32 devices in a mesh: dp: 4 (over z), row: 4 (over x, core), col: 2 (over y).
Axes of the slice: x: 2, y: 2, z: 4, core: 2. Of those that a mesh axis runs over, the one named last changes fastest.
Arguments:
- inputs: float32 [768, 16384], P('row', ('dp', 'col')), may hold values from -6 to 6
- teacher: float32 [768, 16384], P('row', ('dp', 'col')), may hold values from -6 to 6
- lengths: int32 [8], P('dp'), may hold values from 1024 to 2048, as said below
- omega: bfloat16 [12, 64, 256], P('col'), may hold values from -4 to 4
- w_query: float32 [768, 768], P('row', 'col'), may hold values from -0.21875 to 0.21875
- b_query: float32 [768], P('col'), may hold values from -1.5 to 1.5
- w_key: float32 [768, 768], P('row', 'col'), may hold values from -0.21875 to 0.21875
- b_key: float32 [768], P('col'), may hold values from -1.5 to 1.5
- w_value: float32 [768, 768], P('row', 'col'), may hold values from -0.21875 to 0.21875
- b_value: float32 [768], P('col'), may hold values from -1.5 to 1.5
- w_out: float32 [768, 768], P('row', 'col'), may hold values from -0.875 to 0.875
- b_out: float32 [768], P('row'), may hold values from -1.5 to 1.5
- norm1_gain: float32 [768], P('row'), may hold values from 0.5 to 1.5
- norm1_bias: float32 [768], P('row'), may hold values from -1.5 to 1.5
- w_up: float32 [768, 3072], P('row', 'col'), may hold values from -0.21875 to 0.21875
- up_bias: float32 [3072], P('col'), may hold values from -1.5 to 1.5
- w_down: float32 [768, 3072], P('row', 'col'), may hold values from -0.109375 to 0.109375
- b_down: float32 [768], P('row'), may hold values from -1.5 to 1.5
- norm2_gain: float32 [768], P('row'), may hold values from 0.5 to 1.5
- norm2_bias: float32 [768], P('row'), may hold values from -1.5 to 1.5
Outputs:
- output: float32 [768, 16384], P('row', ('dp', 'col'))
- loss: float32 [], replicated
- grad_input: float32 [768, 16384], P('row', ('dp', 'col'))
- grad_w_query: float32 [768, 768], P('row', 'col')
- grad_b_query: float32 [768], P('col')
- grad_w_key: float32 [768, 768], P('row', 'col')
- grad_b_key: float32 [768], P('col')
- grad_w_value: float32 [768, 768], P('row', 'col')
- grad_b_value: float32 [768], P('col')
- grad_w_out: float32 [768, 768], P('row', 'col')
- grad_b_out: float32 [768], P('row')
- grad_norm1_gain: float32 [768], P('row')
- grad_norm1_bias: float32 [768], P('row')
- grad_w_up: float32 [768, 3072], P('row', 'col')
- grad_b_up: float32 [3072], P('col')
- grad_w_down: float32 [768, 3072], P('row', 'col')
- grad_b_down: float32 [768], P('row')
- grad_norm2_gain: float32 [768], P('row')
- grad_norm2_bias: float32 [768], P('row')
The draws below stay inside these ranges and needn't reach their ends.
Inputs may be any that keep to these rules, and one draw needn't show every extreme that they name: `lengths`: every draw has a sequence with all 2048 tokens valid and one with 1024.
All inputs are finite; a program needn't handle non-finite values.
Results may differ from the reference program's by a relative error of at most 0.025.
Values may be sent and summed in bfloat16 or wider, within the bound.
No kernel may reach another device: no remote copies, remote signals or barrier semaphores. Data moves between devices by JAX's collectives and lax.ppermute only.
A program may use at most 256 MiB of HBM per device.

```python
import jax
import jax.numpy as jnp
from jax import lax

D = 768
HEADS = 12
FF = 3072
FEATS = 256
SEQ_LEN = 2048
LOSS_SCALE = 16777216
HEAD_DIM = 64
SEQS = 8
TOKENS = 16384


def draw_lengths(key, part):
    first_key, second_key = jax.random.split(jax.random.fold_in(key, 7))
    values = jax.random.randint(first_key, (SEQS,), SEQ_LEN // 2, SEQ_LEN + 1)
    full_at = jax.random.randint(second_key, (), 0, SEQS)
    indices = jnp.arange(SEQS, dtype=jnp.int32)
    values = jnp.where(indices == full_at, SEQ_LEN, values)
    values = jnp.where(indices == (full_at + 1) % SEQS, SEQ_LEN // 2, values)
    return values.astype(jnp.int32)


def level_of(stream_key, shape, pieces, least, largest):
    level = 1.0
    for position, shards_of in pieces:
        steps = jax.random.uniform(jax.random.fold_in(jax.random.fold_in(stream_key, 6), position), (shards_of,), jnp.float32, least / len(pieces), largest / len(pieces))
        level = level * jnp.repeat(jnp.exp(steps), shape[position] // shards_of).reshape((-1,) + (1,) * (len(shape) - 1 - position))
    return level


def centred(rng, shape, deviation, limit, pieces=(), held_as=jnp.bfloat16):
    values = jax.random.normal(rng, shape, jnp.float32) * deviation
    if len(pieces) > 0:
        values = level_of(rng, shape, pieces, -0.22, 0.18) * values
    return jnp.clip(values, min=-limit, max=limit).astype(held_as)


def setup_inputs(seed: int = 0) -> dict:
    arg_keys = jax.random.split(jax.random.key(seed), 21)
    return {
        "inputs": centred(arg_keys[0], (D, TOKENS), 1.0, 6.0, ((0, 4), (1, 8)), jnp.float32),
        "teacher": centred(arg_keys[1], (D, TOKENS), 1.0, 6.0, ((0, 4), (1, 8)), jnp.float32),
        "lengths": draw_lengths(jax.random.fold_in(arg_keys[20], 71), 0),
        "omega": centred(arg_keys[3], (HEADS, HEAD_DIM, FEATS), 1.0, 4.0, ((0, 2),)),
        "w_query": centred(arg_keys[4], (D, D), D ** -0.5, 0.21875, ((0, 4), (1, 2)), jnp.float32),
        "b_query": centred(arg_keys[5], (D,), 0.3, 1.5, ((0, 2),), jnp.float32),
        "w_key": centred(arg_keys[6], (D, D), D ** -0.5, 0.21875, ((0, 4), (1, 2)), jnp.float32),
        "b_key": centred(arg_keys[7], (D,), 0.3, 1.5, ((0, 2),), jnp.float32),
        "w_value": centred(arg_keys[8], (D, D), D ** -0.5, 0.21875, ((0, 4), (1, 2)), jnp.float32),
        "b_value": centred(arg_keys[9], (D,), 0.3, 1.5, ((0, 2),), jnp.float32),
        "w_out": centred(arg_keys[10], (D, D), (D // 16) ** -0.5, 0.875, ((0, 4), (1, 2)), jnp.float32),
        "b_out": centred(arg_keys[11], (D,), 0.3, 1.5, ((0, 4),), jnp.float32),
        "norm1_gain": jnp.clip(1.0 + 0.1 * jax.random.normal(arg_keys[12], (D,), jnp.float32), 0.5, 1.5),
        "norm1_bias": centred(arg_keys[13], (D,), 0.3, 1.5, ((0, 4),), jnp.float32),
        "w_up": centred(arg_keys[14], (D, FF), D ** -0.5, 0.21875, ((0, 4), (1, 2)), jnp.float32),
        "up_bias": centred(arg_keys[15], (FF,), 0.3, 1.5, ((0, 2),), jnp.float32),
        "w_down": centred(arg_keys[16], (D, FF), FF ** -0.5, 0.109375, ((0, 4), (1, 2)), jnp.float32),
        "b_down": centred(arg_keys[17], (D,), 0.3, 1.5, ((0, 4),), jnp.float32),
        "norm2_gain": jnp.clip(1.0 + 0.1 * jax.random.normal(arg_keys[18], (D,), jnp.float32), 0.5, 1.5),
        "norm2_bias": centred(arg_keys[19], (D,), 0.3, 1.5, ((0, 4),), jnp.float32),
    }


stabilizer = 2.0
norm_eps = 1e-12
highest = lax.Precision.HIGHEST

@jax.custom_vjp
def low(v):
    return lax.optimization_barrier(v.astype(jnp.bfloat16)).astype(jnp.float32)

@jax.custom_vjp
def low_back(v):
    return v

def low_keep(v):
    return (low(v), None)

def low_pass(kept, grad):
    return (grad,)

def back_keep(v):
    return (v, None)

def back_low(kept, grad):
    return (low(grad),)
low.defvjp(low_keep, low_pass)
low_back.defvjp(back_keep, back_low)

def layer_norm(summed, gain, shift):
    average = lax.optimization_barrier(jnp.mean(summed, axis=-1, keepdims=True))
    centered = summed - average
    spread = lax.optimization_barrier(jnp.mean(centered * centered, axis=-1, keepdims=True))
    return centered * lax.rsqrt(spread + norm_eps) * gain + shift

def project(lowered, weight, bias):
    return jnp.einsum('bld,de->ble', lowered, low(weight), precision=highest) + bias

def positive_features(projected, omega_full, keeper):
    scaled = projected * HEAD_DIM ** (-0.25)
    exponent = low_back(jnp.einsum('blhd,hdm->blhm', low(scaled), omega_full, precision=highest))
    return keeper * jnp.exp(exponent - 0.5 * lax.optimization_barrier(jnp.sum(scaled * scaled, axis=-1, keepdims=True)) - stabilizer)

def forward(states, params, omega_full, keeper, target, count):
    w_query, b_query, w_key, b_key, w_value, b_value, w_out, b_out, norm1_gain, norm1_bias, w_up, up_bias, w_down, b_down, norm2_gain, norm2_bias = params
    blocks, length, width = states.shape
    states_low = low(states)
    query = low_back(project(states_low, w_query, b_query)).reshape(blocks, length, HEADS, HEAD_DIM)
    key_states = low_back(project(states_low, w_key, b_key)).reshape(blocks, length, HEADS, HEAD_DIM)
    value_states = low_back(project(states_low, w_value, b_value)).reshape(blocks, length, HEADS, HEAD_DIM)
    feat_query = positive_features(query, omega_full, 1.0)
    feat_key = positive_features(key_states, omega_full, keeper[:, :, None, None])
    query_low = low(feat_query)
    key_low = low(feat_key)
    key_value = low(low_back(jnp.einsum('blhm,blhd->bhmd', key_low, low(value_states), precision=highest)))
    key_total = low(lax.optimization_barrier(jnp.sum(feat_key, axis=1)))
    numerator = low_back(jnp.einsum('blhm,bhmd->blhd', query_low, key_value, precision=highest))
    denominator = low_back(jnp.einsum('blhm,bhm->blh', query_low, key_total, precision=highest))
    attended = (numerator / denominator[..., None]).reshape(blocks, length, width)
    out_branch = low_back(project(low(attended), jnp.transpose(w_out), b_out))
    normed = layer_norm(states + out_branch, norm1_gain, norm1_bias)
    expanded_states = low_back(project(low(normed), w_up, up_bias))
    hidden = jax.nn.gelu(expanded_states, approximate=False)
    down_branch = low_back(project(low(hidden), jnp.transpose(w_down), b_down))
    output = layer_norm(normed + down_branch, norm2_gain, norm2_bias)
    differ = output - target
    partial_loss = jnp.sum(keeper[:, :, None] * differ * differ) / (count * D)
    return (partial_loss, output)

def reference(inputs, teacher, lengths, omega, w_query, b_query, w_key, b_key, w_value, b_value, w_out, b_out, norm1_gain, norm1_bias, w_up, up_bias, w_down, b_down, norm2_gain, norm2_bias):
    count = jnp.sum(lengths).astype(jnp.float32)
    params = (w_query, b_query, w_key, b_key, w_value, b_value, w_out, b_out, norm1_gain, norm1_bias, w_up, up_bias, w_down, b_down, norm2_gain, norm2_bias)
    omega_full = omega.astype(jnp.float32)
    pairs = SEQS // 2
    input_blocks = jnp.transpose(inputs).reshape(pairs, 2, SEQ_LEN, D)
    target_blocks = jnp.transpose(teacher).reshape(pairs, 2, SEQ_LEN, D)
    length_blocks = lengths.reshape(pairs, 2)
    positions = jnp.arange(SEQ_LEN, dtype=jnp.int32)

    def one_block(totals, item):
        block_inputs, block_target, block_lengths = item
        keeper = (positions[None, :] < block_lengths[:, None]).astype(jnp.float32)

        def loss_of(values, weights):
            return forward(values, weights, omega_full, keeper, block_target, count)
        partial_loss, pull_back, output = jax.vjp(loss_of, block_inputs, params, has_aux=True)
        input_grad, weight_grads = pull_back(jnp.float32(LOSS_SCALE))
        totals = jax.tree.map(jnp.add, totals, (partial_loss, weight_grads))
        return (totals, (output, input_grad))
    starting = (jnp.float32(0.0), jax.tree.map(jnp.zeros_like, params))
    (loss, grads), (outputs, input_grads) = lax.scan(one_block, starting, (input_blocks, target_blocks, length_blocks))
    grad_w_query, grad_b_query, grad_w_key, grad_b_key, grad_w_value, grad_b_value, grad_w_out, grad_b_out, grad_norm1_gain, grad_norm1_bias, grad_w_up, grad_b_up, grad_w_down, grad_b_down, grad_norm2_gain, grad_norm2_bias = grads
    return (jnp.transpose(outputs.reshape(TOKENS, D)), loss, jnp.transpose(input_grads.reshape(TOKENS, D)), grad_w_query, grad_b_query, grad_w_key, grad_b_key, grad_w_value, grad_b_value, grad_w_out, grad_b_out, grad_norm1_gain, grad_norm1_bias, grad_w_up, grad_b_up, grad_w_down, grad_b_down, grad_norm2_gain, grad_norm2_bias)
```

```python
import jax
import jax.numpy as jnp
from jax import lax
from jax.sharding import PartitionSpec as P

LOSS_SCALE = 16777216

stabilizer = 2.0
norm_eps = 1e-12
root_half = 0.7071067811865476
inv_root_two_pi = 0.3989422804014327
f32 = jnp.float32
bf16 = jnp.bfloat16


def swap(value, axis, mask):
    size = lax.axis_size(axis)
    return lax.ppermute(value, axis, [(s, s ^ mask) for s in range(size)])


def dot(a, b, dims):
    return lax.dot_general(a, b, (dims, ((), ())), preferred_element_type=f32)


def gather_plane(own, share):
    cut = own.shape[0] * share // 4
    by_core = swap(own, "row", 1)
    by_x = swap(own, "row", 2)
    by_y = swap(own, "col", 1)
    far_x = swap(by_y[:cut], "row", 2)
    far_y = swap(by_x[cut:], "col", 1)
    far = jnp.concatenate((far_x, far_y), axis=0)
    x_core = swap(by_x, "row", 1)
    y_core = swap(by_y, "row", 1)
    far_core = swap(far, "row", 1)
    return ((own, by_core, by_x, x_core), (by_y, y_core, far, far_core))


def rows_of(blocks):
    return jnp.concatenate(blocks, axis=0)


def reduce_plane(mine, theirs, share):
    got = swap(jnp.stack(theirs).astype(bf16), "row", 1)
    near = mine[0] + got[0]
    far = mine[1] + got[1]
    cut = near.shape[0] * share // 4
    far_low = far[:, 1].astype(bf16)
    from_x = swap(far_low[:cut], "row", 2)
    from_y = swap(far_low[cut:], "col", 1)
    to_x = far[:, 0]
    to_y = near[:, 1]
    to_y = jnp.concatenate((to_y[:cut] + from_x, to_y[cut:]), axis=0).astype(bf16)
    to_x = jnp.concatenate((to_x[:cut], to_x[cut:] + from_y), axis=0).astype(bf16)
    from_x = swap(to_x, "row", 2)
    from_y = swap(to_y, "col", 1)
    return near[:, 0] + from_x + from_y


def reduce_dp(value):
    parts = lax.axis_size("dp")
    if parts != 4:
        return lax.psum(value.astype(bf16), "dp").astype(f32)
    index = lax.axis_index("dp")
    n = value.shape[0] // parts
    low = value.astype(bf16).reshape(parts, n, value.shape[1])
    total = lax.dynamic_index_in_dim(value.reshape(low.shape), index, 0, False)
    for mask in (1, 2, 3):
        total = total + swap(lax.dynamic_index_in_dim(low, index ^ mask, 0, False), "dp", mask)
    total = total.astype(bf16)
    out = jnp.zeros(low.shape, bf16)
    out = lax.dynamic_update_index_in_dim(out, total, index, 0)
    for mask in (1, 2, 3):
        out = lax.dynamic_update_index_in_dim(out, swap(total, "dp", mask), index ^ mask, 0)
    return out.reshape(value.shape).astype(f32)


def reduce_small(value, axes):
    for axis in axes:
        step = 1
        while step < lax.axis_size(axis):
            value = value + swap(value, axis, step)
            step *= 2
    return value


def to_positions(shard, row_parts):
    row = lax.axis_index("row")
    n = shard.shape[1] // row_parts
    blocks = []
    for j in range(row_parts):
        block = lax.dynamic_slice_in_dim(shard, (row ^ j) * n, n, 1).astype(bf16)
        blocks.append(swap(block, "row", j) if j else block)
    return jnp.concatenate(blocks, axis=0)


def to_features(value, row_parts):
    row = lax.axis_index("row")
    k = value.shape[0] // row_parts
    n = value.shape[1]
    out = jnp.zeros((k, n * row_parts), f32)
    for j in range(row_parts):
        block = value[j * k : (j + 1) * k]
        if j:
            block = swap(block.astype(bf16), "row", j).astype(f32)
        out = lax.dynamic_update_slice_in_dim(out, block, (row ^ j) * n, 1)
    return out


def row_vectors(packed):
    return jnp.concatenate([packed] + [swap(packed, "row", j) for j in (1, 2, 3)], axis=1)


def norm_forward(summed, gain, shift):
    average = jnp.mean(summed, axis=0, keepdims=True)
    centered = summed - average
    spread = jnp.mean(centered * centered, axis=0, keepdims=True)
    scaling = lax.rsqrt(spread + norm_eps)
    normal = centered * scaling
    return normal * gain[:, None] + shift[:, None], normal, scaling


def norm_backward(grad_out, normal, scaling, gain):
    scaled_grad = grad_out * gain[:, None]
    first = jnp.mean(scaled_grad, axis=0, keepdims=True)
    second = jnp.mean(scaled_grad * normal, axis=0, keepdims=True)
    grad_in = scaling * (scaled_grad - first - normal * second)
    return grad_in, jnp.sum(grad_out * normal, axis=1), jnp.sum(grad_out, axis=1)


def weight_grad(left, right, row_parts, share):
    n = left.shape[0] // row_parts
    cols, k, _ = right.shape
    flat = right.reshape(cols * k, -1)
    parts = [
        dot(left[j * n : (j + 1) * n], flat, ((1,), (1,))).reshape(n, cols, k)
        for j in range(row_parts)
    ]
    return reduce_dp(reduce_plane(parts[0::2], parts[1::2], share))


def shards(
    inputs, teacher, lengths, omega,
    w_query, b_query, w_key, b_key, w_value, b_value, w_out, b_out,
    norm1_gain, norm1_bias, w_up, up_bias, w_down, b_down, norm2_gain, norm2_bias,
):
    row_parts = lax.axis_size("row")
    cols = lax.axis_size("col")
    feat_local, seq_length = inputs.shape
    width = feat_local * row_parts
    head_local, head_width, feats = omega.shape
    heads = head_local * cols
    tokens = seq_length // row_parts
    head_block = head_local * head_width
    factor = head_width ** (-0.25)
    row = lax.axis_index("row")
    col = lax.axis_index("col")
    share = 1

    own_triple = jnp.concatenate((w_query, w_key, w_value), axis=1).astype(bf16)
    states = to_positions(inputs, row_parts)
    triple_blocks = gather_plane(own_triple, share)
    omega_all = jnp.concatenate((omega, swap(omega, "col", 1)), axis=0)
    col_pack = jnp.concatenate((b_query, b_key, b_value, up_bias))
    col_other = swap(col_pack, "col", 1)
    row_pack = row_vectors(jnp.stack((b_out, norm1_gain, norm1_bias, b_down, norm2_gain, norm2_bias)))
    b_out_all, gain1, shift1, b_down_all, gain2, shift2 = [row_pack[m] for m in range(6)]
    triple_bias = jnp.stack((col_pack[: 3 * head_block], col_other[: 3 * head_block]))
    up_bias_all = jnp.concatenate((col_pack[3 * head_block :], col_other[3 * head_block :]))
    out_blocks = gather_plane(w_out.astype(bf16), share)
    up_blocks = gather_plane(w_up.astype(bf16), share)
    down_blocks = gather_plane(w_down.astype(bf16), share)
    target = to_positions(teacher, row_parts)

    count = reduce_small(jnp.sum(lengths).astype(f32).reshape(1, 1) + jnp.zeros((8, 128), f32), ("dp",))[0, 0]
    length = lax.dynamic_index_in_dim(lengths, col, 0, False)
    keep = ((row * tokens + jnp.arange(tokens, dtype=jnp.int32)) < length).astype(f32)

    triple_weight = [rows_of(b) for b in triple_blocks]
    out_weight = jnp.concatenate([rows_of(b) for b in out_blocks], axis=1)
    up_weight = jnp.concatenate([rows_of(b) for b in up_blocks], axis=1)
    down_weight = jnp.concatenate([rows_of(b) for b in down_blocks], axis=1)

    triple = jnp.stack([dot(w, states, ((0,), (0,))) for w in triple_weight]) + triple_bias[:, :, None]
    triple = triple.reshape(cols, 3, head_local, head_width, tokens)
    split = [triple[:, p].reshape(heads, head_width, tokens) for p in range(3)]
    query_scaled = split[0] * factor
    key_scaled = split[1] * factor
    value_low = split[2].astype(bf16)

    def positive(scaled, keeper):
        exponent = jnp.einsum("hdt,hdm->hmt", scaled.astype(bf16), omega_all, preferred_element_type=f32)
        return keeper * jnp.exp(exponent - 0.5 * jnp.sum(scaled * scaled, axis=1, keepdims=True) - stabilizer)

    feat_query = positive(query_scaled, 1.0)
    feat_key = positive(key_scaled, keep)
    query_low = feat_query.astype(bf16)
    key_low = feat_key.astype(bf16)

    def over_row(kv, total):
        packed = jnp.concatenate((kv.reshape(heads * head_width, feats), total, jnp.zeros((4, feats), f32)))
        packed = packed + swap(packed.astype(bf16), "row", 1)
        packed = packed + swap(packed.astype(bf16), "row", 2)
        return packed[: heads * head_width].reshape(kv.shape), packed[heads * head_width : heads * (head_width + 1)]

    kv, key_total = over_row(
        jnp.einsum("hmt,hdt->hdm", key_low, value_low, preferred_element_type=f32), jnp.sum(feat_key, axis=2)
    )
    kv_low = kv.astype(bf16)
    total_low = key_total.astype(bf16)
    numerator = jnp.einsum("hdm,hmt->hdt", kv_low, query_low, preferred_element_type=f32)
    denominator = jnp.einsum("hm,hmt->ht", total_low, query_low, preferred_element_type=f32)
    inverse = 1.0 / denominator
    attended = numerator * inverse[:, None, :]
    attended_low = attended.astype(bf16).reshape(width, tokens)

    summed = states.astype(f32) + dot(out_weight, attended_low, ((1,), (0,))) + b_out_all[:, None]
    normed, normal1, scale1 = norm_forward(summed, gain1, shift1)
    normed_low = normed.astype(bf16)
    up = dot(up_weight, normed_low, ((0,), (0,))) + up_bias_all[:, None]
    gate = 0.5 * (1.0 + lax.erf(up * root_half))
    hidden_low = (up * gate).astype(bf16)
    slope = gate + up * inv_root_two_pi * jnp.exp(-0.5 * up * up)
    summed = normed + dot(down_weight, hidden_low, ((1,), (0,))) + b_down_all[:, None]
    output, normal2, scale2 = norm_forward(summed, gain2, shift2)
    out_result = to_features(output, row_parts)

    differ = (output - target.astype(f32)) * keep
    loss_part = jnp.sum(differ * differ)
    grad_output = (2.0 * LOSS_SCALE / (count * width)) * differ
    grad2, gain2_grad, shift2_grad = norm_backward(grad_output, normal2, scale2, gain2)
    grad2_low = grad2.astype(bf16)

    ff = up_weight.shape[1]
    w_down_grad = weight_grad(grad2_low, hidden_low.reshape(cols, ff // cols, tokens), row_parts, share)
    b_down_grad = jnp.sum(grad2_low.astype(f32), axis=1)
    grad_up_low = (dot(down_weight, grad2_low, ((0,), (0,))) * slope).astype(bf16)
    w_up_grad = weight_grad(normed_low, grad_up_low.reshape(cols, ff // cols, tokens), row_parts, share)
    b_up_grad = jnp.sum(grad_up_low.astype(f32), axis=1)
    grad_normed = grad2 + dot(up_weight, grad_up_low, ((1,), (0,)))
    grad1, gain1_grad, shift1_grad = norm_backward(grad_normed, normal1, scale1, gain1)
    grad1_low = grad1.astype(bf16)

    w_out_grad = weight_grad(grad1_low, attended_low.reshape(cols, head_block, tokens), row_parts, share)
    b_out_grad = jnp.sum(grad1_low.astype(f32), axis=1)
    grad_att = dot(out_weight, grad1_low, ((0,), (0,))).reshape(heads, head_width, tokens)
    grad_num = (grad_att * inverse[:, None, :]).astype(bf16)
    grad_den = (-jnp.sum(grad_att * attended, axis=1) * inverse).astype(bf16)
    grad_kv, grad_total = over_row(
        jnp.einsum("hmt,hdt->hdm", query_low, grad_num, preferred_element_type=f32),
        jnp.einsum("hmt,ht->hm", query_low, grad_den, preferred_element_type=f32),
    )
    grad_kv_low = grad_kv.astype(bf16)

    def feature_back(grad_feat, feat, scaled):
        grad_expo = grad_feat * feat
        back = jnp.einsum("hmt,hdm->hdt", grad_expo.astype(bf16), omega_all, preferred_element_type=f32)
        back = back - jnp.sum(grad_expo, axis=1, keepdims=True) * scaled
        return (factor * back).astype(bf16)

    grad_feat_query = jnp.einsum("hdt,hdm->hmt", grad_num, kv_low, preferred_element_type=f32)
    grad_feat_query = grad_feat_query + grad_den.astype(f32)[:, None, :] * total_low.astype(f32)[:, :, None]
    grad_query = feature_back(grad_feat_query, feat_query, query_scaled)
    grad_feat_key = jnp.einsum("hdt,hdm->hmt", value_low, grad_kv_low, preferred_element_type=f32)
    grad_feat_key = grad_feat_key + grad_total[:, :, None]
    grad_key = feature_back(grad_feat_key, feat_key, key_scaled)
    grad_value = jnp.einsum("hmt,hdm->hdt", key_low, grad_kv_low, preferred_element_type=f32) if False else jnp.einsum(
        "hdm,hmt->hdt", grad_kv_low, key_low, preferred_element_type=f32
    ).astype(bf16)
    grad_triple = jnp.stack(
        [g.reshape(cols, head_block, tokens) for g in (grad_query, grad_key, grad_value)], axis=1
    ).reshape(cols, 3 * head_block, tokens)
    w_triple_grad = weight_grad(states, grad_triple, row_parts, share)
    b_triple_grad = jnp.sum(grad_triple.astype(f32), axis=2)
    grad_input = grad1
    for i in range(cols):
        grad_input = grad_input + dot(triple_weight[i], grad_triple[i], ((1,), (0,)))
    grad_input = to_features(grad_input, row_parts)

    row_small = jnp.stack(
        (b_out_grad, gain1_grad, shift1_grad, b_down_grad, gain2_grad, shift2_grad)
    ).reshape(6, row_parts, feat_local)
    row_small = jnp.transpose(row_small, (1, 0, 2)).reshape(row_parts, 6 * feat_local)
    col_small = jnp.concatenate((b_triple_grad, b_up_grad.reshape(cols, ff // cols)), axis=1)
    got = row_small[0]
    for j in (1, 2, 3):
        got = got + swap(row_small[j], "row", j)
    got_col = col_small[0] + swap(col_small[1], "col", 1)
    got = got + swap(got, "col", 1)
    got_col = reduce_small(got_col, ("row",))
    loss_all = reduce_small(jnp.broadcast_to(loss_part.reshape(1), (128,)), ("row", "col"))
    small = reduce_small(jnp.concatenate((got, got_col, loss_all)), ("dp",))
    row_part = small[: 6 * feat_local].reshape(6, feat_local)
    col_part = small[6 * feat_local : 6 * feat_local + col_small.shape[1]]
    loss = small[-1] / (count * width)

    return (
        out_result,
        loss,
        grad_input,
        w_triple_grad[:, :head_block],
        col_part[:head_block],
        w_triple_grad[:, head_block : 2 * head_block],
        col_part[head_block : 2 * head_block],
        w_triple_grad[:, 2 * head_block :],
        col_part[2 * head_block : 3 * head_block],
        w_out_grad,
        row_part[0],
        row_part[1],
        row_part[2],
        w_up_grad,
        col_part[3 * head_block :],
        w_down_grad,
        row_part[3],
        row_part[4],
        row_part[5],
    )


def solution(mesh):
    both = P("row", ("dp", "col"))
    in_specs = (
        both, both, P("dp"), P("col", None, None),
        P("row", "col"), P("col"), P("row", "col"), P("col"), P("row", "col"), P("col"),
        P("row", "col"), P("row"), P("row"), P("row"),
        P("row", "col"), P("col"), P("row", "col"), P("row"), P("row"), P("row"),
    )
    out_specs = (
        both, P(), both,
        P("row", "col"), P("col"), P("row", "col"), P("col"), P("row", "col"), P("col"),
        P("row", "col"), P("row"), P("row"), P("row"),
        P("row", "col"), P("col"), P("row", "col"), P("row"), P("row"), P("row"),
    )
    return jax.shard_map(shards, mesh=mesh, in_specs=in_specs, out_specs=out_specs, check_vma=False)
```

```python
import jax
import jax.numpy as jnp
from jax import lax
from jax.sharding import PartitionSpec as P

LOSS_SCALE = 16777216

stabilizer = 2.0
norm_eps = 1e-12
root_half = 0.7071067811865476
inv_root_two_pi = 0.3989422804014327
f32 = jnp.float32
bf16 = jnp.bfloat16


def swap(value, axis, mask):
    size = lax.axis_size(axis)
    return lax.ppermute(value, axis, [(s, s ^ mask) for s in range(size)])


def dot(a, b, dims):
    return lax.dot_general(a, b, (dims, ((), ())), preferred_element_type=f32)


def gather_plane(own, share):
    cut = own.shape[0] * share // 4
    by_x = swap(own, "row", 2)
    by_y = swap(own, "col", 1)
    far = swap(by_x[cut:], "col", 1)
    if cut:
        far = jnp.concatenate((swap(by_y[:cut], "row", 2), far), axis=0)
    near = jnp.concatenate((own, by_x), axis=0)
    other = jnp.concatenate((by_y, far), axis=0)
    return (
        jnp.concatenate((near, swap(near, "row", 1)), axis=0),
        jnp.concatenate((other, swap(other, "row", 1)), axis=0),
    )


def reduce_plane(mine, theirs, share):
    got = swap(theirs.astype(bf16), "row", 1)
    total = mine + got
    near = total[0]
    far = total[1]
    cut = near.shape[0] * share // 4
    far_low = far[:, 1].astype(bf16)
    from_x = swap(far_low[:cut], "row", 2)
    from_y = swap(far_low[cut:], "col", 1)
    to_x = far[:, 0]
    to_y = near[:, 1]
    to_y = jnp.concatenate((to_y[:cut] + from_x, to_y[cut:]), axis=0).astype(bf16)
    to_x = jnp.concatenate((to_x[:cut], to_x[cut:] + from_y), axis=0).astype(bf16)
    from_x = swap(to_x, "row", 2)
    from_y = swap(to_y, "col", 1)
    return near[:, 0] + from_x + from_y


def reduce_dp(value):
    parts = lax.axis_size("dp")
    if parts != 4:
        return lax.psum(value.astype(bf16), "dp").astype(f32)
    index = lax.axis_index("dp")
    middle = jnp.logical_or(index == 1, index == 2)
    low = value.astype(bf16)
    value = value + lax.ppermute(low, "dp", [(0, 1), (3, 2)])
    other = lax.ppermute(value.astype(bf16), "dp", [(1, 2), (2, 1)])
    low = (value + other).astype(bf16)
    back = lax.ppermute(low, "dp", [(1, 0), (2, 3)])
    return jnp.where(middle, low, back).astype(f32)


def reduce_small(value, axes):
    for axis in axes:
        step = 1
        while step < lax.axis_size(axis):
            value = value + swap(value, axis, step)
            step *= 2
    return value


ORDER = (0, 2, 1, 3)


def to_positions(shard, row_parts):
    row = lax.axis_index("row")
    k = shard.shape[0]
    n = shard.shape[1] // row_parts
    blocks = [lax.dynamic_slice_in_dim(shard, (row ^ j) * n, n, 1).astype(bf16) for j in range(4)]
    got = swap(jnp.concatenate((blocks[1], blocks[3]), axis=0), "row", 1)
    here = jnp.concatenate((blocks[0], got[:k]), axis=0)
    there = swap(jnp.concatenate((blocks[2], got[k:]), axis=0), "row", 2)
    return jnp.concatenate((here[:k], there[:k], here[k:], there[k:]), axis=0)


def to_features(value, row_parts):
    row = lax.axis_index("row")
    k = value.shape[0] // row_parts
    n = value.shape[1]
    low = value.astype(bf16)
    got = swap(jnp.concatenate((low[k : 2 * k], low[3 * k :]), axis=0), "row", 2)
    core = swap(jnp.concatenate((low[2 * k : 3 * k], got[k:]), axis=0), "row", 1)
    out = jnp.zeros((k, n * row_parts), f32)
    for j, block in ((0, value[:k]), (2, got[:k]), (1, core[:k]), (3, core[k:])):
        out = lax.dynamic_update_slice_in_dim(out, block.astype(f32), (row ^ j) * n, 1)
    return out


def row_vectors(packed):
    got = jnp.concatenate((packed, swap(packed, "row", 2)), axis=1)
    return jnp.concatenate((got, swap(got, "row", 1)), axis=1)


def norm_forward(summed, gain, shift):
    average = jnp.mean(summed, axis=0, keepdims=True)
    centered = summed - average
    spread = jnp.mean(centered * centered, axis=0, keepdims=True)
    scaling = lax.rsqrt(spread + norm_eps)
    normal = centered * scaling
    return normal * gain[:, None] + shift[:, None], normal, scaling


def norm_backward(grad_out, normal, scaling, gain):
    scaled_grad = grad_out * gain[:, None]
    first = jnp.mean(scaled_grad, axis=0, keepdims=True)
    second = jnp.mean(scaled_grad * normal, axis=0, keepdims=True)
    grad_in = scaling * (scaled_grad - first - normal * second)
    return grad_in, jnp.sum(grad_out * normal, axis=1), jnp.sum(grad_out, axis=1)


def partial_grad(left, right, row_parts):
    n = left.shape[0] // row_parts
    cols, k, tokens = right.shape
    flat = right.reshape(cols * k, tokens)
    theirs = dot(left[2 * n :], flat, ((1,), (1,))).reshape(2, n, cols, k)
    mine = dot(left[: 2 * n], flat, ((1,), (1,))).reshape(2, n, cols, k)
    return mine, theirs


def finish_grad(parts, share):
    return reduce_dp(reduce_plane(*parts, share))


def shards(
    inputs, teacher, lengths, omega,
    w_query, b_query, w_key, b_key, w_value, b_value, w_out, b_out,
    norm1_gain, norm1_bias, w_up, up_bias, w_down, b_down, norm2_gain, norm2_bias,
):
    row_parts = lax.axis_size("row")
    cols = lax.axis_size("col")
    feat_local, seq_length = inputs.shape
    width = feat_local * row_parts
    head_local, head_width, feats = omega.shape
    heads = head_local * cols
    tokens = seq_length // row_parts
    head_block = head_local * head_width
    factor = head_width ** (-0.25)
    row = lax.axis_index("row")
    col = lax.axis_index("col")
    share = 1

    own_triple = jnp.concatenate((w_query, w_key, w_value), axis=1).astype(bf16)
    states = to_positions(inputs, row_parts)
    triple_weight = gather_plane(own_triple, 0)
    omega_all = jnp.concatenate((omega, swap(omega, "col", 1)), axis=0)
    col_pack = jnp.concatenate((b_query, b_key, b_value, up_bias))
    col_other = swap(col_pack, "col", 1)
    row_pack = row_vectors(jnp.stack((b_out, norm1_gain, norm1_bias, b_down, norm2_gain, norm2_bias)))
    b_out_all, gain1, shift1, b_down_all, gain2, shift2 = [row_pack[m] for m in range(6)]
    triple_bias = jnp.stack((col_pack[: 3 * head_block], col_other[: 3 * head_block]))
    up_bias_all = jnp.concatenate((col_pack[3 * head_block :], col_other[3 * head_block :]))
    rest = gather_plane(jnp.concatenate((w_out, w_up, w_down), axis=1).astype(bf16), share)
    target = to_positions(teacher, row_parts)

    count = reduce_small(jnp.sum(lengths).astype(f32).reshape(1, 1) + jnp.zeros((8, 128), f32), ("dp",))[0, 0]
    length = lax.dynamic_index_in_dim(lengths, col, 0, False)
    keep = ((row * tokens + jnp.arange(tokens, dtype=jnp.int32)) < length).astype(f32)

    hid_local = w_up.shape[1]
    out_weight = jnp.concatenate([w[:, :head_block] for w in rest], axis=1)
    up_weight = jnp.concatenate([w[:, head_block : head_block + hid_local] for w in rest], axis=1)
    down_weight = jnp.concatenate([w[:, head_block + hid_local :] for w in rest], axis=1)

    triple = jnp.stack([dot(w, states, ((0,), (0,))) for w in triple_weight]) + triple_bias[:, :, None]
    triple = triple.reshape(cols, 3, head_local, head_width, tokens)
    split = [triple[:, p].reshape(heads, head_width, tokens) for p in range(3)]
    query_scaled = split[0] * factor
    key_scaled = split[1] * factor
    value_low = split[2].astype(bf16)

    def positive(scaled, keeper):
        exponent = jnp.einsum("hdt,hdm->hmt", scaled.astype(bf16), omega_all, preferred_element_type=f32)
        return keeper * jnp.exp(exponent - 0.5 * jnp.sum(scaled * scaled, axis=1, keepdims=True) - stabilizer)

    feat_query = positive(query_scaled, 1.0)
    feat_key = positive(key_scaled, keep)
    query_low = feat_query.astype(bf16)
    key_low = feat_key.astype(bf16)

    def over_row(kv, total):
        packed = jnp.concatenate((kv.reshape(heads * head_width, feats), total, jnp.zeros((4, feats), f32)))
        packed = packed + swap(packed.astype(bf16), "row", 1)
        packed = packed + swap(packed.astype(bf16), "row", 2)
        return packed[: heads * head_width].reshape(kv.shape), packed[heads * head_width : heads * (head_width + 1)]

    kv, key_total = over_row(
        jnp.einsum("hmt,hdt->hdm", key_low, value_low, preferred_element_type=f32), jnp.sum(feat_key, axis=2)
    )
    kv_low = kv.astype(bf16)
    total_low = key_total.astype(bf16)
    numerator = jnp.einsum("hdm,hmt->hdt", kv_low, query_low, preferred_element_type=f32)
    denominator = jnp.einsum("hm,hmt->ht", total_low, query_low, preferred_element_type=f32)
    inverse = 1.0 / denominator
    attended = numerator * inverse[:, None, :]
    attended_low = attended.astype(bf16).reshape(width, tokens)

    summed = states.astype(f32) + dot(out_weight, attended_low, ((1,), (0,))) + b_out_all[:, None]
    normed, normal1, scale1 = norm_forward(summed, gain1, shift1)
    normed_low = normed.astype(bf16)
    up = dot(up_weight, normed_low, ((0,), (0,))) + up_bias_all[:, None]
    gate = 0.5 * (1.0 + lax.erf(up * root_half))
    hidden_low = (up * gate).astype(bf16)
    slope = gate + up * inv_root_two_pi * jnp.exp(-0.5 * up * up)
    summed = normed + dot(down_weight, hidden_low, ((1,), (0,))) + b_down_all[:, None]
    output, normal2, scale2 = norm_forward(summed, gain2, shift2)
    out_result = to_features(output, row_parts)

    differ = (output - target.astype(f32)) * keep
    loss_part = jnp.sum(differ * differ)
    grad_output = (2.0 * LOSS_SCALE / (count * width)) * differ
    grad2, gain2_grad, shift2_grad = norm_backward(grad_output, normal2, scale2, gain2)
    grad2_low = grad2.astype(bf16)

    ff = up_weight.shape[1]
    w_down_grad = finish_grad(partial_grad(grad2_low, hidden_low.reshape(cols, ff // cols, tokens), row_parts), share)
    b_down_grad = jnp.sum(grad2_low.astype(f32), axis=1)
    grad_up_low = (dot(down_weight, grad2_low, ((0,), (0,))) * slope).astype(bf16)
    w_up_grad = finish_grad(partial_grad(normed_low, grad_up_low.reshape(cols, ff // cols, tokens), row_parts), share)
    b_up_grad = jnp.sum(grad_up_low.astype(f32), axis=1)
    grad_normed = grad2 + dot(up_weight, grad_up_low, ((1,), (0,)))
    grad1, gain1_grad, shift1_grad = norm_backward(grad_normed, normal1, scale1, gain1)
    grad1_low = grad1.astype(bf16)

    out_parts = partial_grad(grad1_low, attended_low.reshape(cols, head_block, tokens), row_parts)
    b_out_grad = jnp.sum(grad1_low.astype(f32), axis=1)
    grad_att = dot(out_weight, grad1_low, ((0,), (0,))).reshape(heads, head_width, tokens)
    grad_num = (grad_att * inverse[:, None, :]).astype(bf16)
    grad_den = (-jnp.sum(grad_att * attended, axis=1) * inverse).astype(bf16)
    grad_kv, grad_total = over_row(
        jnp.einsum("hmt,hdt->hdm", query_low, grad_num, preferred_element_type=f32),
        jnp.einsum("hmt,ht->hm", query_low, grad_den, preferred_element_type=f32),
    )
    grad_kv_low = grad_kv.astype(bf16)

    def feature_back(grad_feat, feat, scaled):
        grad_expo = grad_feat * feat
        back = jnp.einsum("hmt,hdm->hdt", grad_expo.astype(bf16), omega_all, preferred_element_type=f32)
        back = back - jnp.sum(grad_expo, axis=1, keepdims=True) * scaled
        return (factor * back).astype(bf16)

    grad_feat_query = jnp.einsum("hdt,hdm->hmt", grad_num, kv_low, preferred_element_type=f32)
    grad_feat_query = grad_feat_query + grad_den.astype(f32)[:, None, :] * total_low.astype(f32)[:, :, None]
    grad_query = feature_back(grad_feat_query, feat_query, query_scaled)
    grad_feat_key = jnp.einsum("hdt,hdm->hmt", value_low, grad_kv_low, preferred_element_type=f32)
    grad_feat_key = grad_feat_key + grad_total[:, :, None]
    grad_key = feature_back(grad_feat_key, feat_key, key_scaled)
    grad_value = jnp.einsum(
        "hdm,hmt->hdt", grad_kv_low, key_low, preferred_element_type=f32
    ).astype(bf16)
    grad_triple = jnp.stack(
        [g.reshape(cols, head_block, tokens) for g in (grad_query, grad_key, grad_value)], axis=1
    ).reshape(cols, 3 * head_block, tokens)
    triple_parts = partial_grad(states, grad_triple, row_parts)
    both = [jnp.concatenate((a, b), axis=3) for a, b in zip(triple_parts, out_parts)]
    both = finish_grad(both, share)
    w_triple_grad = both[:, : 3 * head_block]
    w_out_grad = both[:, 3 * head_block :]
    b_triple_grad = jnp.sum(grad_triple.astype(f32), axis=2)
    grad_input = grad1
    for i in range(cols):
        grad_input = grad_input + dot(triple_weight[i], grad_triple[i], ((1,), (0,)))
    grad_input = to_features(grad_input, row_parts)

    row_small = jnp.stack(
        (b_out_grad, gain1_grad, shift1_grad, b_down_grad, gain2_grad, shift2_grad)
    ).reshape(6, row_parts, feat_local)
    row_small = jnp.transpose(row_small, (1, 0, 2)).reshape(row_parts, 6 * feat_local)
    col_small = jnp.concatenate((b_triple_grad, b_up_grad.reshape(cols, ff // cols)), axis=1)
    got = row_small[:2] + swap(row_small[2:], "row", 1)
    got = got[0] + swap(got[1], "row", 2)
    got_col = col_small[0] + swap(col_small[1], "col", 1)
    got = got + swap(got, "col", 1)
    got_col = reduce_small(got_col, ("row",))
    loss_all = reduce_small(jnp.broadcast_to(loss_part.reshape(1), (128,)), ("row", "col"))
    small = reduce_small(jnp.concatenate((got, got_col, loss_all)), ("dp",))
    row_part = small[: 6 * feat_local].reshape(6, feat_local)
    col_part = small[6 * feat_local : 6 * feat_local + col_small.shape[1]]
    loss = small[-1] / (count * width)

    return (
        out_result,
        loss,
        grad_input,
        w_triple_grad[:, :head_block],
        col_part[:head_block],
        w_triple_grad[:, head_block : 2 * head_block],
        col_part[head_block : 2 * head_block],
        w_triple_grad[:, 2 * head_block :],
        col_part[2 * head_block : 3 * head_block],
        w_out_grad,
        row_part[0],
        row_part[1],
        row_part[2],
        w_up_grad,
        col_part[3 * head_block :],
        w_down_grad,
        row_part[3],
        row_part[4],
        row_part[5],
    )


def solution(mesh):
    both = P("row", ("dp", "col"))
    in_specs = (
        both, both, P("dp"), P("col", None, None),
        P("row", "col"), P("col"), P("row", "col"), P("col"), P("row", "col"), P("col"),
        P("row", "col"), P("row"), P("row"), P("row"),
        P("row", "col"), P("col"), P("row", "col"), P("row"), P("row"), P("row"),
    )
    out_specs = (
        both, P(), both,
        P("row", "col"), P("col"), P("row", "col"), P("col"), P("row", "col"), P("col"),
        P("row", "col"), P("row"), P("row"), P("row"),
        P("row", "col"), P("col"), P("row", "col"), P("row"), P("row"), P("row"),
    )
    return jax.shard_map(shards, mesh=mesh, in_specs=in_specs, out_specs=out_specs, check_vma=False)
```

```python
import jax
import jax.numpy as jnp
from jax import lax
from jax.experimental import pallas as pl
from jax.experimental.pallas import tpu as pltpu
from jax.sharding import PartitionSpec as P

LOSS_SCALE = 16777216
stabilizer = 2.0
norm_eps = 1e-12
root_half = 0.7071067811865476
inv_root_two_pi = 0.3989422804014327
f32 = jnp.float32
bf16 = jnp.bfloat16
PAD = 8


def dot(a, b, dims):
    return lax.dot_general(a, b, (dims, ((), ())), preferred_element_type=f32)


def nn(a, b):
    return dot(a, b, ((1,), (0,)))


def nt(a, b):
    return dot(a, b, ((1,), (1,)))


def tn(a, b):
    return dot(a, b, ((0,), (0,)))


def call(body, outs, *args, name):
    return pl.pallas_call(
        body,
        out_shape=[jax.ShapeDtypeStruct(s, d) for s, d in outs],
        compiler_params=pltpu.CompilerParams(vmem_limit_bytes=58 * 1024 * 1024),
        cost_estimate=pl.CostEstimate(flops=1000, bytes_accessed=1000, transcendentals=0),
        name=name,
    )(*args)


def attention_in(x, blocks, bias, omega_t, keep, head_local, head_width):
    tokens = x.shape[1]
    feats = omega_t.shape[1]
    heads = omega_t.shape[0]
    hb = head_local * head_width
    rows = head_width + PAD
    factor = head_width ** (-0.25)

    def body(x_ref, m0, t0, m1, t1, bias_ref, omega_ref, keep_ref, fq_ref, fk_ref, uq_ref, uk_ref, v_ref, kv_ref):
        xv = x_ref[...]
        columns = jnp.transpose(bias_ref[...])
        ones = jnp.ones((PAD, tokens), bf16)
        for i, (m, t) in enumerate(((m0, t0), (m1, t1))):
            half = m.shape[0]
            triple = tn(m[...], xv[:half]) + tn(t[...], xv[half:])
            triple = triple + columns[:, i : i + 1]
            for hl in range(head_local):
                h = i * head_local + hl
                at = h * head_width
                lo = hl * head_width
                value = triple[2 * hb + lo : 2 * hb + lo + head_width].astype(bf16)
                v_ref[at : at + head_width] = value
                for base, u_ref, f_ref, mask in ((0, uq_ref, fq_ref, False), (hb, uk_ref, fk_ref, True)):
                    u = triple[base + lo : base + lo + head_width] * factor
                    ub = u.astype(bf16)
                    u_ref[at : at + head_width] = ub
                    z = nn(omega_ref[h], ub)
                    feat = jnp.exp(z - (0.5 * jnp.sum(u * u, axis=0, keepdims=True) + stabilizer))
                    if mask:
                        feat = feat * keep_ref[0:1]
                    feat = feat.astype(bf16)
                    f_ref[h * feats : (h + 1) * feats] = feat
                kv_ref[h * rows : (h + 1) * rows] = nt(jnp.concatenate((value, ones), axis=0), feat).astype(bf16)

    n = heads * head_width
    outs = [((heads * feats, tokens), bf16)] * 2 + [((n, tokens), bf16)] * 3 + [((heads * rows, feats), bf16)]
    return call(body, outs, x, *blocks, bias, omega_t, keep, name="attention_in")


def middle(kv, fq, x, blocks, vecs, up_bias, target, keep, scale, heads, head_width, hid_local):
    width, tokens = x.shape
    feats = kv.shape[1]
    rows = head_width + PAD
    hb = heads * head_width // 2

    def body(kv_ref, fq_ref, x_ref, m0, t0, m1, t1, vec_ref, upb_ref, tgt_ref, keep_ref, scale_ref,
             att_ref, inv_ref, xh1_ref, r1_ref, x1_ref, hid_ref, slope_ref, out_ref, gf_ref, sum_ref, loss_ref):
        half = m0.shape[0]
        vec = jnp.transpose(vec_ref[...])
        upb = jnp.transpose(upb_ref[...])
        for h in range(heads):
            both = nn(kv_ref[h * rows : (h + 1) * rows], fq_ref[h * feats : (h + 1) * feats])
            inverse = 1.0 / both[head_width : head_width + 1]
            inv_ref[h : h + 1] = inverse
            att_ref[h * head_width : (h + 1) * head_width] = (both[:head_width] * inverse).astype(bf16)
        parts = []
        for a, b in ((m0, m1), (t0, t1)):
            parts.append(nn(a[:, :hb], att_ref[:hb]) + nn(b[:, :hb], att_ref[hb:]))
        h1 = jnp.concatenate(parts, axis=0) + x_ref[...].astype(f32) + vec[:, 0:1]
        mean = jnp.sum(h1, axis=0, keepdims=True) * (1.0 / width)
        h1 = h1 - mean
        r1 = lax.rsqrt(jnp.sum(h1 * h1, axis=0, keepdims=True) * (1.0 / width) + norm_eps)
        h1 = h1 * r1
        r1_ref[...] = jnp.broadcast_to(r1, (8, tokens))
        xh1_ref[...] = h1.astype(bf16)
        x1 = h1 * vec[:, 1:2] + vec[:, 2:3]
        x1b = x1.astype(bf16)
        x1_ref[...] = x1b
        step = 512
        h2 = x1 + vec[:, 3:4]
        for i, (m, t) in enumerate(((m0, t0), (m1, t1))):
            for c in range(0, hid_local, step):
                at = i * hid_local + c
                lo = hb + c
                up = tn(m[:, lo : lo + step], x1b[:half]) + tn(t[:, lo : lo + step], x1b[half:])
                up = up + upb[at : at + step, 0:1]
                gate = 0.5 * (1.0 + lax.erf(up * root_half))
                slope_ref[at : at + step] = (gate + up * inv_root_two_pi * jnp.exp(-0.5 * up * up)).astype(bf16)
                hid_ref[at : at + step] = (up * gate).astype(bf16)
            lo = hb + hid_local
            hid = hid_ref[i * hid_local : (i + 1) * hid_local]
            h2 = h2 + jnp.concatenate((nn(m[:, lo:], hid), nn(t[:, lo:], hid)), axis=0)
        mean = jnp.sum(h2, axis=0, keepdims=True) * (1.0 / width)
        h2 = h2 - mean
        r2 = lax.rsqrt(jnp.sum(h2 * h2, axis=0, keepdims=True) * (1.0 / width) + norm_eps)
        h2 = h2 * r2
        out = h2 * vec[:, 4:5] + vec[:, 5:6]
        out_ref[...] = out.astype(bf16)
        diff = (out - tgt_ref[...].astype(f32)) * keep_ref[0:1]
        loss_ref[...] = jnp.full((8, 128), jnp.sum(diff * diff), f32)
        g = diff * scale_ref[0:1, 0:1]
        ones = jnp.ones((8, tokens), bf16)
        sum_ref[0:8] = nt(ones, (g * h2).astype(bf16))
        sum_ref[8:16] = nt(ones, g.astype(bf16))
        a = g * vec[:, 4:5]
        first = jnp.sum(a, axis=0, keepdims=True) * (1.0 / width)
        second = jnp.sum(a * h2, axis=0, keepdims=True) * (1.0 / width)
        gf_ref[...] = (r2 * (a - first - h2 * second)).astype(bf16)

    ff = 2 * hid_local
    outs = [
        ((width, tokens), bf16), ((16, tokens), f32), ((width, tokens), bf16), ((8, tokens), f32),
        ((width, tokens), bf16), ((ff, tokens), bf16), ((ff, tokens), bf16), ((width, tokens), bf16),
        ((width, tokens), bf16), ((16, width), f32), ((8, 128), f32),
    ]
    return call(body, outs, kv, fq, x, *blocks, vecs, up_bias, target, keep, scale, name="middle")


def half_grad(left, right, which, name):
    n, tokens = left.shape
    k = right.shape[0] // 2
    half = n // 2

    def body(l_ref, r_ref, o_ref):
        l = l_ref[which * half : (which + 1) * half]
        for i in range(2):
            o_ref[i] = nt(l, r_ref[i * k : (i + 1) * k]).astype(bf16)

    return call(body, [((2, half, k), bf16)], left, right, name=name)[0]


def down_back(gf, slope, blocks, hb, hid_local):
    width, tokens = gf.shape

    def body(gf_ref, slope_ref, m0, t0, m1, t1, gu_ref, sum_ref, bd_ref):
        half = m0.shape[0]
        lo = hb + hid_local
        step = 512
        g = gf_ref[...]
        ones = jnp.ones((8, tokens), bf16)
        bd_ref[...] = nt(ones, g)
        for i, (m, t) in enumerate(((m0, t0), (m1, t1))):
            for c in range(0, hid_local, step):
                at = i * hid_local + c
                v = tn(m[:, lo + c : lo + c + step], g[:half]) + tn(t[:, lo + c : lo + c + step], g[half:])
                v = (v * slope_ref[at : at + step].astype(f32)).astype(bf16)
                gu_ref[at : at + step] = v
                sum_ref[:, at : at + step] = nt(ones, v)

    ff = 2 * hid_local
    return call(body, [((ff, tokens), bf16), ((8, ff), f32), ((8, width), f32)], gf, slope, *blocks, name="down_back")


def up_back(gu, gf, xh1, r1, vecs, blocks, hb, hid_local):
    width, tokens = gf.shape

    def body(gu_ref, gf_ref, xh_ref, r1_ref, vec_ref, m0, t0, m1, t1, go_ref, sum_ref):
        vec = jnp.transpose(vec_ref[...])
        parts = []
        for a, b in ((m0, m1), (t0, t1)):
            parts.append(nn(a[:, hb : hb + hid_local], gu_ref[:hid_local]) + nn(b[:, hb : hb + hid_local], gu_ref[hid_local:]))
        g = jnp.concatenate(parts, axis=0) + gf_ref[...].astype(f32)
        xh = xh_ref[...].astype(f32)
        ones = jnp.ones((8, tokens), bf16)
        sum_ref[0:8] = nt(ones, (g * xh).astype(bf16))
        sum_ref[8:16] = nt(ones, g.astype(bf16))
        a = g * vec[:, 1:2]
        first = jnp.sum(a, axis=0, keepdims=True) * (1.0 / width)
        second = jnp.sum(a * xh, axis=0, keepdims=True) * (1.0 / width)
        go = (r1_ref[0:1] * (a - first - xh * second)).astype(bf16)
        go_ref[...] = go
        sum_ref[16:24] = nt(ones, go)

    return call(body, [((width, tokens), bf16), ((24, width), f32)], gu, gf, xh1, r1, vecs, *blocks, name="up_back")


def attention_mid(go, att, inv, fq, blocks, heads, head_width):
    width, tokens = go.shape
    feats = fq.shape[0] // heads
    hb = heads * head_width // 2
    rows = head_width + PAD

    def body(go_ref, att_ref, inv_ref, fq_ref, m0, t0, m1, t1, gn_ref, kv_ref):
        half = m0.shape[0]
        g = go_ref[...]
        zeros = jnp.zeros((PAD - 1, tokens), f32)
        for i, (m, t) in enumerate(((m0, t0), (m1, t1))):
            ga = tn(m[:, :hb], g[:half]) + tn(t[:, :hb], g[half:])
            for hl in range(heads // 2):
                h = i * (heads // 2) + hl
                gh = ga[hl * head_width : (hl + 1) * head_width]
                inverse = inv_ref[h : h + 1]
                a = att_ref[h * head_width : (h + 1) * head_width].astype(f32)
                gd = -jnp.sum(gh * a, axis=0, keepdims=True) * inverse
                both = jnp.concatenate((gh * inverse, gd, zeros), axis=0).astype(bf16)
                gn_ref[h * rows : (h + 1) * rows] = both
                kv_ref[h * rows : (h + 1) * rows] = nt(both, fq_ref[h * feats : (h + 1) * feats]).astype(bf16)

    return call(
        body, [((heads * rows, tokens), bf16), ((heads * rows, feats), bf16)], go, att, inv, fq, *blocks, name="attention_mid"
    )


def query_back(gn, kv, fq, uq, omega, heads, head_width):
    n, tokens = uq.shape
    feats = fq.shape[0] // heads
    rows = head_width + PAD
    factor = head_width ** (-0.25)

    def body(gn_ref, kv_ref, fq_ref, uq_ref, om_ref, gq_ref, sum_ref):
        for h in range(heads):
            e = tn(kv_ref[h * rows : (h + 1) * rows], gn_ref[h * rows : (h + 1) * rows])
            e = e * fq_ref[h * feats : (h + 1) * feats].astype(f32)
            s = jnp.sum(e, axis=0, keepdims=True)
            u = uq_ref[h * head_width : (h + 1) * head_width].astype(f32)
            gq_ref[h * head_width : (h + 1) * head_width] = (factor * (nn(om_ref[h], e.astype(bf16)) - s * u)).astype(bf16)

        sum_ref[...] = nt(jnp.ones((8, tokens), bf16), gq_ref[...])

    return call(body, [((n, tokens), bf16), ((8, n), f32)], gn, kv, fq, uq, omega, name="query_back")


def key_back(gkv, fk, uk, v, omega, heads, head_width):
    n, tokens = uk.shape
    feats = fk.shape[0] // heads
    rows = head_width + PAD
    factor = head_width ** (-0.25)
    hl_n = heads // 2
    hb = hl_n * head_width

    def body(gkv_ref, fk_ref, uk_ref, v_ref, om_ref, g_ref, sum_ref):
        ones = jnp.ones((PAD, tokens), bf16)
        for h in range(heads):
            i, hl = divmod(h, hl_n)
            base = i * 2 * hb + hl * head_width
            kv = gkv_ref[h * rows : (h + 1) * rows]
            f = fk_ref[h * feats : (h + 1) * feats]
            at = h * head_width
            value = jnp.concatenate((v_ref[at : at + head_width], ones), axis=0)
            e = tn(kv, value) * f.astype(f32)
            s = jnp.sum(e, axis=0, keepdims=True)
            u = uk_ref[at : at + head_width].astype(f32)
            g_ref[base : base + head_width] = (factor * (nn(om_ref[h], e.astype(bf16)) - s * u)).astype(bf16)
            g_ref[base + hb : base + hb + head_width] = nn(kv[:head_width], f).astype(bf16)
        sum_ref[...] = nt(jnp.ones((8, tokens), bf16), g_ref[...])

    return call(body, [((2 * n, tokens), bf16), ((8, 2 * n), f32)], gkv, fk, uk, v, omega, name="key_back")


def tail_grad(x, g, go, att, which, name):
    n, tokens = x.shape
    half = n // 2
    k = g.shape[0] // 2
    hb = n // 2

    def body(x_ref, g_ref, go_ref, att_ref, o_ref):
        for i in range(2):
            o_ref[i, :, :k] = nt(x_ref[which * half : (which + 1) * half], g_ref[i * k : (i + 1) * k]).astype(bf16)
            o_ref[i, :, k:] = nt(go_ref[which * half : (which + 1) * half], att_ref[i * hb : (i + 1) * hb]).astype(bf16)

    return call(body, [((2, half, k + hb), bf16)], x, g, go, att, name=name)[0]


def input_grad(gq, g, go, blocks):
    width, tokens = go.shape
    hb = gq.shape[0] // 2

    def body(gq_ref, g_ref, go_ref, m0, t0, m1, t1, o_ref):
        half = m0.shape[0]
        for w, pair in enumerate(((m0, m1), (t0, t1))):
            at = w * half
            total = go_ref[at : at + half].astype(f32)
            for i, a in enumerate(pair):
                total = total + nn(a[:, :hb], gq_ref[i * hb : (i + 1) * hb])
                total = total + nn(a[:, hb:], g_ref[i * 2 * hb : (i + 1) * 2 * hb])
            o_ref[at : at + half] = total.astype(bf16)

    return call(body, [((width, tokens), bf16)], gq, g, go, *blocks, name="input_grad")[0]


def swap(value, axis, mask):
    size = lax.axis_size(axis)
    return lax.ppermute(value, axis, [(s, s ^ mask) for s in range(size)])


def after(value, *others):
    return lax.optimization_barrier((value, *others))[0]


def gather_plane(own, by_x, by_y, cut):
    far = swap(by_x[cut:], "col", 1)
    if cut:
        far = jnp.concatenate((swap(by_y[:cut], "row", 2), far), axis=0)
    near = jnp.concatenate((own, by_x), axis=0)
    other = jnp.concatenate((by_y, far), axis=0)
    return near, swap(near, "row", 1), other, swap(other, "row", 1)


def far_sum(mine, got):
    n = mine.shape[1] // 2
    return mine[1, n:] + got[1, n:]


def send_far(low, cut):
    from_x = swap(low[:cut], "row", 2) if cut else None
    return from_x, swap(low[cut:], "col", 1)


def near_sums(mine, got, from_x, from_y, cut):
    n = mine.shape[1] // 2
    to_x = mine[0, n:].astype(f32) + got[0, n:].astype(f32)
    to_y = mine[1, :n].astype(f32) + got[1, :n].astype(f32)
    to_x = jnp.concatenate((to_x[:cut], to_x[cut:] + from_y), axis=0)
    if cut:
        to_y = jnp.concatenate((to_y[:cut] + from_x, to_y[cut:]), axis=0)
    return to_x.astype(bf16), to_y.astype(bf16)


def own_sum(mine, got, from_x, from_y):
    n = mine.shape[1] // 2
    return mine[0, :n].astype(f32) + got[0, :n].astype(f32) + from_x.astype(f32) + from_y.astype(f32)


def reduce_dp(value):
    parts = lax.axis_size("dp")
    if parts != 4:
        return lax.psum(value.astype(bf16), "dp").astype(f32)
    index = lax.axis_index("dp")
    inner = jnp.logical_or(index == 1, index == 2)
    value = value + lax.ppermute(value.astype(bf16), "dp", [(0, 1), (3, 2)]).astype(f32)
    other = lax.ppermute(value.astype(bf16), "dp", [(1, 2), (2, 1)])
    low = (value + other.astype(f32)).astype(bf16)
    back = lax.ppermute(low, "dp", [(1, 0), (2, 3)])
    return jnp.where(inner, low, back).astype(f32)


def reduce_small(value, axis):
    step = 1
    while step < lax.axis_size(axis):
        value = value + swap(value, axis, step)
        step *= 2
    return value


def position_blocks(shard, row_parts):
    row = lax.axis_index("row")
    n = shard.shape[1] // row_parts
    blocks = [lax.dynamic_slice_in_dim(shard, (row ^ j) * n, n, 1).astype(bf16) for j in range(4)]
    return jnp.concatenate((blocks[0], blocks[2]), axis=0), jnp.concatenate((blocks[1], blocks[3]), axis=0)


def to_features(low, row_parts):
    row = lax.axis_index("row")
    k = low.shape[0] // row_parts
    n = low.shape[1]
    got = swap(jnp.concatenate((low[k : 2 * k], low[3 * k :]), axis=0), "row", 2)
    core = swap(jnp.concatenate((low[2 * k : 3 * k], got[k:]), axis=0), "row", 1)
    out = jnp.zeros((k, n * row_parts), f32)
    for j, block in ((0, low[:k]), (2, got[:k]), (1, core[:k]), (3, core[k:])):
        out = lax.dynamic_update_slice_in_dim(out, block.astype(f32), (row ^ j) * n, 1)
    return out


def shards(
    inputs, teacher, lengths, omega,
    w_query, b_query, w_key, b_key, w_value, b_value, w_out, b_out,
    norm1_gain, norm1_bias, w_up, up_bias, w_down, b_down, norm2_gain, norm2_bias,
):
    row_parts = lax.axis_size("row")
    cols = lax.axis_size("col")
    feat_local, seq_length = inputs.shape
    width = feat_local * row_parts
    head_local, head_width, feats = omega.shape
    heads = head_local * cols
    tokens = seq_length // row_parts
    hb = head_local * head_width
    hid_local = w_up.shape[1]
    row = lax.axis_index("row")
    col = lax.axis_index("col")
    cut = CUT

    here, there = position_blocks(inputs, row_parts)
    k = feat_local
    got = swap(there, "row", 1)
    own_a = jnp.concatenate((w_query, w_key, w_value), axis=1).astype(bf16)
    a_y = swap(own_a, "col", 1)
    mid = jnp.concatenate((here[k:], got[k:]), axis=0)
    far = swap(mid, "row", 2)
    x = jnp.concatenate((here[:k], far[:k], got[:k], far[k:]), axis=0)
    a_x = swap(after(own_a, mid), "row", 2)
    col_pack = jnp.concatenate((b_query, b_key, b_value, up_bias))
    col_other = swap(col_pack, "col", 1)
    omega_all = jnp.concatenate((omega, swap(omega, "col", 1)), axis=0)
    vecs = jnp.stack((b_out, norm1_gain, norm1_bias, b_down, norm2_gain, norm2_bias, b_out, b_out))
    vecs = jnp.concatenate((vecs, swap(vecs, "row", 2)), axis=1)
    vecs = jnp.concatenate((vecs, swap(vecs, "row", 1)), axis=1)
    bias_a = jnp.concatenate((jnp.stack((col_pack[: 3 * hb], col_other[: 3 * hb])), jnp.zeros((6, 3 * hb), f32)))
    up_bias_all = jnp.concatenate((col_pack[3 * hb :], col_other[3 * hb :])).reshape(1, -1)
    up_bias_all = jnp.broadcast_to(up_bias_all, (8, up_bias_all.shape[1]))
    own_b = jnp.concatenate((w_out, w_up, w_down), axis=1).astype(bf16)
    own_b = after(own_b, own_a, mid)
    b_x = swap(own_b, "row", 2)
    b_y = swap(own_b, "col", 1)
    blocks_a = gather_plane(own_a, a_x, a_y, 0)
    blocks_b = gather_plane(own_b, b_x, b_y, cut)
    t_here, t_there = position_blocks(teacher, row_parts)
    t_got = swap(t_there, "row", 1)
    t_far = swap(jnp.concatenate((t_here[k:], t_got[k:]), axis=0), "row", 2)
    target = jnp.concatenate((t_here[:k], t_far[:k], t_got[:k], t_far[k:]), axis=0)

    count = reduce_small(jnp.sum(lengths).astype(f32).reshape(1, 1) + jnp.zeros((8, 128), f32), "dp")
    length = lax.dynamic_index_in_dim(lengths, col, 0, False)
    keep = ((row * tokens + jnp.arange(tokens, dtype=jnp.int32)) < length).astype(f32)
    keep = jnp.broadcast_to(keep[None, :], (8, tokens))
    scale = (2.0 * LOSS_SCALE) / (count * width)

    omega_t = jnp.transpose(omega_all, (0, 2, 1))
    fq, fk, uq, uk, v, kv = attention_in(x, blocks_a, bias_a, omega_t, keep, head_local, head_width)
    kv = kv + swap(kv, "row", 1)
    kv = kv + swap(kv, "row", 2)
    att, inv, xh1, r1, x1, hid, slope, out, gf, sum2, loss_part = middle(
        kv, fq, x, blocks_b, vecs, up_bias_all, target, keep, scale, heads, head_width, hid_local
    )

    theirs = half_grad(gf, hid, 1, "down_theirs")
    got1 = swap(theirs, "row", 1)
    mine1 = half_grad(after(gf, theirs), hid, 0, "down_mine")
    low1 = far_sum(mine1, got1)
    far1 = send_far(low1, cut)
    gu, bu, bd = down_back(after(gf, low1), slope, blocks_b, hb, hid_local)
    to1 = near_sums(mine1, got1, *far1, cut)
    from1 = (swap(to1[0], "row", 2), swap(to1[1], "col", 1))

    theirs = half_grad(after(x1, *to1), gu, 1, "up_theirs")
    got2 = swap(theirs, "row", 1)
    mine2 = half_grad(after(x1, theirs), gu, 0, "up_mine")
    low2 = far_sum(mine2, got2)
    far2 = send_far(low2, cut)
    go, sum1 = up_back(after(gu, low2), gf, xh1, r1, vecs, blocks_b, hb, hid_local)
    to2 = near_sums(mine2, got2, *far2, cut)
    from2 = (swap(to2[0], "row", 2), swap(to2[1], "col", 1))
    grad_down = reduce_dp(own_sum(mine1, got1, *from1))

    gn, gkv = attention_mid(after(go, *to2), att, inv, fq, blocks_b, heads, head_width)
    gkv = gkv + swap(gkv, "row", 1)
    gkv_x = swap(gkv, "row", 2)
    gq, sum_q = query_back(after(gn, gkv), kv, fq, uq, omega_all, heads, head_width)
    theirs = tail_grad(x, gq, go, att, 1, "tail_theirs")
    got3 = swap(theirs, "row", 1)
    mine3 = tail_grad(after(x, theirs), gq, go, att, 0, "tail_mine")
    grad_up = reduce_dp(own_sum(mine2, got2, *from2))
    gkv = gkv + gkv_x
    low3 = far_sum(mine3, got3)
    far3 = send_far(low3, cut)
    g, sum_kv = key_back(after(gkv, low3), fk, uk, v, omega_all, heads, head_width)
    to3 = near_sums(mine3, got3, *far3, cut)
    from3 = (swap(to3[0], "row", 2), swap(to3[1], "col", 1))
    theirs = half_grad(after(x, *to3), g, 1, "kv_theirs")
    got4 = swap(theirs, "row", 1)
    mine4 = half_grad(after(x, theirs), g, 0, "kv_mine")
    low4 = far_sum(mine4, got4)
    far4 = send_far(low4, cut)
    grad_in = input_grad(gq, g, after(go, low4), blocks_a)
    to4 = near_sums(mine4, got4, *far4, cut)
    from4 = (swap(to4[0], "row", 2), swap(to4[1], "col", 1))
    grad_tail = reduce_dp(own_sum(mine3, got3, *from3))
    grad_kv = reduce_dp(own_sum(mine4, got4, *from4))
    out = to_features(out, row_parts)
    grad_in = to_features(grad_in, row_parts)

    small = jnp.stack((sum1[16], sum1[0], sum1[8], bd[0], sum2[0], sum2[8])).reshape(6, row_parts, feat_local)
    small = jnp.transpose(small, (1, 0, 2)).reshape(row_parts * 6 * feat_local)
    q = sum_q[0].reshape(cols, hb)
    pair = sum_kv[0].reshape(cols, 2 * hb)
    ups = bu[0].reshape(cols, hid_local)
    col_small = jnp.concatenate((q, pair, ups), axis=1)
    loss_row = loss_part[0]
    packed = jnp.concatenate((small, col_small[0], loss_row)) + swap(jnp.concatenate((small, col_small[1], loss_row)), "col", 1)
    for mask in (1, 2):
        half = small.shape[0] // (2 if mask == 1 else 4)
        packed = jnp.concatenate((packed[:half], packed[2 * half :])) + swap(packed[half:], "row", mask)
    packed = reduce_small(packed, "dp")
    rows = packed[: 6 * feat_local].reshape(6, feat_local)
    col_part = packed[6 * feat_local : 6 * feat_local + 3 * hb + hid_local]
    loss = packed[-1] / (count[0, 0] * width)

    return (
        out,
        loss,
        grad_in,
        grad_tail[:, :hb],
        col_part[:hb],
        grad_kv[:, :hb],
        col_part[hb : 2 * hb],
        grad_kv[:, hb:],
        col_part[2 * hb : 3 * hb],
        grad_tail[:, hb:],
        rows[0],
        rows[1],
        rows[2],
        grad_up,
        col_part[3 * hb :],
        grad_down,
        rows[3],
        rows[4],
        rows[5],
    )


CUT = 32

def solution(mesh):
    both = P("row", ("dp", "col"))
    in_specs = (
        both, both, P("dp"), P("col", None, None),
        P("row", "col"), P("col"), P("row", "col"), P("col"), P("row", "col"), P("col"),
        P("row", "col"), P("row"), P("row"), P("row"),
        P("row", "col"), P("col"), P("row", "col"), P("row"), P("row"), P("row"),
    )
    out_specs = (
        both, P(), both,
        P("row", "col"), P("col"), P("row", "col"), P("col"), P("row", "col"), P("col"),
        P("row", "col"), P("row"), P("row"), P("row"),
        P("row", "col"), P("col"), P("row", "col"), P("row"), P("row"), P("row"),
    )
    return jax.shard_map(shards, mesh=mesh, in_specs=in_specs, out_specs=out_specs, check_vma=False)
```

```python
import jax
import jax.numpy as jnp
from jax import lax
from jax.experimental import pallas as pl
from jax.experimental.pallas import tpu as pltpu
from jax.sharding import PartitionSpec as P

LOSS_SCALE = 16777216
stabilizer = 2.0
norm_eps = 1e-12
root_half = 0.7071067811865476
inv_root_two_pi = 0.3989422804014327
f32 = jnp.float32
bf16 = jnp.bfloat16
PAD = 8
EXTRA = 16
CUT = 32


def dot(a, b, dims):
    return lax.dot_general(a, b, (dims, ((), ())), preferred_element_type=f32)


def nn(a, b):
    return dot(a, b, ((1,), (0,)))


def nt(a, b):
    return dot(a, b, ((1,), (1,)))


def tn(a, b):
    return dot(a, b, ((0,), (0,)))


def ones_rows(tokens):
    return jnp.ones((8, tokens), bf16)


def call(body, outs, args, name, grid=None, in_specs=None, out_specs=None, scratch=(), limit=40):
    extra = {}
    if grid is not None:
        extra = dict(grid=grid, in_specs=in_specs, out_specs=out_specs)
    elif in_specs is not None:
        extra = dict(in_specs=in_specs)
    return pl.pallas_call(
        body,
        out_shape=[jax.ShapeDtypeStruct(s, d) for s, d in outs],
        scratch_shapes=list(scratch),
        compiler_params=pltpu.CompilerParams(vmem_limit_bytes=limit * 1024 * 1024),
        cost_estimate=pl.CostEstimate(flops=1000, bytes_accessed=1000, transcendentals=0),
        name=name,
        **extra,
    )(*args)


def whole(a):
    zeros = (0,) * a.ndim
    return pl.BlockSpec(a.shape, lambda s: zeros)


def whole_out(shape):
    zeros = (0,) * len(shape)
    return pl.BlockSpec(shape, lambda s: zeros)


VMEM = pl.BlockSpec(memory_space=pltpu.VMEM)
SMEM = pl.BlockSpec(memory_space=pltpu.SMEM)


def split_positions(shard, row, row_parts):
    k, length = shard.shape
    n = length // row_parts

    def body(row_ref, in_ref, *out_refs):
        r = row_ref[0]
        for j, o_ref in enumerate(out_refs):
            at = pl.multiple_of(jnp.bitwise_xor(r, j) * n, n)
            o_ref[...] = in_ref[:, pl.ds(at, n)].astype(bf16)

    return call(body, [((k, n), bf16)] * row_parts, (row, shard), "split_positions", in_specs=[SMEM, VMEM])


def join_positions(blocks, row):
    k, n = blocks[0].shape
    parts = len(blocks)

    def body(row_ref, *refs):
        r = row_ref[0]
        o_ref = refs[parts]
        for j in range(parts):
            at = pl.multiple_of(jnp.bitwise_xor(r, j) * n, n)
            o_ref[:, pl.ds(at, n)] = refs[j][...].astype(f32)

    return call(body, [((k, n * parts), f32)], (row, *blocks), "join_positions", in_specs=[SMEM] + [VMEM] * parts)[0]


def narrow(parts, name):
    n = parts[0].shape[0]
    widths = [p.shape[1] for p in parts]

    def body(*refs):
        at = 0
        for ref, w in zip(refs, widths):
            refs[-1][:, at : at + w] = ref[...].astype(bf16)
            at += w

    return call(body, [((n, sum(widths)), bf16)], parts, name)[0]


def attention_in(xs, near, other, bias, omega_t, keep, head_local, head_width):
    k, tokens = xs[0].shape
    feats = omega_t.shape[1]
    heads = omega_t.shape[0]
    hb = head_local * head_width
    rows = head_width + PAD
    factor = head_width ** (-0.25)
    n_near, n_other = len(near), len(other)

    def body(*refs):
        x_in = refs[:4]
        near_refs = refs[4 : 4 + n_near]
        other_refs = refs[4 + n_near : 4 + n_near + n_other]
        bias_ref, omega_ref, keep_ref, x_ref, fq_ref, fk_ref, uq_ref, uk_ref, v_ref, kv_ref = refs[4 + n_near + n_other :]
        for p in range(4):
            x_ref[p * k : (p + 1) * k] = x_in[p][...]
        xv = x_ref[...]
        columns = jnp.transpose(bias_ref[...])
        ones = jnp.ones((PAD, tokens), bf16)
        for i, pieces in enumerate((near_refs, other_refs)):
            triple = tn(jnp.concatenate([p[...] for p in pieces], axis=0), xv) + columns[:, i : i + 1]
            for hl in range(head_local):
                h = i * head_local + hl
                at = h * head_width
                lo = hl * head_width
                value = triple[2 * hb + lo : 2 * hb + lo + head_width].astype(bf16)
                v_ref[at : at + head_width] = value
                for base, u_ref, f_ref, mask in ((0, uq_ref, fq_ref, False), (hb, uk_ref, fk_ref, True)):
                    u = triple[base + lo : base + lo + head_width] * factor
                    ub = u.astype(bf16)
                    u_ref[at : at + head_width] = ub
                    z = nn(omega_ref[h], ub)
                    feat = jnp.exp(z - (0.5 * jnp.sum(u * u, axis=0, keepdims=True) + stabilizer))
                    if mask:
                        feat = feat * keep_ref[0:1]
                    feat = feat.astype(bf16)
                    f_ref[h * feats : (h + 1) * feats] = feat
                kv_ref[h * rows : (h + 1) * rows] = nt(jnp.concatenate((value, ones), axis=0), feat).astype(bf16)

    n = heads * head_width
    outs = [((4 * k, tokens), bf16)] + [((heads * feats, tokens), bf16)] * 2 + [((n, tokens), bf16)] * 3
    outs += [((heads * rows, feats), bf16)]
    return call(body, outs, (*xs, *near, *other, bias, omega_t, keep), "attention_in")


def weight_specs(pieces, block, first):
    return [pl.BlockSpec((p.shape[0], block), lambda s, f=first: (0, f + s)) for p in pieces]


def fixed_specs(pieces, block, at):
    return [pl.BlockSpec((p.shape[0], block), lambda s: (0, at)) for p in pieces]


def rows_of(refs):
    return jnp.concatenate([r[...] for r in refs], axis=0)


def middle(kv0, kv1, fq, x, near, other, vecs, up_bias, target, keep, scale, heads, head_width, hid_local):
    width, tokens = x.shape
    feats = kv0.shape[1]
    rows = head_width + PAD
    hb = heads * head_width // 2
    steps = hid_local // hb
    k = width // 4
    nn_, no = len(near), len(other)
    np_ = nn_ + no

    def body(*refs):
        kv0_ref, kv1_ref, fq_ref, x_ref = refs[:4]
        out_w = refs[4 : 4 + np_]
        up_w = refs[4 + np_ : 4 + 2 * np_]
        down_w = refs[4 + 2 * np_ : 4 + 3 * np_]
        (vec_ref, upb_ref, t0, t1, t2, t3, keep_ref, scale_ref,
         kv_ref, att_ref, inv_ref, xh1_ref, r1_ref, x1_ref, hid_ref, slope_ref, gf_ref, sum_ref,
         o0, o1, o2, o3, acc_ref, vec_s) = refs[4 + 3 * np_ :]
        step = pl.program_id(0)

        @pl.when(step == 0)
        def _():
            vec = jnp.transpose(vec_ref[...])
            vec_s[...] = vec
            kv_ref[...] = (kv0_ref[...].astype(f32) + kv1_ref[...].astype(f32)).astype(bf16)
            for h in range(heads):
                both = nn(kv_ref[h * rows : (h + 1) * rows], fq_ref[h * feats : (h + 1) * feats])
                inverse = 1.0 / both[head_width : head_width + 1]
                inv_ref[h : h + 1] = inverse
                att_ref[h * head_width : (h + 1) * head_width] = (both[:head_width] * inverse).astype(bf16)
            w = jnp.concatenate((rows_of(out_w[:nn_]), rows_of(out_w[nn_:])), axis=1)
            h1 = nn(w, att_ref[...]) + x_ref[...].astype(f32) + vec[:, 0:1]
            mean = jnp.sum(h1, axis=0, keepdims=True) * (1.0 / width)
            h1 = h1 - mean
            r1 = lax.rsqrt(jnp.sum(h1 * h1, axis=0, keepdims=True) * (1.0 / width) + norm_eps)
            h1 = h1 * r1
            r1_ref[...] = jnp.broadcast_to(r1, (8, tokens))
            xh1_ref[...] = h1.astype(bf16)
            x1 = h1 * vec[:, 1:2] + vec[:, 2:3]
            x1_ref[...] = x1.astype(bf16)
            acc_ref[...] = x1 + vec[:, 3:4]

        x1b = x1_ref[...]
        bias = jnp.transpose(upb_ref[...])
        total = acc_ref[...]
        for i, (a, b) in enumerate(((0, nn_), (nn_, np_))):
            up = tn(rows_of(up_w[a:b]), x1b) + bias[:, i : i + 1]
            gate = 0.5 * (1.0 + lax.erf(up * root_half))
            slope_ref[i] = (gate + up * inv_root_two_pi * jnp.exp(-0.5 * up * up)).astype(bf16)
            hid = (up * gate).astype(bf16)
            hid_ref[i] = hid
            total = total + nn(rows_of(down_w[a:b]), hid)
        acc_ref[...] = total

        @pl.when(step == steps - 1)
        def _():
            vec = vec_s[...]
            h2 = acc_ref[...]
            mean = jnp.sum(h2, axis=0, keepdims=True) * (1.0 / width)
            h2 = h2 - mean
            r2 = lax.rsqrt(jnp.sum(h2 * h2, axis=0, keepdims=True) * (1.0 / width) + norm_eps)
            h2 = h2 * r2
            out = h2 * vec[:, 4:5] + vec[:, 5:6]
            for p, o_ref in enumerate((o0, o1, o2, o3)):
                o_ref[...] = out[p * k : (p + 1) * k].astype(bf16)
            target = jnp.concatenate((t0[...], t1[...], t2[...], t3[...]), axis=0).astype(f32)
            diff = (out - target) * keep_ref[0:1]
            g = diff * scale_ref[0:1, 0:1]
            ones = ones_rows(tokens)
            sum_ref[0:8] = nt(ones, (g * h2).astype(bf16))
            sum_ref[8:16] = nt(ones, g.astype(bf16))
            sum_ref[16:24] = jnp.full((8, width), jnp.sum(diff * diff), f32)
            a = g * vec[:, 4:5]
            first = jnp.sum(a, axis=0, keepdims=True) * (1.0 / width)
            second = jnp.sum(a * h2, axis=0, keepdims=True) * (1.0 / width)
            gf_ref[...] = (r2 * (a - first - h2 * second)).astype(bf16)

    outs = [
        ((heads * rows, feats), bf16), ((width, tokens), bf16), ((16, tokens), f32), ((width, tokens), bf16),
        ((8, tokens), f32), ((width, tokens), bf16), ((2, hid_local, tokens), bf16), ((2, hid_local, tokens), bf16),
        ((width, tokens), bf16), ((24, width), f32),
    ] + [((k, tokens), bf16)] * 4
    pieces = (*near, *other)
    args = (kv0, kv1, fq, x, *pieces, *pieces, *pieces, vecs, up_bias, *target, keep, scale)
    in_specs = [whole(a) for a in (kv0, kv1, fq, x)]
    in_specs += fixed_specs(pieces, hb, 0) + weight_specs(pieces, hb, 1) + weight_specs(pieces, hb, 1 + steps)
    in_specs += [whole(vecs), pl.BlockSpec((8, hb), lambda s: (0, s))] + [whole(t) for t in target] + [whole(keep), whole(scale)]
    out_specs = [whole_out(s) for s, _ in outs]
    out_specs[6] = out_specs[7] = pl.BlockSpec((2, hb, tokens), lambda s: (0, s, 0))
    scratch = [pltpu.VMEM((width, tokens), f32), pltpu.VMEM((width, 8), f32)]
    return call(body, outs, args, "middle", (steps,), in_specs, out_specs, scratch, limit=56)


def grad_theirs(left, right, block, name):
    n, tokens = left.shape
    k = right.shape[1]
    half = n // 2

    def body(l_ref, r_ref, o_ref):
        for i in range(2):
            o_ref[i] = nt(l_ref[...], r_ref[i]).astype(bf16)

    return call(
        body, [((2, half, k), bf16)], (left, right), name, (k // block,),
        [pl.BlockSpec((half, tokens), lambda s: (1, 0)), pl.BlockSpec((2, block, tokens), lambda s: (0, s, 0))],
        [pl.BlockSpec((2, half, block), lambda s: (0, 0, s))],
    )[0]


def grad_mine(left, right, got, block, name):
    n, tokens = left.shape
    k = right.shape[1]
    half = n // 2

    def body(l_ref, r_ref, got_ref, keep_ref, send_ref):
        for i, o_ref in enumerate((keep_ref, send_ref)):
            o_ref[...] = (nt(l_ref[...], r_ref[i]) + got_ref[i].astype(f32)).astype(bf16)

    return call(
        body, [((half, k), bf16)] * 2, (left, right, got), name, (k // block,),
        [
            pl.BlockSpec((half, tokens), lambda s: (0, 0)),
            pl.BlockSpec((2, block, tokens), lambda s: (0, s, 0)),
            pl.BlockSpec((2, half, block), lambda s: (0, 0, s)),
        ],
        [pl.BlockSpec((half, block), lambda s: (0, s))] * 2,
    )


def pair_theirs(x, gq, go, att, name):
    n, tokens = x.shape
    half = n // 2
    k = gq.shape[1]

    def body(x_ref, gq_ref, go_ref, att_ref, o_ref):
        for i in range(2):
            o_ref[i, :, :k] = nt(x_ref[half:], gq_ref[i]).astype(bf16)
            o_ref[i, :, k:] = nt(go_ref[half:], att_ref[i]).astype(bf16)

    return call(body, [((2, half, 2 * k), bf16)], (x, gq, go, att), name)[0]


def pair_mine(x, gq, go, att, got, name):
    n, tokens = x.shape
    half = n // 2
    k = gq.shape[1]

    def body(x_ref, gq_ref, go_ref, att_ref, got_ref, keep_ref, send_ref):
        for i, o_ref in enumerate((keep_ref, send_ref)):
            o_ref[:, :k] = (nt(x_ref[:half], gq_ref[i]) + got_ref[i, :, :k].astype(f32)).astype(bf16)
            o_ref[:, k:] = (nt(go_ref[:half], att_ref[i]) + got_ref[i, :, k:].astype(f32)).astype(bf16)

    return call(body, [((half, 2 * k), bf16)] * 2, (x, gq, go, att, got), name)


def down_back(gf, slope, near, other, hb, hid_local):
    width, tokens = gf.shape
    steps = hid_local // hb
    nn_, no = len(near), len(other)
    pieces = (*near, *other)

    def body(gf_ref, slope_ref, *refs):
        gu_ref, sum_ref, bd_ref = refs[nn_ + no :]
        g = gf_ref[...]
        ones = ones_rows(tokens)

        @pl.when(pl.program_id(0) == 0)
        def _():
            bd_ref[...] = nt(ones, g)

        for i, w in enumerate((refs[:nn_], refs[nn_ : nn_ + no])):
            v = (tn(rows_of(w), g) * slope_ref[i].astype(f32)).astype(bf16)
            gu_ref[i] = v
            sum_ref[i] = nt(ones, v)

    spec = pl.BlockSpec((2, hb, tokens), lambda s: (0, s, 0))
    return call(
        body, [((2, hid_local, tokens), bf16), ((2, 8, hid_local), f32), ((8, width), f32)], (gf, slope, *pieces), "down_back",
        (steps,), [whole(gf), spec] + weight_specs(pieces, hb, 1 + steps),
        [spec, pl.BlockSpec((2, 8, hb), lambda s: (0, 0, s)), whole_out((8, width))],
    )


def up_back(gu, gf, xh1, r1, vecs, near, other, hb):
    width, tokens = gf.shape
    steps = gu.shape[1] // hb
    nn_, no = len(near), len(other)
    pieces = (*near, *other)

    def body(gu_ref, gf_ref, xh_ref, r1_ref, vec_ref, *refs):
        go_ref, sum_ref, acc_ref = refs[nn_ + no :]
        step = pl.program_id(0)

        @pl.when(step == 0)
        def _():
            acc_ref[...] = gf_ref[...].astype(f32)

        acc_ref[...] += nn(rows_of(refs[:nn_]), gu_ref[0]) + nn(rows_of(refs[nn_ : nn_ + no]), gu_ref[1])

        @pl.when(step == steps - 1)
        def _():
            vec = jnp.transpose(vec_ref[...])
            g = acc_ref[...]
            xh = xh_ref[...].astype(f32)
            ones = ones_rows(tokens)
            sum_ref[0:8] = nt(ones, (g * xh).astype(bf16))
            sum_ref[8:16] = nt(ones, g.astype(bf16))
            a = g * vec[:, 1:2]
            first = jnp.sum(a, axis=0, keepdims=True) * (1.0 / width)
            second = jnp.sum(a * xh, axis=0, keepdims=True) * (1.0 / width)
            go = (r1_ref[0:1] * (a - first - xh * second)).astype(bf16)
            go_ref[...] = go
            sum_ref[16:24] = nt(ones, go)

    return call(
        body, [((width, tokens), bf16), ((24, width), f32)], (gu, gf, xh1, r1, vecs, *pieces), "up_back", (steps,),
        [pl.BlockSpec((2, hb, tokens), lambda s: (0, s, 0))] + [whole(a) for a in (gf, xh1, r1, vecs)] + weight_specs(pieces, hb, 1),
        [whole_out((width, tokens)), whole_out((24, width))], [pltpu.VMEM((width, tokens), f32)],
    )


def attention_mid(go, att, inv, fq, near, other, heads, head_width):
    width, tokens = go.shape
    feats = fq.shape[0] // heads
    hb = heads * head_width // 2
    rows = head_width + PAD
    nn_, no = len(near), len(other)
    pieces = (*near, *other)

    def body(go_ref, att_ref, inv_ref, fq_ref, *refs):
        gn_ref, kv_ref = refs[nn_ + no :]
        g = go_ref[...]
        zeros = jnp.zeros((PAD - 1, tokens), f32)
        for i, w in enumerate((refs[:nn_], refs[nn_ : nn_ + no])):
            ga = tn(rows_of(w), g)
            for hl in range(heads // 2):
                h = i * (heads // 2) + hl
                gh = ga[hl * head_width : (hl + 1) * head_width]
                inverse = inv_ref[h : h + 1]
                a = att_ref[h * head_width : (h + 1) * head_width].astype(f32)
                gd = -jnp.sum(gh * a, axis=0, keepdims=True) * inverse
                both = jnp.concatenate((gh * inverse, gd, zeros), axis=0).astype(bf16)
                gn_ref[h * rows : (h + 1) * rows] = both
                kv_ref[h * rows : (h + 1) * rows] = nt(both, fq_ref[h * feats : (h + 1) * feats]).astype(bf16)

    outs = [((heads * rows, tokens), bf16), ((heads * rows, feats), bf16)]
    args = (go, att, inv, fq, *pieces)
    return call(
        body, outs, args, "attention_mid", (1,), [whole(a) for a in args[:4]] + fixed_specs(pieces, hb, 0),
        [whole_out(s) for s, _ in outs],
    )


def query_back(gn, kv, fq, uq, omega, heads, head_width):
    n, tokens = uq.shape
    feats = fq.shape[0] // heads
    rows = head_width + PAD
    factor = head_width ** (-0.25)

    def body(gn_ref, kv_ref, fq_ref, uq_ref, om_ref, gq_ref, sum_ref):
        for h in range(heads):
            e = tn(kv_ref[h * rows : (h + 1) * rows], gn_ref[h * rows : (h + 1) * rows])
            e = e * fq_ref[h * feats : (h + 1) * feats].astype(f32)
            s = jnp.sum(e, axis=0, keepdims=True)
            u = uq_ref[h * head_width : (h + 1) * head_width].astype(f32)
            gq_ref[h * head_width : (h + 1) * head_width] = (factor * (nn(om_ref[h], e.astype(bf16)) - s * u)).astype(bf16)
        sum_ref[...] = nt(ones_rows(tokens), gq_ref[...])

    return call(body, [((n, tokens), bf16), ((8, n), f32)], (gn, kv, fq, uq, omega), "query_back")


def key_back(gkv0, gkv1, fk, uk, v, omega, heads, head_width):
    n, tokens = uk.shape
    feats = fk.shape[0] // heads
    rows = head_width + PAD
    factor = head_width ** (-0.25)
    hl_n = heads // 2
    hb = hl_n * head_width

    def body(gkv0_ref, gkv1_ref, fk_ref, uk_ref, v_ref, om_ref, g_ref, sum_ref):
        ones = jnp.ones((PAD, tokens), bf16)
        for h in range(heads):
            i, hl = divmod(h, hl_n)
            base = i * 2 * hb + hl * head_width
            kv = (gkv0_ref[h * rows : (h + 1) * rows].astype(f32) + gkv1_ref[h * rows : (h + 1) * rows].astype(f32)).astype(bf16)
            f = fk_ref[h * feats : (h + 1) * feats]
            at = h * head_width
            value = jnp.concatenate((v_ref[at : at + head_width], ones), axis=0)
            e = tn(kv, value) * f.astype(f32)
            s = jnp.sum(e, axis=0, keepdims=True)
            u = uk_ref[at : at + head_width].astype(f32)
            g_ref[base : base + head_width] = (factor * (nn(om_ref[h], e.astype(bf16)) - s * u)).astype(bf16)
            g_ref[base + hb : base + hb + head_width] = nn(kv[:head_width], f).astype(bf16)
        sum_ref[...] = nt(ones_rows(tokens), g_ref[...])

    return call(body, [((2 * n, tokens), bf16), ((8, 2 * n), f32)], (gkv0, gkv1, fk, uk, v, omega), "key_back")


def last_parts(x, g, sums, got, name):
    sum1, sum2, bd, bu, sum_q, sum_kv = sums
    n, tokens = x.shape
    q = n // 4
    k = g.shape[1]
    hb = k // 2
    hid_local = bu.shape[2]
    ups = hid_local // hb
    rows = q + EXTRA
    which = 0 if got is not None else 1

    def body(x_ref, g_ref, s1_ref, s2_ref, bd_ref, bu_ref, sq_ref, skv_ref, *refs):
        if got is None:
            o_ref, row_s, col_s = refs
        else:
            got_ref, keep_ref, send_ref, row_s, col_s = refs
        for m, v in enumerate((s1_ref[16:17], s1_ref[0:1], s1_ref[8:9], bd_ref[0:1], s2_ref[0:1], s2_ref[8:9], s2_ref[16:17])):
            row_s[m : m + 1] = v
        row_s[7:8] = jnp.zeros((1, n), f32)
        col_s[...] = jnp.zeros(col_s.shape, f32)
        for i in range(2):
            col_s[i, 0:1] = sq_ref[0:1, i * hb : (i + 1) * hb]
            col_s[i, 1:2] = skv_ref[0:1, i * k : i * k + hb]
            col_s[i, 2:3] = skv_ref[0:1, i * k + hb : (i + 1) * k]
            for u in range(ups):
                col_s[i, 3 + u : 4 + u] = bu_ref[i, 0:1, u * hb : (u + 1) * hb]
        for i in range(2):
            for jx in range(2):
                p = 2 * which + jx
                main = nt(x_ref[p * q : (p + 1) * q], g_ref[i])
                small = row_s[:, p * q : (p + 1) * q]
                small = jnp.concatenate((small, jnp.zeros((8, hb - q), f32), col_s[i]), axis=1)
                small = jnp.concatenate((small, jnp.zeros((EXTRA - 8, k), f32)), axis=0)
                if got is None:
                    o_ref[i, jx, :q] = main.astype(bf16)
                    o_ref[i, jx, q:] = small.astype(bf16)
                else:
                    o = send_ref if jx else keep_ref
                    o[i * rows : i * rows + q] = (main + got_ref[i, jx, :q].astype(f32)).astype(bf16)
                    o[i * rows + q : (i + 1) * rows] = (small + got_ref[i, jx, q:].astype(f32)).astype(bf16)

    outs = [((2, 2, rows, k), bf16)] if got is None else [((2 * rows, k), bf16)] * 2
    args = (x, g, *sums) if got is None else (x, g, *sums, got)
    return call(body, outs, args, name, scratch=[pltpu.VMEM((8, n), f32), pltpu.VMEM((2, 8, hb), f32)])


def input_grad(gq, g, go, near, other):
    width, tokens = go.shape
    hb = gq.shape[1]
    k = width // 4
    nn_, no = len(near), len(other)

    def body(gq_ref, g_ref, go_ref, *refs):
        total = go_ref[...].astype(f32)
        for i, w in enumerate((refs[:nn_], refs[nn_ : nn_ + no])):
            w = rows_of(w)
            total = total + nn(w[:, :hb], gq_ref[i]) + nn(w[:, hb:], g_ref[i])
        for p, o_ref in enumerate(refs[nn_ + no :]):
            o_ref[...] = total[p * k : (p + 1) * k].astype(bf16)

    return call(body, [((k, tokens), bf16)] * 4, (gq, g, go, *near, *other), "input_grad")


def swap(value, axis, mask):
    size = lax.axis_size(axis)
    return lax.ppermute(value, axis, [(s, s ^ mask) for s in range(size)])


def after(value, *others):
    return lax.optimization_barrier((value, *others))[0]


def finish(keep, got, last, second):
    n = keep.shape[0] // 2
    value = keep[:n] + got[:n] + last
    parts = lax.axis_size("dp")
    if parts != 4:
        return lax.psum(value, "dp")
    index = lax.axis_index("dp")
    inner = jnp.logical_or(index == 1, index == 2)
    value = value + lax.ppermute(value, "dp", [(0, 1), (3, 2)])
    low = value + lax.ppermute(value, "dp", [(1, 2), (2, 1)])
    back = lax.ppermute(low, "dp", [(1, 0), (2, 3)])
    return jnp.where(inner, low, back)


def far_half(keep, got):
    n = keep.shape[0] // 2
    return keep[n:] + got[n:]


def exchange(blocks):
    return [blocks[0]] + [swap(blocks[j], "row", j) for j in (1, 2, 3)]


def reduce_small(value, axis):
    step = 1
    while step < lax.axis_size(axis):
        value = value + swap(value, axis, step)
        step *= 2
    return value


def shards(
    inputs, teacher, lengths, omega,
    w_query, b_query, w_key, b_key, w_value, b_value, w_out, b_out,
    norm1_gain, norm1_bias, w_up, up_bias, w_down, b_down, norm2_gain, norm2_bias,
):
    row_parts = lax.axis_size("row")
    feat_local, seq_length = inputs.shape
    width = feat_local * row_parts
    head_local, head_width, feats = omega.shape
    heads = head_local * lax.axis_size("col")
    tokens = seq_length // row_parts
    hb = head_local * head_width
    hid_local = w_up.shape[1]
    row = lax.axis_index("row")
    col = lax.axis_index("col")
    row_ref = row.astype(jnp.int32).reshape(1)

    ins = split_positions(inputs, row_ref, row_parts)
    ins_got = exchange(ins)
    xs = [ins_got[j] for j in (0, 2, 1, 3)]
    own_a = narrow((w_query, w_key, w_value), "narrow_a")
    a_y = swap(own_a, "col", 1)
    a_x = swap(after(own_a, *ins), "row", 2)
    own_b = narrow((w_out, w_up, w_down), "narrow_b")
    b_x = swap(after(own_b, own_a), "row", 2)
    a_far = swap(a_x, "col", 1)
    near_a = (own_a, a_x, swap(own_a, "row", 1), swap(a_x, "row", 1))
    other_a = (a_y, a_far, swap(a_y, "row", 1), swap(a_far, "row", 1))
    col_pack = jnp.concatenate((b_query, b_key, b_value, up_bias))
    col_other = swap(col_pack, "col", 1)
    omega_all = jnp.concatenate((omega, swap(omega, "col", 1)), axis=0)
    vecs = jnp.stack((b_out, norm1_gain, norm1_bias, b_down, norm2_gain, norm2_bias, b_out, b_out))
    vecs = jnp.concatenate((vecs, swap(vecs, "row", 2)), axis=1)
    vecs = jnp.concatenate((vecs, swap(vecs, "row", 1)), axis=1)
    both = jnp.stack((col_pack, col_other))
    bias_all = jnp.concatenate((both, jnp.zeros((6, both.shape[1]), f32)))
    bias_a = bias_all[:, : 3 * hb]
    up_bias_all = bias_all[:, 3 * hb :]
    b_y = swap(after(own_b, a_x), "col", 1)
    b_far_y = swap(b_x[CUT:], "col", 1)
    b_far_x = swap(b_y[:CUT], "row", 2)
    near_b = (own_b, b_x)
    near_b = near_b + tuple(swap(p, "row", 1) for p in near_b)
    other_b = (b_y, b_far_x, b_far_y)
    other_b = other_b + tuple(swap(p, "row", 1) for p in other_b)

    count = reduce_small(jnp.sum(lengths).astype(f32).reshape(1, 1) + jnp.zeros((8, 128), f32), "dp")
    length = lax.dynamic_index_in_dim(lengths, col, 0, False)
    keep = ((row * tokens + jnp.arange(tokens, dtype=jnp.int32)) < length).astype(f32)
    keep = jnp.broadcast_to(keep[None, :], (8, tokens))
    scale = (2.0 * LOSS_SCALE) / (count * width)

    omega_t = jnp.transpose(omega_all, (0, 2, 1))
    x, fq, fk, uq, uk, v, kv = attention_in(xs, near_a, other_a, bias_a, omega_t, keep, head_local, head_width)
    kv0 = kv + swap(kv, "row", 1)
    kv1 = swap(kv0, "row", 2)
    teach = exchange(split_positions(after(teacher, kv0), row_ref, row_parts))
    target = [teach[j] for j in (0, 2, 1, 3)]
    kv, att, inv, xh1, r1, x1, hid, slope, gf, sum2, *out = middle(
        kv0, kv1, fq, x, near_b, other_b, vecs, up_bias_all, target, keep, scale, heads, head_width, hid_local
    )
    out = [out[j] for j in (0, 2, 1, 3)]

    theirs = grad_theirs(gf, hid, hb, "down_theirs")
    got1 = swap(theirs, "row", 1)
    gu, bu, bd = down_back(after(gf, theirs), slope, near_b, other_b, hb, hid_local)
    theirs = grad_theirs(x1, gu, hb, "up_theirs")
    got2 = swap(theirs, "row", 1)
    keep1, send1 = grad_mine(after(gf, theirs), hid, got1, hb, "down_mine")
    r_y1 = swap(send1, "col", 1)
    go, sum1 = up_back(after(gu, send1), gf, xh1, r1, vecs, near_b, other_b, hb)
    keep2, send2 = grad_mine(after(x1, go), gu, got2, hb, "up_mine")
    r_y2 = swap(send2, "col", 1)
    gn, gkv = attention_mid(after(go, send2), att, inv, fq, near_b, other_b, heads, head_width)
    gkv0 = gkv + swap(gkv, "row", 1)
    gkv1 = swap(gkv0, "row", 2)
    far1 = far_half(keep1, r_y1)
    r_x1 = swap(after(far1, gkv0), "row", 2)
    gq, sum_q = query_back(after(gn, gkv0), kv, fq, uq, omega_all, heads, head_width)
    gq = gq.reshape(2, hb, tokens)
    att2 = att.reshape(2, hb, tokens)
    theirs = pair_theirs(x, gq, go, att2, "pair_theirs")
    got3 = swap(theirs, "row", 1)
    g, sum_kv = key_back(after(gkv0, theirs), gkv1, fk, uk, v, omega_all, heads, head_width)
    g = g.reshape(2, 2 * hb, tokens)
    sums = (sum1, sum2, bd, bu, sum_q, sum_kv)
    theirs = last_parts(x, g, sums, None, "last_theirs")[0]
    got4 = swap(theirs, "row", 1)
    keep3, send3 = pair_mine(after(x, theirs), gq, go, att2, got3, "pair_mine")
    r_y3 = swap(send3, "col", 1)
    keep4, send4 = last_parts(after(x, send3), g, sums, got4, "last_mine")
    r_x4 = swap(send4, "row", 2)
    gin = input_grad(gq, g, after(go, send4), near_a, other_a)
    gin = [gin[j] for j in (0, 2, 1, 3)]
    grad_down = finish(keep1, r_y1, r_x1, "row")
    r_x2 = swap(far_half(keep2, r_y2), "row", 2)
    grad_up = finish(keep2, r_y2, r_x2, "row")
    r_x3 = swap(far_half(keep3, r_y3), "row", 2)
    grad_pair = finish(keep3, r_y3, r_x3, "row").astype(f32)
    r_y4 = swap(far_half(keep4, r_x4), "col", 1)
    last = finish(keep4, r_x4, r_y4, "col").astype(f32)
    out = join_positions(exchange(out), row_ref)
    grad_in = join_positions(exchange(gin), row_ref)

    extra = last[feat_local:]
    rows = extra[:7, :feat_local]
    cols = extra[:7, hb:]
    loss = rows[6, 0] / (count[0, 0] * width)
    return (
        out,
        loss,
        grad_in,
        grad_pair[:, :hb],
        cols[0],
        last[:feat_local, :hb],
        cols[1],
        last[:feat_local, hb:],
        cols[2],
        grad_pair[:, hb:],
        rows[0],
        rows[1],
        rows[2],
        grad_up.astype(f32),
        cols[3:].reshape(hid_local),
        grad_down.astype(f32),
        rows[3],
        rows[4],
        rows[5],
    )


def solution(mesh):
    both = P("row", ("dp", "col"))
    in_specs = (
        both, both, P("dp"), P("col", None, None),
        P("row", "col"), P("col"), P("row", "col"), P("col"), P("row", "col"), P("col"),
        P("row", "col"), P("row"), P("row"), P("row"),
        P("row", "col"), P("col"), P("row", "col"), P("row"), P("row"), P("row"),
    )
    out_specs = (
        both, P(), both,
        P("row", "col"), P("col"), P("row", "col"), P("col"), P("row", "col"), P("col"),
        P("row", "col"), P("row"), P("row"), P("row"),
        P("row", "col"), P("col"), P("row", "col"), P("row"), P("row"), P("row"),
    )
    return jax.shard_map(shards, mesh=mesh, in_specs=in_specs, out_specs=out_specs, check_vma=False)
```

```python
import jax
import jax.numpy as jnp
from jax import lax
from jax.experimental import pallas as pl
from jax.experimental.pallas import tpu as pltpu
from jax.sharding import PartitionSpec as P

LOSS_SCALE = 16777216
stabilizer = 2.0
norm_eps = 1e-12
root_half = 0.7071067811865476
inv_root_two_pi = 0.3989422804014327
f32 = jnp.float32
bf16 = jnp.bfloat16
PAD = 8
EXTRA = 16
CUT = 48
ASIDE = 256


def dot(a, b, dims):
    return lax.dot_general(a, b, (dims, ((), ())), preferred_element_type=f32)


def nn(a, b):
    return dot(a, b, ((1,), (0,)))


def nt(a, b):
    return dot(a, b, ((1,), (1,)))


def tn(a, b):
    return dot(a, b, ((0,), (0,)))


def ones_rows(tokens):
    return jnp.ones((8, tokens), bf16)


def call(body, outs, args, name, grid=None, in_specs=None, out_specs=None, scratch=(), limit=40):
    if grid is None:
        grid = (1,)
        in_specs = [single(a.shape) for a in args] if in_specs is None else in_specs
        out_specs = [single(s) for s, _ in outs]
    extra = dict(grid=grid, in_specs=in_specs, out_specs=out_specs)
    return pl.pallas_call(
        body,
        out_shape=[jax.ShapeDtypeStruct(s, d) for s, d in outs],
        scratch_shapes=list(scratch),
        compiler_params=pltpu.CompilerParams(vmem_limit_bytes=limit * 1024 * 1024),
        cost_estimate=pl.CostEstimate(flops=1000, bytes_accessed=1000, transcendentals=0),
        name=name,
        **extra,
    )(*args)


def single(shape):
    zeros = (0,) * len(shape)
    return pl.BlockSpec(shape, lambda s: zeros, pipeline_mode=pl.Buffered(1))


def whole(a):
    zeros = (0,) * a.ndim
    return pl.BlockSpec(a.shape, lambda s: zeros)


def whole_out(shape):
    zeros = (0,) * len(shape)
    return pl.BlockSpec(shape, lambda s: zeros)


SMEM = pl.BlockSpec(memory_space=pltpu.SMEM)


def split_positions(shard, row, row_parts):
    k, length = shard.shape
    n = length // row_parts

    def body(row_ref, in_ref, *out_refs):
        r = row_ref[0]
        for j, o_ref in enumerate(out_refs):
            at = pl.multiple_of(jnp.bitwise_xor(r, j) * n, n)
            o_ref[...] = in_ref[:, pl.ds(at, n)].astype(bf16)

    return call(body, [((k, n), bf16)] * row_parts, (row, shard), "split_positions", in_specs=[SMEM, single(shard.shape)])


def join_positions(blocks, row):
    k, n = blocks[0].shape
    parts = len(blocks)

    def body(row_ref, *refs):
        r = row_ref[0]
        o_ref = refs[parts]
        for j in range(parts):
            at = pl.multiple_of(jnp.bitwise_xor(r, j) * n, n)
            o_ref[:, pl.ds(at, n)] = refs[j][...].astype(f32)

    return call(body, [((k, n * parts), f32)], (row, *blocks), "join_positions", in_specs=[SMEM] + [single(b.shape) for b in blocks])[0]


def narrow(parts, steps, name):
    n = parts[0].shape[0]
    widths = [p.shape[1] for p in parts]

    def body(*refs):
        at = 0
        for ref, w in zip(refs, widths):
            refs[-1][:, at : at + w] = ref[...].astype(bf16)
            at += w

    return call(
        body, [((n, sum(widths)), bf16)], parts, name, (steps,),
        [pl.BlockSpec((n // steps, w), lambda s: (s, 0)) for w in widths],
        [pl.BlockSpec((n // steps, sum(widths)), lambda s: (s, 0))],
    )[0]


def narrow_small(parts, vecs, biases, up_bias, name):
    n, hb = parts[0].shape
    width = hb * len(parts)
    small = [v.reshape(1, v.shape[0]) for v in (*vecs, *biases, up_bias)]
    nv = len(vecs)
    rest = up_bias.shape[0] - width

    def body(*refs):
        p_refs = refs[: len(parts)]
        v_refs = refs[len(parts) : len(parts) + nv]
        b_refs = refs[len(parts) + nv : len(parts) + nv + len(biases)]
        up_ref, o_ref, small_ref = refs[len(parts) + nv + len(biases) :]
        small_ref[...] = jnp.zeros(small_ref.shape, f32)
        for m, ref in enumerate(v_refs):
            small_ref[m : m + 1, :n] = ref[...]
        for m, (ref, b_ref) in enumerate(zip(p_refs, b_refs)):
            o_ref[:n, m * hb : (m + 1) * hb] = ref[...].astype(bf16)
            small_ref[nv : nv + 1, m * hb : (m + 1) * hb] = b_ref[...]
        small_ref[nv + 1 : nv + 2] = up_ref[:, :width]
        small_ref[0:1, ASIDE : ASIDE + rest] = up_ref[:, width:]
        value = small_ref[...]
        high = value.astype(bf16).astype(f32)
        o_ref[n:] = jnp.concatenate((high, value - high), axis=0).astype(bf16)

    return call(body, [((n + EXTRA, width), bf16)], (*parts, *small), name, scratch=[pltpu.VMEM((8, width), f32)])[0]


def small_rows(ref, k):
    v = ref[k : k + EXTRA].astype(f32)
    return v[0:8] + v[8:16]


def attention_in(xs, near, other, omegas, keep, head_local, head_width, hid_local):
    k, tokens = xs[0].shape
    feats = omegas[0].shape[2]
    heads = 2 * head_local
    hb = head_local * head_width
    rows = head_width + PAD
    factor = head_width ** (-0.25)
    n_near, n_other = len(near), len(other)

    def body(*refs):
        x_in = refs[:4]
        near_refs = refs[4 : 4 + n_near]
        other_refs = refs[4 + n_near : 4 + n_near + n_other]
        (om0_ref, om1_ref, keep_ref, x_ref, fq_ref, fk_ref, uq_ref, uk_ref, v_ref, kv_ref, vec_ref, up_ref) = refs[
            4 + n_near + n_other :
        ]
        for p in range(4):
            vec_ref[:, p * k : (p + 1) * k] = small_rows(near_refs[p], k)[:, :k]
        up_ref[...] = jnp.zeros(up_ref.shape, f32)
        for p in range(4):
            x_ref[p * k : (p + 1) * k] = x_in[p][...]
        xv = x_ref[...]
        ones = jnp.ones((PAD, tokens), bf16)
        for i, pieces in enumerate((near_refs, other_refs)):
            omega_ref = (om0_ref, om1_ref)[i]
            small = small_rows(pieces[0], k)
            up_ref[i : i + 1, : 3 * hb] = small[7:8]
            up_ref[i : i + 1, 3 * hb :] = small[0:1, ASIDE : ASIDE + hid_local - 3 * hb]
            triple = tn(jnp.concatenate([p[:k] for p in pieces], axis=0), xv) + jnp.transpose(small)[:, 6:7]
            for hl in range(head_local):
                h = i * head_local + hl
                at = h * head_width
                lo = hl * head_width
                value = triple[2 * hb + lo : 2 * hb + lo + head_width].astype(bf16)
                v_ref[at : at + head_width] = value
                for base, u_ref, f_ref, mask in ((0, uq_ref, fq_ref, False), (hb, uk_ref, fk_ref, True)):
                    u = triple[base + lo : base + lo + head_width] * factor
                    ub = u.astype(bf16)
                    u_ref[at : at + head_width] = ub
                    z = tn(omega_ref[hl], ub)
                    feat = jnp.exp(z - (0.5 * jnp.sum(u * u, axis=0, keepdims=True) + stabilizer))
                    if mask:
                        feat = feat * keep_ref[0:1]
                    feat = feat.astype(bf16)
                    f_ref[h * feats : (h + 1) * feats] = feat
                kv_ref[h * rows : (h + 1) * rows] = nt(jnp.concatenate((value, ones), axis=0), feat).astype(bf16)

    n = heads * head_width
    outs = [((4 * k, tokens), bf16)] + [((heads * feats, tokens), bf16)] * 2 + [((n, tokens), bf16)] * 3
    outs += [((heads * rows, feats), bf16), ((8, 4 * k), f32), ((8, hid_local), f32)]
    return call(body, outs, (*xs, *near, *other, *omegas, keep), "attention_in")


def weight_specs(pieces, block, first):
    return [pl.BlockSpec((p.shape[0], block), lambda s, f=first: (0, f + s)) for p in pieces]


def fixed_specs(pieces, block, at):
    return [pl.BlockSpec((p.shape[0], block), lambda s: (0, at)) for p in pieces]


def rows_of(refs):
    return jnp.concatenate([r[...] for r in refs], axis=0)


def middle(kv0, kv1, fq, x, near, other, vecs, up_bias, target, keep, scale, heads, head_width, hid_local):
    width, tokens = x.shape
    feats = kv0.shape[1]
    rows = head_width + PAD
    hb = heads * head_width // 2
    steps = hid_local // hb
    k = width // 4
    nn_, no = len(near), len(other)
    np_ = nn_ + no

    def body(*refs):
        kv0_ref, kv1_ref, fq_ref, x_ref = refs[:4]
        out_w = refs[4 : 4 + np_]
        up_w = refs[4 + np_ : 4 + 2 * np_]
        down_w = refs[4 + 2 * np_ : 4 + 3 * np_]
        (vec_ref, upb_ref, t0, t1, t2, t3, keep_ref, scale_ref,
         kv_ref, att_ref, inv_ref, xh1_ref, r1_ref, x1_ref, hid_ref, slope_ref, gf_ref, sum_ref,
         o0, o1, o2, o3, acc_ref, vec_s) = refs[4 + 3 * np_ :]
        step = pl.program_id(0)

        @pl.when(step == 0)
        def _():
            vec = jnp.transpose(vec_ref[...])
            vec_s[...] = vec
            kv_ref[...] = (kv0_ref[...].astype(f32) + kv1_ref[...].astype(f32)).astype(bf16)
            for h in range(heads):
                both = nn(kv_ref[h * rows : (h + 1) * rows], fq_ref[h * feats : (h + 1) * feats])
                inverse = 1.0 / both[head_width : head_width + 1]
                inv_ref[h : h + 1] = inverse
                att_ref[h * head_width : (h + 1) * head_width] = (both[:head_width] * inverse).astype(bf16)
            w = jnp.concatenate((rows_of(out_w[:nn_]), rows_of(out_w[nn_:])), axis=1)
            h1 = nn(w, att_ref[...]) + x_ref[...].astype(f32) + vec[:, 0:1]
            mean = jnp.sum(h1, axis=0, keepdims=True) * (1.0 / width)
            h1 = h1 - mean
            r1 = lax.rsqrt(jnp.sum(h1 * h1, axis=0, keepdims=True) * (1.0 / width) + norm_eps)
            h1 = h1 * r1
            r1_ref[...] = jnp.broadcast_to(r1, (8, tokens))
            xh1_ref[...] = h1.astype(bf16)
            x1 = h1 * vec[:, 1:2] + vec[:, 2:3]
            x1_ref[...] = x1.astype(bf16)
            acc_ref[...] = x1 + vec[:, 3:4]

        x1b = x1_ref[...]
        bias = jnp.transpose(upb_ref[...])
        total = acc_ref[...]
        for i, (a, b) in enumerate(((0, nn_), (nn_, np_))):
            up = tn(rows_of(up_w[a:b]), x1b) + bias[:, i : i + 1]
            gate = 0.5 * (1.0 + lax.erf(up * root_half))
            slope_ref[i] = (gate + up * inv_root_two_pi * jnp.exp(-0.5 * up * up)).astype(bf16)
            hid = (up * gate).astype(bf16)
            hid_ref[i] = hid
            total = total + nn(rows_of(down_w[a:b]), hid)
        acc_ref[...] = total

        @pl.when(step == steps - 1)
        def _():
            vec = vec_s[...]
            h2 = acc_ref[...]
            mean = jnp.sum(h2, axis=0, keepdims=True) * (1.0 / width)
            h2 = h2 - mean
            r2 = lax.rsqrt(jnp.sum(h2 * h2, axis=0, keepdims=True) * (1.0 / width) + norm_eps)
            h2 = h2 * r2
            out = h2 * vec[:, 4:5] + vec[:, 5:6]
            for p, o_ref in enumerate((o0, o1, o2, o3)):
                o_ref[...] = out[p * k : (p + 1) * k].astype(bf16)
            target = jnp.concatenate((t0[...], t1[...], t2[...], t3[...]), axis=0).astype(f32)
            diff = (out - target) * keep_ref[0:1]
            g = diff * scale_ref[0:1, 0:1]
            ones = ones_rows(tokens)
            sum_ref[0:8] = nt(ones, (g * h2).astype(bf16))
            sum_ref[8:16] = nt(ones, g.astype(bf16))
            sum_ref[16:24] = jnp.full((8, width), jnp.sum(diff * diff), f32)
            a = g * vec[:, 4:5]
            first = jnp.sum(a, axis=0, keepdims=True) * (1.0 / width)
            second = jnp.sum(a * h2, axis=0, keepdims=True) * (1.0 / width)
            gf_ref[...] = (r2 * (a - first - h2 * second)).astype(bf16)

    outs = [
        ((heads * rows, feats), bf16), ((width, tokens), bf16), ((16, tokens), f32), ((width, tokens), bf16),
        ((8, tokens), f32), ((width, tokens), bf16), ((2, hid_local, tokens), bf16), ((2, hid_local, tokens), bf16),
        ((width, tokens), bf16), ((24, width), f32),
    ] + [((k, tokens), bf16)] * 4
    pieces = (*near, *other)
    args = (kv0, kv1, fq, x, *pieces, *pieces, *pieces, vecs, up_bias, *target, keep, scale)
    in_specs = [whole(a) for a in (kv0, kv1, fq, x)]
    in_specs += fixed_specs(pieces, hb, 0) + weight_specs(pieces, hb, 1) + weight_specs(pieces, hb, 1 + steps)
    in_specs += [whole(vecs), pl.BlockSpec((8, hb), lambda s: (0, s))] + [whole(t) for t in target] + [whole(keep), whole(scale)]
    out_specs = [whole_out(s) for s, _ in outs]
    out_specs[6] = out_specs[7] = pl.BlockSpec((2, hb, tokens), lambda s: (0, s, 0))
    scratch = [pltpu.VMEM((width, tokens), f32), pltpu.VMEM((width, 8), f32)]
    return call(body, outs, args, "middle", (steps,), in_specs, out_specs, scratch, limit=56)


def grad_theirs(left, right, block, name):
    n, tokens = left.shape
    k = right.shape[1]
    half = n // 2

    def body(l_ref, r_ref, o_ref):
        for i in range(2):
            o_ref[i] = nt(l_ref[...], r_ref[i]).astype(bf16)

    return call(
        body, [((2, half, k), bf16)], (left, right), name, (k // block,),
        [pl.BlockSpec((half, tokens), lambda s: (1, 0)), pl.BlockSpec((2, block, tokens), lambda s: (0, s, 0))],
        [pl.BlockSpec((2, half, block), lambda s: (0, 0, s))],
    )[0]


def grad_mine(left, right, got, block, name):
    n, tokens = left.shape
    k = right.shape[1]
    half = n // 2
    share = k // block // 2

    def body(l_ref, r_ref, got_ref, keep0, keep1, send0, send1):
        step = pl.program_id(0)

        def part(keep_ref, send_ref):
            for i, o_ref in enumerate((keep_ref, send_ref)):
                o_ref[...] = (nt(l_ref[...], r_ref[i]) + got_ref[i].astype(f32)).astype(bf16)

        pl.when(step < share)(lambda: part(keep0, send0))
        pl.when(step >= share)(lambda: part(keep1, send1))

    first = pl.BlockSpec((half, block), lambda s: (0, jnp.minimum(s, share - 1)))
    second = pl.BlockSpec((half, block), lambda s: (0, jnp.maximum(s - share, 0)))
    return call(
        body, [((half, k // 2), bf16)] * 4, (left, right, got), name, (2 * share,),
        [
            pl.BlockSpec((half, tokens), lambda s: (0, 0)),
            pl.BlockSpec((2, block, tokens), lambda s: (0, s, 0)),
            pl.BlockSpec((2, half, block), lambda s: (0, 0, s)),
        ],
        [first, second, first, second],
    )


def pair_theirs(x, gq, go, att, name):
    n, tokens = x.shape
    half = n // 2
    k = gq.shape[1]

    def body(x_ref, gq_ref, go_ref, att_ref, o_ref):
        for i in range(2):
            o_ref[i, :, :k] = nt(x_ref[half:], gq_ref[i]).astype(bf16)
            o_ref[i, :, k:] = nt(go_ref[half:], att_ref[i]).astype(bf16)

    return call(body, [((2, half, 2 * k), bf16)], (x, gq, go, att), name)[0]


def pair_mine(x, gq, go, att, got, name):
    n, tokens = x.shape
    half = n // 2
    k = gq.shape[1]

    def body(x_ref, gq_ref, go_ref, att_ref, got_ref, keep_ref, send_ref):
        for i, o_ref in enumerate((keep_ref, send_ref)):
            o_ref[:, :k] = (nt(x_ref[:half], gq_ref[i]) + got_ref[i, :, :k].astype(f32)).astype(bf16)
            o_ref[:, k:] = (nt(go_ref[:half], att_ref[i]) + got_ref[i, :, k:].astype(f32)).astype(bf16)

    return call(body, [((half, 2 * k), bf16)] * 2, (x, gq, go, att, got), name)


def down_back(gf, slope, near, other, hb, hid_local):
    width, tokens = gf.shape
    steps = hid_local // hb
    nn_, no = len(near), len(other)
    pieces = (*near, *other)

    def body(gf_ref, slope_ref, *refs):
        gu_ref, sum_ref, bd_ref = refs[nn_ + no :]
        g = gf_ref[...]
        ones = ones_rows(tokens)

        @pl.when(pl.program_id(0) == 0)
        def _():
            bd_ref[...] = nt(ones, g)

        for i, w in enumerate((refs[:nn_], refs[nn_ : nn_ + no])):
            v = (tn(rows_of(w), g) * slope_ref[i].astype(f32)).astype(bf16)
            gu_ref[i] = v
            sum_ref[i] = nt(ones, v)

    spec = pl.BlockSpec((2, hb, tokens), lambda s: (0, s, 0))
    return call(
        body, [((2, hid_local, tokens), bf16), ((2, 8, hid_local), f32), ((8, width), f32)], (gf, slope, *pieces), "down_back",
        (steps,), [whole(gf), spec] + weight_specs(pieces, hb, 1 + steps),
        [spec, pl.BlockSpec((2, 8, hb), lambda s: (0, 0, s)), whole_out((8, width))],
    )


def up_back(gu, gf, xh1, r1, vecs, near, other, hb):
    width, tokens = gf.shape
    steps = gu.shape[1] // hb
    nn_, no = len(near), len(other)
    pieces = (*near, *other)

    def body(gu_ref, gf_ref, xh_ref, r1_ref, vec_ref, *refs):
        go_ref, sum_ref, acc_ref = refs[nn_ + no :]
        step = pl.program_id(0)

        @pl.when(step == 0)
        def _():
            acc_ref[...] = gf_ref[...].astype(f32)

        acc_ref[...] += nn(rows_of(refs[:nn_]), gu_ref[0]) + nn(rows_of(refs[nn_ : nn_ + no]), gu_ref[1])

        @pl.when(step == steps - 1)
        def _():
            vec = jnp.transpose(vec_ref[...])
            g = acc_ref[...]
            xh = xh_ref[...].astype(f32)
            ones = ones_rows(tokens)
            sum_ref[0:8] = nt(ones, (g * xh).astype(bf16))
            sum_ref[8:16] = nt(ones, g.astype(bf16))
            a = g * vec[:, 1:2]
            first = jnp.sum(a, axis=0, keepdims=True) * (1.0 / width)
            second = jnp.sum(a * xh, axis=0, keepdims=True) * (1.0 / width)
            go = (r1_ref[0:1] * (a - first - xh * second)).astype(bf16)
            go_ref[...] = go
            sum_ref[16:24] = nt(ones, go)

    return call(
        body, [((width, tokens), bf16), ((24, width), f32)], (gu, gf, xh1, r1, vecs, *pieces), "up_back", (steps,),
        [pl.BlockSpec((2, hb, tokens), lambda s: (0, s, 0))] + [whole(a) for a in (gf, xh1, r1, vecs)] + weight_specs(pieces, hb, 1),
        [whole_out((width, tokens)), whole_out((24, width))], [pltpu.VMEM((width, tokens), f32)],
    )


def attention_mid(go, att, inv, fq, near, other, heads, head_width):
    width, tokens = go.shape
    feats = fq.shape[0] // heads
    hb = heads * head_width // 2
    rows = head_width + PAD
    nn_, no = len(near), len(other)
    pieces = (*near, *other)

    def body(go_ref, att_ref, inv_ref, fq_ref, *refs):
        gn_ref, kv_ref = refs[nn_ + no :]
        g = go_ref[...]
        zeros = jnp.zeros((PAD - 1, tokens), f32)
        for i, w in enumerate((refs[:nn_], refs[nn_ : nn_ + no])):
            ga = tn(rows_of(w), g)
            for hl in range(heads // 2):
                h = i * (heads // 2) + hl
                gh = ga[hl * head_width : (hl + 1) * head_width]
                inverse = inv_ref[h : h + 1]
                a = att_ref[h * head_width : (h + 1) * head_width].astype(f32)
                gd = -jnp.sum(gh * a, axis=0, keepdims=True) * inverse
                both = jnp.concatenate((gh * inverse, gd, zeros), axis=0).astype(bf16)
                gn_ref[h * rows : (h + 1) * rows] = both
                kv_ref[h * rows : (h + 1) * rows] = nt(both, fq_ref[h * feats : (h + 1) * feats]).astype(bf16)

    outs = [((heads * rows, tokens), bf16), ((heads * rows, feats), bf16)]
    args = (go, att, inv, fq, *pieces)
    return call(
        body, outs, args, "attention_mid", (1,), [whole(a) for a in args[:4]] + fixed_specs(pieces, hb, 0),
        [whole_out(s) for s, _ in outs],
    )


def query_back(gn, kv, fq, uq, omegas, heads, head_width):
    n, tokens = uq.shape
    feats = fq.shape[0] // heads
    rows = head_width + PAD
    factor = head_width ** (-0.25)

    def body(gn_ref, kv_ref, fq_ref, uq_ref, om0_ref, om1_ref, gq_ref, sum_ref):
        for h in range(heads):
            om_ref = (om0_ref, om1_ref)[h // (heads // 2)]
            e = tn(kv_ref[h * rows : (h + 1) * rows], gn_ref[h * rows : (h + 1) * rows])
            e = e * fq_ref[h * feats : (h + 1) * feats].astype(f32)
            s = jnp.sum(e, axis=0, keepdims=True)
            u = uq_ref[h * head_width : (h + 1) * head_width].astype(f32)
            gq_ref[h * head_width : (h + 1) * head_width] = (
                factor * (nn(om_ref[h % (heads // 2)], e.astype(bf16)) - s * u)
            ).astype(bf16)
        sum_ref[...] = nt(ones_rows(tokens), gq_ref[...])

    return call(body, [((n, tokens), bf16), ((8, n), f32)], (gn, kv, fq, uq, *omegas), "query_back")


def key_back(gkv0, gkv1, fk, uk, v, omegas, heads, head_width):
    n, tokens = uk.shape
    feats = fk.shape[0] // heads
    rows = head_width + PAD
    factor = head_width ** (-0.25)
    hl_n = heads // 2
    hb = hl_n * head_width

    def body(gkv0_ref, gkv1_ref, fk_ref, uk_ref, v_ref, om0_ref, om1_ref, g_ref, sum_ref):
        ones = jnp.ones((PAD, tokens), bf16)
        for h in range(heads):
            i, hl = divmod(h, hl_n)
            base = i * 2 * hb + hl * head_width
            kv = (gkv0_ref[h * rows : (h + 1) * rows].astype(f32) + gkv1_ref[h * rows : (h + 1) * rows].astype(f32)).astype(bf16)
            f = fk_ref[h * feats : (h + 1) * feats]
            at = h * head_width
            value = jnp.concatenate((v_ref[at : at + head_width], ones), axis=0)
            e = tn(kv, value) * f.astype(f32)
            s = jnp.sum(e, axis=0, keepdims=True)
            u = uk_ref[at : at + head_width].astype(f32)
            g_ref[base : base + head_width] = (
                factor * (nn((om0_ref, om1_ref)[i][hl], e.astype(bf16)) - s * u)
            ).astype(bf16)
            g_ref[base + hb : base + hb + head_width] = nn(kv[:head_width], f).astype(bf16)
        sum_ref[...] = nt(ones_rows(tokens), g_ref[...])

    return call(body, [((2 * n, tokens), bf16), ((8, 2 * n), f32)], (gkv0, gkv1, fk, uk, v, *omegas), "key_back")


def last_parts(x, g, sums, got, name):
    sum1, sum2, bd, bu, sum_q, sum_kv = sums
    n, tokens = x.shape
    q = n // 4
    k = g.shape[1]
    hb = k // 2
    hid_local = bu.shape[2]
    ups = hid_local // hb
    rows = q + EXTRA
    which = 0 if got is not None else 1

    def body(x_ref, g_ref, s1_ref, s2_ref, bd_ref, bu_ref, sq_ref, skv_ref, *refs):
        if got is None:
            o_ref, row_s, col_s = refs
        else:
            got_ref, keep_ref, send_ref, row_s, col_s = refs
        for m, v in enumerate((s1_ref[16:17], s1_ref[0:1], s1_ref[8:9], bd_ref[0:1], s2_ref[0:1], s2_ref[8:9], s2_ref[16:17])):
            row_s[m : m + 1] = v
        row_s[7:8] = jnp.zeros((1, n), f32)
        col_s[...] = jnp.zeros(col_s.shape, f32)
        for i in range(2):
            col_s[i, 0:1] = sq_ref[0:1, i * hb : (i + 1) * hb]
            col_s[i, 1:2] = skv_ref[0:1, i * k : i * k + hb]
            col_s[i, 2:3] = skv_ref[0:1, i * k + hb : (i + 1) * k]
            for u in range(ups):
                col_s[i, 3 + u : 4 + u] = bu_ref[i, 0:1, u * hb : (u + 1) * hb]
        for i in range(2):
            for jx in range(2):
                p = 2 * which + jx
                main = nt(x_ref[p * q : (p + 1) * q], g_ref[i])
                small = row_s[:, p * q : (p + 1) * q]
                small = jnp.concatenate((small, jnp.zeros((8, hb - q), f32), col_s[i]), axis=1)
                small = jnp.concatenate((small, jnp.zeros((EXTRA - 8, k), f32)), axis=0)
                if got is None:
                    o_ref[i, jx, :q] = main.astype(bf16)
                    o_ref[i, jx, q:] = small.astype(bf16)
                else:
                    o = send_ref if jx else keep_ref
                    o[i * rows : i * rows + q] = (main + got_ref[i, jx, :q].astype(f32)).astype(bf16)
                    o[i * rows + q : (i + 1) * rows] = (small + got_ref[i, jx, q:].astype(f32)).astype(bf16)

    outs = [((2, 2, rows, k), bf16)] if got is None else [((2 * rows, k), bf16)] * 2
    args = (x, g, *sums) if got is None else (x, g, *sums, got)
    return call(body, outs, args, name, scratch=[pltpu.VMEM((8, n), f32), pltpu.VMEM((2, 8, hb), f32)])


def input_grad(gq, g, go, near, other):
    width, tokens = go.shape
    hb = gq.shape[1]
    k = width // 4
    nn_, no = len(near), len(other)

    def body(gq_ref, g_ref, go_ref, *refs):
        total = go_ref[...].astype(f32)
        for i, w in enumerate((refs[:nn_], refs[nn_ : nn_ + no])):
            w = jnp.concatenate([r[:k] for r in w], axis=0)
            total = total + nn(w[:, :hb], gq_ref[i]) + nn(w[:, hb:], g_ref[i])
        for p, o_ref in enumerate(refs[nn_ + no :]):
            o_ref[...] = total[p * k : (p + 1) * k].astype(bf16)

    return call(body, [((k, tokens), bf16)] * 4, (gq, g, go, *near, *other), "input_grad")


def swap(value, axis, mask):
    size = lax.axis_size(axis)
    return lax.ppermute(value, axis, [(s, s ^ mask) for s in range(size)])


def after(value, *others):
    return lax.optimization_barrier((value, *others))[0]


class Fold:
    def __init__(self, value):
        self.value = value
        self.four = lax.axis_size("dp") == 4
        if self.four:
            self.got = lax.ppermute(value, "dp", [(0, 1), (3, 2)])
        else:
            self.value = lax.psum(value, "dp")

    def middle(self, order):
        if not self.four:
            return order
        self.value = after(self.value, order) + self.got
        self.got = lax.ppermute(self.value, "dp", [(1, 2), (2, 1)])
        return self.value

    def back(self, order):
        if not self.four:
            return order
        self.value = after(self.value, order) + self.got
        self.got = lax.ppermute(self.value, "dp", [(1, 0), (2, 3)])
        return self.value

    def result(self):
        if not self.four:
            return self.value
        index = lax.axis_index("dp")
        inner = jnp.logical_or(index == 1, index == 2)
        return jnp.where(inner, self.value, self.got)


def total(keep, got, last):
    n = keep.shape[0] // 2
    return keep[:n] + got[:n] + last


def far_half(keep, got):
    n = keep.shape[0] // 2
    return keep[n:] + got[n:]


def exchange(blocks):
    return [blocks[0]] + [swap(blocks[j], "row", j) for j in (1, 2, 3)]


def reduce_small(value, axis):
    step = 1
    while step < lax.axis_size(axis):
        value = value + swap(value, axis, step)
        step *= 2
    return value


def shards(
    inputs, teacher, lengths, omega,
    w_query, b_query, w_key, b_key, w_value, b_value, w_out, b_out,
    norm1_gain, norm1_bias, w_up, up_bias, w_down, b_down, norm2_gain, norm2_bias,
):
    row_parts = lax.axis_size("row")
    feat_local, seq_length = inputs.shape
    width = feat_local * row_parts
    head_local, head_width, feats = omega.shape
    heads = head_local * lax.axis_size("col")
    tokens = seq_length // row_parts
    hb = head_local * head_width
    hid_local = w_up.shape[1]
    row = lax.axis_index("row")
    col = lax.axis_index("col")
    row_ref = row.astype(jnp.int32).reshape(1)

    omegas = (omega, swap(omega, "col", 1))
    vecs = (b_out, norm1_gain, norm1_bias, b_down, norm2_gain, norm2_bias)
    own_a = narrow_small((w_query, w_key, w_value), vecs, (b_query, b_key, b_value), up_bias, "narrow_a")
    a_y = swap(own_a, "col", 1)
    a_x = swap(own_a, "row", 2)
    ins = split_positions(after(inputs, own_a, omegas[1]), row_ref, row_parts)
    ins_got = exchange(ins)
    xs = [ins_got[j] for j in (0, 2, 1, 3)]
    a_far = swap(after(a_x, a_y, omegas[1]), "col", 1)
    near_a = (own_a, a_x, swap(own_a, "row", 1), swap(a_x, "row", 1))
    other_a = (a_y, a_far, swap(a_y, "row", 1), swap(a_far, "row", 1))
    own_b = narrow((after(w_out, *ins), w_up, w_down), 3, "narrow_b")
    b_x = swap(after(own_b, a_x, ins_got[2], ins_got[3]), "row", 2)
    b_y = swap(after(own_b, a_far), "col", 1)
    count = reduce_small(jnp.sum(lengths).astype(f32).reshape(1, 1) + jnp.zeros((8, 128), f32), "dp")
    length = lax.dynamic_index_in_dim(lengths, col, 0, False)
    keep = ((row * tokens + jnp.arange(tokens, dtype=jnp.int32)) < length).astype(f32)
    keep = jnp.broadcast_to(keep[None, :], (8, tokens))
    scale = (2.0 * LOSS_SCALE) / (count * width)

    x, fq, fk, uq, uk, v, kv, vecs, up_bias_all = attention_in(
        xs, near_a, other_a, omegas, keep, head_local, head_width, hid_local
    )
    kv0 = kv + swap(kv, "row", 1)
    kv1 = swap(kv0, "row", 2)
    teach = split_positions(after(teacher, kv0), row_ref, row_parts)
    teach = exchange([teach[0], teach[1], *[after(t, kv1) for t in teach[2:]]])
    target = [teach[j] for j in (0, 2, 1, 3)]
    b_x = after(b_x, kv)
    b_y = after(b_y, kv)
    b_far_y = swap(b_x[CUT:], "col", 1)
    b_far_x = swap(after(b_y[:CUT], kv1, teach[2], teach[3]), "row", 2)
    near_b = (own_b, b_x)
    near_b = near_b + tuple(swap(p, "row", 1) for p in near_b)
    other_b = (b_y, b_far_x, after(b_far_y, teach[2], teach[3]))
    other_b = other_b + tuple(swap(p, "row", 1) for p in other_b)
    kv, att, inv, xh1, r1, x1, hid, slope, gf, sum2, *out = middle(
        kv0, kv1, fq, x, near_b, other_b, vecs, up_bias_all, target, keep, scale, heads, head_width, hid_local
    )
    out = exchange([out[j] for j in (0, 2, 1, 3)])

    theirs = grad_theirs(gf, hid, hb, "down_theirs")
    got1 = swap(theirs, "row", 1)
    gu, bu, bd = down_back(after(gf, theirs), slope, near_b, other_b, hb, hid_local)
    kept0, kept1, send0, send1 = grad_mine(after(gf, gu), hid, got1, hb, "down_mine")
    down = ((kept0, swap(send0, "col", 1)), (kept1, swap(send1, "col", 1)))
    theirs = grad_theirs(after(x1, send0), gu, hb, "up_theirs")
    got2 = swap(theirs, "row", 1)
    go, sum1 = up_back(after(gu, theirs), gf, xh1, r1, vecs, near_b, other_b, hb)
    far = far_half(after(down[0][0], go), down[0][1])
    r_down0 = swap(far, "row", 2)
    gn, gkv = attention_mid(after(go, *out, far), att, inv, fq, near_b, other_b, heads, head_width)
    gkv0 = gkv + swap(gkv, "row", 1)
    gkv1 = swap(gkv0, "row", 2)
    kept0, kept1, send0, send1 = grad_mine(after(x1, gkv0), gu, got2, hb, "up_mine")
    up = ((kept0, swap(send0, "col", 1)), (kept1, swap(send1, "col", 1)))
    far = far_half(after(down[1][0], send0), down[1][1])
    r_down1 = swap(far, "row", 2)
    gq, sum_q = query_back(after(gn, far), kv, fq, uq, omegas, heads, head_width)
    down0 = total(after(down[0][0], gq), down[0][1], r_down0)
    z_down0 = Fold(down0)
    gq = gq.reshape(2, hb, tokens)
    att2 = att.reshape(2, hb, tokens)
    theirs = pair_theirs(after(x, down0), gq, go, att2, "pair_theirs")
    got3 = swap(theirs, "row", 1)
    g, sum_kv = key_back(after(gkv0, theirs), gkv1, fk, uk, v, omegas, heads, head_width)
    down1 = total(after(down[1][0], g), down[1][1], r_down1)
    z_down1 = Fold(down1)
    g = g.reshape(2, 2 * hb, tokens)
    sums = (sum1, sum2, bd, bu, sum_q, sum_kv)
    theirs = last_parts(after(x, down1), g, sums, None, "last_theirs")[0]
    got4 = swap(theirs, "row", 1)
    keep3, send3 = pair_mine(after(x, theirs), gq, go, att2, got3, "pair_mine")
    r_y3 = swap(send3, "col", 1)
    far = far_half(after(up[0][0], send3), up[0][1])
    r_up0 = swap(far, "row", 2)
    order = z_down0.middle(far)
    keep4, send4 = last_parts(after(x, order), g, sums, got4, "last_mine")
    r_x4 = swap(send4, "row", 2)
    gin = input_grad(gq, g, after(go, send4), near_a, other_a)
    far = far_half(after(up[1][0], gin[0]), up[1][1])
    r_up1 = swap(far, "row", 2)
    order = z_down1.middle(far)
    far = far_half(after(keep4, order), r_x4)
    r_y4 = swap(far, "col", 1)
    up0 = total(after(up[0][0], far), up[0][1], r_up0)
    z_up0 = Fold(up0)
    order = z_down0.back(up0)
    far = far_half(after(keep3, order), r_y3)
    r_x3 = swap(far, "row", 2)
    gin = [after(gin[0], far), *[after(b, far) for b in gin[1:]]]
    gin = exchange([gin[j] for j in (0, 2, 1, 3)])
    up1 = total(after(up[1][0], far), up[1][1], r_up1)
    z_up1 = Fold(up1)
    order = z_up0.middle(up1)
    order = z_down1.back(order)
    last = total(after(keep4, order), r_x4, r_y4)
    z_last = Fold(last)
    pair = total(after(keep3, last), r_y3, r_x3)
    z_pair = Fold(pair)
    order = z_up1.middle(pair)
    order = z_up0.back(order)
    order = z_last.middle(order)
    order = z_pair.middle(order)
    order = z_up1.back(order)
    out[0] = after(out[0], order)
    out = join_positions(out, row_ref)
    grad_in = join_positions([after(gin[0], out), *gin[1:]], row_ref)
    grad_down = jnp.concatenate((z_down0.result(), z_down1.result()), axis=1).astype(f32)
    grad_up = jnp.concatenate((z_up0.result(), z_up1.result()), axis=1).astype(f32)
    order = z_last.back(grad_in)
    z_pair.back(order)
    last = z_last.result().astype(f32)
    grad_pair = z_pair.result().astype(f32)

    extra = last[feat_local:]
    rows = extra[:7, :feat_local]
    cols = extra[:7, hb:]
    loss = rows[6, 0] / (count[0, 0] * width)
    return (
        out,
        loss,
        grad_in,
        grad_pair[:, :hb],
        cols[0],
        last[:feat_local, :hb],
        cols[1],
        last[:feat_local, hb:],
        cols[2],
        grad_pair[:, hb:],
        rows[0],
        rows[1],
        rows[2],
        grad_up,
        cols[3:].reshape(hid_local),
        grad_down,
        rows[3],
        rows[4],
        rows[5],
    )


def solution(mesh):
    both = P("row", ("dp", "col"))
    in_specs = (
        both, both, P("dp"), P("col", None, None),
        P("row", "col"), P("col"), P("row", "col"), P("col"), P("row", "col"), P("col"),
        P("row", "col"), P("row"), P("row"), P("row"),
        P("row", "col"), P("col"), P("row", "col"), P("row"), P("row"), P("row"),
    )
    out_specs = (
        both, P(), both,
        P("row", "col"), P("col"), P("row", "col"), P("col"), P("row", "col"), P("col"),
        P("row", "col"), P("row"), P("row"), P("row"),
        P("row", "col"), P("col"), P("row", "col"), P("row"), P("row"), P("row"),
    )
    return jax.shard_map(shards, mesh=mesh, in_specs=in_specs, out_specs=out_specs, check_vma=False)
```

```python
import jax
import jax.numpy as jnp
from jax import lax
from jax.experimental import pallas as pl
from jax.experimental.pallas import tpu as pltpu
from jax.sharding import PartitionSpec as P

LOSS_SCALE = 16777216
stabilizer = 2.0
norm_eps = 1e-12
root_half = 0.7071067811865476
inv_root_two_pi = 0.3989422804014327
f32 = jnp.float32
bf16 = jnp.bfloat16
PAD = 8
EXTRA = 16
CUT = 48
ASIDE = 256


def dot(a, b, dims):
    return lax.dot_general(a, b, (dims, ((), ())), preferred_element_type=f32)


def nn(a, b):
    return dot(a, b, ((1,), (0,)))


def nt(a, b):
    return dot(a, b, ((1,), (1,)))


def tn(a, b):
    return dot(a, b, ((0,), (0,)))


def ones_rows(tokens):
    return jnp.ones((8, tokens), bf16)


def call(body, outs, args, name, grid=None, in_specs=None, out_specs=None, scratch=(), limit=40):
    if grid is None:
        grid = (1,)
        in_specs = [single(a.shape) for a in args] if in_specs is None else in_specs
        out_specs = [single(s) for s, _ in outs]
    extra = dict(grid=grid, in_specs=in_specs, out_specs=out_specs)
    args = [a if spec is SMEM else pltpu.with_memory_space_constraint(a, pltpu.HBM) for a, spec in zip(args, in_specs)]
    return pl.pallas_call(
        body,
        out_shape=[pltpu.HBM(s, d) for s, d in outs],
        scratch_shapes=list(scratch),
        compiler_params=pltpu.CompilerParams(vmem_limit_bytes=limit * 1024 * 1024),
        cost_estimate=pl.CostEstimate(flops=1000, bytes_accessed=1000, transcendentals=0),
        name=name,
        **extra,
    )(*args)


def single(shape):
    zeros = (0,) * len(shape)
    return pl.BlockSpec(shape, lambda s: zeros, pipeline_mode=pl.Buffered(1))


def whole(a):
    zeros = (0,) * a.ndim
    return pl.BlockSpec(a.shape, lambda s: zeros)


def whole_out(shape):
    zeros = (0,) * len(shape)
    return pl.BlockSpec(shape, lambda s: zeros)


SMEM = pl.BlockSpec(memory_space=pltpu.SMEM)


def split_positions(shard, row, row_parts):
    k, length = shard.shape
    n = length // row_parts

    def body(row_ref, in_ref, *out_refs):
        r = row_ref[0]
        for j, o_ref in enumerate(out_refs):
            at = pl.multiple_of(jnp.bitwise_xor(r, j) * n, n)
            o_ref[...] = in_ref[:, pl.ds(at, n)].astype(bf16)

    return call(body, [((k, n), bf16)] * row_parts, (row, shard), "split_positions", in_specs=[SMEM, single(shard.shape)])


def join_positions(blocks, row):
    k, n = blocks[0].shape
    parts = len(blocks)

    def body(row_ref, *refs):
        r = row_ref[0]
        o_ref = refs[parts]
        for j in range(parts):
            at = pl.multiple_of(jnp.bitwise_xor(r, j) * n, n)
            o_ref[:, pl.ds(at, n)] = refs[j][...].astype(f32)

    return call(body, [((k, n * parts), f32)], (row, *blocks), "join_positions", in_specs=[SMEM] + [single(b.shape) for b in blocks])[0]


def narrow(parts, steps, name):
    n = parts[0].shape[0]
    widths = [p.shape[1] for p in parts]

    def body(*refs):
        at = 0
        for ref, w in zip(refs, widths):
            refs[-1][:, at : at + w] = ref[...].astype(bf16)
            at += w

    return call(
        body, [((n, sum(widths)), bf16)], parts, name, (steps,),
        [pl.BlockSpec((n // steps, w), lambda s: (s, 0)) for w in widths],
        [pl.BlockSpec((n // steps, sum(widths)), lambda s: (s, 0))],
    )[0]


def narrow_small(parts, vecs, biases, up_bias, name):
    n, hb = parts[0].shape
    width = hb * len(parts)
    small = [v.reshape(1, v.shape[0]) for v in (*vecs, *biases, up_bias)]
    nv = len(vecs)
    rest = up_bias.shape[0] - width

    def body(*refs):
        p_refs = refs[: len(parts)]
        v_refs = refs[len(parts) : len(parts) + nv]
        b_refs = refs[len(parts) + nv : len(parts) + nv + len(biases)]
        up_ref, o_ref, small_ref = refs[len(parts) + nv + len(biases) :]
        small_ref[...] = jnp.zeros(small_ref.shape, f32)
        for m, ref in enumerate(v_refs):
            small_ref[m : m + 1, :n] = ref[...]
        for m, (ref, b_ref) in enumerate(zip(p_refs, b_refs)):
            o_ref[:n, m * hb : (m + 1) * hb] = ref[...].astype(bf16)
            small_ref[nv : nv + 1, m * hb : (m + 1) * hb] = b_ref[...]
        small_ref[nv + 1 : nv + 2] = up_ref[:, :width]
        small_ref[0:1, ASIDE : ASIDE + rest] = up_ref[:, width:]
        value = small_ref[...]
        high = value.astype(bf16).astype(f32)
        o_ref[n:] = jnp.concatenate((high, value - high), axis=0).astype(bf16)

    return call(body, [((n + EXTRA, width), bf16)], (*parts, *small), name, scratch=[pltpu.VMEM((8, width), f32)])[0]


def small_rows(ref, k):
    v = ref[k : k + EXTRA].astype(f32)
    return v[0:8] + v[8:16]


def attention_in(xs, near, other, omegas, keep, head_local, head_width, hid_local):
    k, tokens = xs[0].shape
    feats = omegas[0].shape[2]
    heads = 2 * head_local
    hb = head_local * head_width
    rows = head_width + PAD
    factor = head_width ** (-0.25)
    n_near, n_other = len(near), len(other)

    def body(*refs):
        x_in = refs[:4]
        near_refs = refs[4 : 4 + n_near]
        other_refs = refs[4 + n_near : 4 + n_near + n_other]
        (om0_ref, om1_ref, keep_ref, x_ref, fq_ref, fk_ref, uq_ref, uk_ref, v_ref, kv_ref, vec_ref, up_ref) = refs[
            4 + n_near + n_other :
        ]
        for p in range(4):
            vec_ref[:, p * k : (p + 1) * k] = small_rows(near_refs[p], k)[:, :k]
        up_ref[...] = jnp.zeros(up_ref.shape, f32)
        for p in range(4):
            x_ref[p * k : (p + 1) * k] = x_in[p][...]
        xv = x_ref[...]
        ones = jnp.ones((PAD, tokens), bf16)
        for i, pieces in enumerate((near_refs, other_refs)):
            omega_ref = (om0_ref, om1_ref)[i]
            small = small_rows(pieces[0], k)
            up_ref[i : i + 1, : 3 * hb] = small[7:8]
            up_ref[i : i + 1, 3 * hb :] = small[0:1, ASIDE : ASIDE + hid_local - 3 * hb]
            triple = tn(jnp.concatenate([p[:k] for p in pieces], axis=0), xv) + jnp.transpose(small)[:, 6:7]
            for hl in range(head_local):
                h = i * head_local + hl
                at = h * head_width
                lo = hl * head_width
                value = triple[2 * hb + lo : 2 * hb + lo + head_width].astype(bf16)
                v_ref[at : at + head_width] = value
                for base, u_ref, f_ref, mask in ((0, uq_ref, fq_ref, False), (hb, uk_ref, fk_ref, True)):
                    u = triple[base + lo : base + lo + head_width] * factor
                    ub = u.astype(bf16)
                    u_ref[at : at + head_width] = ub
                    z = tn(omega_ref[hl], ub)
                    feat = jnp.exp(z - (0.5 * jnp.sum(u * u, axis=0, keepdims=True) + stabilizer))
                    if mask:
                        feat = feat * keep_ref[0:1]
                    feat = feat.astype(bf16)
                    f_ref[h * feats : (h + 1) * feats] = feat
                kv_ref[h * rows : (h + 1) * rows] = nt(jnp.concatenate((value, ones), axis=0), feat).astype(bf16)

    n = heads * head_width
    outs = [((4 * k, tokens), bf16)] + [((heads * feats, tokens), bf16)] * 2 + [((n, tokens), bf16)] * 3
    outs += [((heads * rows, feats), bf16), ((8, 4 * k), f32), ((8, hid_local), f32)]
    return call(body, outs, (*xs, *near, *other, *omegas, keep), "attention_in")


def weight_specs(pieces, block, first):
    return [pl.BlockSpec((p.shape[0], block), lambda s, f=first: (0, f + s)) for p in pieces]


def fixed_specs(pieces, block, at):
    return [pl.BlockSpec((p.shape[0], block), lambda s: (0, at)) for p in pieces]


def rows_of(refs):
    return jnp.concatenate([r[...] for r in refs], axis=0)


def middle(kv0, kv1, fq, x, near, other, vecs, up_bias, target, keep, scale, heads, head_width, hid_local):
    width, tokens = x.shape
    feats = kv0.shape[1]
    rows = head_width + PAD
    hb = heads * head_width // 2
    steps = hid_local // hb
    k = width // 4
    nn_, no = len(near), len(other)
    np_ = nn_ + no

    def body(*refs):
        kv0_ref, kv1_ref, fq_ref, x_ref = refs[:4]
        out_w = refs[4 : 4 + np_]
        up_w = refs[4 + np_ : 4 + 2 * np_]
        down_w = refs[4 + 2 * np_ : 4 + 3 * np_]
        (vec_ref, upb_ref, t0, t1, t2, t3, keep_ref, scale_ref,
         kv_ref, att_ref, inv_ref, xh1_ref, r1_ref, x1_ref, hid_ref, slope_ref, gf_ref, sum_ref,
         o0, o1, o2, o3, acc_ref, vec_s) = refs[4 + 3 * np_ :]
        step = pl.program_id(0)

        @pl.when(step == 0)
        def _():
            vec = jnp.transpose(vec_ref[...])
            vec_s[...] = vec
            kv_ref[...] = (kv0_ref[...].astype(f32) + kv1_ref[...].astype(f32)).astype(bf16)
            for h in range(heads):
                both = nn(kv_ref[h * rows : (h + 1) * rows], fq_ref[h * feats : (h + 1) * feats])
                inverse = 1.0 / both[head_width : head_width + 1]
                inv_ref[h : h + 1] = inverse
                att_ref[h * head_width : (h + 1) * head_width] = (both[:head_width] * inverse).astype(bf16)
            w = jnp.concatenate((rows_of(out_w[:nn_]), rows_of(out_w[nn_:])), axis=1)
            h1 = nn(w, att_ref[...]) + x_ref[...].astype(f32) + vec[:, 0:1]
            mean = jnp.sum(h1, axis=0, keepdims=True) * (1.0 / width)
            h1 = h1 - mean
            r1 = lax.rsqrt(jnp.sum(h1 * h1, axis=0, keepdims=True) * (1.0 / width) + norm_eps)
            h1 = h1 * r1
            r1_ref[...] = jnp.broadcast_to(r1, (8, tokens))
            xh1_ref[...] = h1.astype(bf16)
            x1 = h1 * vec[:, 1:2] + vec[:, 2:3]
            x1_ref[...] = x1.astype(bf16)
            acc_ref[...] = x1 + vec[:, 3:4]

        x1b = x1_ref[...]
        bias = jnp.transpose(upb_ref[...])
        total = acc_ref[...]
        for i, (a, b) in enumerate(((0, nn_), (nn_, np_))):
            up = tn(rows_of(up_w[a:b]), x1b) + bias[:, i : i + 1]
            gate = 0.5 * (1.0 + lax.erf(up * root_half))
            slope_ref[i] = (gate + up * inv_root_two_pi * jnp.exp(-0.5 * up * up)).astype(bf16)
            hid = (up * gate).astype(bf16)
            hid_ref[i] = hid
            total = total + nn(rows_of(down_w[a:b]), hid)
        acc_ref[...] = total

        @pl.when(step == steps - 1)
        def _():
            vec = vec_s[...]
            h2 = acc_ref[...]
            mean = jnp.sum(h2, axis=0, keepdims=True) * (1.0 / width)
            h2 = h2 - mean
            r2 = lax.rsqrt(jnp.sum(h2 * h2, axis=0, keepdims=True) * (1.0 / width) + norm_eps)
            h2 = h2 * r2
            out = h2 * vec[:, 4:5] + vec[:, 5:6]
            for p, o_ref in enumerate((o0, o1, o2, o3)):
                o_ref[...] = out[p * k : (p + 1) * k].astype(bf16)
            target = jnp.concatenate((t0[...], t1[...], t2[...], t3[...]), axis=0).astype(f32)
            diff = (out - target) * keep_ref[0:1]
            g = diff * scale_ref[0:1, 0:1]
            ones = ones_rows(tokens)
            sum_ref[0:8] = nt(ones, (g * h2).astype(bf16))
            sum_ref[8:16] = nt(ones, g.astype(bf16))
            sum_ref[16:24] = jnp.full((8, width), jnp.sum(diff * diff), f32)
            a = g * vec[:, 4:5]
            first = jnp.sum(a, axis=0, keepdims=True) * (1.0 / width)
            second = jnp.sum(a * h2, axis=0, keepdims=True) * (1.0 / width)
            gf_ref[...] = (r2 * (a - first - h2 * second)).astype(bf16)

    outs = [
        ((heads * rows, feats), bf16), ((width, tokens), bf16), ((16, tokens), f32), ((width, tokens), bf16),
        ((8, tokens), f32), ((width, tokens), bf16), ((2, hid_local, tokens), bf16), ((2, hid_local, tokens), bf16),
        ((width, tokens), bf16), ((24, width), f32),
    ] + [((k, tokens), bf16)] * 4
    pieces = (*near, *other)
    args = (kv0, kv1, fq, x, *pieces, *pieces, *pieces, vecs, up_bias, *target, keep, scale)
    in_specs = [whole(a) for a in (kv0, kv1, fq, x)]
    in_specs += fixed_specs(pieces, hb, 0) + weight_specs(pieces, hb, 1) + weight_specs(pieces, hb, 1 + steps)
    in_specs += [whole(vecs), pl.BlockSpec((8, hb), lambda s: (0, s))] + [whole(t) for t in target] + [whole(keep), whole(scale)]
    out_specs = [whole_out(s) for s, _ in outs]
    out_specs[6] = out_specs[7] = pl.BlockSpec((2, hb, tokens), lambda s: (0, s, 0))
    scratch = [pltpu.VMEM((width, tokens), f32), pltpu.VMEM((width, 8), f32)]
    return call(body, outs, args, "middle", (steps,), in_specs, out_specs, scratch, limit=56)


def grad_theirs(left, right, block, name):
    n, tokens = left.shape
    k = right.shape[1]
    half = n // 2

    def body(l_ref, r_ref, o_ref):
        for i in range(2):
            o_ref[i] = nt(l_ref[...], r_ref[i]).astype(bf16)

    return call(
        body, [((2, half, k), bf16)], (left, right), name, (k // block,),
        [pl.BlockSpec((half, tokens), lambda s: (1, 0)), pl.BlockSpec((2, block, tokens), lambda s: (0, s, 0))],
        [pl.BlockSpec((2, half, block), lambda s: (0, 0, s))],
    )[0]


def grad_mine(left, right, got, block, name):
    n, tokens = left.shape
    k = right.shape[1]
    half = n // 2
    share = k // block // 2

    def body(l_ref, r_ref, got_ref, keep0, keep1, send0, send1):
        step = pl.program_id(0)

        def part(keep_ref, send_ref):
            for i, o_ref in enumerate((keep_ref, send_ref)):
                o_ref[...] = (nt(l_ref[...], r_ref[i]) + got_ref[i].astype(f32)).astype(bf16)

        pl.when(step < share)(lambda: part(keep0, send0))
        pl.when(step >= share)(lambda: part(keep1, send1))

    first = pl.BlockSpec((half, block), lambda s: (0, jnp.minimum(s, share - 1)))
    second = pl.BlockSpec((half, block), lambda s: (0, jnp.maximum(s - share, 0)))
    return call(
        body, [((half, k // 2), bf16)] * 4, (left, right, got), name, (2 * share,),
        [
            pl.BlockSpec((half, tokens), lambda s: (0, 0)),
            pl.BlockSpec((2, block, tokens), lambda s: (0, s, 0)),
            pl.BlockSpec((2, half, block), lambda s: (0, 0, s)),
        ],
        [first, second, first, second],
    )


def pair_theirs(x, gq, go, att, name):
    n, tokens = x.shape
    half = n // 2
    k = gq.shape[1]

    def body(x_ref, gq_ref, go_ref, att_ref, o_ref):
        for i in range(2):
            o_ref[i, :, :k] = nt(x_ref[half:], gq_ref[i]).astype(bf16)
            o_ref[i, :, k:] = nt(go_ref[half:], att_ref[i]).astype(bf16)

    return call(body, [((2, half, 2 * k), bf16)], (x, gq, go, att), name)[0]


def pair_mine(x, gq, go, att, got, name):
    n, tokens = x.shape
    half = n // 2
    k = gq.shape[1]

    def body(x_ref, gq_ref, go_ref, att_ref, got_ref, keep_ref, send_ref):
        for i, o_ref in enumerate((keep_ref, send_ref)):
            o_ref[:, :k] = (nt(x_ref[:half], gq_ref[i]) + got_ref[i, :, :k].astype(f32)).astype(bf16)
            o_ref[:, k:] = (nt(go_ref[:half], att_ref[i]) + got_ref[i, :, k:].astype(f32)).astype(bf16)

    return call(body, [((half, 2 * k), bf16)] * 2, (x, gq, go, att, got), name)


def down_back(gf, slope, near, other, hb, hid_local):
    width, tokens = gf.shape
    steps = hid_local // hb
    nn_, no = len(near), len(other)
    pieces = (*near, *other)

    def body(gf_ref, slope_ref, *refs):
        gu_ref, sum_ref, bd_ref = refs[nn_ + no :]
        g = gf_ref[...]
        ones = ones_rows(tokens)

        @pl.when(pl.program_id(0) == 0)
        def _():
            bd_ref[...] = nt(ones, g)

        for i, w in enumerate((refs[:nn_], refs[nn_ : nn_ + no])):
            v = (tn(rows_of(w), g) * slope_ref[i].astype(f32)).astype(bf16)
            gu_ref[i] = v
            sum_ref[i] = nt(ones, v)

    spec = pl.BlockSpec((2, hb, tokens), lambda s: (0, s, 0))
    return call(
        body, [((2, hid_local, tokens), bf16), ((2, 8, hid_local), f32), ((8, width), f32)], (gf, slope, *pieces), "down_back",
        (steps,), [whole(gf), spec] + weight_specs(pieces, hb, 1 + steps),
        [spec, pl.BlockSpec((2, 8, hb), lambda s: (0, 0, s)), whole_out((8, width))],
    )


def up_back(gu, gf, xh1, r1, vecs, near, other, hb):
    width, tokens = gf.shape
    steps = gu.shape[1] // hb
    nn_, no = len(near), len(other)
    pieces = (*near, *other)

    def body(gu_ref, gf_ref, xh_ref, r1_ref, vec_ref, *refs):
        go_ref, sum_ref, acc_ref = refs[nn_ + no :]
        step = pl.program_id(0)

        @pl.when(step == 0)
        def _():
            acc_ref[...] = gf_ref[...].astype(f32)

        acc_ref[...] += nn(rows_of(refs[:nn_]), gu_ref[0]) + nn(rows_of(refs[nn_ : nn_ + no]), gu_ref[1])

        @pl.when(step == steps - 1)
        def _():
            vec = jnp.transpose(vec_ref[...])
            g = acc_ref[...]
            xh = xh_ref[...].astype(f32)
            ones = ones_rows(tokens)
            sum_ref[0:8] = nt(ones, (g * xh).astype(bf16))
            sum_ref[8:16] = nt(ones, g.astype(bf16))
            a = g * vec[:, 1:2]
            first = jnp.sum(a, axis=0, keepdims=True) * (1.0 / width)
            second = jnp.sum(a * xh, axis=0, keepdims=True) * (1.0 / width)
            go = (r1_ref[0:1] * (a - first - xh * second)).astype(bf16)
            go_ref[...] = go
            sum_ref[16:24] = nt(ones, go)

    return call(
        body, [((width, tokens), bf16), ((24, width), f32)], (gu, gf, xh1, r1, vecs, *pieces), "up_back", (steps,),
        [pl.BlockSpec((2, hb, tokens), lambda s: (0, s, 0))] + [whole(a) for a in (gf, xh1, r1, vecs)] + weight_specs(pieces, hb, 1),
        [whole_out((width, tokens)), whole_out((24, width))], [pltpu.VMEM((width, tokens), f32)],
    )


def attention_mid(go, att, inv, fq, near, other, heads, head_width):
    width, tokens = go.shape
    feats = fq.shape[0] // heads
    hb = heads * head_width // 2
    rows = head_width + PAD
    nn_, no = len(near), len(other)
    pieces = (*near, *other)

    def body(go_ref, att_ref, inv_ref, fq_ref, *refs):
        gn_ref, kv_ref = refs[nn_ + no :]
        g = go_ref[...]
        zeros = jnp.zeros((PAD - 1, tokens), f32)
        for i, w in enumerate((refs[:nn_], refs[nn_ : nn_ + no])):
            ga = tn(rows_of(w), g)
            for hl in range(heads // 2):
                h = i * (heads // 2) + hl
                gh = ga[hl * head_width : (hl + 1) * head_width]
                inverse = inv_ref[h : h + 1]
                a = att_ref[h * head_width : (h + 1) * head_width].astype(f32)
                gd = -jnp.sum(gh * a, axis=0, keepdims=True) * inverse
                both = jnp.concatenate((gh * inverse, gd, zeros), axis=0).astype(bf16)
                gn_ref[h * rows : (h + 1) * rows] = both
                kv_ref[h * rows : (h + 1) * rows] = nt(both, fq_ref[h * feats : (h + 1) * feats]).astype(bf16)

    outs = [((heads * rows, tokens), bf16), ((heads * rows, feats), bf16)]
    args = (go, att, inv, fq, *pieces)
    return call(
        body, outs, args, "attention_mid", (1,), [whole(a) for a in args[:4]] + fixed_specs(pieces, hb, 0),
        [whole_out(s) for s, _ in outs],
    )


def query_back(gn, kv, fq, uq, omegas, heads, head_width):
    n, tokens = uq.shape
    feats = fq.shape[0] // heads
    rows = head_width + PAD
    factor = head_width ** (-0.25)

    def body(gn_ref, kv_ref, fq_ref, uq_ref, om0_ref, om1_ref, gq_ref, sum_ref):
        for h in range(heads):
            om_ref = (om0_ref, om1_ref)[h // (heads // 2)]
            e = tn(kv_ref[h * rows : (h + 1) * rows], gn_ref[h * rows : (h + 1) * rows])
            e = e * fq_ref[h * feats : (h + 1) * feats].astype(f32)
            s = jnp.sum(e, axis=0, keepdims=True)
            u = uq_ref[h * head_width : (h + 1) * head_width].astype(f32)
            gq_ref[h * head_width : (h + 1) * head_width] = (
                factor * (nn(om_ref[h % (heads // 2)], e.astype(bf16)) - s * u)
            ).astype(bf16)
        sum_ref[...] = nt(ones_rows(tokens), gq_ref[...])

    return call(body, [((n, tokens), bf16), ((8, n), f32)], (gn, kv, fq, uq, *omegas), "query_back")


def key_back(gkv0, gkv1, fk, uk, v, omegas, heads, head_width):
    n, tokens = uk.shape
    feats = fk.shape[0] // heads
    rows = head_width + PAD
    factor = head_width ** (-0.25)
    hl_n = heads // 2
    hb = hl_n * head_width

    def body(gkv0_ref, gkv1_ref, fk_ref, uk_ref, v_ref, om0_ref, om1_ref, g_ref, sum_ref):
        ones = jnp.ones((PAD, tokens), bf16)
        for h in range(heads):
            i, hl = divmod(h, hl_n)
            base = i * 2 * hb + hl * head_width
            kv = (gkv0_ref[h * rows : (h + 1) * rows].astype(f32) + gkv1_ref[h * rows : (h + 1) * rows].astype(f32)).astype(bf16)
            f = fk_ref[h * feats : (h + 1) * feats]
            at = h * head_width
            value = jnp.concatenate((v_ref[at : at + head_width], ones), axis=0)
            e = tn(kv, value) * f.astype(f32)
            s = jnp.sum(e, axis=0, keepdims=True)
            u = uk_ref[at : at + head_width].astype(f32)
            g_ref[base : base + head_width] = (
                factor * (nn((om0_ref, om1_ref)[i][hl], e.astype(bf16)) - s * u)
            ).astype(bf16)
            g_ref[base + hb : base + hb + head_width] = nn(kv[:head_width], f).astype(bf16)
        sum_ref[...] = nt(ones_rows(tokens), g_ref[...])

    return call(body, [((2 * n, tokens), bf16), ((8, 2 * n), f32)], (gkv0, gkv1, fk, uk, v, *omegas), "key_back")


def last_parts(x, g, sums, got, name):
    sum1, sum2, bd, bu, sum_q, sum_kv = sums
    n, tokens = x.shape
    q = n // 4
    k = g.shape[1]
    hb = k // 2
    hid_local = bu.shape[2]
    ups = hid_local // hb
    rows = q + EXTRA
    which = 0 if got is not None else 1

    def body(x_ref, g_ref, s1_ref, s2_ref, bd_ref, bu_ref, sq_ref, skv_ref, *refs):
        if got is None:
            o_ref, row_s, col_s = refs
        else:
            got_ref, keep_ref, send_ref, row_s, col_s = refs
        for m, v in enumerate((s1_ref[16:17], s1_ref[0:1], s1_ref[8:9], bd_ref[0:1], s2_ref[0:1], s2_ref[8:9], s2_ref[16:17])):
            row_s[m : m + 1] = v
        row_s[7:8] = jnp.zeros((1, n), f32)
        col_s[...] = jnp.zeros(col_s.shape, f32)
        for i in range(2):
            col_s[i, 0:1] = sq_ref[0:1, i * hb : (i + 1) * hb]
            col_s[i, 1:2] = skv_ref[0:1, i * k : i * k + hb]
            col_s[i, 2:3] = skv_ref[0:1, i * k + hb : (i + 1) * k]
            for u in range(ups):
                col_s[i, 3 + u : 4 + u] = bu_ref[i, 0:1, u * hb : (u + 1) * hb]
        for i in range(2):
            for jx in range(2):
                p = 2 * which + jx
                main = nt(x_ref[p * q : (p + 1) * q], g_ref[i])
                small = row_s[:, p * q : (p + 1) * q]
                small = jnp.concatenate((small, jnp.zeros((8, hb - q), f32), col_s[i]), axis=1)
                small = jnp.concatenate((small, jnp.zeros((EXTRA - 8, k), f32)), axis=0)
                if got is None:
                    o_ref[i, jx, :q] = main.astype(bf16)
                    o_ref[i, jx, q:] = small.astype(bf16)
                else:
                    o = send_ref if jx else keep_ref
                    o[i * rows : i * rows + q] = (main + got_ref[i, jx, :q].astype(f32)).astype(bf16)
                    o[i * rows + q : (i + 1) * rows] = (small + got_ref[i, jx, q:].astype(f32)).astype(bf16)

    outs = [((2, 2, rows, k), bf16)] if got is None else [((2 * rows, k), bf16)] * 2
    args = (x, g, *sums) if got is None else (x, g, *sums, got)
    return call(body, outs, args, name, scratch=[pltpu.VMEM((8, n), f32), pltpu.VMEM((2, 8, hb), f32)])


def input_grad(gq, g, go, near, other):
    width, tokens = go.shape
    hb = gq.shape[1]
    k = width // 4
    nn_, no = len(near), len(other)

    def body(gq_ref, g_ref, go_ref, *refs):
        total = go_ref[...].astype(f32)
        for i, w in enumerate((refs[:nn_], refs[nn_ : nn_ + no])):
            w = jnp.concatenate([r[:k] for r in w], axis=0)
            total = total + nn(w[:, :hb], gq_ref[i]) + nn(w[:, hb:], g_ref[i])
        for p, o_ref in enumerate(refs[nn_ + no :]):
            o_ref[...] = total[p * k : (p + 1) * k].astype(bf16)

    return call(body, [((k, tokens), bf16)] * 4, (gq, g, go, *near, *other), "input_grad")


def swap(value, axis, mask):
    size = lax.axis_size(axis)
    return lax.ppermute(value, axis, [(s, s ^ mask) for s in range(size)])


def after(value, *others):
    return lax.optimization_barrier((value, *others))[0]


class Fold:
    def __init__(self, value):
        self.value = value
        self.four = lax.axis_size("dp") == 4
        if self.four:
            self.got = lax.ppermute(value, "dp", [(0, 1), (3, 2)])
        else:
            self.value = lax.psum(value, "dp")

    def middle(self, order):
        if not self.four:
            return order
        self.value = after(self.value, order) + self.got
        self.got = lax.ppermute(self.value, "dp", [(1, 2), (2, 1)])
        return self.value

    def back(self, order):
        if not self.four:
            return order
        self.value = after(self.value, order) + self.got
        self.got = lax.ppermute(self.value, "dp", [(1, 0), (2, 3)])
        return self.value

    def result(self):
        if not self.four:
            return self.value
        index = lax.axis_index("dp")
        inner = jnp.logical_or(index == 1, index == 2)
        return jnp.where(inner, self.value, self.got)


def total(keep, got, last):
    n = keep.shape[0] // 2
    return keep[:n] + got[:n] + last


def far_half(keep, got):
    n = keep.shape[0] // 2
    return keep[n:] + got[n:]


def exchange(blocks):
    return [blocks[0]] + [swap(blocks[j], "row", j) for j in (1, 2, 3)]


def reduce_small(value, axis):
    step = 1
    while step < lax.axis_size(axis):
        value = value + swap(value, axis, step)
        step *= 2
    return value


def shards(
    inputs, teacher, lengths, omega,
    w_query, b_query, w_key, b_key, w_value, b_value, w_out, b_out,
    norm1_gain, norm1_bias, w_up, up_bias, w_down, b_down, norm2_gain, norm2_bias,
):
    row_parts = lax.axis_size("row")
    feat_local, seq_length = inputs.shape
    width = feat_local * row_parts
    head_local, head_width, feats = omega.shape
    heads = head_local * lax.axis_size("col")
    tokens = seq_length // row_parts
    hb = head_local * head_width
    hid_local = w_up.shape[1]
    row = lax.axis_index("row")
    col = lax.axis_index("col")
    row_ref = row.astype(jnp.int32).reshape(1)

    omegas = (omega, swap(omega, "col", 1))
    vecs = (b_out, norm1_gain, norm1_bias, b_down, norm2_gain, norm2_bias)
    ins = split_positions(inputs, row_ref, row_parts)
    ins_got = exchange(ins)
    xs = [ins_got[j] for j in (0, 2, 1, 3)]
    own_a = narrow_small((after(w_query, *ins), w_key, w_value), vecs, (b_query, b_key, b_value), up_bias, "narrow_a")
    a_y = swap(own_a, "col", 1)
    a_x = swap(own_a, "row", 2)
    a_far = swap(after(a_x, a_y, omegas[1]), "col", 1)
    near_a = (own_a, a_x, swap(own_a, "row", 1), swap(a_x, "row", 1))
    other_a = (a_y, a_far, swap(a_y, "row", 1), swap(a_far, "row", 1))
    count = reduce_small(jnp.sum(lengths).astype(f32).reshape(1, 1) + jnp.zeros((8, 128), f32), "dp")
    own_b = narrow((after(w_out, own_a, omegas[1], count), w_up, w_down), 3, "narrow_b")
    b_x = swap(after(own_b, a_x, ins_got[2], ins_got[3]), "row", 2)
    b_y = swap(after(own_b, a_far), "col", 1)
    length = lax.dynamic_index_in_dim(lengths, col, 0, False)
    keep = ((row * tokens + jnp.arange(tokens, dtype=jnp.int32)) < length).astype(f32)
    keep = jnp.broadcast_to(keep[None, :], (8, tokens))
    scale = (2.0 * LOSS_SCALE) / (count * width)

    x, fq, fk, uq, uk, v, kv, vecs, up_bias_all = attention_in(
        xs, near_a, other_a, omegas, keep, head_local, head_width, hid_local
    )
    kv0 = kv + swap(kv, "row", 1)
    kv1 = swap(kv0, "row", 2)
    theirs = split_positions(after(teacher, kv0), row_ref, row_parts)
    teach = exchange(theirs)
    target = [teach[j] for j in (0, 2, 1, 3)]
    b_x = after(b_x, kv0, theirs[0])
    b_y = after(b_y, kv0, theirs[0])
    b_far_y = swap(b_x[CUT:], "col", 1)
    b_far_x = swap(b_y[:CUT], "row", 2)
    near_b = (own_b, b_x)
    near_b = near_b + tuple(swap(p, "row", 1) for p in near_b)
    other_b = (b_y, b_far_x, after(b_far_y, kv1, b_far_x, teach[2], teach[3]))
    other_b = other_b + tuple(swap(p, "row", 1) for p in other_b)
    kv, att, inv, xh1, r1, x1, hid, slope, gf, sum2, *out = middle(
        kv0, kv1, fq, x, near_b, other_b, vecs, up_bias_all, target, keep, scale, heads, head_width, hid_local
    )
    out = exchange([out[j] for j in (0, 2, 1, 3)])

    theirs = grad_theirs(gf, hid, hb, "down_theirs")
    got1 = swap(theirs, "row", 1)
    gu, bu, bd = down_back(after(gf, theirs), slope, near_b, other_b, hb, hid_local)
    kept0, kept1, send0, send1 = grad_mine(after(gf, gu), hid, got1, hb, "down_mine")
    down = ((kept0, swap(send0, "col", 1)), (kept1, swap(send1, "col", 1)))
    theirs = grad_theirs(after(x1, send0), gu, hb, "up_theirs")
    got2 = swap(theirs, "row", 1)
    go, sum1 = up_back(after(gu, theirs), gf, xh1, r1, vecs, near_b, other_b, hb)
    far = far_half(after(down[0][0], go), down[0][1])
    r_down0 = swap(far, "row", 2)
    gn, gkv = attention_mid(after(go, *out, far), att, inv, fq, near_b, other_b, heads, head_width)
    gkv0 = gkv + swap(gkv, "row", 1)
    gkv1 = swap(gkv0, "row", 2)
    kept0, kept1, send0, send1 = grad_mine(after(x1, gkv0), gu, got2, hb, "up_mine")
    up = ((kept0, swap(send0, "col", 1)), (kept1, swap(send1, "col", 1)))
    far = far_half(after(down[1][0], send0), down[1][1])
    r_down1 = swap(far, "row", 2)
    gq, sum_q = query_back(after(gn, far), kv, fq, uq, omegas, heads, head_width)
    down0 = total(after(down[0][0], gq), down[0][1], r_down0)
    z_down0 = Fold(down0)
    gq = gq.reshape(2, hb, tokens)
    att2 = att.reshape(2, hb, tokens)
    theirs = pair_theirs(after(x, down0), gq, go, att2, "pair_theirs")
    got3 = swap(theirs, "row", 1)
    g, sum_kv = key_back(after(gkv0, theirs), gkv1, fk, uk, v, omegas, heads, head_width)
    down1 = total(after(down[1][0], g), down[1][1], r_down1)
    z_down1 = Fold(down1)
    far = far_half(after(up[0][0], down1), up[0][1])
    r_up0 = swap(far, "row", 2)
    g = g.reshape(2, 2 * hb, tokens)
    sums = (sum1, sum2, bd, bu, sum_q, sum_kv)
    theirs = last_parts(after(x, far), g, sums, None, "last_theirs")[0]
    got4 = swap(theirs, "row", 1)
    keep3, send3 = pair_mine(after(x, theirs), gq, go, att2, got3, "pair_mine")
    r_y3 = swap(send3, "col", 1)
    order = z_down0.middle(send3)
    keep4, send4 = last_parts(after(x, order), g, sums, got4, "last_mine")
    r_x4 = swap(send4, "row", 2)
    gin = input_grad(gq, g, after(go, send4), near_a, other_a)
    far = far_half(after(up[1][0], gin[0]), up[1][1])
    r_up1 = swap(far, "row", 2)
    order = z_down1.middle(far)
    up0 = total(after(up[0][0], order), up[0][1], r_up0)
    z_up0 = Fold(up0)
    order = z_down0.back(up0)
    far = far_half(after(keep3, order), r_y3)
    r_x3 = swap(far, "row", 2)
    far = far_half(after(keep4, far), r_x4)
    r_y4 = swap(far, "col", 1)
    gin = exchange([after(gin[j], far) for j in (0, 2, 1, 3)])
    up1 = total(after(up[1][0], far), up[1][1], r_up1)
    z_up1 = Fold(up1)
    order = z_up0.middle(up1)
    order = z_down1.back(order)
    pair = total(after(keep3, order), r_y3, r_x3)
    z_pair = Fold(pair)
    last = total(after(keep4, pair), r_x4, r_y4)
    z_last = Fold(last)
    order = z_up1.middle(last)
    order = z_up0.back(order)
    order = z_pair.middle(order)
    order = z_last.middle(order)
    order = z_up1.back(order)
    out[0] = after(out[0], order)
    out = join_positions(out, row_ref)
    grad_in = join_positions([after(gin[0], out), *gin[1:]], row_ref)
    grad_down = jnp.concatenate((z_down0.result(), z_down1.result()), axis=1).astype(f32)
    grad_up = jnp.concatenate((z_up0.result(), z_up1.result()), axis=1).astype(f32)
    order = z_pair.back(grad_in)
    z_last.back(order)
    last = z_last.result().astype(f32)
    grad_pair = z_pair.result().astype(f32)

    extra = last[feat_local:]
    rows = extra[:7, :feat_local]
    cols = extra[:7, hb:]
    loss = rows[6, 0] / (count[0, 0] * width)
    return (
        out,
        loss,
        grad_in,
        grad_pair[:, :hb],
        cols[0],
        last[:feat_local, :hb],
        cols[1],
        last[:feat_local, hb:],
        cols[2],
        grad_pair[:, hb:],
        rows[0],
        rows[1],
        rows[2],
        grad_up,
        cols[3:].reshape(hid_local),
        grad_down,
        rows[3],
        rows[4],
        rows[5],
    )


def solution(mesh):
    both = P("row", ("dp", "col"))
    in_specs = (
        both, both, P("dp"), P("col", None, None),
        P("row", "col"), P("col"), P("row", "col"), P("col"), P("row", "col"), P("col"),
        P("row", "col"), P("row"), P("row"), P("row"),
        P("row", "col"), P("col"), P("row", "col"), P("row"), P("row"), P("row"),
    )
    out_specs = (
        both, P(), both,
        P("row", "col"), P("col"), P("row", "col"), P("col"), P("row", "col"), P("col"),
        P("row", "col"), P("row"), P("row"), P("row"),
        P("row", "col"), P("col"), P("row", "col"), P("row"), P("row"), P("row"),
    )
    return jax.shard_map(shards, mesh=mesh, in_specs=in_specs, out_specs=out_specs, check_vma=False)
```

```python
import jax
import jax.numpy as jnp
from jax import lax
from jax.experimental import pallas as pl
from jax.experimental.pallas import tpu as pltpu
from jax.sharding import PartitionSpec as P

LOSS_SCALE = 16777216
stabilizer = 2.0
norm_eps = 1e-12
root_half = 0.7071067811865476
inv_root_two_pi = 0.3989422804014327
f32 = jnp.float32
bf16 = jnp.bfloat16
PAD = 8
EXTRA = 16
CUT = 48
ASIDE = 256


def dot(a, b, dims):
    return lax.dot_general(a, b, (dims, ((), ())), preferred_element_type=f32)


def nn(a, b):
    return dot(a, b, ((1,), (0,)))


def nt(a, b):
    return dot(a, b, ((1,), (1,)))


def tn(a, b):
    return dot(a, b, ((0,), (0,)))


def ones_rows(tokens):
    return jnp.ones((8, tokens), bf16)


def call(body, outs, args, name, grid=None, in_specs=None, out_specs=None, scratch=(), limit=40, pinned=False):
    if grid is None:
        grid = (1,)
        in_specs = [single(a.shape) for a in args] if in_specs is None else in_specs
        out_specs = [single(s) for s, _ in outs]
    extra = dict(grid=grid, in_specs=in_specs, out_specs=out_specs)
    if pinned:
        args = [a if p is SMEM else pltpu.with_memory_space_constraint(a, pltpu.HBM) for a, p in zip(args, in_specs)]
    make = pltpu.HBM if pinned else jax.ShapeDtypeStruct
    return pl.pallas_call(
        body,
        out_shape=[make(s, d) for s, d in outs],
        scratch_shapes=list(scratch),
        compiler_params=pltpu.CompilerParams(vmem_limit_bytes=limit * 1024 * 1024),
        cost_estimate=pl.CostEstimate(flops=1000, bytes_accessed=1000, transcendentals=0),
        name=name,
        **extra,
    )(*args)


def single(shape):
    zeros = (0,) * len(shape)
    return pl.BlockSpec(shape, lambda s: zeros, pipeline_mode=pl.Buffered(1))


def whole(a):
    zeros = (0,) * a.ndim
    return pl.BlockSpec(a.shape, lambda s: zeros)


def whole_out(shape):
    zeros = (0,) * len(shape)
    return pl.BlockSpec(shape, lambda s: zeros)


SMEM = pl.BlockSpec(memory_space=pltpu.SMEM)


def split_positions(shard, row, row_parts):
    k, length = shard.shape
    n = length // row_parts

    def body(row_ref, in_ref, *out_refs):
        r = row_ref[0]
        for j, o_ref in enumerate(out_refs):
            at = pl.multiple_of(jnp.bitwise_xor(r, j) * n, n)
            o_ref[...] = in_ref[:, pl.ds(at, n)].astype(bf16)

    return call(body, [((k, n), bf16)] * row_parts, (row, shard), "split_positions", in_specs=[SMEM, single(shard.shape)], pinned=True)


def join_positions(blocks, row):
    k, n = blocks[0].shape
    parts = len(blocks)

    def body(row_ref, *refs):
        r = row_ref[0]
        o_ref = refs[parts]
        for j in range(parts):
            at = pl.multiple_of(jnp.bitwise_xor(r, j) * n, n)
            o_ref[:, pl.ds(at, n)] = refs[j][...].astype(f32)

    return call(body, [((k, n * parts), f32)], (row, *blocks), "join_positions", in_specs=[SMEM] + [single(b.shape) for b in blocks])[0]


def narrow(parts, steps, name):
    n = parts[0].shape[0]
    widths = [p.shape[1] for p in parts]

    def body(*refs):
        at = 0
        for ref, w in zip(refs, widths):
            refs[-1][:, at : at + w] = ref[...].astype(bf16)
            at += w

    return call(
        body, [((n, sum(widths)), bf16)], parts, name, (steps,),
        [pl.BlockSpec((n // steps, w), lambda s: (s, 0)) for w in widths],
        [pl.BlockSpec((n // steps, sum(widths)), lambda s: (s, 0))],
        pinned=True,
    )[0]


def narrow_small(parts, vecs, biases, up_bias, name):
    n, hb = parts[0].shape
    width = hb * len(parts)
    nv = len(vecs)
    rest = up_bias.shape[0] - width
    small = [v.reshape(1, v.shape[0]) for v in vecs] + [jnp.concatenate((*biases, up_bias)).reshape(-1, hb)]

    def body(*refs):
        p_refs = refs[: len(parts)]
        v_refs = refs[len(parts) : len(parts) + nv]
        b_ref, o_ref, small_ref = refs[len(parts) + nv :]
        small_ref[...] = jnp.zeros(small_ref.shape, f32)
        for m, ref in enumerate(v_refs):
            small_ref[m : m + 1, :n] = ref[...]
        for m, ref in enumerate(p_refs):
            o_ref[:n, m * hb : (m + 1) * hb] = ref[...].astype(bf16)
            small_ref[nv : nv + 1, m * hb : (m + 1) * hb] = b_ref[m : m + 1]
            small_ref[nv + 1 : nv + 2, m * hb : (m + 1) * hb] = b_ref[len(parts) + m : len(parts) + m + 1]
        small_ref[0:1, ASIDE : ASIDE + rest] = b_ref[2 * len(parts) : 2 * len(parts) + 1]
        value = small_ref[...]
        high = value.astype(bf16).astype(f32)
        o_ref[n:] = jnp.concatenate((high, value - high), axis=0).astype(bf16)

    scratch = [pltpu.VMEM((8, width), f32)]
    return call(body, [((n + EXTRA, width), bf16)], (*parts, *small), name, scratch=scratch, pinned=True)[0]


def small_rows(ref, k):
    v = ref[k : k + EXTRA].astype(f32)
    return v[0:8] + v[8:16]


def attention_in(xs, near, other, omegas, keep, head_local, head_width, hid_local):
    k, tokens = xs[0].shape
    feats = omegas[0].shape[2]
    heads = 2 * head_local
    hb = head_local * head_width
    rows = head_width + PAD
    factor = head_width ** (-0.25)
    n_near, n_other = len(near), len(other)

    def body(*refs):
        x_in = refs[:4]
        near_refs = refs[4 : 4 + n_near]
        other_refs = refs[4 + n_near : 4 + n_near + n_other]
        (om0_ref, om1_ref, keep_ref, x_ref, fq_ref, fk_ref, uq_ref, uk_ref, v_ref, kv_ref, vec_ref, up_ref) = refs[
            4 + n_near + n_other :
        ]
        for p in range(4):
            vec_ref[:, p * k : (p + 1) * k] = small_rows(near_refs[p], k)[:, :k]
        up_ref[...] = jnp.zeros(up_ref.shape, f32)
        for p in range(4):
            x_ref[p * k : (p + 1) * k] = x_in[p][...]
        xv = x_ref[...]
        ones = jnp.ones((PAD, tokens), bf16)
        for i, pieces in enumerate((near_refs, other_refs)):
            omega_ref = (om0_ref, om1_ref)[i]
            small = small_rows(pieces[0], k)
            up_ref[i : i + 1, : 3 * hb] = small[7:8]
            up_ref[i : i + 1, 3 * hb :] = small[0:1, ASIDE : ASIDE + hid_local - 3 * hb]
            triple = tn(jnp.concatenate([p[:k] for p in pieces], axis=0), xv) + jnp.transpose(small)[:, 6:7]
            for hl in range(head_local):
                h = i * head_local + hl
                at = h * head_width
                lo = hl * head_width
                value = triple[2 * hb + lo : 2 * hb + lo + head_width].astype(bf16)
                v_ref[at : at + head_width] = value
                for base, u_ref, f_ref, mask in ((0, uq_ref, fq_ref, False), (hb, uk_ref, fk_ref, True)):
                    u = triple[base + lo : base + lo + head_width] * factor
                    ub = u.astype(bf16)
                    u_ref[at : at + head_width] = ub
                    z = tn(omega_ref[hl], ub)
                    feat = jnp.exp(z - (0.5 * jnp.sum(u * u, axis=0, keepdims=True) + stabilizer))
                    if mask:
                        feat = feat * keep_ref[0:1]
                    feat = feat.astype(bf16)
                    f_ref[h * feats : (h + 1) * feats] = feat
                kv_ref[h * rows : (h + 1) * rows] = nt(jnp.concatenate((value, ones), axis=0), feat).astype(bf16)

    n = heads * head_width
    outs = [((4 * k, tokens), bf16)] + [((heads * feats, tokens), bf16)] * 2 + [((n, tokens), bf16)] * 3
    outs += [((heads * rows, feats), bf16), ((8, 4 * k), f32), ((8, hid_local), f32)]
    return call(body, outs, (*xs, *near, *other, *omegas, keep), "attention_in", pinned=True)


def weight_specs(pieces, block, first):
    return [pl.BlockSpec((p.shape[0], block), lambda s, f=first: (0, f + s)) for p in pieces]


def fixed_specs(pieces, block, at):
    return [pl.BlockSpec((p.shape[0], block), lambda s: (0, at)) for p in pieces]


def rows_of(refs):
    return jnp.concatenate([r[...] for r in refs], axis=0)


def middle(kv0, kv1, fq, x, near, other, vecs, up_bias, target, keep, scale, heads, head_width, hid_local):
    width, tokens = x.shape
    feats = kv0.shape[1]
    rows = head_width + PAD
    hb = heads * head_width // 2
    steps = hid_local // hb
    k = width // 4
    nn_, no = len(near), len(other)
    np_ = nn_ + no

    def body(*refs):
        kv0_ref, kv1_ref, fq_ref, x_ref = refs[:4]
        out_w = refs[4 : 4 + np_]
        up_w = refs[4 + np_ : 4 + 2 * np_]
        down_w = refs[4 + 2 * np_ : 4 + 3 * np_]
        (vec_ref, upb_ref, t0, t1, t2, t3, keep_ref, scale_ref,
         kv_ref, att_ref, inv_ref, xh1_ref, r1_ref, x1_ref, hid_ref, slope_ref, gf_ref, sum_ref,
         o0, o1, o2, o3, acc_ref, vec_s) = refs[4 + 3 * np_ :]
        step = pl.program_id(0)

        @pl.when(step == 0)
        def _():
            vec = jnp.transpose(vec_ref[...])
            vec_s[...] = vec
            kv_ref[...] = (kv0_ref[...].astype(f32) + kv1_ref[...].astype(f32)).astype(bf16)
            for h in range(heads):
                both = nn(kv_ref[h * rows : (h + 1) * rows], fq_ref[h * feats : (h + 1) * feats])
                inverse = 1.0 / both[head_width : head_width + 1]
                inv_ref[h : h + 1] = inverse
                att_ref[h * head_width : (h + 1) * head_width] = (both[:head_width] * inverse).astype(bf16)
            w = jnp.concatenate((rows_of(out_w[:nn_]), rows_of(out_w[nn_:])), axis=1)
            h1 = nn(w, att_ref[...]) + x_ref[...].astype(f32) + vec[:, 0:1]
            mean = jnp.sum(h1, axis=0, keepdims=True) * (1.0 / width)
            h1 = h1 - mean
            r1 = lax.rsqrt(jnp.sum(h1 * h1, axis=0, keepdims=True) * (1.0 / width) + norm_eps)
            h1 = h1 * r1
            r1_ref[...] = jnp.broadcast_to(r1, (8, tokens))
            xh1_ref[...] = h1.astype(bf16)
            x1 = h1 * vec[:, 1:2] + vec[:, 2:3]
            x1_ref[...] = x1.astype(bf16)
            acc_ref[...] = x1 + vec[:, 3:4]

        x1b = x1_ref[...]
        bias = jnp.transpose(upb_ref[...])
        total = acc_ref[...]
        for i, (a, b) in enumerate(((0, nn_), (nn_, np_))):
            up = tn(rows_of(up_w[a:b]), x1b) + bias[:, i : i + 1]
            gate = 0.5 * (1.0 + lax.erf(up * root_half))
            slope_ref[i] = (gate + up * inv_root_two_pi * jnp.exp(-0.5 * up * up)).astype(bf16)
            hid = (up * gate).astype(bf16)
            hid_ref[i] = hid
            total = total + nn(rows_of(down_w[a:b]), hid)
        acc_ref[...] = total

        @pl.when(step == steps - 1)
        def _():
            vec = vec_s[...]
            h2 = acc_ref[...]
            mean = jnp.sum(h2, axis=0, keepdims=True) * (1.0 / width)
            h2 = h2 - mean
            r2 = lax.rsqrt(jnp.sum(h2 * h2, axis=0, keepdims=True) * (1.0 / width) + norm_eps)
            h2 = h2 * r2
            out = h2 * vec[:, 4:5] + vec[:, 5:6]
            for p, o_ref in enumerate((o0, o1, o2, o3)):
                o_ref[...] = out[p * k : (p + 1) * k].astype(bf16)
            target = jnp.concatenate((t0[...], t1[...], t2[...], t3[...]), axis=0).astype(f32)
            diff = (out - target) * keep_ref[0:1]
            g = diff * scale_ref[0:1, 0:1]
            ones = ones_rows(tokens)
            sum_ref[0:8] = nt(ones, (g * h2).astype(bf16))
            sum_ref[8:16] = nt(ones, g.astype(bf16))
            sum_ref[16:24] = jnp.full((8, width), jnp.sum(diff * diff), f32)
            a = g * vec[:, 4:5]
            first = jnp.sum(a, axis=0, keepdims=True) * (1.0 / width)
            second = jnp.sum(a * h2, axis=0, keepdims=True) * (1.0 / width)
            gf_ref[...] = (r2 * (a - first - h2 * second)).astype(bf16)

    outs = [
        ((heads * rows, feats), bf16), ((width, tokens), bf16), ((16, tokens), f32), ((width, tokens), bf16),
        ((8, tokens), f32), ((width, tokens), bf16), ((2, hid_local, tokens), bf16), ((2, hid_local, tokens), bf16),
        ((width, tokens), bf16), ((24, width), f32),
    ] + [((k, tokens), bf16)] * 4
    pieces = (*near, *other)
    args = (kv0, kv1, fq, x, *pieces, *pieces, *pieces, vecs, up_bias, *target, keep, scale)
    in_specs = [whole(a) for a in (kv0, kv1, fq, x)]
    in_specs += fixed_specs(pieces, hb, 0) + weight_specs(pieces, hb, 1) + weight_specs(pieces, hb, 1 + steps)
    in_specs += [whole(vecs), pl.BlockSpec((8, hb), lambda s: (0, s))] + [whole(t) for t in target] + [whole(keep), whole(scale)]
    out_specs = [whole_out(s) for s, _ in outs]
    out_specs[6] = out_specs[7] = pl.BlockSpec((2, hb, tokens), lambda s: (0, s, 0))
    scratch = [pltpu.VMEM((width, tokens), f32), pltpu.VMEM((width, 8), f32)]
    return call(body, outs, args, "middle", (steps,), in_specs, out_specs, scratch, limit=56)


def grad_theirs(left, right, block, name):
    n, tokens = left.shape
    k = right.shape[1]
    half = n // 2

    def body(l_ref, r_ref, o_ref):
        for i in range(2):
            o_ref[i] = nt(l_ref[...], r_ref[i]).astype(bf16)

    return call(
        body, [((2, half, k), bf16)], (left, right), name, (k // block,),
        [pl.BlockSpec((half, tokens), lambda s: (1, 0)), pl.BlockSpec((2, block, tokens), lambda s: (0, s, 0))],
        [pl.BlockSpec((2, half, block), lambda s: (0, 0, s))],
    )[0]


def grad_mine(left, right, got, block, name):
    n, tokens = left.shape
    k = right.shape[1]
    half = n // 2
    share = k // block // 2

    def body(l_ref, r_ref, got_ref, keep0, keep1, send0, send1):
        step = pl.program_id(0)

        def part(keep_ref, send_ref):
            for i, o_ref in enumerate((keep_ref, send_ref)):
                o_ref[...] = (nt(l_ref[...], r_ref[i]) + got_ref[i].astype(f32)).astype(bf16)

        pl.when(step < share)(lambda: part(keep0, send0))
        pl.when(step >= share)(lambda: part(keep1, send1))

    first = pl.BlockSpec((half, block), lambda s: (0, jnp.minimum(s, share - 1)))
    second = pl.BlockSpec((half, block), lambda s: (0, jnp.maximum(s - share, 0)))
    return call(
        body, [((half, k // 2), bf16)] * 4, (left, right, got), name, (2 * share,),
        [
            pl.BlockSpec((half, tokens), lambda s: (0, 0)),
            pl.BlockSpec((2, block, tokens), lambda s: (0, s, 0)),
            pl.BlockSpec((2, half, block), lambda s: (0, 0, s)),
        ],
        [first, second, first, second],
    )


def pair_theirs(x, gq, go, att, name):
    n, tokens = x.shape
    half = n // 2
    k = gq.shape[1]

    def body(x_ref, gq_ref, go_ref, att_ref, o_ref):
        for i in range(2):
            o_ref[i, :, :k] = nt(x_ref[half:], gq_ref[i]).astype(bf16)
            o_ref[i, :, k:] = nt(go_ref[half:], att_ref[i]).astype(bf16)

    return call(body, [((2, half, 2 * k), bf16)], (x, gq, go, att), name)[0]


def pair_mine(x, gq, go, att, got, name):
    n, tokens = x.shape
    half = n // 2
    k = gq.shape[1]

    def body(x_ref, gq_ref, go_ref, att_ref, got_ref, keep_ref, send_ref):
        for i, o_ref in enumerate((keep_ref, send_ref)):
            o_ref[:, :k] = (nt(x_ref[:half], gq_ref[i]) + got_ref[i, :, :k].astype(f32)).astype(bf16)
            o_ref[:, k:] = (nt(go_ref[:half], att_ref[i]) + got_ref[i, :, k:].astype(f32)).astype(bf16)

    return call(body, [((half, 2 * k), bf16)] * 2, (x, gq, go, att, got), name)


def down_back(gf, slope, near, other, hb, hid_local):
    width, tokens = gf.shape
    steps = hid_local // hb
    nn_, no = len(near), len(other)
    pieces = (*near, *other)

    def body(gf_ref, slope_ref, *refs):
        gu_ref, sum_ref, bd_ref = refs[nn_ + no :]
        g = gf_ref[...]
        ones = ones_rows(tokens)

        @pl.when(pl.program_id(0) == 0)
        def _():
            bd_ref[...] = nt(ones, g)

        for i, w in enumerate((refs[:nn_], refs[nn_ : nn_ + no])):
            v = (tn(rows_of(w), g) * slope_ref[i].astype(f32)).astype(bf16)
            gu_ref[i] = v
            sum_ref[i] = nt(ones, v)

    spec = pl.BlockSpec((2, hb, tokens), lambda s: (0, s, 0))
    return call(
        body, [((2, hid_local, tokens), bf16), ((2, 8, hid_local), f32), ((8, width), f32)], (gf, slope, *pieces), "down_back",
        (steps,), [whole(gf), spec] + weight_specs(pieces, hb, 1 + steps),
        [spec, pl.BlockSpec((2, 8, hb), lambda s: (0, 0, s)), whole_out((8, width))],
    )


def up_back(gu, gf, xh1, r1, vecs, near, other, hb):
    width, tokens = gf.shape
    steps = gu.shape[1] // hb
    nn_, no = len(near), len(other)
    pieces = (*near, *other)

    def body(gu_ref, gf_ref, xh_ref, r1_ref, vec_ref, *refs):
        go_ref, sum_ref, acc_ref = refs[nn_ + no :]
        step = pl.program_id(0)

        @pl.when(step == 0)
        def _():
            acc_ref[...] = gf_ref[...].astype(f32)

        acc_ref[...] += nn(rows_of(refs[:nn_]), gu_ref[0]) + nn(rows_of(refs[nn_ : nn_ + no]), gu_ref[1])

        @pl.when(step == steps - 1)
        def _():
            vec = jnp.transpose(vec_ref[...])
            g = acc_ref[...]
            xh = xh_ref[...].astype(f32)
            ones = ones_rows(tokens)
            sum_ref[0:8] = nt(ones, (g * xh).astype(bf16))
            sum_ref[8:16] = nt(ones, g.astype(bf16))
            a = g * vec[:, 1:2]
            first = jnp.sum(a, axis=0, keepdims=True) * (1.0 / width)
            second = jnp.sum(a * xh, axis=0, keepdims=True) * (1.0 / width)
            go = (r1_ref[0:1] * (a - first - xh * second)).astype(bf16)
            go_ref[...] = go
            sum_ref[16:24] = nt(ones, go)

    return call(
        body, [((width, tokens), bf16), ((24, width), f32)], (gu, gf, xh1, r1, vecs, *pieces), "up_back", (steps,),
        [pl.BlockSpec((2, hb, tokens), lambda s: (0, s, 0))] + [whole(a) for a in (gf, xh1, r1, vecs)] + weight_specs(pieces, hb, 1),
        [whole_out((width, tokens)), whole_out((24, width))], [pltpu.VMEM((width, tokens), f32)],
    )


def attention_mid(go, att, inv, fq, near, other, heads, head_width):
    width, tokens = go.shape
    feats = fq.shape[0] // heads
    hb = heads * head_width // 2
    rows = head_width + PAD
    nn_, no = len(near), len(other)
    pieces = (*near, *other)

    def body(go_ref, att_ref, inv_ref, fq_ref, *refs):
        gn_ref, kv_ref = refs[nn_ + no :]
        g = go_ref[...]
        zeros = jnp.zeros((PAD - 1, tokens), f32)
        for i, w in enumerate((refs[:nn_], refs[nn_ : nn_ + no])):
            ga = tn(rows_of(w), g)
            for hl in range(heads // 2):
                h = i * (heads // 2) + hl
                gh = ga[hl * head_width : (hl + 1) * head_width]
                inverse = inv_ref[h : h + 1]
                a = att_ref[h * head_width : (h + 1) * head_width].astype(f32)
                gd = -jnp.sum(gh * a, axis=0, keepdims=True) * inverse
                both = jnp.concatenate((gh * inverse, gd, zeros), axis=0).astype(bf16)
                gn_ref[h * rows : (h + 1) * rows] = both
                kv_ref[h * rows : (h + 1) * rows] = nt(both, fq_ref[h * feats : (h + 1) * feats]).astype(bf16)

    outs = [((heads * rows, tokens), bf16), ((heads * rows, feats), bf16)]
    args = (go, att, inv, fq, *pieces)
    return call(
        body, outs, args, "attention_mid", (1,), [whole(a) for a in args[:4]] + fixed_specs(pieces, hb, 0),
        [whole_out(s) for s, _ in outs],
    )


def query_back(gn, kv, fq, uq, omegas, heads, head_width):
    n, tokens = uq.shape
    feats = fq.shape[0] // heads
    rows = head_width + PAD
    factor = head_width ** (-0.25)

    def body(gn_ref, kv_ref, fq_ref, uq_ref, om0_ref, om1_ref, gq_ref, sum_ref):
        for h in range(heads):
            om_ref = (om0_ref, om1_ref)[h // (heads // 2)]
            e = tn(kv_ref[h * rows : (h + 1) * rows], gn_ref[h * rows : (h + 1) * rows])
            e = e * fq_ref[h * feats : (h + 1) * feats].astype(f32)
            s = jnp.sum(e, axis=0, keepdims=True)
            u = uq_ref[h * head_width : (h + 1) * head_width].astype(f32)
            gq_ref[h * head_width : (h + 1) * head_width] = (
                factor * (nn(om_ref[h % (heads // 2)], e.astype(bf16)) - s * u)
            ).astype(bf16)
        sum_ref[...] = nt(ones_rows(tokens), gq_ref[...])

    return call(body, [((n, tokens), bf16), ((8, n), f32)], (gn, kv, fq, uq, *omegas), "query_back")


def key_back(gkv0, gkv1, fk, uk, v, omegas, heads, head_width):
    n, tokens = uk.shape
    feats = fk.shape[0] // heads
    rows = head_width + PAD
    factor = head_width ** (-0.25)
    hl_n = heads // 2
    hb = hl_n * head_width

    def body(gkv0_ref, gkv1_ref, fk_ref, uk_ref, v_ref, om0_ref, om1_ref, g_ref, sum_ref):
        ones = jnp.ones((PAD, tokens), bf16)
        for h in range(heads):
            i, hl = divmod(h, hl_n)
            base = i * 2 * hb + hl * head_width
            kv = (gkv0_ref[h * rows : (h + 1) * rows].astype(f32) + gkv1_ref[h * rows : (h + 1) * rows].astype(f32)).astype(bf16)
            f = fk_ref[h * feats : (h + 1) * feats]
            at = h * head_width
            value = jnp.concatenate((v_ref[at : at + head_width], ones), axis=0)
            e = tn(kv, value) * f.astype(f32)
            s = jnp.sum(e, axis=0, keepdims=True)
            u = uk_ref[at : at + head_width].astype(f32)
            g_ref[base : base + head_width] = (
                factor * (nn((om0_ref, om1_ref)[i][hl], e.astype(bf16)) - s * u)
            ).astype(bf16)
            g_ref[base + hb : base + hb + head_width] = nn(kv[:head_width], f).astype(bf16)
        sum_ref[...] = nt(ones_rows(tokens), g_ref[...])

    return call(body, [((2 * n, tokens), bf16), ((8, 2 * n), f32)], (gkv0, gkv1, fk, uk, v, *omegas), "key_back")


def last_parts(x, g, sums, got, name):
    sum1, sum2, bd, bu, sum_q, sum_kv = sums
    n, tokens = x.shape
    q = n // 4
    k = g.shape[1]
    hb = k // 2
    hid_local = bu.shape[2]
    ups = hid_local // hb
    rows = q + EXTRA
    which = 0 if got is not None else 1

    def body(x_ref, g_ref, s1_ref, s2_ref, bd_ref, bu_ref, sq_ref, skv_ref, *refs):
        if got is None:
            o_ref, row_s, col_s = refs
        else:
            got_ref, keep_ref, send_ref, row_s, col_s = refs
        for m, v in enumerate((s1_ref[16:17], s1_ref[0:1], s1_ref[8:9], bd_ref[0:1], s2_ref[0:1], s2_ref[8:9], s2_ref[16:17])):
            row_s[m : m + 1] = v
        row_s[7:8] = jnp.zeros((1, n), f32)
        col_s[...] = jnp.zeros(col_s.shape, f32)
        for i in range(2):
            col_s[i, 0:1] = sq_ref[0:1, i * hb : (i + 1) * hb]
            col_s[i, 1:2] = skv_ref[0:1, i * k : i * k + hb]
            col_s[i, 2:3] = skv_ref[0:1, i * k + hb : (i + 1) * k]
            for u in range(ups):
                col_s[i, 3 + u : 4 + u] = bu_ref[i, 0:1, u * hb : (u + 1) * hb]
        for i in range(2):
            for jx in range(2):
                p = 2 * which + jx
                main = nt(x_ref[p * q : (p + 1) * q], g_ref[i])
                small = row_s[:, p * q : (p + 1) * q]
                small = jnp.concatenate((small, jnp.zeros((8, hb - q), f32), col_s[i]), axis=1)
                small = jnp.concatenate((small, jnp.zeros((EXTRA - 8, k), f32)), axis=0)
                if got is None:
                    o_ref[i, jx, :q] = main.astype(bf16)
                    o_ref[i, jx, q:] = small.astype(bf16)
                else:
                    o = send_ref if jx else keep_ref
                    o[i * rows : i * rows + q] = (main + got_ref[i, jx, :q].astype(f32)).astype(bf16)
                    o[i * rows + q : (i + 1) * rows] = (small + got_ref[i, jx, q:].astype(f32)).astype(bf16)

    outs = [((2, 2, rows, k), bf16)] if got is None else [((2 * rows, k), bf16)] * 2
    args = (x, g, *sums) if got is None else (x, g, *sums, got)
    return call(body, outs, args, name, scratch=[pltpu.VMEM((8, n), f32), pltpu.VMEM((2, 8, hb), f32)])


def input_grad(gq, g, go, near, other):
    width, tokens = go.shape
    hb = gq.shape[1]
    k = width // 4
    nn_, no = len(near), len(other)

    def body(gq_ref, g_ref, go_ref, *refs):
        total = go_ref[...].astype(f32)
        for i, w in enumerate((refs[:nn_], refs[nn_ : nn_ + no])):
            w = jnp.concatenate([r[:k] for r in w], axis=0)
            total = total + nn(w[:, :hb], gq_ref[i]) + nn(w[:, hb:], g_ref[i])
        for p, o_ref in enumerate(refs[nn_ + no :]):
            o_ref[...] = total[p * k : (p + 1) * k].astype(bf16)

    return call(body, [((k, tokens), bf16)] * 4, (gq, g, go, *near, *other), "input_grad")


def swap(value, axis, mask):
    size = lax.axis_size(axis)
    return lax.ppermute(value, axis, [(s, s ^ mask) for s in range(size)])


def after(value, *others):
    return lax.optimization_barrier((value, *others))[0]


class Fold:
    def __init__(self, value):
        self.value = value
        self.four = lax.axis_size("dp") == 4
        if not self.four:
            self.value = lax.psum(value, "dp")
            return
        self.odd = lax.axis_index("dp") % 2 == 1
        n = value.shape[1] // 2
        low, high = value[:, :n], value[:, n:]
        self.value = jnp.where(self.odd, high, low)
        self.got = swap(jnp.where(self.odd, low, high), "dp", 1)

    def step(self, order, mask):
        if not self.four:
            return order
        self.value = after(self.value, order) + self.got
        self.got = swap(self.value, "dp", mask)
        return self.value

    def middle(self, order):
        return self.step(order, 2)

    def back(self, order):
        return self.step(order, 1)

    def result(self):
        if not self.four:
            return self.value.astype(f32)
        a, b = self.value.astype(f32), self.got.astype(f32)
        return jnp.concatenate((jnp.where(self.odd, b, a), jnp.where(self.odd, a, b)), axis=1)


def total(keep, got, last):
    n = keep.shape[0] // 2
    return keep[:n] + got[:n] + last


def far_half(keep, got):
    n = keep.shape[0] // 2
    return keep[n:] + got[n:]


def exchange(blocks):
    return [blocks[0]] + [swap(blocks[j], "row", j) for j in (1, 2, 3)]


def reduce_small(value, axis):
    step = 1
    while step < lax.axis_size(axis):
        value = value + swap(value, axis, step)
        step *= 2
    return value


def shards(
    inputs, teacher, lengths, omega,
    w_query, b_query, w_key, b_key, w_value, b_value, w_out, b_out,
    norm1_gain, norm1_bias, w_up, up_bias, w_down, b_down, norm2_gain, norm2_bias,
):
    row_parts = lax.axis_size("row")
    feat_local, seq_length = inputs.shape
    width = feat_local * row_parts
    head_local, head_width, feats = omega.shape
    heads = head_local * lax.axis_size("col")
    tokens = seq_length // row_parts
    hb = head_local * head_width
    hid_local = w_up.shape[1]
    row = lax.axis_index("row")
    col = lax.axis_index("col")
    row_ref = row.astype(jnp.int32).reshape(1)

    omegas = (omega, swap(omega, "col", 1))
    vecs = (b_out, norm1_gain, norm1_bias, b_down, norm2_gain, norm2_bias)
    ins = split_positions(inputs, row_ref, row_parts)
    ins_got = exchange(ins)
    xs = [ins_got[j] for j in (0, 2, 1, 3)]
    own_a = narrow_small((after(w_query, *ins), w_key, w_value), vecs, (b_query, b_key, b_value), up_bias, "narrow_a")
    a_y = swap(own_a, "col", 1)
    a_x = swap(own_a, "row", 2)
    a_far = swap(after(a_x, a_y, omegas[1]), "col", 1)
    near_a = (own_a, a_x, swap(own_a, "row", 1), swap(a_x, "row", 1))
    other_a = (a_y, a_far, swap(a_y, "row", 1), swap(a_far, "row", 1))
    count = reduce_small(jnp.sum(lengths).astype(f32).reshape(1, 1) + jnp.zeros((8, 128), f32), "dp")
    own_b = narrow((after(w_out, own_a, count), w_up, w_down), 3, "narrow_b")
    b_x = swap(after(own_b, a_x, ins_got[2], ins_got[3]), "row", 2)
    b_y = swap(after(own_b, a_far), "col", 1)
    length = lax.dynamic_index_in_dim(lengths, col, 0, False)
    keep = ((row * tokens + jnp.arange(tokens, dtype=jnp.int32)) < length).astype(f32)
    keep = jnp.broadcast_to(keep[None, :], (8, tokens))
    scale = (2.0 * LOSS_SCALE) / (count * width)

    x, fq, fk, uq, uk, v, kv, vecs, up_bias_all = attention_in(
        xs, near_a, other_a, omegas, keep, head_local, head_width, hid_local
    )
    kv0 = kv + swap(kv, "row", 1)
    kv1 = swap(kv0, "row", 2)
    theirs = split_positions(after(teacher, kv0), row_ref, row_parts)
    teach = exchange(theirs)
    target = [teach[j] for j in (0, 2, 1, 3)]
    b_x = after(b_x, kv0, theirs[0])
    b_y = after(b_y, kv0, theirs[0])
    b_far_y = swap(b_x[CUT:], "col", 1)
    b_far_x = swap(b_y[:CUT], "row", 2)
    near_b = (own_b, b_x)
    near_b = near_b + tuple(swap(p, "row", 1) for p in near_b)
    other_b = (b_y, b_far_x, after(b_far_y, kv1, b_far_x, teach[2], teach[3]))
    other_b = other_b + tuple(swap(p, "row", 1) for p in other_b)
    kv, att, inv, xh1, r1, x1, hid, slope, gf, sum2, *out = middle(
        kv0, kv1, fq, x, near_b, other_b, vecs, up_bias_all, target, keep, scale, heads, head_width, hid_local
    )
    out = exchange([out[j] for j in (0, 2, 1, 3)])

    theirs = grad_theirs(gf, hid, hb, "down_theirs")
    got1 = swap(theirs, "row", 1)
    gu, bu, bd = down_back(after(gf, theirs), slope, near_b, other_b, hb, hid_local)
    kept0, kept1, send0, send1 = grad_mine(after(gf, gu), hid, got1, hb, "down_mine")
    down = ((kept0, swap(send0, "col", 1)), (kept1, swap(send1, "col", 1)))
    theirs = grad_theirs(after(x1, send0), gu, hb, "up_theirs")
    got2 = swap(theirs, "row", 1)
    go, sum1 = up_back(after(gu, theirs), gf, xh1, r1, vecs, near_b, other_b, hb)
    far = far_half(after(down[0][0], go), down[0][1])
    r_down0 = swap(far, "row", 2)
    gn, gkv = attention_mid(after(go, *out, far), att, inv, fq, near_b, other_b, heads, head_width)
    gkv0 = gkv + swap(gkv, "row", 1)
    gkv1 = swap(gkv0, "row", 2)
    kept0, kept1, send0, send1 = grad_mine(after(x1, gkv0), gu, got2, hb, "up_mine")
    up = ((kept0, swap(send0, "col", 1)), (kept1, swap(send1, "col", 1)))
    far = far_half(after(down[1][0], send0), down[1][1])
    r_down1 = swap(far, "row", 2)
    gq, sum_q = query_back(after(gn, far), kv, fq, uq, omegas, heads, head_width)
    down0 = total(after(down[0][0], gq), down[0][1], r_down0)
    z_down0 = Fold(down0)
    gq = gq.reshape(2, hb, tokens)
    att2 = att.reshape(2, hb, tokens)
    theirs = pair_theirs(after(x, down0), gq, go, att2, "pair_theirs")
    got3 = swap(theirs, "row", 1)
    g, sum_kv = key_back(after(gkv0, theirs), gkv1, fk, uk, v, omegas, heads, head_width)
    down1 = total(after(down[1][0], g), down[1][1], r_down1)
    z_down1 = Fold(down1)
    order = z_down0.middle(down1)
    far = far_half(after(up[0][0], order), up[0][1])
    r_up0 = swap(far, "row", 2)
    far = far_half(after(up[1][0], far), up[1][1])
    r_up1 = swap(far, "row", 2)
    g = g.reshape(2, 2 * hb, tokens)
    sums = (sum1, sum2, bd, bu, sum_q, sum_kv)
    theirs = last_parts(after(x, far), g, sums, None, "last_theirs")[0]
    got4 = swap(theirs, "row", 1)
    keep3, send3 = pair_mine(after(x, theirs), gq, go, att2, got3, "pair_mine")
    r_y3 = swap(send3, "col", 1)
    order = z_down1.middle(send3)
    keep4, send4 = last_parts(after(x, order), g, sums, got4, "last_mine")
    r_x4 = swap(send4, "row", 2)
    order = z_down0.back(send4)
    up0 = total(after(up[0][0], order), up[0][1], r_up0)
    z_up0 = Fold(up0)
    gin = input_grad(gq, g, after(go, up0), near_a, other_a)
    far = far_half(after(keep4, gin[0]), r_x4)
    r_y4 = swap(far, "col", 1)
    far = far_half(after(keep3, far), r_y3)
    r_x3 = swap(far, "row", 2)
    up1 = total(after(up[1][0], far), up[1][1], r_up1)
    z_up1 = Fold(up1)
    order = z_down1.back(up1)
    gin = exchange([after(gin[j], order) for j in (0, 2, 1, 3)])
    order = z_up0.middle(order)
    last = total(after(keep4, order), r_x4, r_y4)
    z_last = Fold(last)
    pair = total(after(keep3, last), r_y3, r_x3)
    z_pair = Fold(pair)
    order = z_up1.middle(pair)
    order = z_up0.back(order)
    order = z_last.middle(order)
    order = z_pair.middle(order)
    order = z_up1.back(order)
    order = z_last.back(order)
    order = z_pair.back(order)
    out[0] = after(out[0], order)
    out = join_positions(out, row_ref)
    grad_in = join_positions([after(gin[0], out), *gin[1:]], row_ref)
    grad_down = jnp.concatenate((z_down0.result(), z_down1.result()), axis=1)
    grad_up = jnp.concatenate((z_up0.result(), z_up1.result()), axis=1)
    last = z_last.result().astype(f32)
    grad_pair = z_pair.result().astype(f32)

    extra = last[feat_local:]
    rows = extra[:7, :feat_local]
    cols = extra[:7, hb:]
    loss = rows[6, 0] / (count[0, 0] * width)
    return (
        out,
        loss,
        grad_in,
        grad_pair[:, :hb],
        cols[0],
        last[:feat_local, :hb],
        cols[1],
        last[:feat_local, hb:],
        cols[2],
        grad_pair[:, hb:],
        rows[0],
        rows[1],
        rows[2],
        grad_up,
        cols[3:].reshape(hid_local),
        grad_down,
        rows[3],
        rows[4],
        rows[5],
    )


def solution(mesh):
    both = P("row", ("dp", "col"))
    in_specs = (
        both, both, P("dp"), P("col", None, None),
        P("row", "col"), P("col"), P("row", "col"), P("col"), P("row", "col"), P("col"),
        P("row", "col"), P("row"), P("row"), P("row"),
        P("row", "col"), P("col"), P("row", "col"), P("row"), P("row"), P("row"),
    )
    out_specs = (
        both, P(), both,
        P("row", "col"), P("col"), P("row", "col"), P("col"), P("row", "col"), P("col"),
        P("row", "col"), P("row"), P("row"), P("row"),
        P("row", "col"), P("col"), P("row", "col"), P("row"), P("row"), P("row"),
    )
    return jax.shard_map(shards, mesh=mesh, in_specs=in_specs, out_specs=out_specs, check_vma=False)
```

```python
import jax
import jax.numpy as jnp
from jax import lax
from jax.experimental import pallas as pl
from jax.experimental.pallas import tpu as pltpu
from jax.sharding import PartitionSpec as P

LOSS_SCALE = 16777216
stabilizer = 2.0
norm_eps = 1e-12
root_half = 0.7071067811865476
inv_root_two_pi = 0.3989422804014327
f32 = jnp.float32
bf16 = jnp.bfloat16
PAD = 8
EXTRA = 16
CUT = 48
ASIDE = 256


def dot(a, b, dims):
    return lax.dot_general(a, b, (dims, ((), ())), preferred_element_type=f32)


def nn(a, b):
    return dot(a, b, ((1,), (0,)))


def nt(a, b):
    return dot(a, b, ((1,), (1,)))


def tn(a, b):
    return dot(a, b, ((0,), (0,)))


def ones_rows(tokens):
    return jnp.ones((8, tokens), bf16)


def call(body, outs, args, name, grid=None, in_specs=None, out_specs=None, scratch=(), limit=40, pinned=False):
    if grid is None:
        grid = (1,)
        in_specs = [single(a.shape) for a in args] if in_specs is None else in_specs
        out_specs = [single(s) for s, _ in outs]
    extra = dict(grid=grid, in_specs=in_specs, out_specs=out_specs)
    if pinned:
        args = [a if p is SMEM else pltpu.with_memory_space_constraint(a, pltpu.HBM) for a, p in zip(args, in_specs)]
    make = pltpu.HBM if pinned else jax.ShapeDtypeStruct
    return pl.pallas_call(
        body,
        out_shape=[make(s, d) for s, d in outs],
        scratch_shapes=list(scratch),
        compiler_params=pltpu.CompilerParams(vmem_limit_bytes=limit * 1024 * 1024),
        cost_estimate=pl.CostEstimate(flops=1000, bytes_accessed=1000, transcendentals=0),
        name=name,
        **extra,
    )(*args)


def single(shape):
    zeros = (0,) * len(shape)
    return pl.BlockSpec(shape, lambda s: zeros, pipeline_mode=pl.Buffered(1))


def whole(a):
    zeros = (0,) * a.ndim
    return pl.BlockSpec(a.shape, lambda s: zeros)


def whole_out(shape):
    zeros = (0,) * len(shape)
    return pl.BlockSpec(shape, lambda s: zeros)


SMEM = pl.BlockSpec(memory_space=pltpu.SMEM)


def split_positions(shard, row, row_parts):
    k, length = shard.shape
    n = length // row_parts

    def body(row_ref, in_ref, *out_refs):
        r = row_ref[0]
        for j, o_ref in enumerate(out_refs):
            at = pl.multiple_of(jnp.bitwise_xor(r, j) * n, n)
            o_ref[...] = in_ref[:, pl.ds(at, n)].astype(bf16)

    return call(body, [((k, n), bf16)] * row_parts, (row, shard), "split_positions", in_specs=[SMEM, single(shard.shape)], pinned=True)


def join_positions(blocks, row):
    k, n = blocks[0].shape
    parts = len(blocks)

    def body(row_ref, *refs):
        r = row_ref[0]
        o_ref = refs[parts]
        for j in range(parts):
            at = pl.multiple_of(jnp.bitwise_xor(r, j) * n, n)
            o_ref[:, pl.ds(at, n)] = refs[j][...].astype(f32)

    return call(body, [((k, n * parts), f32)], (row, *blocks), "join_positions", in_specs=[SMEM] + [single(b.shape) for b in blocks])[0]


def narrow(parts, steps, name):
    n = parts[0].shape[0]
    widths = [p.shape[1] for p in parts]

    def body(*refs):
        at = 0
        for ref, w in zip(refs, widths):
            refs[-1][:, at : at + w] = ref[...].astype(bf16)
            at += w

    return call(
        body, [((n, sum(widths)), bf16)], parts, name, (steps,),
        [pl.BlockSpec((n // steps, w), lambda s: (s, 0)) for w in widths],
        [pl.BlockSpec((n // steps, sum(widths)), lambda s: (s, 0))],
        pinned=True,
    )[0]


def narrow_small(parts, vecs, biases, up_bias, name):
    n, hb = parts[0].shape
    width = hb * len(parts)
    nv = len(vecs)
    rest = up_bias.shape[0] - width
    small = [v.reshape(1, v.shape[0]) for v in vecs] + [jnp.concatenate((*biases, up_bias)).reshape(-1, hb)]

    def body(*refs):
        p_refs = refs[: len(parts)]
        v_refs = refs[len(parts) : len(parts) + nv]
        b_ref, o_ref, small_ref = refs[len(parts) + nv :]
        small_ref[...] = jnp.zeros(small_ref.shape, f32)
        for m, ref in enumerate(v_refs):
            small_ref[m : m + 1, :n] = ref[...]
        for m, ref in enumerate(p_refs):
            o_ref[:n, m * hb : (m + 1) * hb] = ref[...].astype(bf16)
            small_ref[nv : nv + 1, m * hb : (m + 1) * hb] = b_ref[m : m + 1]
            small_ref[nv + 1 : nv + 2, m * hb : (m + 1) * hb] = b_ref[len(parts) + m : len(parts) + m + 1]
        small_ref[0:1, ASIDE : ASIDE + rest] = b_ref[2 * len(parts) : 2 * len(parts) + 1]
        value = small_ref[...]
        high = value.astype(bf16).astype(f32)
        o_ref[n:] = jnp.concatenate((high, value - high), axis=0).astype(bf16)

    scratch = [pltpu.VMEM((8, width), f32)]
    return call(body, [((n + EXTRA, width), bf16)], (*parts, *small), name, scratch=scratch, pinned=True)[0]


def small_rows(ref, k):
    v = ref[k : k + EXTRA].astype(f32)
    return v[0:8] + v[8:16]


def attention_in(xs, near, other, omegas, keep, head_local, head_width, hid_local):
    k, tokens = xs[0].shape
    feats = omegas[0].shape[2]
    heads = 2 * head_local
    hb = head_local * head_width
    rows = head_width + PAD
    factor = head_width ** (-0.25)
    n_near, n_other = len(near), len(other)

    def body(*refs):
        x_in = refs[:4]
        near_refs = refs[4 : 4 + n_near]
        other_refs = refs[4 + n_near : 4 + n_near + n_other]
        (om0_ref, om1_ref, keep_ref, x_ref, fq_ref, fk_ref, uq_ref, uk_ref, v_ref, kv_ref, vec_ref, up_ref) = refs[
            4 + n_near + n_other :
        ]
        for p in range(4):
            vec_ref[:, p * k : (p + 1) * k] = small_rows(near_refs[p], k)[:, :k]
        up_ref[...] = jnp.zeros(up_ref.shape, f32)
        for p in range(4):
            x_ref[p * k : (p + 1) * k] = x_in[p][...]
        xv = x_ref[...]
        ones = jnp.ones((PAD, tokens), bf16)
        for i, pieces in enumerate((near_refs, other_refs)):
            omega_ref = (om0_ref, om1_ref)[i]
            small = small_rows(pieces[0], k)
            up_ref[i : i + 1, : 3 * hb] = small[7:8]
            up_ref[i : i + 1, 3 * hb :] = small[0:1, ASIDE : ASIDE + hid_local - 3 * hb]
            triple = tn(jnp.concatenate([p[:k] for p in pieces], axis=0), xv) + jnp.transpose(small)[:, 6:7]
            for hl in range(head_local):
                h = i * head_local + hl
                at = h * head_width
                lo = hl * head_width
                value = triple[2 * hb + lo : 2 * hb + lo + head_width].astype(bf16)
                v_ref[at : at + head_width] = value
                for base, u_ref, f_ref, mask in ((0, uq_ref, fq_ref, False), (hb, uk_ref, fk_ref, True)):
                    u = triple[base + lo : base + lo + head_width] * factor
                    ub = u.astype(bf16)
                    u_ref[at : at + head_width] = ub
                    z = tn(omega_ref[hl], ub)
                    feat = jnp.exp(z - (0.5 * jnp.sum(u * u, axis=0, keepdims=True) + stabilizer))
                    if mask:
                        feat = feat * keep_ref[0:1]
                    feat = feat.astype(bf16)
                    f_ref[h * feats : (h + 1) * feats] = feat
                kv_ref[h * rows : (h + 1) * rows] = nt(jnp.concatenate((value, ones), axis=0), feat).astype(bf16)

    n = heads * head_width
    outs = [((4 * k, tokens), bf16)] + [((heads * feats, tokens), bf16)] * 2 + [((n, tokens), bf16)] * 3
    outs += [((heads * rows, feats), bf16), ((8, 4 * k), f32), ((8, hid_local), f32)]
    return call(body, outs, (*xs, *near, *other, *omegas, keep), "attention_in", pinned=True)


def weight_specs(pieces, block, first):
    return [pl.BlockSpec((p.shape[0], block), lambda s, f=first: (0, f + s)) for p in pieces]


def fixed_specs(pieces, block, at):
    return [pl.BlockSpec((p.shape[0], block), lambda s: (0, at)) for p in pieces]


def rows_of(refs):
    return jnp.concatenate([r[...] for r in refs], axis=0)


def middle(kv0, kv1, fq, x, near, other, vecs, up_bias, target, keep, scale, heads, head_width, hid_local):
    width, tokens = x.shape
    feats = kv0.shape[1]
    rows = head_width + PAD
    hb = heads * head_width // 2
    steps = hid_local // hb
    k = width // 4
    nn_, no = len(near), len(other)
    np_ = nn_ + no

    def body(*refs):
        kv0_ref, kv1_ref, fq_ref, x_ref = refs[:4]
        out_w = refs[4 : 4 + np_]
        up_w = refs[4 + np_ : 4 + 2 * np_]
        down_w = refs[4 + 2 * np_ : 4 + 3 * np_]
        (vec_ref, upb_ref, t0, t1, t2, t3, keep_ref, scale_ref,
         kv_ref, att_ref, inv_ref, xh1_ref, r1_ref, x1_ref, hid_ref, slope_ref, gf_ref, sum_ref,
         o0, o1, o2, o3, acc_ref, vec_s) = refs[4 + 3 * np_ :]
        step = pl.program_id(0)

        @pl.when(step == 0)
        def _():
            vec = jnp.transpose(vec_ref[...])
            vec_s[...] = vec
            kv_ref[...] = (kv0_ref[...].astype(f32) + kv1_ref[...].astype(f32)).astype(bf16)
            for h in range(heads):
                both = nn(kv_ref[h * rows : (h + 1) * rows], fq_ref[h * feats : (h + 1) * feats])
                inverse = 1.0 / both[head_width : head_width + 1]
                inv_ref[h : h + 1] = inverse
                att_ref[h * head_width : (h + 1) * head_width] = (both[:head_width] * inverse).astype(bf16)
            w = jnp.concatenate((rows_of(out_w[:nn_]), rows_of(out_w[nn_:])), axis=1)
            h1 = nn(w, att_ref[...]) + x_ref[...].astype(f32) + vec[:, 0:1]
            mean = jnp.sum(h1, axis=0, keepdims=True) * (1.0 / width)
            h1 = h1 - mean
            r1 = lax.rsqrt(jnp.sum(h1 * h1, axis=0, keepdims=True) * (1.0 / width) + norm_eps)
            h1 = h1 * r1
            r1_ref[...] = jnp.broadcast_to(r1, (8, tokens))
            xh1_ref[...] = h1.astype(bf16)
            x1 = h1 * vec[:, 1:2] + vec[:, 2:3]
            x1_ref[...] = x1.astype(bf16)
            acc_ref[...] = x1 + vec[:, 3:4]

        x1b = x1_ref[...]
        bias = jnp.transpose(upb_ref[...])
        total = acc_ref[...]
        for i, (a, b) in enumerate(((0, nn_), (nn_, np_))):
            up = tn(rows_of(up_w[a:b]), x1b) + bias[:, i : i + 1]
            gate = 0.5 * (1.0 + lax.erf(up * root_half))
            slope_ref[i] = (gate + up * inv_root_two_pi * jnp.exp(-0.5 * up * up)).astype(bf16)
            hid = (up * gate).astype(bf16)
            hid_ref[i] = hid
            total = total + nn(rows_of(down_w[a:b]), hid)
        acc_ref[...] = total

        @pl.when(step == steps - 1)
        def _():
            vec = vec_s[...]
            h2 = acc_ref[...]
            mean = jnp.sum(h2, axis=0, keepdims=True) * (1.0 / width)
            h2 = h2 - mean
            r2 = lax.rsqrt(jnp.sum(h2 * h2, axis=0, keepdims=True) * (1.0 / width) + norm_eps)
            h2 = h2 * r2
            out = h2 * vec[:, 4:5] + vec[:, 5:6]
            for p, o_ref in enumerate((o0, o1, o2, o3)):
                o_ref[...] = out[p * k : (p + 1) * k].astype(bf16)
            target = jnp.concatenate((t0[...], t1[...], t2[...], t3[...]), axis=0).astype(f32)
            diff = (out - target) * keep_ref[0:1]
            g = diff * scale_ref[0:1, 0:1]
            ones = ones_rows(tokens)
            sum_ref[0:8] = nt(ones, (g * h2).astype(bf16))
            sum_ref[8:16] = nt(ones, g.astype(bf16))
            sum_ref[16:24] = jnp.full((8, width), jnp.sum(diff * diff), f32)
            a = g * vec[:, 4:5]
            first = jnp.sum(a, axis=0, keepdims=True) * (1.0 / width)
            second = jnp.sum(a * h2, axis=0, keepdims=True) * (1.0 / width)
            gf_ref[...] = (r2 * (a - first - h2 * second)).astype(bf16)

    outs = [
        ((heads * rows, feats), bf16), ((width, tokens), bf16), ((16, tokens), f32), ((width, tokens), bf16),
        ((8, tokens), f32), ((width, tokens), bf16), ((2, hid_local, tokens), bf16), ((2, hid_local, tokens), bf16),
        ((width, tokens), bf16), ((24, width), f32),
    ] + [((k, tokens), bf16)] * 4
    pieces = (*near, *other)
    args = (kv0, kv1, fq, x, *pieces, *pieces, *pieces, vecs, up_bias, *target, keep, scale)
    in_specs = [whole(a) for a in (kv0, kv1, fq, x)]
    in_specs += fixed_specs(pieces, hb, 0) + weight_specs(pieces, hb, 1) + weight_specs(pieces, hb, 1 + steps)
    in_specs += [whole(vecs), pl.BlockSpec((8, hb), lambda s: (0, s))] + [whole(t) for t in target] + [whole(keep), whole(scale)]
    out_specs = [whole_out(s) for s, _ in outs]
    out_specs[6] = out_specs[7] = pl.BlockSpec((2, hb, tokens), lambda s: (0, s, 0))
    scratch = [pltpu.VMEM((width, tokens), f32), pltpu.VMEM((width, 8), f32)]
    return call(body, outs, args, "middle", (steps,), in_specs, out_specs, scratch, limit=56, pinned=True)


def grad_theirs(left, right, block, name):
    n, tokens = left.shape
    k = right.shape[1]
    half = n // 2

    def body(l_ref, r_ref, o_ref):
        for i in range(2):
            o_ref[i] = nt(l_ref[...], r_ref[i]).astype(bf16)

    return call(
        body, [((2, half, k), bf16)], (left, right), name, (k // block,),
        [pl.BlockSpec((half, tokens), lambda s: (1, 0)), pl.BlockSpec((2, block, tokens), lambda s: (0, s, 0))],
        [pl.BlockSpec((2, half, block), lambda s: (0, 0, s))],
    )[0]


def grad_mine(left, right, got, block, name):
    n, tokens = left.shape
    k = right.shape[1]
    half = n // 2
    share = k // block // 2

    def body(l_ref, r_ref, got_ref, keep0, keep1, send0, send1):
        step = pl.program_id(0)

        def part(keep_ref, send_ref):
            for i, o_ref in enumerate((keep_ref, send_ref)):
                o_ref[...] = (nt(l_ref[...], r_ref[i]) + got_ref[i].astype(f32)).astype(bf16)

        pl.when(step < share)(lambda: part(keep0, send0))
        pl.when(step >= share)(lambda: part(keep1, send1))

    first = pl.BlockSpec((half, block), lambda s: (0, jnp.minimum(s, share - 1)))
    second = pl.BlockSpec((half, block), lambda s: (0, jnp.maximum(s - share, 0)))
    return call(
        body, [((half, k // 2), bf16)] * 4, (left, right, got), name, (2 * share,),
        [
            pl.BlockSpec((half, tokens), lambda s: (0, 0)),
            pl.BlockSpec((2, block, tokens), lambda s: (0, s, 0)),
            pl.BlockSpec((2, half, block), lambda s: (0, 0, s)),
        ],
        [first, second, first, second],
    )


def pair_theirs(x, gq, go, att, name):
    n, tokens = x.shape
    half = n // 2
    k = gq.shape[1]

    def body(x_ref, gq_ref, go_ref, att_ref, o_ref):
        for i in range(2):
            o_ref[i, :, :k] = nt(x_ref[half:], gq_ref[i]).astype(bf16)
            o_ref[i, :, k:] = nt(go_ref[half:], att_ref[i]).astype(bf16)

    return call(body, [((2, half, 2 * k), bf16)], (x, gq, go, att), name)[0]


def pair_mine(x, gq, go, att, got, name):
    n, tokens = x.shape
    half = n // 2
    k = gq.shape[1]

    def body(x_ref, gq_ref, go_ref, att_ref, got_ref, keep_ref, send_ref):
        for i, o_ref in enumerate((keep_ref, send_ref)):
            o_ref[:, :k] = (nt(x_ref[:half], gq_ref[i]) + got_ref[i, :, :k].astype(f32)).astype(bf16)
            o_ref[:, k:] = (nt(go_ref[:half], att_ref[i]) + got_ref[i, :, k:].astype(f32)).astype(bf16)

    return call(body, [((half, 2 * k), bf16)] * 2, (x, gq, go, att, got), name)


def down_back(gf, slope, near, other, hb, hid_local):
    width, tokens = gf.shape
    steps = hid_local // hb
    nn_, no = len(near), len(other)
    pieces = (*near, *other)

    def body(gf_ref, slope_ref, *refs):
        gu_ref, sum_ref, bd_ref = refs[nn_ + no :]
        g = gf_ref[...]
        ones = ones_rows(tokens)

        @pl.when(pl.program_id(0) == 0)
        def _():
            bd_ref[...] = nt(ones, g)

        for i, w in enumerate((refs[:nn_], refs[nn_ : nn_ + no])):
            v = (tn(rows_of(w), g) * slope_ref[i].astype(f32)).astype(bf16)
            gu_ref[i] = v
            sum_ref[i] = nt(ones, v)

    spec = pl.BlockSpec((2, hb, tokens), lambda s: (0, s, 0))
    return call(
        body, [((2, hid_local, tokens), bf16), ((2, 8, hid_local), f32), ((8, width), f32)], (gf, slope, *pieces), "down_back",
        (steps,), [whole(gf), spec] + weight_specs(pieces, hb, 1 + steps),
        [spec, pl.BlockSpec((2, 8, hb), lambda s: (0, 0, s)), whole_out((8, width))],
    )


def up_back(gu, gf, xh1, r1, vecs, near, other, hb):
    width, tokens = gf.shape
    steps = gu.shape[1] // hb
    nn_, no = len(near), len(other)
    pieces = (*near, *other)

    def body(gu_ref, gf_ref, xh_ref, r1_ref, vec_ref, *refs):
        go_ref, sum_ref, acc_ref = refs[nn_ + no :]
        step = pl.program_id(0)

        @pl.when(step == 0)
        def _():
            acc_ref[...] = gf_ref[...].astype(f32)

        acc_ref[...] += nn(rows_of(refs[:nn_]), gu_ref[0]) + nn(rows_of(refs[nn_ : nn_ + no]), gu_ref[1])

        @pl.when(step == steps - 1)
        def _():
            vec = jnp.transpose(vec_ref[...])
            g = acc_ref[...]
            xh = xh_ref[...].astype(f32)
            ones = ones_rows(tokens)
            sum_ref[0:8] = nt(ones, (g * xh).astype(bf16))
            sum_ref[8:16] = nt(ones, g.astype(bf16))
            a = g * vec[:, 1:2]
            first = jnp.sum(a, axis=0, keepdims=True) * (1.0 / width)
            second = jnp.sum(a * xh, axis=0, keepdims=True) * (1.0 / width)
            go = (r1_ref[0:1] * (a - first - xh * second)).astype(bf16)
            go_ref[...] = go
            sum_ref[16:24] = nt(ones, go)

    return call(
        body, [((width, tokens), bf16), ((24, width), f32)], (gu, gf, xh1, r1, vecs, *pieces), "up_back", (steps,),
        [pl.BlockSpec((2, hb, tokens), lambda s: (0, s, 0))] + [whole(a) for a in (gf, xh1, r1, vecs)] + weight_specs(pieces, hb, 1),
        [whole_out((width, tokens)), whole_out((24, width))], [pltpu.VMEM((width, tokens), f32)],
    )


def attention_mid(go, att, inv, fq, near, other, heads, head_width):
    width, tokens = go.shape
    feats = fq.shape[0] // heads
    hb = heads * head_width // 2
    rows = head_width + PAD
    nn_, no = len(near), len(other)
    pieces = (*near, *other)

    def body(go_ref, att_ref, inv_ref, fq_ref, *refs):
        gn_ref, kv_ref = refs[nn_ + no :]
        g = go_ref[...]
        zeros = jnp.zeros((PAD - 1, tokens), f32)
        for i, w in enumerate((refs[:nn_], refs[nn_ : nn_ + no])):
            ga = tn(rows_of(w), g)
            for hl in range(heads // 2):
                h = i * (heads // 2) + hl
                gh = ga[hl * head_width : (hl + 1) * head_width]
                inverse = inv_ref[h : h + 1]
                a = att_ref[h * head_width : (h + 1) * head_width].astype(f32)
                gd = -jnp.sum(gh * a, axis=0, keepdims=True) * inverse
                both = jnp.concatenate((gh * inverse, gd, zeros), axis=0).astype(bf16)
                gn_ref[h * rows : (h + 1) * rows] = both
                kv_ref[h * rows : (h + 1) * rows] = nt(both, fq_ref[h * feats : (h + 1) * feats]).astype(bf16)

    outs = [((heads * rows, tokens), bf16), ((heads * rows, feats), bf16)]
    args = (go, att, inv, fq, *pieces)
    return call(
        body, outs, args, "attention_mid", (1,), [whole(a) for a in args[:4]] + fixed_specs(pieces, hb, 0),
        [whole_out(s) for s, _ in outs],
    )


def query_back(gn, kv, fq, uq, omegas, heads, head_width):
    n, tokens = uq.shape
    feats = fq.shape[0] // heads
    rows = head_width + PAD
    factor = head_width ** (-0.25)

    def body(gn_ref, kv_ref, fq_ref, uq_ref, om0_ref, om1_ref, gq_ref, sum_ref):
        for h in range(heads):
            om_ref = (om0_ref, om1_ref)[h // (heads // 2)]
            e = tn(kv_ref[h * rows : (h + 1) * rows], gn_ref[h * rows : (h + 1) * rows])
            e = e * fq_ref[h * feats : (h + 1) * feats].astype(f32)
            s = jnp.sum(e, axis=0, keepdims=True)
            u = uq_ref[h * head_width : (h + 1) * head_width].astype(f32)
            gq_ref[h * head_width : (h + 1) * head_width] = (
                factor * (nn(om_ref[h % (heads // 2)], e.astype(bf16)) - s * u)
            ).astype(bf16)
        sum_ref[...] = nt(ones_rows(tokens), gq_ref[...])

    return call(body, [((n, tokens), bf16), ((8, n), f32)], (gn, kv, fq, uq, *omegas), "query_back")


def key_back(gkv0, gkv1, fk, uk, v, omegas, heads, head_width):
    n, tokens = uk.shape
    feats = fk.shape[0] // heads
    rows = head_width + PAD
    factor = head_width ** (-0.25)
    hl_n = heads // 2
    hb = hl_n * head_width

    def body(gkv0_ref, gkv1_ref, fk_ref, uk_ref, v_ref, om0_ref, om1_ref, g_ref, sum_ref):
        ones = jnp.ones((PAD, tokens), bf16)
        for h in range(heads):
            i, hl = divmod(h, hl_n)
            base = i * 2 * hb + hl * head_width
            kv = (gkv0_ref[h * rows : (h + 1) * rows].astype(f32) + gkv1_ref[h * rows : (h + 1) * rows].astype(f32)).astype(bf16)
            f = fk_ref[h * feats : (h + 1) * feats]
            at = h * head_width
            value = jnp.concatenate((v_ref[at : at + head_width], ones), axis=0)
            e = tn(kv, value) * f.astype(f32)
            s = jnp.sum(e, axis=0, keepdims=True)
            u = uk_ref[at : at + head_width].astype(f32)
            g_ref[base : base + head_width] = (
                factor * (nn((om0_ref, om1_ref)[i][hl], e.astype(bf16)) - s * u)
            ).astype(bf16)
            g_ref[base + hb : base + hb + head_width] = nn(kv[:head_width], f).astype(bf16)
        sum_ref[...] = nt(ones_rows(tokens), g_ref[...])

    return call(body, [((2 * n, tokens), bf16), ((8, 2 * n), f32)], (gkv0, gkv1, fk, uk, v, *omegas), "key_back")


def last_parts(x, g, sums, got, name):
    sum1, sum2, bd, bu, sum_q, sum_kv = sums
    n, tokens = x.shape
    q = n // 4
    k = g.shape[1]
    hb = k // 2
    hid_local = bu.shape[2]
    ups = hid_local // hb
    rows = q + EXTRA
    which = 0 if got is not None else 1

    def body(x_ref, g_ref, s1_ref, s2_ref, bd_ref, bu_ref, sq_ref, skv_ref, *refs):
        if got is None:
            o_ref, row_s, col_s = refs
        else:
            got_ref, keep_ref, send_ref, row_s, col_s = refs
        for m, v in enumerate((s1_ref[16:17], s1_ref[0:1], s1_ref[8:9], bd_ref[0:1], s2_ref[0:1], s2_ref[8:9], s2_ref[16:17])):
            row_s[m : m + 1] = v
        row_s[7:8] = jnp.zeros((1, n), f32)
        col_s[...] = jnp.zeros(col_s.shape, f32)
        for i in range(2):
            col_s[i, 0:1] = sq_ref[0:1, i * hb : (i + 1) * hb]
            col_s[i, 1:2] = skv_ref[0:1, i * k : i * k + hb]
            col_s[i, 2:3] = skv_ref[0:1, i * k + hb : (i + 1) * k]
            for u in range(ups):
                col_s[i, 3 + u : 4 + u] = bu_ref[i, 0:1, u * hb : (u + 1) * hb]
        for i in range(2):
            for jx in range(2):
                p = 2 * which + jx
                main = nt(x_ref[p * q : (p + 1) * q], g_ref[i])
                small = row_s[:, p * q : (p + 1) * q]
                small = jnp.concatenate((small, jnp.zeros((8, hb - q), f32), col_s[i]), axis=1)
                small = jnp.concatenate((small, jnp.zeros((EXTRA - 8, k), f32)), axis=0)
                if got is None:
                    o_ref[i, jx, :q] = main.astype(bf16)
                    o_ref[i, jx, q:] = small.astype(bf16)
                else:
                    o = send_ref if jx else keep_ref
                    o[i * rows : i * rows + q] = (main + got_ref[i, jx, :q].astype(f32)).astype(bf16)
                    o[i * rows + q : (i + 1) * rows] = (small + got_ref[i, jx, q:].astype(f32)).astype(bf16)

    outs = [((2, 2, rows, k), bf16)] if got is None else [((2 * rows, k), bf16)] * 2
    args = (x, g, *sums) if got is None else (x, g, *sums, got)
    return call(body, outs, args, name, scratch=[pltpu.VMEM((8, n), f32), pltpu.VMEM((2, 8, hb), f32)])


def input_grad(gq, g, go, near, other):
    width, tokens = go.shape
    hb = gq.shape[1]
    k = width // 4
    nn_, no = len(near), len(other)

    def body(gq_ref, g_ref, go_ref, *refs):
        total = go_ref[...].astype(f32)
        for i, w in enumerate((refs[:nn_], refs[nn_ : nn_ + no])):
            w = jnp.concatenate([r[:k] for r in w], axis=0)
            total = total + nn(w[:, :hb], gq_ref[i]) + nn(w[:, hb:], g_ref[i])
        for p, o_ref in enumerate(refs[nn_ + no :]):
            o_ref[...] = total[p * k : (p + 1) * k].astype(bf16)

    return call(body, [((k, tokens), bf16)] * 4, (gq, g, go, *near, *other), "input_grad")


def swap(value, axis, mask):
    size = lax.axis_size(axis)
    return lax.ppermute(value, axis, [(s, s ^ mask) for s in range(size)])


def after(value, *others):
    return lax.optimization_barrier((value, *others))[0]


class Fold:
    def __init__(self, value):
        self.value = value
        self.four = lax.axis_size("dp") == 4
        if not self.four:
            self.value = lax.psum(value, "dp")
            return
        self.odd = lax.axis_index("dp") % 2 == 1
        n = value.shape[1] // 2
        low, high = value[:, :n], value[:, n:]
        self.value = jnp.where(self.odd, high, low)
        self.got = swap(jnp.where(self.odd, low, high), "dp", 1)

    def step(self, order, mask):
        if not self.four:
            return order
        self.value = after(self.value, order) + self.got
        self.got = swap(self.value, "dp", mask)
        return self.value

    def middle(self, order):
        return self.step(order, 2)

    def back(self, order):
        return self.step(order, 1)

    def result(self):
        if not self.four:
            return self.value.astype(f32)
        a, b = self.value.astype(f32), self.got.astype(f32)
        return jnp.concatenate((jnp.where(self.odd, b, a), jnp.where(self.odd, a, b)), axis=1)


def total(keep, got, last):
    n = keep.shape[0] // 2
    return keep[:n] + got[:n] + last


def far_half(keep, got):
    n = keep.shape[0] // 2
    return keep[n:] + got[n:]


def exchange(blocks):
    return [blocks[0]] + [swap(blocks[j], "row", j) for j in (1, 2, 3)]


def reduce_small(value, axis):
    step = 1
    while step < lax.axis_size(axis):
        value = value + swap(value, axis, step)
        step *= 2
    return value


def shards(
    inputs, teacher, lengths, omega,
    w_query, b_query, w_key, b_key, w_value, b_value, w_out, b_out,
    norm1_gain, norm1_bias, w_up, up_bias, w_down, b_down, norm2_gain, norm2_bias,
):
    row_parts = lax.axis_size("row")
    feat_local, seq_length = inputs.shape
    width = feat_local * row_parts
    head_local, head_width, feats = omega.shape
    heads = head_local * lax.axis_size("col")
    tokens = seq_length // row_parts
    hb = head_local * head_width
    hid_local = w_up.shape[1]
    row = lax.axis_index("row")
    col = lax.axis_index("col")
    row_ref = row.astype(jnp.int32).reshape(1)

    omegas = (omega, swap(omega, "col", 1))
    vecs = (b_out, norm1_gain, norm1_bias, b_down, norm2_gain, norm2_bias)
    ins = split_positions(inputs, row_ref, row_parts)
    ins_got = exchange(ins)
    xs = [ins_got[j] for j in (0, 2, 1, 3)]
    own_a = narrow_small((after(w_query, *ins), w_key, w_value), vecs, (b_query, b_key, b_value), up_bias, "narrow_a")
    a_y = swap(own_a, "col", 1)
    a_x = swap(own_a, "row", 2)
    a_far = swap(after(a_x, a_y, omegas[1]), "col", 1)
    near_a = (own_a, a_x, swap(own_a, "row", 1), swap(a_x, "row", 1))
    other_a = (a_y, a_far, swap(a_y, "row", 1), swap(a_far, "row", 1))
    count = reduce_small(jnp.sum(lengths).astype(f32).reshape(1, 1) + jnp.zeros((8, 128), f32), "dp")
    own_b = narrow((after(w_out, own_a, count), w_up, w_down), 3, "narrow_b")
    b_x = swap(after(own_b, a_x, ins_got[2], ins_got[3]), "row", 2)
    b_y = swap(after(own_b, a_far), "col", 1)
    length = lax.dynamic_index_in_dim(lengths, col, 0, False)
    keep = ((row * tokens + jnp.arange(tokens, dtype=jnp.int32)) < length).astype(f32)
    keep = jnp.broadcast_to(keep[None, :], (8, tokens))
    scale = (2.0 * LOSS_SCALE) / (count * width)

    x, fq, fk, uq, uk, v, kv, vecs, up_bias_all = attention_in(
        xs, near_a, other_a, omegas, keep, head_local, head_width, hid_local
    )
    kv0 = kv + swap(kv, "row", 1)
    kv1 = swap(kv0, "row", 2)
    theirs = split_positions(after(teacher, kv0), row_ref, row_parts)
    teach = exchange(theirs)
    target = [teach[j] for j in (0, 2, 1, 3)]
    b_x = after(b_x, kv0, theirs[0])
    b_y = after(b_y, kv0, theirs[0])
    b_far_y = swap(b_x[CUT:], "col", 1)
    b_far_x = swap(b_y[:CUT], "row", 2)
    near_b = (own_b, b_x)
    near_b = near_b + tuple(swap(p, "row", 1) for p in near_b)
    other_b = (b_y, b_far_x, after(b_far_y, kv1, b_far_x, teach[2], teach[3]))
    other_b = other_b + tuple(swap(p, "row", 1) for p in other_b)
    kv, att, inv, xh1, r1, x1, hid, slope, gf, sum2, *out = middle(
        kv0, kv1, fq, x, near_b, other_b, vecs, up_bias_all, target, keep, scale, heads, head_width, hid_local
    )
    out = exchange([out[j] for j in (0, 2, 1, 3)])

    theirs = grad_theirs(gf, hid, hb, "down_theirs")
    got1 = swap(theirs, "row", 1)
    gu, bu, bd = down_back(after(gf, theirs), slope, near_b, other_b, hb, hid_local)
    kept0, kept1, send0, send1 = grad_mine(after(gf, gu), hid, got1, hb, "down_mine")
    down = ((kept0, swap(send0, "col", 1)), (kept1, swap(send1, "col", 1)))
    go, sum1 = up_back(after(gu, send0), gf, xh1, r1, vecs, near_b, other_b, hb)
    gn, gkv = attention_mid(go, att, inv, fq, near_b, other_b, heads, head_width)
    gkv0 = gkv + swap(gkv, "row", 1)
    gkv1 = swap(gkv0, "row", 2)
    far = far_half(after(down[0][0], gn, *out), down[0][1])
    r_down0 = swap(far, "row", 2)
    theirs = grad_theirs(after(x1, far), gu, hb, "up_theirs")
    got2 = swap(theirs, "row", 1)
    gq, sum_q = query_back(after(gn, theirs), kv, fq, uq, omegas, heads, head_width)
    kept0, kept1, send0, send1 = grad_mine(after(x1, gq, gkv0), gu, got2, hb, "up_mine")
    up = ((kept0, swap(send0, "col", 1)), (kept1, swap(send1, "col", 1)))
    far = far_half(after(down[1][0], send0), down[1][1])
    r_down1 = swap(far, "row", 2)
    gq = gq.reshape(2, hb, tokens)
    att2 = att.reshape(2, hb, tokens)
    theirs = pair_theirs(after(x, far), gq, go, att2, "pair_theirs")
    got3 = swap(theirs, "row", 1)
    down0 = total(after(down[0][0], theirs), down[0][1], r_down0)
    z_down0 = Fold(down0)
    g, sum_kv = key_back(after(gkv0, down0), gkv1, fk, uk, v, omegas, heads, head_width)
    g = g.reshape(2, 2 * hb, tokens)
    sums = (sum1, sum2, bd, bu, sum_q, sum_kv)
    far = far_half(after(up[0][0], g), up[0][1])
    r_up0 = swap(far, "row", 2)
    theirs = last_parts(after(x, far), g, sums, None, "last_theirs")[0]
    got4 = swap(theirs, "row", 1)
    keep3, send3 = pair_mine(after(x, theirs), gq, go, att2, got3, "pair_mine")
    r_y3 = swap(send3, "col", 1)
    keep4, send4 = last_parts(after(x, send3), g, sums, got4, "last_mine")
    r_x4 = swap(send4, "row", 2)
    down1 = total(after(down[1][0], send4), down[1][1], r_down1)
    z_down1 = Fold(down1)
    order = z_down0.middle(down1)
    far = far_half(after(up[1][0], order), up[1][1])
    r_up1 = swap(far, "row", 2)
    gin = input_grad(gq, g, after(go, far), near_a, other_a)
    far = far_half(after(keep4, gin[0]), r_x4)
    r_y4 = swap(far, "col", 1)
    up0 = total(after(up[0][0], far), up[0][1], r_up0)
    z_up0 = Fold(up0)
    order = z_down1.middle(up0)
    order = z_down0.back(order)
    far = far_half(after(keep3, order), r_y3)
    r_x3 = swap(far, "row", 2)
    gin = exchange([after(gin[j], far) for j in (0, 2, 1, 3)])
    order = z_up0.middle(far)
    up1 = total(after(up[1][0], order), up[1][1], r_up1)
    z_up1 = Fold(up1)
    order = z_down1.back(up1)
    last = total(after(keep4, order), r_x4, r_y4)
    last = jnp.concatenate((last, total(keep3, r_y3, r_x3)), axis=0)
    z_last = Fold(last)
    order = z_up1.middle(last)
    order = z_up0.back(order)
    order = z_last.middle(order)
    order = z_up1.back(order)
    order = z_last.back(order)
    out[0] = after(out[0], order)
    out = join_positions(out, row_ref)
    grad_in = join_positions([after(gin[0], out), *gin[1:]], row_ref)
    grad_down = jnp.concatenate((z_down0.result(), z_down1.result()), axis=1)
    grad_up = jnp.concatenate((z_up0.result(), z_up1.result()), axis=1)
    last = z_last.result()
    grad_pair = last[keep4.shape[0] // 2 :]

    extra = last[feat_local : keep4.shape[0] // 2]
    rows = extra[:7, :feat_local]
    cols = extra[:7, hb:]
    loss = rows[6, 0] / (count[0, 0] * width)
    return (
        out,
        loss,
        grad_in,
        grad_pair[:, :hb],
        cols[0],
        last[:feat_local, :hb],
        cols[1],
        last[:feat_local, hb:],
        cols[2],
        grad_pair[:, hb:],
        rows[0],
        rows[1],
        rows[2],
        grad_up,
        cols[3:].reshape(hid_local),
        grad_down,
        rows[3],
        rows[4],
        rows[5],
    )


def solution(mesh):
    both = P("row", ("dp", "col"))
    in_specs = (
        both, both, P("dp"), P("col", None, None),
        P("row", "col"), P("col"), P("row", "col"), P("col"), P("row", "col"), P("col"),
        P("row", "col"), P("row"), P("row"), P("row"),
        P("row", "col"), P("col"), P("row", "col"), P("row"), P("row"), P("row"),
    )
    out_specs = (
        both, P(), both,
        P("row", "col"), P("col"), P("row", "col"), P("col"), P("row", "col"), P("col"),
        P("row", "col"), P("row"), P("row"), P("row"),
        P("row", "col"), P("col"), P("row", "col"), P("row"), P("row"), P("row"),
    )
    return jax.shard_map(shards, mesh=mesh, in_specs=in_specs, out_specs=out_specs, check_vma=False)
```

```python
import jax
import jax.numpy as jnp
from jax import lax
from jax.experimental import pallas as pl
from jax.experimental.pallas import tpu as pltpu
from jax.sharding import PartitionSpec as P

LOSS_SCALE = 16777216
stabilizer = 2.0
norm_eps = 1e-12
root_half = 0.7071067811865476
inv_root_two_pi = 0.3989422804014327
f32 = jnp.float32
bf16 = jnp.bfloat16
PAD = 8
EXTRA = 16
CUT = 48
ASIDE = 256


def dot(a, b, dims):
    return lax.dot_general(a, b, (dims, ((), ())), preferred_element_type=f32)


def nn(a, b):
    return dot(a, b, ((1,), (0,)))


def nt(a, b):
    return dot(a, b, ((1,), (1,)))


def tn(a, b):
    return dot(a, b, ((0,), (0,)))


def ones_rows(tokens):
    return jnp.ones((8, tokens), bf16)


def call(body, outs, args, name, grid=None, in_specs=None, out_specs=None, scratch=(), limit=40, pinned=False):
    if grid is None:
        grid = (1,)
        in_specs = [single(a.shape) for a in args] if in_specs is None else in_specs
        out_specs = [single(s) for s, _ in outs]
    extra = dict(grid=grid, in_specs=in_specs, out_specs=out_specs)
    if pinned:
        args = [a if p is SMEM else pltpu.with_memory_space_constraint(a, pltpu.HBM) for a, p in zip(args, in_specs)]
    make = pltpu.HBM if pinned else jax.ShapeDtypeStruct
    return pl.pallas_call(
        body,
        out_shape=[make(s, d) for s, d in outs],
        scratch_shapes=list(scratch),
        compiler_params=pltpu.CompilerParams(vmem_limit_bytes=limit * 1024 * 1024),
        cost_estimate=pl.CostEstimate(flops=1000, bytes_accessed=1000, transcendentals=0),
        name=name,
        **extra,
    )(*args)


def single(shape):
    zeros = (0,) * len(shape)
    return pl.BlockSpec(shape, lambda s: zeros, pipeline_mode=pl.Buffered(1))


def whole(a):
    zeros = (0,) * a.ndim
    return pl.BlockSpec(a.shape, lambda s: zeros)


def whole_out(shape):
    zeros = (0,) * len(shape)
    return pl.BlockSpec(shape, lambda s: zeros)


SMEM = pl.BlockSpec(memory_space=pltpu.SMEM)


def split_positions(shard, row, row_parts):
    k, length = shard.shape
    n = length // row_parts

    def body(row_ref, in_ref, *out_refs):
        r = row_ref[0]
        for j, o_ref in enumerate(out_refs):
            at = pl.multiple_of(jnp.bitwise_xor(r, j) * n, n)
            o_ref[...] = in_ref[:, pl.ds(at, n)].astype(bf16)

    return call(body, [((k, n), bf16)] * row_parts, (row, shard), "split_positions", in_specs=[SMEM, single(shard.shape)], pinned=True)


def join_positions(blocks, row):
    k, n = blocks[0].shape
    parts = len(blocks)

    def body(row_ref, *refs):
        r = row_ref[0]
        o_ref = refs[parts]
        for j in range(parts):
            at = pl.multiple_of(jnp.bitwise_xor(r, j) * n, n)
            o_ref[:, pl.ds(at, n)] = refs[j][...].astype(f32)

    return call(body, [((k, n * parts), f32)], (row, *blocks), "join_positions", in_specs=[SMEM] + [single(b.shape) for b in blocks])[0]


def narrow(parts, steps, name):
    n = parts[0].shape[0]
    widths = [p.shape[1] for p in parts]

    def body(*refs):
        at = 0
        for ref, w in zip(refs, widths):
            refs[-1][:, at : at + w] = ref[...].astype(bf16)
            at += w

    return call(
        body, [((n, sum(widths)), bf16)], parts, name, (steps,),
        [pl.BlockSpec((n // steps, w), lambda s: (s, 0)) for w in widths],
        [pl.BlockSpec((n // steps, sum(widths)), lambda s: (s, 0))],
        pinned=True,
    )[0]


def narrow_small(parts, vecs, biases, up_bias, name):
    n, hb = parts[0].shape
    width = hb * len(parts)
    nv = len(vecs)
    rest = up_bias.shape[0] - width
    small = [v.reshape(1, v.shape[0]) for v in vecs] + [jnp.concatenate((*biases, up_bias)).reshape(-1, hb)]

    def body(*refs):
        p_refs = refs[: len(parts)]
        v_refs = refs[len(parts) : len(parts) + nv]
        b_ref, o_ref, small_ref = refs[len(parts) + nv :]
        small_ref[...] = jnp.zeros(small_ref.shape, f32)
        for m, ref in enumerate(v_refs):
            small_ref[m : m + 1, :n] = ref[...]
        for m, ref in enumerate(p_refs):
            o_ref[:n, m * hb : (m + 1) * hb] = ref[...].astype(bf16)
            small_ref[nv : nv + 1, m * hb : (m + 1) * hb] = b_ref[m : m + 1]
            small_ref[nv + 1 : nv + 2, m * hb : (m + 1) * hb] = b_ref[len(parts) + m : len(parts) + m + 1]
        small_ref[0:1, ASIDE : ASIDE + rest] = b_ref[2 * len(parts) : 2 * len(parts) + 1]
        value = small_ref[...]
        high = value.astype(bf16).astype(f32)
        o_ref[n:] = jnp.concatenate((high, value - high), axis=0).astype(bf16)

    scratch = [pltpu.VMEM((8, width), f32)]
    return call(body, [((n + EXTRA, width), bf16)], (*parts, *small), name, scratch=scratch, pinned=True)[0]


def small_rows(ref, k):
    v = ref[k : k + EXTRA].astype(f32)
    return v[0:8] + v[8:16]


def attention_in(xs, near, other, omegas, keep, head_local, head_width, hid_local):
    k, tokens = xs[0].shape
    feats = omegas[0].shape[2]
    heads = 2 * head_local
    hb = head_local * head_width
    rows = head_width + PAD
    factor = head_width ** (-0.25)
    n_near, n_other = len(near), len(other)

    def body(*refs):
        x_in = refs[:4]
        near_refs = refs[4 : 4 + n_near]
        other_refs = refs[4 + n_near : 4 + n_near + n_other]
        (om0_ref, om1_ref, keep_ref, x_ref, fq_ref, fk_ref, uq_ref, uk_ref, v_ref, kv_ref, vec_ref, up_ref) = refs[
            4 + n_near + n_other :
        ]
        for p in range(4):
            vec_ref[:, p * k : (p + 1) * k] = small_rows(near_refs[p], k)[:, :k]
        up_ref[...] = jnp.zeros(up_ref.shape, f32)
        for p in range(4):
            x_ref[p * k : (p + 1) * k] = x_in[p][...]
        xv = x_ref[...]
        ones = jnp.ones((PAD, tokens), bf16)
        for i, pieces in enumerate((near_refs, other_refs)):
            omega_ref = (om0_ref, om1_ref)[i]
            small = small_rows(pieces[0], k)
            up_ref[i : i + 1, : 3 * hb] = small[7:8]
            up_ref[i : i + 1, 3 * hb :] = small[0:1, ASIDE : ASIDE + hid_local - 3 * hb]
            triple = tn(jnp.concatenate([p[:k] for p in pieces], axis=0), xv) + jnp.transpose(small)[:, 6:7]
            for hl in range(head_local):
                h = i * head_local + hl
                at = h * head_width
                lo = hl * head_width
                value = triple[2 * hb + lo : 2 * hb + lo + head_width].astype(bf16)
                v_ref[at : at + head_width] = value
                for base, u_ref, f_ref, mask in ((0, uq_ref, fq_ref, False), (hb, uk_ref, fk_ref, True)):
                    u = triple[base + lo : base + lo + head_width] * factor
                    ub = u.astype(bf16)
                    u_ref[at : at + head_width] = ub
                    z = tn(omega_ref[hl], ub)
                    feat = jnp.exp(z - (0.5 * jnp.sum(u * u, axis=0, keepdims=True) + stabilizer))
                    if mask:
                        feat = feat * keep_ref[0:1]
                    feat = feat.astype(bf16)
                    f_ref[h * feats : (h + 1) * feats] = feat
                kv_ref[h * rows : (h + 1) * rows] = nt(jnp.concatenate((value, ones), axis=0), feat).astype(bf16)

    n = heads * head_width
    outs = [((4 * k, tokens), bf16)] + [((heads * feats, tokens), bf16)] * 2 + [((n, tokens), bf16)] * 3
    outs += [((heads * rows, feats), bf16), ((8, 4 * k), f32), ((8, hid_local), f32)]
    return call(body, outs, (*xs, *near, *other, *omegas, keep), "attention_in", pinned=True)


def weight_specs(pieces, block, first):
    return [pl.BlockSpec((p.shape[0], block), lambda s, f=first: (0, f + s)) for p in pieces]


def fixed_specs(pieces, block, at):
    return [pl.BlockSpec((p.shape[0], block), lambda s: (0, at)) for p in pieces]


def rows_of(refs):
    return jnp.concatenate([r[...] for r in refs], axis=0)


def middle(kv0, kv1, fq, x, near, other, vecs, up_bias, target, keep, scale, heads, head_width, hid_local):
    width, tokens = x.shape
    feats = kv0.shape[1]
    rows = head_width + PAD
    hb = heads * head_width // 2
    steps = hid_local // hb
    k = width // 4
    nn_, no = len(near), len(other)
    np_ = nn_ + no

    def body(*refs):
        kv0_ref, kv1_ref, fq_ref, x_ref = refs[:4]
        out_w = refs[4 : 4 + np_]
        up_w = refs[4 + np_ : 4 + 2 * np_]
        down_w = refs[4 + 2 * np_ : 4 + 3 * np_]
        (vec_ref, upb_ref, t0, t1, t2, t3, keep_ref, scale_ref,
         kv_ref, att_ref, inv_ref, xh1_ref, r1_ref, x1_ref, hid_ref, slope_ref, gf_ref, sum_ref,
         o0, o1, o2, o3, acc_ref, vec_s) = refs[4 + 3 * np_ :]
        step = pl.program_id(0)

        @pl.when(step == 0)
        def _():
            vec = jnp.transpose(vec_ref[...])
            vec_s[...] = vec
            kv_ref[...] = (kv0_ref[...].astype(f32) + kv1_ref[...].astype(f32)).astype(bf16)
            for h in range(heads):
                both = nn(kv_ref[h * rows : (h + 1) * rows], fq_ref[h * feats : (h + 1) * feats])
                inverse = 1.0 / both[head_width : head_width + 1]
                inv_ref[h : h + 1] = inverse
                att_ref[h * head_width : (h + 1) * head_width] = (both[:head_width] * inverse).astype(bf16)
            w = jnp.concatenate((rows_of(out_w[:nn_]), rows_of(out_w[nn_:])), axis=1)
            h1 = nn(w, att_ref[...]) + x_ref[...].astype(f32) + vec[:, 0:1]
            mean = jnp.sum(h1, axis=0, keepdims=True) * (1.0 / width)
            h1 = h1 - mean
            r1 = lax.rsqrt(jnp.sum(h1 * h1, axis=0, keepdims=True) * (1.0 / width) + norm_eps)
            h1 = h1 * r1
            r1_ref[...] = jnp.broadcast_to(r1, (8, tokens))
            xh1_ref[...] = h1.astype(bf16)
            x1 = h1 * vec[:, 1:2] + vec[:, 2:3]
            x1_ref[...] = x1.astype(bf16)
            acc_ref[...] = x1 + vec[:, 3:4]

        x1b = x1_ref[...]
        bias = jnp.transpose(upb_ref[...])
        total = acc_ref[...]
        for i, (a, b) in enumerate(((0, nn_), (nn_, np_))):
            up = tn(rows_of(up_w[a:b]), x1b) + bias[:, i : i + 1]
            gate = 0.5 * (1.0 + lax.erf(up * root_half))
            slope_ref[i] = (gate + up * inv_root_two_pi * jnp.exp(-0.5 * up * up)).astype(bf16)
            hid = (up * gate).astype(bf16)
            hid_ref[i] = hid
            total = total + nn(rows_of(down_w[a:b]), hid)
        acc_ref[...] = total

        @pl.when(step == steps - 1)
        def _():
            vec = vec_s[...]
            h2 = acc_ref[...]
            mean = jnp.sum(h2, axis=0, keepdims=True) * (1.0 / width)
            h2 = h2 - mean
            r2 = lax.rsqrt(jnp.sum(h2 * h2, axis=0, keepdims=True) * (1.0 / width) + norm_eps)
            h2 = h2 * r2
            out = h2 * vec[:, 4:5] + vec[:, 5:6]
            for p, o_ref in enumerate((o0, o1, o2, o3)):
                o_ref[...] = out[p * k : (p + 1) * k].astype(bf16)
            target = jnp.concatenate((t0[...], t1[...], t2[...], t3[...]), axis=0).astype(f32)
            diff = (out - target) * keep_ref[0:1]
            g = diff * scale_ref[0:1, 0:1]
            ones = ones_rows(tokens)
            sum_ref[0:8] = nt(ones, (g * h2).astype(bf16))
            sum_ref[8:16] = nt(ones, g.astype(bf16))
            sum_ref[16:24] = jnp.full((8, width), jnp.sum(diff * diff), f32)
            a = g * vec[:, 4:5]
            first = jnp.sum(a, axis=0, keepdims=True) * (1.0 / width)
            second = jnp.sum(a * h2, axis=0, keepdims=True) * (1.0 / width)
            gf_ref[...] = (r2 * (a - first - h2 * second)).astype(bf16)

    outs = [
        ((heads * rows, feats), bf16), ((width, tokens), bf16), ((16, tokens), f32), ((width, tokens), bf16),
        ((8, tokens), f32), ((width, tokens), bf16), ((2, hid_local, tokens), bf16), ((2, hid_local, tokens), bf16),
        ((width, tokens), bf16), ((24, width), f32),
    ] + [((k, tokens), bf16)] * 4
    pieces = (*near, *other)
    args = (kv0, kv1, fq, x, *pieces, *pieces, *pieces, vecs, up_bias, *target, keep, scale)
    in_specs = [whole(a) for a in (kv0, kv1, fq, x)]
    in_specs += fixed_specs(pieces, hb, 0) + weight_specs(pieces, hb, 1) + weight_specs(pieces, hb, 1 + steps)
    in_specs += [whole(vecs), pl.BlockSpec((8, hb), lambda s: (0, s))] + [whole(t) for t in target] + [whole(keep), whole(scale)]
    out_specs = [whole_out(s) for s, _ in outs]
    out_specs[6] = out_specs[7] = pl.BlockSpec((2, hb, tokens), lambda s: (0, s, 0))
    scratch = [pltpu.VMEM((width, tokens), f32), pltpu.VMEM((width, 8), f32)]
    return call(body, outs, args, "middle", (steps,), in_specs, out_specs, scratch, limit=56, pinned=True)


def grad_theirs(left, right, block, name):
    n, tokens = left.shape
    k = right.shape[1]
    half = n // 2

    def body(l_ref, r_ref, o_ref):
        for i in range(2):
            o_ref[i] = nt(l_ref[...], r_ref[i]).astype(bf16)

    return call(
        body, [((2, half, k), bf16)], (left, right), name, (k // block,),
        [pl.BlockSpec((half, tokens), lambda s: (1, 0)), pl.BlockSpec((2, block, tokens), lambda s: (0, s, 0))],
        [pl.BlockSpec((2, half, block), lambda s: (0, 0, s))],
    )[0]


def grad_mine(left, right, got, block, name):
    n, tokens = left.shape
    k = right.shape[1]
    half = n // 2
    share = k // block // 2

    def body(l_ref, r_ref, got_ref, keep0, keep1, send0, send1):
        step = pl.program_id(0)

        def part(keep_ref, send_ref):
            for i, o_ref in enumerate((keep_ref, send_ref)):
                o_ref[...] = (nt(l_ref[...], r_ref[i]) + got_ref[i].astype(f32)).astype(bf16)

        pl.when(step < share)(lambda: part(keep0, send0))
        pl.when(step >= share)(lambda: part(keep1, send1))

    first = pl.BlockSpec((half, block), lambda s: (0, jnp.minimum(s, share - 1)))
    second = pl.BlockSpec((half, block), lambda s: (0, jnp.maximum(s - share, 0)))
    return call(
        body, [((half, k // 2), bf16)] * 4, (left, right, got), name, (2 * share,),
        [
            pl.BlockSpec((half, tokens), lambda s: (0, 0)),
            pl.BlockSpec((2, block, tokens), lambda s: (0, s, 0)),
            pl.BlockSpec((2, half, block), lambda s: (0, 0, s)),
        ],
        [first, second, first, second],
    )


def pair_theirs(x, gq, go, att, name):
    n, tokens = x.shape
    half = n // 2
    k = gq.shape[1]

    def body(x_ref, gq_ref, go_ref, att_ref, o_ref):
        for i in range(2):
            o_ref[i, :, :k] = nt(x_ref[half:], gq_ref[i]).astype(bf16)
            o_ref[i, :, k:] = nt(go_ref[half:], att_ref[i]).astype(bf16)

    return call(body, [((2, half, 2 * k), bf16)], (x, gq, go, att), name)[0]


def pair_mine(x, gq, go, att, got, name):
    n, tokens = x.shape
    half = n // 2
    k = gq.shape[1]

    def body(x_ref, gq_ref, go_ref, att_ref, got_ref, keep_ref, send_ref):
        for i, o_ref in enumerate((keep_ref, send_ref)):
            o_ref[:, :k] = (nt(x_ref[:half], gq_ref[i]) + got_ref[i, :, :k].astype(f32)).astype(bf16)
            o_ref[:, k:] = (nt(go_ref[:half], att_ref[i]) + got_ref[i, :, k:].astype(f32)).astype(bf16)

    return call(body, [((half, 2 * k), bf16)] * 2, (x, gq, go, att, got), name)


def down_back(gf, slope, near, other, hb, hid_local):
    width, tokens = gf.shape
    steps = hid_local // hb
    nn_, no = len(near), len(other)
    pieces = (*near, *other)

    def body(gf_ref, slope_ref, *refs):
        gu_ref, sum_ref, bd_ref = refs[nn_ + no :]
        g = gf_ref[...]
        ones = ones_rows(tokens)

        @pl.when(pl.program_id(0) == 0)
        def _():
            bd_ref[...] = nt(ones, g)

        for i, w in enumerate((refs[:nn_], refs[nn_ : nn_ + no])):
            v = (tn(rows_of(w), g) * slope_ref[i].astype(f32)).astype(bf16)
            gu_ref[i] = v
            sum_ref[i] = nt(ones, v)

    spec = pl.BlockSpec((2, hb, tokens), lambda s: (0, s, 0))
    return call(
        body, [((2, hid_local, tokens), bf16), ((2, 8, hid_local), f32), ((8, width), f32)], (gf, slope, *pieces), "down_back",
        (steps,), [whole(gf), spec] + weight_specs(pieces, hb, 1 + steps),
        [spec, pl.BlockSpec((2, 8, hb), lambda s: (0, 0, s)), whole_out((8, width))],
    )


def up_back(gu, gf, xh1, r1, vecs, near, other, hb):
    width, tokens = gf.shape
    steps = gu.shape[1] // hb
    nn_, no = len(near), len(other)
    pieces = (*near, *other)

    def body(gu_ref, gf_ref, xh_ref, r1_ref, vec_ref, *refs):
        go_ref, sum_ref, acc_ref = refs[nn_ + no :]
        step = pl.program_id(0)

        @pl.when(step == 0)
        def _():
            acc_ref[...] = gf_ref[...].astype(f32)

        acc_ref[...] += nn(rows_of(refs[:nn_]), gu_ref[0]) + nn(rows_of(refs[nn_ : nn_ + no]), gu_ref[1])

        @pl.when(step == steps - 1)
        def _():
            vec = jnp.transpose(vec_ref[...])
            g = acc_ref[...]
            xh = xh_ref[...].astype(f32)
            ones = ones_rows(tokens)
            sum_ref[0:8] = nt(ones, (g * xh).astype(bf16))
            sum_ref[8:16] = nt(ones, g.astype(bf16))
            a = g * vec[:, 1:2]
            first = jnp.sum(a, axis=0, keepdims=True) * (1.0 / width)
            second = jnp.sum(a * xh, axis=0, keepdims=True) * (1.0 / width)
            go = (r1_ref[0:1] * (a - first - xh * second)).astype(bf16)
            go_ref[...] = go
            sum_ref[16:24] = nt(ones, go)

    return call(
        body, [((width, tokens), bf16), ((24, width), f32)], (gu, gf, xh1, r1, vecs, *pieces), "up_back", (steps,),
        [pl.BlockSpec((2, hb, tokens), lambda s: (0, s, 0))] + [whole(a) for a in (gf, xh1, r1, vecs)] + weight_specs(pieces, hb, 1),
        [whole_out((width, tokens)), whole_out((24, width))], [pltpu.VMEM((width, tokens), f32)],
    )


def attention_mid(go, att, inv, fq, near, other, heads, head_width):
    width, tokens = go.shape
    feats = fq.shape[0] // heads
    hb = heads * head_width // 2
    rows = head_width + PAD
    nn_, no = len(near), len(other)
    pieces = (*near, *other)

    def body(go_ref, att_ref, inv_ref, fq_ref, *refs):
        gn_ref, kv_ref = refs[nn_ + no :]
        g = go_ref[...]
        zeros = jnp.zeros((PAD - 1, tokens), f32)
        for i, w in enumerate((refs[:nn_], refs[nn_ : nn_ + no])):
            ga = tn(rows_of(w), g)
            for hl in range(heads // 2):
                h = i * (heads // 2) + hl
                gh = ga[hl * head_width : (hl + 1) * head_width]
                inverse = inv_ref[h : h + 1]
                a = att_ref[h * head_width : (h + 1) * head_width].astype(f32)
                gd = -jnp.sum(gh * a, axis=0, keepdims=True) * inverse
                both = jnp.concatenate((gh * inverse, gd, zeros), axis=0).astype(bf16)
                gn_ref[h * rows : (h + 1) * rows] = both
                kv_ref[h * rows : (h + 1) * rows] = nt(both, fq_ref[h * feats : (h + 1) * feats]).astype(bf16)

    outs = [((heads * rows, tokens), bf16), ((heads * rows, feats), bf16)]
    args = (go, att, inv, fq, *pieces)
    return call(
        body, outs, args, "attention_mid", (1,), [whole(a) for a in args[:4]] + fixed_specs(pieces, hb, 0),
        [whole_out(s) for s, _ in outs],
    )


def query_back(gn, kv, fq, uq, omegas, heads, head_width):
    n, tokens = uq.shape
    feats = fq.shape[0] // heads
    rows = head_width + PAD
    factor = head_width ** (-0.25)

    def body(gn_ref, kv_ref, fq_ref, uq_ref, om0_ref, om1_ref, gq_ref, sum_ref):
        for h in range(heads):
            om_ref = (om0_ref, om1_ref)[h // (heads // 2)]
            e = tn(kv_ref[h * rows : (h + 1) * rows], gn_ref[h * rows : (h + 1) * rows])
            e = e * fq_ref[h * feats : (h + 1) * feats].astype(f32)
            s = jnp.sum(e, axis=0, keepdims=True)
            u = uq_ref[h * head_width : (h + 1) * head_width].astype(f32)
            gq_ref[h * head_width : (h + 1) * head_width] = (
                factor * (nn(om_ref[h % (heads // 2)], e.astype(bf16)) - s * u)
            ).astype(bf16)
        sum_ref[...] = nt(ones_rows(tokens), gq_ref[...])

    return call(body, [((n, tokens), bf16), ((8, n), f32)], (gn, kv, fq, uq, *omegas), "query_back")


def key_back(gkv0, gkv1, fk, uk, v, omegas, heads, head_width):
    n, tokens = uk.shape
    feats = fk.shape[0] // heads
    rows = head_width + PAD
    factor = head_width ** (-0.25)
    hl_n = heads // 2
    hb = hl_n * head_width

    def body(gkv0_ref, gkv1_ref, fk_ref, uk_ref, v_ref, om0_ref, om1_ref, g_ref, sum_ref):
        ones = jnp.ones((PAD, tokens), bf16)
        for h in range(heads):
            i, hl = divmod(h, hl_n)
            base = i * 2 * hb + hl * head_width
            kv = (gkv0_ref[h * rows : (h + 1) * rows].astype(f32) + gkv1_ref[h * rows : (h + 1) * rows].astype(f32)).astype(bf16)
            f = fk_ref[h * feats : (h + 1) * feats]
            at = h * head_width
            value = jnp.concatenate((v_ref[at : at + head_width], ones), axis=0)
            e = tn(kv, value) * f.astype(f32)
            s = jnp.sum(e, axis=0, keepdims=True)
            u = uk_ref[at : at + head_width].astype(f32)
            g_ref[base : base + head_width] = (
                factor * (nn((om0_ref, om1_ref)[i][hl], e.astype(bf16)) - s * u)
            ).astype(bf16)
            g_ref[base + hb : base + hb + head_width] = nn(kv[:head_width], f).astype(bf16)
        sum_ref[...] = nt(ones_rows(tokens), g_ref[...])

    return call(body, [((2 * n, tokens), bf16), ((8, 2 * n), f32)], (gkv0, gkv1, fk, uk, v, *omegas), "key_back")


def last_parts(x, g, sums, got, name):
    sum1, sum2, bd, bu, sum_q, sum_kv = sums
    n, tokens = x.shape
    q = n // 4
    k = g.shape[1]
    hb = k // 2
    hid_local = bu.shape[2]
    ups = hid_local // hb
    rows = q + EXTRA
    which = 0 if got is not None else 1

    def body(x_ref, g_ref, s1_ref, s2_ref, bd_ref, bu_ref, sq_ref, skv_ref, *refs):
        if got is None:
            o_ref, row_s, col_s = refs
        else:
            got_ref, keep_ref, send_ref, row_s, col_s = refs
        for m, v in enumerate((s1_ref[16:17], s1_ref[0:1], s1_ref[8:9], bd_ref[0:1], s2_ref[0:1], s2_ref[8:9], s2_ref[16:17])):
            row_s[m : m + 1] = v
        row_s[7:8] = jnp.zeros((1, n), f32)
        col_s[...] = jnp.zeros(col_s.shape, f32)
        for i in range(2):
            col_s[i, 0:1] = sq_ref[0:1, i * hb : (i + 1) * hb]
            col_s[i, 1:2] = skv_ref[0:1, i * k : i * k + hb]
            col_s[i, 2:3] = skv_ref[0:1, i * k + hb : (i + 1) * k]
            for u in range(ups):
                col_s[i, 3 + u : 4 + u] = bu_ref[i, 0:1, u * hb : (u + 1) * hb]
        for i in range(2):
            for jx in range(2):
                p = 2 * which + jx
                main = nt(x_ref[p * q : (p + 1) * q], g_ref[i])
                small = row_s[:, p * q : (p + 1) * q]
                small = jnp.concatenate((small, jnp.zeros((8, hb - q), f32), col_s[i]), axis=1)
                small = jnp.concatenate((small, jnp.zeros((EXTRA - 8, k), f32)), axis=0)
                if got is None:
                    o_ref[i, jx, :q] = main.astype(bf16)
                    o_ref[i, jx, q:] = small.astype(bf16)
                else:
                    o = send_ref if jx else keep_ref
                    o[i * rows : i * rows + q] = (main + got_ref[i, jx, :q].astype(f32)).astype(bf16)
                    o[i * rows + q : (i + 1) * rows] = (small + got_ref[i, jx, q:].astype(f32)).astype(bf16)

    outs = [((2, 2, rows, k), bf16)] if got is None else [((2 * rows, k), bf16)] * 2
    args = (x, g, *sums) if got is None else (x, g, *sums, got)
    return call(body, outs, args, name, scratch=[pltpu.VMEM((8, n), f32), pltpu.VMEM((2, 8, hb), f32)])


def input_grad(gq, g, go, near, other):
    width, tokens = go.shape
    hb = gq.shape[1]
    k = width // 4
    nn_, no = len(near), len(other)

    def body(gq_ref, g_ref, go_ref, *refs):
        total = go_ref[...].astype(f32)
        for i, w in enumerate((refs[:nn_], refs[nn_ : nn_ + no])):
            w = jnp.concatenate([r[:k] for r in w], axis=0)
            total = total + nn(w[:, :hb], gq_ref[i]) + nn(w[:, hb:], g_ref[i])
        for p, o_ref in enumerate(refs[nn_ + no :]):
            o_ref[...] = total[p * k : (p + 1) * k].astype(bf16)

    return call(body, [((k, tokens), bf16)] * 4, (gq, g, go, *near, *other), "input_grad")


def swap(value, axis, mask):
    size = lax.axis_size(axis)
    return lax.ppermute(value, axis, [(s, s ^ mask) for s in range(size)])


def after(value, *others):
    return lax.optimization_barrier((value, *others))[0]


class Fold:
    def __init__(self, value):
        self.value = value
        self.four = lax.axis_size("dp") == 4
        if not self.four:
            self.value = lax.psum(value, "dp")
            return
        self.odd = lax.axis_index("dp") % 2 == 1
        n = value.shape[1] // 2
        low, high = value[:, :n], value[:, n:]
        self.value = jnp.where(self.odd, high, low)
        self.got = swap(jnp.where(self.odd, low, high), "dp", 1)

    def step(self, order, mask):
        if not self.four:
            return order
        self.value = after(self.value, order) + self.got
        self.got = swap(self.value, "dp", mask)
        return self.value

    def middle(self, order):
        return self.step(order, 2)

    def back(self, order):
        return self.step(order, 1)

    def result(self):
        if not self.four:
            return self.value.astype(f32)
        a, b = self.value.astype(f32), self.got.astype(f32)
        return jnp.concatenate((jnp.where(self.odd, b, a), jnp.where(self.odd, a, b)), axis=1)


def total(keep, got, last):
    n = keep.shape[0] // 2
    return keep[:n] + got[:n] + last


def far_half(keep, got):
    n = keep.shape[0] // 2
    return keep[n:] + got[n:]


def exchange(blocks):
    return [blocks[0]] + [swap(blocks[j], "row", j) for j in (1, 2, 3)]


def reduce_small(value, axis):
    step = 1
    while step < lax.axis_size(axis):
        value = value + swap(value, axis, step)
        step *= 2
    return value


def shards(
    inputs, teacher, lengths, omega,
    w_query, b_query, w_key, b_key, w_value, b_value, w_out, b_out,
    norm1_gain, norm1_bias, w_up, up_bias, w_down, b_down, norm2_gain, norm2_bias,
):
    row_parts = lax.axis_size("row")
    feat_local, seq_length = inputs.shape
    width = feat_local * row_parts
    head_local, head_width, feats = omega.shape
    heads = head_local * lax.axis_size("col")
    tokens = seq_length // row_parts
    hb = head_local * head_width
    hid_local = w_up.shape[1]
    row = lax.axis_index("row")
    col = lax.axis_index("col")
    row_ref = row.astype(jnp.int32).reshape(1)

    omegas = (omega, swap(omega, "col", 1))
    vecs = (b_out, norm1_gain, norm1_bias, b_down, norm2_gain, norm2_bias)
    ins = split_positions(inputs, row_ref, row_parts)
    ins_got = exchange(ins)
    xs = [ins_got[j] for j in (0, 2, 1, 3)]
    own_a = narrow_small((after(w_query, *ins), w_key, w_value), vecs, (b_query, b_key, b_value), up_bias, "narrow_a")
    a_y = swap(own_a, "col", 1)
    a_x = swap(own_a, "row", 2)
    a_far = swap(after(a_x, a_y, omegas[1]), "col", 1)
    near_a = (own_a, a_x, swap(own_a, "row", 1), swap(a_x, "row", 1))
    other_a = (a_y, a_far, swap(a_y, "row", 1), swap(a_far, "row", 1))
    count = reduce_small(jnp.sum(lengths).astype(f32).reshape(1, 1) + jnp.zeros((8, 128), f32), "dp")
    own_b = narrow((after(w_out, own_a, count), w_up, w_down), 3, "narrow_b")
    b_x = swap(after(own_b, a_x, ins_got[2], ins_got[3]), "row", 2)
    b_y = swap(after(own_b, a_far), "col", 1)
    length = lax.dynamic_index_in_dim(lengths, col, 0, False)
    keep = ((row * tokens + jnp.arange(tokens, dtype=jnp.int32)) < length).astype(f32)
    keep = jnp.broadcast_to(keep[None, :], (8, tokens))
    scale = (2.0 * LOSS_SCALE) / (count * width)

    x, fq, fk, uq, uk, v, kv, vecs, up_bias_all = attention_in(
        xs, near_a, other_a, omegas, keep, head_local, head_width, hid_local
    )
    kv0 = kv + swap(kv, "row", 1)
    kv1 = swap(kv0, "row", 2)
    theirs = split_positions(after(teacher, kv0), row_ref, row_parts)
    teach = exchange(theirs)
    target = [teach[j] for j in (0, 2, 1, 3)]
    b_x = after(b_x, kv0, theirs[0])
    b_y = after(b_y, kv0, theirs[0])
    b_far_y = swap(b_x[CUT:], "col", 1)
    b_far_x = swap(b_y[:CUT], "row", 2)
    near_b = (own_b, b_x)
    near_b = near_b + tuple(swap(p, "row", 1) for p in near_b)
    other_b = (b_y, b_far_x, after(b_far_y, kv1, b_far_x, teach[2], teach[3]))
    other_b = other_b + tuple(swap(p, "row", 1) for p in other_b)
    kv, att, inv, xh1, r1, x1, hid, slope, gf, sum2, *out = middle(
        kv0, kv1, fq, x, near_b, other_b, vecs, up_bias_all, target, keep, scale, heads, head_width, hid_local
    )
    out = exchange([out[j] for j in (0, 2, 1, 3)])

    theirs = grad_theirs(gf, hid, hb, "down_theirs")
    got1 = swap(theirs, "row", 1)
    gu, bu, bd = down_back(after(gf, theirs), slope, near_b, other_b, hb, hid_local)
    kept0, kept1, send0, send1 = grad_mine(after(gf, gu), hid, got1, hb, "down_mine")
    down = ((kept0, swap(send0, "col", 1)), (kept1, swap(send1, "col", 1)))
    go, sum1 = up_back(after(gu, send0), gf, xh1, r1, vecs, near_b, other_b, hb)
    gn, gkv = attention_mid(go, att, inv, fq, near_b, other_b, heads, head_width)
    gkv0 = gkv + swap(gkv, "row", 1)
    gkv1 = swap(gkv0, "row", 2)
    far = far_half(after(down[0][0], gn, *out), down[0][1])
    r_down0 = swap(far, "row", 2)
    theirs = grad_theirs(after(x1, far), gu, hb, "up_theirs")
    got2 = swap(theirs, "row", 1)
    gq, sum_q = query_back(after(gn, theirs), kv, fq, uq, omegas, heads, head_width)
    down0 = total(after(down[0][0], gq), down[0][1], r_down0)
    z_down0 = Fold(down0)
    kept0, kept1, send0, send1 = grad_mine(after(x1, down0, gkv0), gu, got2, hb, "up_mine")
    up = ((kept0, swap(send0, "col", 1)), (kept1, swap(send1, "col", 1)))
    far = far_half(after(down[1][0], send0), down[1][1])
    r_down1 = swap(far, "row", 2)
    gq = gq.reshape(2, hb, tokens)
    att2 = att.reshape(2, hb, tokens)
    theirs = pair_theirs(after(x, far, gkv1), gq, go, att2, "pair_theirs")
    got3 = swap(theirs, "row", 1)
    g, sum_kv = key_back(after(gkv0, theirs), gkv1, fk, uk, v, omegas, heads, head_width)
    g = g.reshape(2, 2 * hb, tokens)
    sums = (sum1, sum2, bd, bu, sum_q, sum_kv)
    far = far_half(after(up[0][0], g), up[0][1])
    r_up0 = swap(far, "row", 2)
    theirs = last_parts(after(x, far), g, sums, None, "last_theirs")[0]
    got4 = swap(theirs, "row", 1)
    keep3, send3 = pair_mine(after(x, theirs), gq, go, att2, got3, "pair_mine")
    r_y3 = swap(send3, "col", 1)
    far = far_half(after(up[1][0], send3), up[1][1])
    r_up1 = swap(far, "row", 2)
    keep4, send4 = last_parts(after(x, far), g, sums, got4, "last_mine")
    r_x4 = swap(send4, "row", 2)
    down1 = total(after(down[1][0], send4), down[1][1], r_down1)
    z_down1 = Fold(down1)
    order = z_down0.middle(down1)
    gin = input_grad(gq, g, after(go, order), near_a, other_a)
    far = far_half(after(keep4, gin[0]), r_x4)
    r_y4 = swap(far, "col", 1)
    up0 = total(after(up[0][0], far), up[0][1], r_up0)
    z_up0 = Fold(up0)
    order = z_down1.middle(up0)
    order = z_down0.back(order)
    far = far_half(after(keep3, order), r_y3)
    r_x3 = swap(far, "row", 2)
    gin = exchange([after(gin[j], far) for j in (0, 2, 1, 3)])
    last = total(after(keep4, far), r_x4, r_y4)
    order = z_up0.middle(last)
    up1 = total(after(up[1][0], order), up[1][1], r_up1)
    z_up1 = Fold(up1)
    order = z_down1.back(up1)
    last = jnp.concatenate((last, total(after(keep3, order), r_y3, r_x3)), axis=0)
    z_last = Fold(last)
    order = z_up1.middle(last)
    order = z_up0.back(order)
    order = z_last.middle(order)
    order = z_up1.back(order)
    order = z_last.back(order)
    out[0] = after(out[0], order)
    out = join_positions(out, row_ref)
    grad_in = join_positions([after(gin[0], out), *gin[1:]], row_ref)
    grad_down = jnp.concatenate((z_down0.result(), z_down1.result()), axis=1)
    grad_up = jnp.concatenate((z_up0.result(), z_up1.result()), axis=1)
    last = z_last.result()
    grad_pair = last[keep4.shape[0] // 2 :]

    extra = last[feat_local : keep4.shape[0] // 2]
    rows = extra[:7, :feat_local]
    cols = extra[:7, hb:]
    loss = rows[6, 0] / (count[0, 0] * width)
    return (
        out,
        loss,
        grad_in,
        grad_pair[:, :hb],
        cols[0],
        last[:feat_local, :hb],
        cols[1],
        last[:feat_local, hb:],
        cols[2],
        grad_pair[:, hb:],
        rows[0],
        rows[1],
        rows[2],
        grad_up,
        cols[3:].reshape(hid_local),
        grad_down,
        rows[3],
        rows[4],
        rows[5],
    )


def solution(mesh):
    both = P("row", ("dp", "col"))
    in_specs = (
        both, both, P("dp"), P("col", None, None),
        P("row", "col"), P("col"), P("row", "col"), P("col"), P("row", "col"), P("col"),
        P("row", "col"), P("row"), P("row"), P("row"),
        P("row", "col"), P("col"), P("row", "col"), P("row"), P("row"), P("row"),
    )
    out_specs = (
        both, P(), both,
        P("row", "col"), P("col"), P("row", "col"), P("col"), P("row", "col"), P("col"),
        P("row", "col"), P("row"), P("row"), P("row"),
        P("row", "col"), P("col"), P("row", "col"), P("row"), P("row"), P("row"),
    )
    return jax.shard_map(shards, mesh=mesh, in_specs=in_specs, out_specs=out_specs, check_vma=False)
```

```python
import jax
import jax.numpy as jnp
from jax import lax
from jax.experimental import pallas as pl
from jax.experimental.pallas import tpu as pltpu
from jax.sharding import PartitionSpec as P

LOSS_SCALE = 16777216
stabilizer = 2.0
norm_eps = 1e-12
root_half = 0.7071067811865476
inv_root_two_pi = 0.3989422804014327
f32 = jnp.float32
bf16 = jnp.bfloat16
PAD = 8
EXTRA = 16
CUT = 48
ASIDE = 256


def dot(a, b, dims):
    return lax.dot_general(a, b, (dims, ((), ())), preferred_element_type=f32)


def nn(a, b):
    return dot(a, b, ((1,), (0,)))


def nt(a, b):
    return dot(a, b, ((1,), (1,)))


def tn(a, b):
    return dot(a, b, ((0,), (0,)))


def ones_rows(tokens):
    return jnp.ones((8, tokens), bf16)


def call(body, outs, args, name, grid=None, in_specs=None, out_specs=None, scratch=(), limit=40, pinned=False):
    if grid is None:
        grid = (1,)
        in_specs = [single(a.shape) for a in args] if in_specs is None else in_specs
        out_specs = [single(s) for s, _ in outs]
    extra = dict(grid=grid, in_specs=in_specs, out_specs=out_specs)
    if pinned:
        args = [a if p is SMEM else pltpu.with_memory_space_constraint(a, pltpu.HBM) for a, p in zip(args, in_specs)]
    make = pltpu.HBM if pinned else jax.ShapeDtypeStruct
    return pl.pallas_call(
        body,
        out_shape=[make(s, d) for s, d in outs],
        scratch_shapes=list(scratch),
        compiler_params=pltpu.CompilerParams(vmem_limit_bytes=limit * 1024 * 1024),
        cost_estimate=pl.CostEstimate(flops=1000, bytes_accessed=1000, transcendentals=0),
        name=name,
        **extra,
    )(*args)


def single(shape):
    zeros = (0,) * len(shape)
    return pl.BlockSpec(shape, lambda s: zeros, pipeline_mode=pl.Buffered(1))


def whole(a):
    zeros = (0,) * a.ndim
    return pl.BlockSpec(a.shape, lambda s: zeros)


def whole_out(shape):
    zeros = (0,) * len(shape)
    return pl.BlockSpec(shape, lambda s: zeros)


SMEM = pl.BlockSpec(memory_space=pltpu.SMEM)


def split_positions(shard, row, row_parts):
    k, length = shard.shape
    n = length // row_parts

    def body(row_ref, in_ref, *out_refs):
        r = row_ref[0]
        for j, o_ref in enumerate(out_refs):
            at = pl.multiple_of(jnp.bitwise_xor(r, j) * n, n)
            o_ref[...] = in_ref[:, pl.ds(at, n)].astype(bf16)

    return call(body, [((k, n), bf16)] * row_parts, (row, shard), "split_positions", in_specs=[SMEM, single(shard.shape)], pinned=True)


def join_positions(blocks, row):
    k, n = blocks[0].shape
    parts = len(blocks)

    def body(row_ref, *refs):
        r = row_ref[0]
        o_ref = refs[parts]
        for j in range(parts):
            at = pl.multiple_of(jnp.bitwise_xor(r, j) * n, n)
            o_ref[:, pl.ds(at, n)] = refs[j][...].astype(f32)

    return call(body, [((k, n * parts), f32)], (row, *blocks), "join_positions", in_specs=[SMEM] + [single(b.shape) for b in blocks])[0]


def narrow(parts, steps, name):
    n = parts[0].shape[0]
    widths = [p.shape[1] for p in parts]

    def body(*refs):
        at = 0
        for ref, w in zip(refs, widths):
            refs[-1][:, at : at + w] = ref[...].astype(bf16)
            at += w

    return call(
        body, [((n, sum(widths)), bf16)], parts, name, (steps,),
        [pl.BlockSpec((n // steps, w), lambda s: (s, 0)) for w in widths],
        [pl.BlockSpec((n // steps, sum(widths)), lambda s: (s, 0))],
        pinned=True,
    )[0]


def narrow_small(parts, vecs, biases, up_bias, name):
    n, hb = parts[0].shape
    width = hb * len(parts)
    nv = len(vecs)
    rest = up_bias.shape[0] - width
    small = [v.reshape(1, v.shape[0]) for v in vecs] + [jnp.concatenate((*biases, up_bias)).reshape(-1, hb)]

    def body(*refs):
        p_refs = refs[: len(parts)]
        v_refs = refs[len(parts) : len(parts) + nv]
        b_ref, o_ref, small_ref = refs[len(parts) + nv :]
        small_ref[...] = jnp.zeros(small_ref.shape, f32)
        for m, ref in enumerate(v_refs):
            small_ref[m : m + 1, :n] = ref[...]
        for m, ref in enumerate(p_refs):
            o_ref[:n, m * hb : (m + 1) * hb] = ref[...].astype(bf16)
            small_ref[nv : nv + 1, m * hb : (m + 1) * hb] = b_ref[m : m + 1]
            small_ref[nv + 1 : nv + 2, m * hb : (m + 1) * hb] = b_ref[len(parts) + m : len(parts) + m + 1]
        small_ref[0:1, ASIDE : ASIDE + rest] = b_ref[2 * len(parts) : 2 * len(parts) + 1]
        value = small_ref[...]
        high = value.astype(bf16).astype(f32)
        o_ref[n:] = jnp.concatenate((high, value - high), axis=0).astype(bf16)

    scratch = [pltpu.VMEM((8, width), f32)]
    return call(body, [((n + EXTRA, width), bf16)], (*parts, *small), name, scratch=scratch, pinned=True)[0]


def small_rows(ref, k):
    v = ref[k : k + EXTRA].astype(f32)
    return v[0:8] + v[8:16]


def attention_in(xs, near, other, omegas, keep, head_local, head_width, hid_local):
    k, tokens = xs[0].shape
    feats = omegas[0].shape[2]
    heads = 2 * head_local
    hb = head_local * head_width
    rows = head_width + PAD
    factor = head_width ** (-0.25)
    n_near, n_other = len(near), len(other)

    def body(*refs):
        x_in = refs[:4]
        near_refs = refs[4 : 4 + n_near]
        other_refs = refs[4 + n_near : 4 + n_near + n_other]
        (om0_ref, om1_ref, keep_ref, x_ref, fq_ref, fk_ref, uq_ref, uk_ref, v_ref, kv_ref, vec_ref, up_ref) = refs[
            4 + n_near + n_other :
        ]
        for p in range(4):
            vec_ref[:, p * k : (p + 1) * k] = small_rows(near_refs[p], k)[:, :k]
        up_ref[...] = jnp.zeros(up_ref.shape, f32)
        for p in range(4):
            x_ref[p * k : (p + 1) * k] = x_in[p][...]
        xv = x_ref[...]
        ones = jnp.ones((PAD, tokens), bf16)
        for i, pieces in enumerate((near_refs, other_refs)):
            omega_ref = (om0_ref, om1_ref)[i]
            small = small_rows(pieces[0], k)
            up_ref[i : i + 1, : 3 * hb] = small[7:8]
            up_ref[i : i + 1, 3 * hb :] = small[0:1, ASIDE : ASIDE + hid_local - 3 * hb]
            triple = tn(jnp.concatenate([p[:k] for p in pieces], axis=0), xv) + jnp.transpose(small)[:, 6:7]
            for hl in range(head_local):
                h = i * head_local + hl
                at = h * head_width
                lo = hl * head_width
                value = triple[2 * hb + lo : 2 * hb + lo + head_width].astype(bf16)
                v_ref[at : at + head_width] = value
                for base, u_ref, f_ref, mask in ((0, uq_ref, fq_ref, False), (hb, uk_ref, fk_ref, True)):
                    u = triple[base + lo : base + lo + head_width] * factor
                    ub = u.astype(bf16)
                    u_ref[at : at + head_width] = ub
                    z = tn(omega_ref[hl], ub)
                    feat = jnp.exp(z - (0.5 * jnp.sum(u * u, axis=0, keepdims=True) + stabilizer))
                    if mask:
                        feat = feat * keep_ref[0:1]
                    feat = feat.astype(bf16)
                    f_ref[h * feats : (h + 1) * feats] = feat
                kv_ref[h * rows : (h + 1) * rows] = nt(jnp.concatenate((value, ones), axis=0), feat).astype(bf16)

    n = heads * head_width
    outs = [((4 * k, tokens), bf16)] + [((heads * feats, tokens), bf16)] * 2 + [((n, tokens), bf16)] * 3
    outs += [((heads * rows, feats), bf16), ((8, 4 * k), f32), ((8, hid_local), f32)]
    return call(body, outs, (*xs, *near, *other, *omegas, keep), "attention_in", pinned=True)


def weight_specs(pieces, block, first):
    return [pl.BlockSpec((p.shape[0], block), lambda s, f=first: (0, f + s)) for p in pieces]


def fixed_specs(pieces, block, at):
    return [pl.BlockSpec((p.shape[0], block), lambda s: (0, at)) for p in pieces]


def rows_of(refs):
    return jnp.concatenate([r[...] for r in refs], axis=0)


def middle(kv0, kv1, fq, x, near, other, vecs, up_bias, target, keep, scale, heads, head_width, hid_local):
    width, tokens = x.shape
    feats = kv0.shape[1]
    rows = head_width + PAD
    hb = heads * head_width // 2
    steps = hid_local // hb
    k = width // 4
    nn_, no = len(near), len(other)
    np_ = nn_ + no

    def body(*refs):
        kv0_ref, kv1_ref, fq_ref, x_ref = refs[:4]
        out_w = refs[4 : 4 + np_]
        up_w = refs[4 + np_ : 4 + 2 * np_]
        down_w = refs[4 + 2 * np_ : 4 + 3 * np_]
        (vec_ref, upb_ref, t0, t1, t2, t3, keep_ref, scale_ref,
         kv_ref, att_ref, inv_ref, xh1_ref, r1_ref, x1_ref, hid_ref, slope_ref, gf_ref, sum_ref,
         o0, o1, o2, o3, acc_ref, vec_s) = refs[4 + 3 * np_ :]
        step = pl.program_id(0)

        @pl.when(step == 0)
        def _():
            vec = jnp.transpose(vec_ref[...])
            vec_s[...] = vec
            kv_ref[...] = (kv0_ref[...].astype(f32) + kv1_ref[...].astype(f32)).astype(bf16)
            for h in range(heads):
                both = nn(kv_ref[h * rows : (h + 1) * rows], fq_ref[h * feats : (h + 1) * feats])
                inverse = 1.0 / both[head_width : head_width + 1]
                inv_ref[h : h + 1] = inverse
                att_ref[h * head_width : (h + 1) * head_width] = (both[:head_width] * inverse).astype(bf16)
            w = jnp.concatenate((rows_of(out_w[:nn_]), rows_of(out_w[nn_:])), axis=1)
            h1 = nn(w, att_ref[...]) + x_ref[...].astype(f32) + vec[:, 0:1]
            mean = jnp.sum(h1, axis=0, keepdims=True) * (1.0 / width)
            h1 = h1 - mean
            r1 = lax.rsqrt(jnp.sum(h1 * h1, axis=0, keepdims=True) * (1.0 / width) + norm_eps)
            h1 = h1 * r1
            r1_ref[...] = jnp.broadcast_to(r1, (8, tokens))
            xh1_ref[...] = h1.astype(bf16)
            x1 = h1 * vec[:, 1:2] + vec[:, 2:3]
            x1_ref[...] = x1.astype(bf16)
            acc_ref[...] = x1 + vec[:, 3:4]

        x1b = x1_ref[...]
        bias = jnp.transpose(upb_ref[...])
        total = acc_ref[...]
        for i, (a, b) in enumerate(((0, nn_), (nn_, np_))):
            up = tn(rows_of(up_w[a:b]), x1b) + bias[:, i : i + 1]
            gate = 0.5 * (1.0 + lax.erf(up * root_half))
            slope_ref[i] = (gate + up * inv_root_two_pi * jnp.exp(-0.5 * up * up)).astype(bf16)
            hid = (up * gate).astype(bf16)
            hid_ref[i] = hid
            total = total + nn(rows_of(down_w[a:b]), hid)
        acc_ref[...] = total

        @pl.when(step == steps - 1)
        def _():
            vec = vec_s[...]
            h2 = acc_ref[...]
            mean = jnp.sum(h2, axis=0, keepdims=True) * (1.0 / width)
            h2 = h2 - mean
            r2 = lax.rsqrt(jnp.sum(h2 * h2, axis=0, keepdims=True) * (1.0 / width) + norm_eps)
            h2 = h2 * r2
            out = h2 * vec[:, 4:5] + vec[:, 5:6]
            for p, o_ref in enumerate((o0, o1, o2, o3)):
                o_ref[...] = out[p * k : (p + 1) * k].astype(bf16)
            target = jnp.concatenate((t0[...], t1[...], t2[...], t3[...]), axis=0).astype(f32)
            diff = (out - target) * keep_ref[0:1]
            g = diff * scale_ref[0:1, 0:1]
            ones = ones_rows(tokens)
            sum_ref[0:8] = nt(ones, (g * h2).astype(bf16))
            sum_ref[8:16] = nt(ones, g.astype(bf16))
            sum_ref[16:24] = jnp.full((8, width), jnp.sum(diff * diff), f32)
            a = g * vec[:, 4:5]
            first = jnp.sum(a, axis=0, keepdims=True) * (1.0 / width)
            second = jnp.sum(a * h2, axis=0, keepdims=True) * (1.0 / width)
            gf_ref[...] = (r2 * (a - first - h2 * second)).astype(bf16)

    outs = [
        ((heads * rows, feats), bf16), ((width, tokens), bf16), ((16, tokens), f32), ((width, tokens), bf16),
        ((8, tokens), f32), ((width, tokens), bf16), ((2, hid_local, tokens), bf16), ((2, hid_local, tokens), bf16),
        ((width, tokens), bf16), ((24, width), f32),
    ] + [((k, tokens), bf16)] * 4
    pieces = (*near, *other)
    args = (kv0, kv1, fq, x, *pieces, *pieces, *pieces, vecs, up_bias, *target, keep, scale)
    in_specs = [whole(a) for a in (kv0, kv1, fq, x)]
    in_specs += fixed_specs(pieces, hb, 0) + weight_specs(pieces, hb, 1) + weight_specs(pieces, hb, 1 + steps)
    in_specs += [whole(vecs), pl.BlockSpec((8, hb), lambda s: (0, s))] + [whole(t) for t in target] + [whole(keep), whole(scale)]
    out_specs = [whole_out(s) for s, _ in outs]
    out_specs[6] = out_specs[7] = pl.BlockSpec((2, hb, tokens), lambda s: (0, s, 0))
    scratch = [pltpu.VMEM((width, tokens), f32), pltpu.VMEM((width, 8), f32)]
    return call(body, outs, args, "middle", (steps,), in_specs, out_specs, scratch, limit=56, pinned=True)


def grad_theirs(left, right, block, name):
    n, tokens = left.shape
    k = right.shape[1]
    half = n // 2

    def body(l_ref, r_ref, o_ref):
        for i in range(2):
            o_ref[i] = nt(l_ref[...], r_ref[i]).astype(bf16)

    return call(
        body, [((2, half, k), bf16)], (left, right), name, (k // block,),
        [pl.BlockSpec((half, tokens), lambda s: (1, 0)), pl.BlockSpec((2, block, tokens), lambda s: (0, s, 0))],
        [pl.BlockSpec((2, half, block), lambda s: (0, 0, s))],
    )[0]


def grad_mine(left, right, got, block, name):
    n, tokens = left.shape
    k = right.shape[1]
    half = n // 2
    share = k // block // 2

    def body(l_ref, r_ref, got_ref, keep0, keep1, send0, send1):
        step = pl.program_id(0)

        def part(keep_ref, send_ref):
            for i, o_ref in enumerate((keep_ref, send_ref)):
                o_ref[...] = (nt(l_ref[...], r_ref[i]) + got_ref[i].astype(f32)).astype(bf16)

        pl.when(step < share)(lambda: part(keep0, send0))
        pl.when(step >= share)(lambda: part(keep1, send1))

    first = pl.BlockSpec((half, block), lambda s: (0, jnp.minimum(s, share - 1)))
    second = pl.BlockSpec((half, block), lambda s: (0, jnp.maximum(s - share, 0)))
    return call(
        body, [((half, k // 2), bf16)] * 4, (left, right, got), name, (2 * share,),
        [
            pl.BlockSpec((half, tokens), lambda s: (0, 0)),
            pl.BlockSpec((2, block, tokens), lambda s: (0, s, 0)),
            pl.BlockSpec((2, half, block), lambda s: (0, 0, s)),
        ],
        [first, second, first, second],
    )


def pair_theirs(x, gq, go, att, name):
    n, tokens = x.shape
    half = n // 2
    k = gq.shape[1]

    def body(x_ref, gq_ref, go_ref, att_ref, o_ref):
        for i in range(2):
            o_ref[i, :, :k] = nt(x_ref[half:], gq_ref[i]).astype(bf16)
            o_ref[i, :, k:] = nt(go_ref[half:], att_ref[i]).astype(bf16)

    return call(body, [((2, half, 2 * k), bf16)], (x, gq, go, att), name)[0]


def pair_mine(x, gq, go, att, got, name):
    n, tokens = x.shape
    half = n // 2
    k = gq.shape[1]

    def body(x_ref, gq_ref, go_ref, att_ref, got_ref, keep_ref, send_ref):
        for i, o_ref in enumerate((keep_ref, send_ref)):
            o_ref[:, :k] = (nt(x_ref[:half], gq_ref[i]) + got_ref[i, :, :k].astype(f32)).astype(bf16)
            o_ref[:, k:] = (nt(go_ref[:half], att_ref[i]) + got_ref[i, :, k:].astype(f32)).astype(bf16)

    return call(body, [((half, 2 * k), bf16)] * 2, (x, gq, go, att, got), name)


def down_back(gf, slope, near, other, hb, hid_local):
    width, tokens = gf.shape
    steps = hid_local // hb
    nn_, no = len(near), len(other)
    pieces = (*near, *other)

    def body(gf_ref, slope_ref, *refs):
        gu_ref, sum_ref, bd_ref = refs[nn_ + no :]
        g = gf_ref[...]
        ones = ones_rows(tokens)

        @pl.when(pl.program_id(0) == 0)
        def _():
            bd_ref[...] = nt(ones, g)

        for i, w in enumerate((refs[:nn_], refs[nn_ : nn_ + no])):
            v = (tn(rows_of(w), g) * slope_ref[i].astype(f32)).astype(bf16)
            gu_ref[i] = v
            sum_ref[i] = nt(ones, v)

    spec = pl.BlockSpec((2, hb, tokens), lambda s: (0, s, 0))
    return call(
        body, [((2, hid_local, tokens), bf16), ((2, 8, hid_local), f32), ((8, width), f32)], (gf, slope, *pieces), "down_back",
        (steps,), [whole(gf), spec] + weight_specs(pieces, hb, 1 + steps),
        [spec, pl.BlockSpec((2, 8, hb), lambda s: (0, 0, s)), whole_out((8, width))],
    )


def up_back(gu, gf, xh1, r1, vecs, near, other, hb):
    width, tokens = gf.shape
    steps = gu.shape[1] // hb
    nn_, no = len(near), len(other)
    pieces = (*near, *other)

    def body(gu_ref, gf_ref, xh_ref, r1_ref, vec_ref, *refs):
        go_ref, sum_ref, acc_ref = refs[nn_ + no :]
        step = pl.program_id(0)

        @pl.when(step == 0)
        def _():
            acc_ref[...] = gf_ref[...].astype(f32)

        acc_ref[...] += nn(rows_of(refs[:nn_]), gu_ref[0]) + nn(rows_of(refs[nn_ : nn_ + no]), gu_ref[1])

        @pl.when(step == steps - 1)
        def _():
            vec = jnp.transpose(vec_ref[...])
            g = acc_ref[...]
            xh = xh_ref[...].astype(f32)
            ones = ones_rows(tokens)
            sum_ref[0:8] = nt(ones, (g * xh).astype(bf16))
            sum_ref[8:16] = nt(ones, g.astype(bf16))
            a = g * vec[:, 1:2]
            first = jnp.sum(a, axis=0, keepdims=True) * (1.0 / width)
            second = jnp.sum(a * xh, axis=0, keepdims=True) * (1.0 / width)
            go = (r1_ref[0:1] * (a - first - xh * second)).astype(bf16)
            go_ref[...] = go
            sum_ref[16:24] = nt(ones, go)

    return call(
        body, [((width, tokens), bf16), ((24, width), f32)], (gu, gf, xh1, r1, vecs, *pieces), "up_back", (steps,),
        [pl.BlockSpec((2, hb, tokens), lambda s: (0, s, 0))] + [whole(a) for a in (gf, xh1, r1, vecs)] + weight_specs(pieces, hb, 1),
        [whole_out((width, tokens)), whole_out((24, width))], [pltpu.VMEM((width, tokens), f32)],
    )


def attention_mid(go, att, inv, fq, near, other, heads, head_width):
    width, tokens = go.shape
    feats = fq.shape[0] // heads
    hb = heads * head_width // 2
    rows = head_width + PAD
    nn_, no = len(near), len(other)
    pieces = (*near, *other)

    def body(go_ref, att_ref, inv_ref, fq_ref, *refs):
        gn_ref, kv_ref = refs[nn_ + no :]
        g = go_ref[...]
        zeros = jnp.zeros((PAD - 1, tokens), f32)
        for i, w in enumerate((refs[:nn_], refs[nn_ : nn_ + no])):
            ga = tn(rows_of(w), g)
            for hl in range(heads // 2):
                h = i * (heads // 2) + hl
                gh = ga[hl * head_width : (hl + 1) * head_width]
                inverse = inv_ref[h : h + 1]
                a = att_ref[h * head_width : (h + 1) * head_width].astype(f32)
                gd = -jnp.sum(gh * a, axis=0, keepdims=True) * inverse
                both = jnp.concatenate((gh * inverse, gd, zeros), axis=0).astype(bf16)
                gn_ref[h * rows : (h + 1) * rows] = both
                kv_ref[h * rows : (h + 1) * rows] = nt(both, fq_ref[h * feats : (h + 1) * feats]).astype(bf16)

    outs = [((heads * rows, tokens), bf16), ((heads * rows, feats), bf16)]
    args = (go, att, inv, fq, *pieces)
    return call(
        body, outs, args, "attention_mid", (1,), [whole(a) for a in args[:4]] + fixed_specs(pieces, hb, 0),
        [whole_out(s) for s, _ in outs],
    )


def query_back(gn, kv, fq, uq, omegas, heads, head_width):
    n, tokens = uq.shape
    feats = fq.shape[0] // heads
    rows = head_width + PAD
    factor = head_width ** (-0.25)

    def body(gn_ref, kv_ref, fq_ref, uq_ref, om0_ref, om1_ref, gq_ref, sum_ref):
        for h in range(heads):
            om_ref = (om0_ref, om1_ref)[h // (heads // 2)]
            e = tn(kv_ref[h * rows : (h + 1) * rows], gn_ref[h * rows : (h + 1) * rows])
            e = e * fq_ref[h * feats : (h + 1) * feats].astype(f32)
            s = jnp.sum(e, axis=0, keepdims=True)
            u = uq_ref[h * head_width : (h + 1) * head_width].astype(f32)
            gq_ref[h * head_width : (h + 1) * head_width] = (
                factor * (nn(om_ref[h % (heads // 2)], e.astype(bf16)) - s * u)
            ).astype(bf16)
        sum_ref[...] = nt(ones_rows(tokens), gq_ref[...])

    return call(body, [((n, tokens), bf16), ((8, n), f32)], (gn, kv, fq, uq, *omegas), "query_back")


def key_back(gkv0, gkv1, fk, uk, v, omegas, heads, head_width):
    n, tokens = uk.shape
    feats = fk.shape[0] // heads
    rows = head_width + PAD
    factor = head_width ** (-0.25)
    hl_n = heads // 2
    hb = hl_n * head_width

    def body(gkv0_ref, gkv1_ref, fk_ref, uk_ref, v_ref, om0_ref, om1_ref, g_ref, sum_ref):
        ones = jnp.ones((PAD, tokens), bf16)
        for h in range(heads):
            i, hl = divmod(h, hl_n)
            base = i * 2 * hb + hl * head_width
            kv = (gkv0_ref[h * rows : (h + 1) * rows].astype(f32) + gkv1_ref[h * rows : (h + 1) * rows].astype(f32)).astype(bf16)
            f = fk_ref[h * feats : (h + 1) * feats]
            at = h * head_width
            value = jnp.concatenate((v_ref[at : at + head_width], ones), axis=0)
            e = tn(kv, value) * f.astype(f32)
            s = jnp.sum(e, axis=0, keepdims=True)
            u = uk_ref[at : at + head_width].astype(f32)
            g_ref[base : base + head_width] = (
                factor * (nn((om0_ref, om1_ref)[i][hl], e.astype(bf16)) - s * u)
            ).astype(bf16)
            g_ref[base + hb : base + hb + head_width] = nn(kv[:head_width], f).astype(bf16)
        sum_ref[...] = nt(ones_rows(tokens), g_ref[...])

    return call(body, [((2 * n, tokens), bf16), ((8, 2 * n), f32)], (gkv0, gkv1, fk, uk, v, *omegas), "key_back")


def last_parts(x, g, sums, got, name):
    sum1, sum2, bd, bu, sum_q, sum_kv = sums
    n, tokens = x.shape
    q = n // 4
    k = g.shape[1]
    hb = k // 2
    hid_local = bu.shape[2]
    ups = hid_local // hb
    rows = q + EXTRA
    which = 0 if got is not None else 1

    def body(x_ref, g_ref, s1_ref, s2_ref, bd_ref, bu_ref, sq_ref, skv_ref, *refs):
        if got is None:
            o_ref, row_s, col_s = refs
        else:
            got_ref, keep_ref, send_ref, row_s, col_s = refs
        for m, v in enumerate((s1_ref[16:17], s1_ref[0:1], s1_ref[8:9], bd_ref[0:1], s2_ref[0:1], s2_ref[8:9], s2_ref[16:17])):
            row_s[m : m + 1] = v
        row_s[7:8] = jnp.zeros((1, n), f32)
        col_s[...] = jnp.zeros(col_s.shape, f32)
        for i in range(2):
            col_s[i, 0:1] = sq_ref[0:1, i * hb : (i + 1) * hb]
            col_s[i, 1:2] = skv_ref[0:1, i * k : i * k + hb]
            col_s[i, 2:3] = skv_ref[0:1, i * k + hb : (i + 1) * k]
            for u in range(ups):
                col_s[i, 3 + u : 4 + u] = bu_ref[i, 0:1, u * hb : (u + 1) * hb]
        for i in range(2):
            for jx in range(2):
                p = 2 * which + jx
                main = nt(x_ref[p * q : (p + 1) * q], g_ref[i])
                small = row_s[:, p * q : (p + 1) * q]
                small = jnp.concatenate((small, jnp.zeros((8, hb - q), f32), col_s[i]), axis=1)
                small = jnp.concatenate((small, jnp.zeros((EXTRA - 8, k), f32)), axis=0)
                if got is None:
                    o_ref[i, jx, :q] = main.astype(bf16)
                    o_ref[i, jx, q:] = small.astype(bf16)
                else:
                    o = send_ref if jx else keep_ref
                    o[i * rows : i * rows + q] = (main + got_ref[i, jx, :q].astype(f32)).astype(bf16)
                    o[i * rows + q : (i + 1) * rows] = (small + got_ref[i, jx, q:].astype(f32)).astype(bf16)

    outs = [((2, 2, rows, k), bf16)] if got is None else [((2 * rows, k), bf16)] * 2
    args = (x, g, *sums) if got is None else (x, g, *sums, got)
    return call(body, outs, args, name, scratch=[pltpu.VMEM((8, n), f32), pltpu.VMEM((2, 8, hb), f32)])


def input_grad(gq, g, go, near, other):
    width, tokens = go.shape
    hb = gq.shape[1]
    k = width // 4
    nn_, no = len(near), len(other)

    def body(gq_ref, g_ref, go_ref, *refs):
        total = go_ref[...].astype(f32)
        for i, w in enumerate((refs[:nn_], refs[nn_ : nn_ + no])):
            w = jnp.concatenate([r[:k] for r in w], axis=0)
            total = total + nn(w[:, :hb], gq_ref[i]) + nn(w[:, hb:], g_ref[i])
        for p, o_ref in enumerate(refs[nn_ + no :]):
            o_ref[...] = total[p * k : (p + 1) * k].astype(bf16)

    return call(body, [((k, tokens), bf16)] * 4, (gq, g, go, *near, *other), "input_grad")


def swap(value, axis, mask):
    size = lax.axis_size(axis)
    return lax.ppermute(value, axis, [(s, s ^ mask) for s in range(size)])


def after(value, *others):
    return lax.optimization_barrier((value, *others))[0]


class Fold:
    def __init__(self, value):
        self.value = value
        self.four = lax.axis_size("dp") == 4
        if not self.four:
            self.value = lax.psum(value, "dp")
            return
        self.odd = lax.axis_index("dp") % 2 == 1
        n = value.shape[1] // 2
        low, high = value[:, :n], value[:, n:]
        self.value = jnp.where(self.odd, high, low)
        self.got = swap(jnp.where(self.odd, low, high), "dp", 1)

    def step(self, order, mask):
        if not self.four:
            return order
        self.value = after(self.value, order) + self.got
        self.got = swap(self.value, "dp", mask)
        return self.value

    def middle(self, order):
        return self.step(order, 2)

    def back(self, order):
        return self.step(order, 1)

    def result(self):
        if not self.four:
            return self.value.astype(f32)
        a, b = self.value.astype(f32), self.got.astype(f32)
        return jnp.concatenate((jnp.where(self.odd, b, a), jnp.where(self.odd, a, b)), axis=1)


def total(keep, got, last):
    n = keep.shape[0] // 2
    return keep[:n] + got[:n] + last


def far_half(keep, got):
    n = keep.shape[0] // 2
    return keep[n:] + got[n:]


def exchange(blocks):
    return [blocks[0]] + [swap(blocks[j], "row", j) for j in (1, 2, 3)]


def reduce_small(value, axis):
    step = 1
    while step < lax.axis_size(axis):
        value = value + swap(value, axis, step)
        step *= 2
    return value


def shards(
    inputs, teacher, lengths, omega,
    w_query, b_query, w_key, b_key, w_value, b_value, w_out, b_out,
    norm1_gain, norm1_bias, w_up, up_bias, w_down, b_down, norm2_gain, norm2_bias,
):
    row_parts = lax.axis_size("row")
    feat_local, seq_length = inputs.shape
    width = feat_local * row_parts
    head_local, head_width, feats = omega.shape
    heads = head_local * lax.axis_size("col")
    tokens = seq_length // row_parts
    hb = head_local * head_width
    hid_local = w_up.shape[1]
    row = lax.axis_index("row")
    col = lax.axis_index("col")
    row_ref = row.astype(jnp.int32).reshape(1)

    omegas = (omega, swap(omega, "col", 1))
    vecs = (b_out, norm1_gain, norm1_bias, b_down, norm2_gain, norm2_bias)
    ins = split_positions(inputs, row_ref, row_parts)
    ins_got = exchange(ins)
    xs = [ins_got[j] for j in (0, 2, 1, 3)]
    own_a = narrow_small((after(w_query, *ins), w_key, w_value), vecs, (b_query, b_key, b_value), up_bias, "narrow_a")
    a_y = swap(own_a, "col", 1)
    a_x = swap(own_a, "row", 2)
    a_far = swap(after(a_x, a_y, omegas[1]), "col", 1)
    near_a = (own_a, a_x, swap(own_a, "row", 1), swap(a_x, "row", 1))
    other_a = (a_y, a_far, swap(a_y, "row", 1), swap(a_far, "row", 1))
    count = reduce_small(jnp.sum(lengths).astype(f32).reshape(1, 1) + jnp.zeros((8, 128), f32), "dp")
    own_b = narrow((after(w_out, own_a, count), w_up, w_down), 3, "narrow_b")
    b_x = swap(after(own_b, a_x, ins_got[2], ins_got[3]), "row", 2)
    b_y = swap(after(own_b, a_far), "col", 1)
    length = lax.dynamic_index_in_dim(lengths, col, 0, False)
    keep = ((row * tokens + jnp.arange(tokens, dtype=jnp.int32)) < length).astype(f32)
    keep = jnp.broadcast_to(keep[None, :], (8, tokens))
    scale = (2.0 * LOSS_SCALE) / (count * width)

    x, fq, fk, uq, uk, v, kv, vecs, up_bias_all = attention_in(
        xs, near_a, other_a, omegas, keep, head_local, head_width, hid_local
    )
    kv0 = kv + swap(kv, "row", 1)
    kv1 = swap(kv0, "row", 2)
    theirs = split_positions(after(teacher, kv0), row_ref, row_parts)
    teach = exchange(theirs)
    target = [teach[j] for j in (0, 2, 1, 3)]
    b_x = after(b_x, kv0, theirs[0])
    b_y = after(b_y, kv0, theirs[0])
    b_far_y = swap(b_x[CUT:], "col", 1)
    b_far_x = swap(b_y[:CUT], "row", 2)
    near_b = (own_b, b_x)
    near_b = near_b + tuple(swap(p, "row", 1) for p in near_b)
    other_b = (b_y, b_far_x, after(b_far_y, kv1, b_far_x, teach[2], teach[3]))
    other_b = other_b + tuple(swap(p, "row", 1) for p in other_b)
    kv, att, inv, xh1, r1, x1, hid, slope, gf, sum2, *out = middle(
        kv0, kv1, fq, x, near_b, other_b, vecs, up_bias_all, target, keep, scale, heads, head_width, hid_local
    )
    out = exchange([out[j] for j in (0, 2, 1, 3)])

    theirs = grad_theirs(gf, hid, hb, "down_theirs")
    got1 = swap(theirs, "row", 1)
    gu, bu, bd = down_back(after(gf, theirs), slope, near_b, other_b, hb, hid_local)
    kept0, kept1, send0, send1 = grad_mine(after(gf, gu), hid, got1, hb, "down_mine")
    down = ((kept0, swap(send0, "col", 1)), (kept1, swap(send1, "col", 1)))
    go, sum1 = up_back(after(gu, send0), gf, xh1, r1, vecs, near_b, other_b, hb)
    gn, gkv = attention_mid(go, att, inv, fq, near_b, other_b, heads, head_width)
    gkv0 = gkv + swap(gkv, "row", 1)
    gkv1 = swap(gkv0, "row", 2)
    far = far_half(after(down[0][0], gn, *out), down[0][1])
    r_down0 = swap(far, "row", 2)
    theirs = grad_theirs(after(x1, far), gu, hb, "up_theirs")
    got2 = swap(theirs, "row", 1)
    gq, sum_q = query_back(after(gn, theirs), kv, fq, uq, omegas, heads, head_width)
    down0 = total(after(down[0][0], gq), down[0][1], r_down0)
    z_down0 = Fold(down0)
    kept0, kept1, send0, send1 = grad_mine(after(x1, down0, gkv0), gu, got2, hb, "up_mine")
    up = ((kept0, swap(send0, "col", 1)), (kept1, swap(send1, "col", 1)))
    far = far_half(after(down[1][0], send0), down[1][1])
    r_down1 = swap(far, "row", 2)
    gq = gq.reshape(2, hb, tokens)
    att2 = att.reshape(2, hb, tokens)
    theirs = pair_theirs(after(x, far), gq, go, att2, "pair_theirs")
    got3 = swap(theirs, "row", 1)
    g, sum_kv = key_back(after(gkv0, theirs), gkv1, fk, uk, v, omegas, heads, head_width)
    g = g.reshape(2, 2 * hb, tokens)
    sums = (sum1, sum2, bd, bu, sum_q, sum_kv)
    far = far_half(after(up[0][0], g), up[0][1])
    r_up0 = swap(far, "row", 2)
    down1 = total(after(down[1][0], far), down[1][1], r_down1)
    z_down1 = Fold(down1)
    order = z_down0.middle(down1)
    theirs = last_parts(after(x, order), g, sums, None, "last_theirs")[0]
    got4 = swap(theirs, "row", 1)
    keep3, send3 = pair_mine(after(x, theirs), gq, go, att2, got3, "pair_mine")
    r_y3 = swap(send3, "col", 1)
    up0 = total(after(up[0][0], send3), up[0][1], r_up0)
    z_up0 = Fold(up0)
    keep4, send4 = last_parts(after(x, up0), g, sums, got4, "last_mine")
    r_x4 = swap(send4, "row", 2)
    far = far_half(after(up[1][0], send4), up[1][1])
    r_up1 = swap(far, "row", 2)
    order = z_down1.middle(far)
    order = z_down0.back(order)
    gin = input_grad(gq, g, after(go, order), near_a, other_a)
    far = far_half(after(keep4, gin[0]), r_x4)
    r_y4 = swap(far, "col", 1)
    up1 = total(after(up[1][0], far), up[1][1], r_up1)
    z_up1 = Fold(up1)
    order = z_up0.middle(up1)
    far = far_half(after(keep3, order), r_y3)
    r_x3 = swap(far, "row", 2)
    gin = exchange([after(gin[j], far) for j in (0, 2, 1, 3)])
    order = z_down1.back(far)
    last = total(after(keep4, order), r_x4, r_y4)
    order = z_up1.middle(last)
    last = jnp.concatenate((last, total(after(keep3, order), r_y3, r_x3)), axis=0)
    z_last = Fold(last)
    order = z_up0.back(last)
    order = z_last.middle(order)
    order = z_up1.back(order)
    order = z_last.back(order)
    out[0] = after(out[0], order)
    out = join_positions(out, row_ref)
    grad_in = join_positions([after(gin[0], out), *gin[1:]], row_ref)
    grad_down = jnp.concatenate((z_down0.result(), z_down1.result()), axis=1)
    grad_up = jnp.concatenate((z_up0.result(), z_up1.result()), axis=1)
    last = z_last.result()
    grad_pair = last[keep4.shape[0] // 2 :]

    extra = last[feat_local : keep4.shape[0] // 2]
    rows = extra[:7, :feat_local]
    cols = extra[:7, hb:]
    loss = rows[6, 0] / (count[0, 0] * width)
    return (
        out,
        loss,
        grad_in,
        grad_pair[:, :hb],
        cols[0],
        last[:feat_local, :hb],
        cols[1],
        last[:feat_local, hb:],
        cols[2],
        grad_pair[:, hb:],
        rows[0],
        rows[1],
        rows[2],
        grad_up,
        cols[3:].reshape(hid_local),
        grad_down,
        rows[3],
        rows[4],
        rows[5],
    )


def solution(mesh):
    both = P("row", ("dp", "col"))
    in_specs = (
        both, both, P("dp"), P("col", None, None),
        P("row", "col"), P("col"), P("row", "col"), P("col"), P("row", "col"), P("col"),
        P("row", "col"), P("row"), P("row"), P("row"),
        P("row", "col"), P("col"), P("row", "col"), P("row"), P("row"), P("row"),
    )
    out_specs = (
        both, P(), both,
        P("row", "col"), P("col"), P("row", "col"), P("col"), P("row", "col"), P("col"),
        P("row", "col"), P("row"), P("row"), P("row"),
        P("row", "col"), P("col"), P("row", "col"), P("row"), P("row"), P("row"),
    )
    return jax.shard_map(shards, mesh=mesh, in_specs=in_specs, out_specs=out_specs, check_vma=False)
```

```python
import jax
import jax.numpy as jnp
from jax import lax
from jax.experimental import pallas as pl
from jax.experimental.pallas import tpu as pltpu
from jax.sharding import PartitionSpec as P

LOSS_SCALE = 16777216
stabilizer = 2.0
norm_eps = 1e-12
root_half = 0.7071067811865476
inv_root_two_pi = 0.3989422804014327
f32 = jnp.float32
bf16 = jnp.bfloat16
PAD = 8
EXTRA = 16
CUT = 48
ASIDE = 256


def dot(a, b, dims):
    return lax.dot_general(a, b, (dims, ((), ())), preferred_element_type=f32)


def nn(a, b):
    return dot(a, b, ((1,), (0,)))


def nt(a, b):
    return dot(a, b, ((1,), (1,)))


def tn(a, b):
    return dot(a, b, ((0,), (0,)))


def ones_rows(tokens):
    return jnp.ones((8, tokens), bf16)


def call(body, outs, args, name, grid=None, in_specs=None, out_specs=None, scratch=(), limit=40, pinned=False):
    if grid is None:
        grid = (1,)
        in_specs = [single(a.shape) for a in args] if in_specs is None else in_specs
        out_specs = [single(s) for s, _ in outs]
    extra = dict(grid=grid, in_specs=in_specs, out_specs=out_specs)
    if pinned:
        args = [a if p is SMEM else pltpu.with_memory_space_constraint(a, pltpu.HBM) for a, p in zip(args, in_specs)]
    make = pltpu.HBM if pinned else jax.ShapeDtypeStruct
    return pl.pallas_call(
        body,
        out_shape=[make(s, d) for s, d in outs],
        scratch_shapes=list(scratch),
        compiler_params=pltpu.CompilerParams(vmem_limit_bytes=limit * 1024 * 1024),
        cost_estimate=pl.CostEstimate(flops=1000, bytes_accessed=1000, transcendentals=0),
        name=name,
        **extra,
    )(*args)


def single(shape):
    zeros = (0,) * len(shape)
    return pl.BlockSpec(shape, lambda s: zeros, pipeline_mode=pl.Buffered(1))


def whole(a):
    zeros = (0,) * a.ndim
    return pl.BlockSpec(a.shape, lambda s: zeros)


def whole_out(shape):
    zeros = (0,) * len(shape)
    return pl.BlockSpec(shape, lambda s: zeros)


SMEM = pl.BlockSpec(memory_space=pltpu.SMEM)


def split_positions(shard, row, row_parts):
    k, length = shard.shape
    n = length // row_parts

    def body(row_ref, in_ref, *out_refs):
        r = row_ref[0]
        for j, o_ref in enumerate(out_refs):
            at = pl.multiple_of(jnp.bitwise_xor(r, j) * n, n)
            o_ref[...] = in_ref[:, pl.ds(at, n)].astype(bf16)

    rows = k // 3
    return call(
        body, [((k, n), bf16)] * row_parts, (row, shard), "split_positions", (3,),
        [SMEM, pl.BlockSpec((rows, length), lambda s: (s, 0))], [pl.BlockSpec((rows, n), lambda s: (s, 0))] * row_parts, pinned=True,
    )


def join_positions(blocks, row):
    k, n = blocks[0].shape
    parts = len(blocks)

    def body(row_ref, *refs):
        r = row_ref[0]
        o_ref = refs[parts]
        for j in range(parts):
            at = pl.multiple_of(jnp.bitwise_xor(r, j) * n, n)
            o_ref[:, pl.ds(at, n)] = refs[j][...].astype(f32)

    rows = k // 3
    return call(
        body, [((k, n * parts), f32)], (row, *blocks), "join_positions", (3,),
        [SMEM] + [pl.BlockSpec((rows, n), lambda s: (s, 0))] * parts, [pl.BlockSpec((rows, n * parts), lambda s: (s, 0))],
    )[0]


def narrow(parts, steps, name):
    n = parts[0].shape[0]
    widths = [p.shape[1] for p in parts]

    def body(*refs):
        at = 0
        for ref, w in zip(refs, widths):
            refs[-1][:, at : at + w] = ref[...].astype(bf16)
            at += w

    return call(
        body, [((n, sum(widths)), bf16)], parts, name, (steps,),
        [pl.BlockSpec((n // steps, w), lambda s: (s, 0)) for w in widths],
        [pl.BlockSpec((n // steps, sum(widths)), lambda s: (s, 0))],
        pinned=True,
    )[0]


def narrow_small(parts, vecs, biases, up_bias, name):
    n, hb = parts[0].shape
    width = hb * len(parts)
    nv = len(vecs)
    rest = up_bias.shape[0] - width
    small = [v.reshape(1, v.shape[0]) for v in vecs] + [jnp.concatenate((*biases, up_bias)).reshape(-1, hb)]

    def body(*refs):
        p_refs = refs[: len(parts)]
        v_refs = refs[len(parts) : len(parts) + nv]
        b_ref, o_ref, small_ref = refs[len(parts) + nv :]
        small_ref[...] = jnp.zeros(small_ref.shape, f32)
        for m, ref in enumerate(v_refs):
            small_ref[m : m + 1, :n] = ref[...]
        for m, ref in enumerate(p_refs):
            o_ref[:n, m * hb : (m + 1) * hb] = ref[...].astype(bf16)
            small_ref[nv : nv + 1, m * hb : (m + 1) * hb] = b_ref[m : m + 1]
            small_ref[nv + 1 : nv + 2, m * hb : (m + 1) * hb] = b_ref[len(parts) + m : len(parts) + m + 1]
        small_ref[0:1, ASIDE : ASIDE + rest] = b_ref[2 * len(parts) : 2 * len(parts) + 1]
        value = small_ref[...]
        high = value.astype(bf16).astype(f32)
        o_ref[n:] = jnp.concatenate((high, value - high), axis=0).astype(bf16)

    scratch = [pltpu.VMEM((8, width), f32)]
    return call(body, [((n + EXTRA, width), bf16)], (*parts, *small), name, scratch=scratch, pinned=True)[0]


def small_rows(ref, k):
    v = ref[k : k + EXTRA].astype(f32)
    return v[0:8] + v[8:16]


def attention_in(xs, near, other, omegas, keep, head_local, head_width, hid_local):
    k, tokens = xs[0].shape
    feats = omegas[0].shape[2]
    heads = 2 * head_local
    hb = head_local * head_width
    rows = head_width + PAD
    factor = head_width ** (-0.25)
    n_near, n_other = len(near), len(other)

    def body(*refs):
        x_in = refs[:4]
        near_refs = refs[4 : 4 + n_near]
        other_refs = refs[4 + n_near : 4 + n_near + n_other]
        (om0_ref, om1_ref, keep_ref, x_ref, fq_ref, fk_ref, uq_ref, uk_ref, v_ref, kv_ref, vec_ref, up_ref) = refs[
            4 + n_near + n_other :
        ]
        for p in range(4):
            vec_ref[:, p * k : (p + 1) * k] = small_rows(near_refs[p], k)[:, :k]
        up_ref[...] = jnp.zeros(up_ref.shape, f32)
        for p in range(4):
            x_ref[p * k : (p + 1) * k] = x_in[p][...]
        xv = x_ref[...]
        ones = jnp.ones((PAD, tokens), bf16)
        for i, pieces in enumerate((near_refs, other_refs)):
            omega_ref = (om0_ref, om1_ref)[i]
            small = small_rows(pieces[0], k)
            up_ref[i : i + 1, : 3 * hb] = small[7:8]
            up_ref[i : i + 1, 3 * hb :] = small[0:1, ASIDE : ASIDE + hid_local - 3 * hb]
            triple = tn(jnp.concatenate([p[:k] for p in pieces], axis=0), xv) + jnp.transpose(small)[:, 6:7]
            for hl in range(head_local):
                h = i * head_local + hl
                at = h * head_width
                lo = hl * head_width
                value = triple[2 * hb + lo : 2 * hb + lo + head_width].astype(bf16)
                v_ref[at : at + head_width] = value
                for base, u_ref, f_ref, mask in ((0, uq_ref, fq_ref, False), (hb, uk_ref, fk_ref, True)):
                    u = triple[base + lo : base + lo + head_width] * factor
                    ub = u.astype(bf16)
                    u_ref[at : at + head_width] = ub
                    z = tn(omega_ref[hl], ub)
                    feat = jnp.exp(z - (0.5 * jnp.sum(u * u, axis=0, keepdims=True) + stabilizer))
                    if mask:
                        feat = feat * keep_ref[0:1]
                    feat = feat.astype(bf16)
                    f_ref[h * feats : (h + 1) * feats] = feat
                kv_ref[h * rows : (h + 1) * rows] = nt(jnp.concatenate((value, ones), axis=0), feat).astype(bf16)

    n = heads * head_width
    outs = [((4 * k, tokens), bf16)] + [((heads * feats, tokens), bf16)] * 2 + [((n, tokens), bf16)] * 3
    outs += [((heads * rows, feats), bf16), ((8, 4 * k), f32), ((8, hid_local), f32)]
    return call(body, outs, (*xs, *near, *other, *omegas, keep), "attention_in", pinned=True)


def weight_specs(pieces, block, first):
    return [pl.BlockSpec((p.shape[0], block), lambda s, f=first: (0, f + s)) for p in pieces]


def fixed_specs(pieces, block, at):
    return [pl.BlockSpec((p.shape[0], block), lambda s: (0, at)) for p in pieces]


def rows_of(refs):
    return jnp.concatenate([r[...] for r in refs], axis=0)


def middle(kv0, kv1, fq, x, near, other, vecs, up_bias, target, keep, scale, heads, head_width, hid_local):
    width, tokens = x.shape
    feats = kv0.shape[1]
    rows = head_width + PAD
    hb = heads * head_width // 2
    steps = hid_local // hb
    k = width // 4
    nn_, no = len(near), len(other)
    np_ = nn_ + no

    def body(*refs):
        kv0_ref, kv1_ref, fq_ref, x_ref = refs[:4]
        out_w = refs[4 : 4 + np_]
        up_w = refs[4 + np_ : 4 + 2 * np_]
        down_w = refs[4 + 2 * np_ : 4 + 3 * np_]
        (vec_ref, upb_ref, t0, t1, t2, t3, keep_ref, scale_ref,
         kv_ref, att_ref, inv_ref, xh1_ref, r1_ref, x1_ref, hid_ref, slope_ref, gf_ref, sum_ref,
         o0, o1, o2, o3, acc_ref, vec_s) = refs[4 + 3 * np_ :]
        step = pl.program_id(0)

        @pl.when(step == 0)
        def _():
            vec = jnp.transpose(vec_ref[...])
            vec_s[...] = vec
            kv_ref[...] = (kv0_ref[...].astype(f32) + kv1_ref[...].astype(f32)).astype(bf16)
            for h in range(heads):
                both = nn(kv_ref[h * rows : (h + 1) * rows], fq_ref[h * feats : (h + 1) * feats])
                inverse = 1.0 / both[head_width : head_width + 1]
                inv_ref[h : h + 1] = inverse
                att_ref[h * head_width : (h + 1) * head_width] = (both[:head_width] * inverse).astype(bf16)
            w = jnp.concatenate((rows_of(out_w[:nn_]), rows_of(out_w[nn_:])), axis=1)
            h1 = nn(w, att_ref[...]) + x_ref[...].astype(f32) + vec[:, 0:1]
            mean = jnp.sum(h1, axis=0, keepdims=True) * (1.0 / width)
            h1 = h1 - mean
            r1 = lax.rsqrt(jnp.sum(h1 * h1, axis=0, keepdims=True) * (1.0 / width) + norm_eps)
            h1 = h1 * r1
            r1_ref[...] = jnp.broadcast_to(r1, (8, tokens))
            xh1_ref[...] = h1.astype(bf16)
            x1 = h1 * vec[:, 1:2] + vec[:, 2:3]
            x1_ref[...] = x1.astype(bf16)
            acc_ref[...] = x1 + vec[:, 3:4]

        x1b = x1_ref[...]
        bias = jnp.transpose(upb_ref[...])
        total = acc_ref[...]
        for i, (a, b) in enumerate(((0, nn_), (nn_, np_))):
            up = tn(rows_of(up_w[a:b]), x1b) + bias[:, i : i + 1]
            gate = 0.5 * (1.0 + lax.erf(up * root_half))
            slope_ref[i] = (gate + up * inv_root_two_pi * jnp.exp(-0.5 * up * up)).astype(bf16)
            hid = (up * gate).astype(bf16)
            hid_ref[i] = hid
            total = total + nn(rows_of(down_w[a:b]), hid)
        acc_ref[...] = total

        @pl.when(step == steps - 1)
        def _():
            vec = vec_s[...]
            h2 = acc_ref[...]
            mean = jnp.sum(h2, axis=0, keepdims=True) * (1.0 / width)
            h2 = h2 - mean
            r2 = lax.rsqrt(jnp.sum(h2 * h2, axis=0, keepdims=True) * (1.0 / width) + norm_eps)
            h2 = h2 * r2
            out = h2 * vec[:, 4:5] + vec[:, 5:6]
            for p, o_ref in enumerate((o0, o1, o2, o3)):
                o_ref[...] = out[p * k : (p + 1) * k].astype(bf16)
            target = jnp.concatenate((t0[...], t1[...], t2[...], t3[...]), axis=0).astype(f32)
            diff = (out - target) * keep_ref[0:1]
            g = diff * scale_ref[0:1, 0:1]
            ones = ones_rows(tokens)
            sum_ref[0:8] = nt(ones, (g * h2).astype(bf16))
            sum_ref[8:16] = nt(ones, g.astype(bf16))
            sum_ref[16:24] = jnp.full((8, width), jnp.sum(diff * diff), f32)
            a = g * vec[:, 4:5]
            first = jnp.sum(a, axis=0, keepdims=True) * (1.0 / width)
            second = jnp.sum(a * h2, axis=0, keepdims=True) * (1.0 / width)
            gf_ref[...] = (r2 * (a - first - h2 * second)).astype(bf16)

    outs = [
        ((heads * rows, feats), bf16), ((width, tokens), bf16), ((16, tokens), f32), ((width, tokens), bf16),
        ((8, tokens), f32), ((width, tokens), bf16), ((2, hid_local, tokens), bf16), ((2, hid_local, tokens), bf16),
        ((width, tokens), bf16), ((24, width), f32),
    ] + [((k, tokens), bf16)] * 4
    pieces = (*near, *other)
    args = (kv0, kv1, fq, x, *pieces, *pieces, *pieces, vecs, up_bias, *target, keep, scale)
    in_specs = [whole(a) for a in (kv0, kv1, fq, x)]
    in_specs += fixed_specs(pieces, hb, 0) + weight_specs(pieces, hb, 1) + weight_specs(pieces, hb, 1 + steps)
    in_specs += [whole(vecs), pl.BlockSpec((8, hb), lambda s: (0, s))] + [whole(t) for t in target] + [whole(keep), whole(scale)]
    out_specs = [whole_out(s) for s, _ in outs]
    out_specs[6] = out_specs[7] = pl.BlockSpec((2, hb, tokens), lambda s: (0, s, 0))
    scratch = [pltpu.VMEM((width, tokens), f32), pltpu.VMEM((width, 8), f32)]
    return call(body, outs, args, "middle", (steps,), in_specs, out_specs, scratch, limit=56, pinned=True)


def grad_theirs(left, right, block, name):
    n, tokens = left.shape
    k = right.shape[1]
    half = n // 2

    def body(l_ref, r_ref, o_ref):
        for i in range(2):
            o_ref[i] = nt(l_ref[...], r_ref[i]).astype(bf16)

    return call(
        body, [((2, half, k), bf16)], (left, right), name, (k // block,),
        [pl.BlockSpec((half, tokens), lambda s: (1, 0)), pl.BlockSpec((2, block, tokens), lambda s: (0, s, 0))],
        [pl.BlockSpec((2, half, block), lambda s: (0, 0, s))],
    )[0]


def grad_mine(left, right, got, block, name):
    n, tokens = left.shape
    k = right.shape[1]
    half = n // 2
    share = k // block // 2

    def body(l_ref, r_ref, got_ref, keep0, keep1, send0, send1):
        step = pl.program_id(0)

        sums = [(nt(l_ref[...], r_ref[i]) + got_ref[i].astype(f32)).astype(bf16) for i in range(2)]

        def store(*refs):
            for ref, value in zip(refs, sums):
                ref[...] = value

        pl.when(step < share)(lambda: store(keep0, send0))
        pl.when(step >= share)(lambda: store(keep1, send1))

    first = pl.BlockSpec((half, block), lambda s: (0, jnp.minimum(s, share - 1)))
    second = pl.BlockSpec((half, block), lambda s: (0, jnp.maximum(s - share, 0)))
    return call(
        body, [((half, k // 2), bf16)] * 4, (left, right, got), name, (2 * share,),
        [
            pl.BlockSpec((half, tokens), lambda s: (0, 0)),
            pl.BlockSpec((2, block, tokens), lambda s: (0, s, 0)),
            pl.BlockSpec((2, half, block), lambda s: (0, 0, s)),
        ],
        [first, second, first, second],
    )


def pair_theirs(x, gq, go, att, name):
    n, tokens = x.shape
    half = n // 2
    k = gq.shape[1]

    def body(x_ref, gq_ref, go_ref, att_ref, o_ref):
        for i in range(2):
            o_ref[i, :, :k] = nt(x_ref[half:], gq_ref[i]).astype(bf16)
            o_ref[i, :, k:] = nt(go_ref[half:], att_ref[i]).astype(bf16)

    return call(body, [((2, half, 2 * k), bf16)], (x, gq, go, att), name)[0]


def pair_mine(x, gq, go, att, got, name):
    n, tokens = x.shape
    half = n // 2
    k = gq.shape[1]

    def body(x_ref, gq_ref, go_ref, att_ref, got_ref, keep_ref, send_ref):
        for i, o_ref in enumerate((keep_ref, send_ref)):
            o_ref[:, :k] = (nt(x_ref[:half], gq_ref[i]) + got_ref[i, :, :k].astype(f32)).astype(bf16)
            o_ref[:, k:] = (nt(go_ref[:half], att_ref[i]) + got_ref[i, :, k:].astype(f32)).astype(bf16)

    return call(body, [((half, 2 * k), bf16)] * 2, (x, gq, go, att, got), name)


def down_back(gf, slope, near, other, hb, hid_local):
    width, tokens = gf.shape
    steps = hid_local // hb
    nn_, no = len(near), len(other)
    pieces = (*near, *other)

    def body(gf_ref, slope_ref, *refs):
        gu_ref, sum_ref, bd_ref = refs[nn_ + no :]
        g = gf_ref[...]
        ones = ones_rows(tokens)

        @pl.when(pl.program_id(0) == 0)
        def _():
            bd_ref[...] = nt(ones, g)

        for i, w in enumerate((refs[:nn_], refs[nn_ : nn_ + no])):
            v = (tn(rows_of(w), g) * slope_ref[i].astype(f32)).astype(bf16)
            gu_ref[i] = v
            sum_ref[i] = nt(ones, v)

    spec = pl.BlockSpec((2, hb, tokens), lambda s: (0, s, 0))
    return call(
        body, [((2, hid_local, tokens), bf16), ((2, 8, hid_local), f32), ((8, width), f32)], (gf, slope, *pieces), "down_back",
        (steps,), [whole(gf), spec] + weight_specs(pieces, hb, 1 + steps),
        [spec, pl.BlockSpec((2, 8, hb), lambda s: (0, 0, s)), whole_out((8, width))],
    )


def up_back(gu, gf, xh1, r1, vecs, near, other, hb):
    width, tokens = gf.shape
    steps = gu.shape[1] // hb
    nn_, no = len(near), len(other)
    pieces = (*near, *other)

    def body(gu_ref, gf_ref, xh_ref, r1_ref, vec_ref, *refs):
        go_ref, sum_ref, acc_ref = refs[nn_ + no :]
        step = pl.program_id(0)

        @pl.when(step == 0)
        def _():
            acc_ref[...] = gf_ref[...].astype(f32)

        acc_ref[...] += nn(rows_of(refs[:nn_]), gu_ref[0]) + nn(rows_of(refs[nn_ : nn_ + no]), gu_ref[1])

        @pl.when(step == steps - 1)
        def _():
            vec = jnp.transpose(vec_ref[...])
            g = acc_ref[...]
            xh = xh_ref[...].astype(f32)
            ones = ones_rows(tokens)
            sum_ref[0:8] = nt(ones, (g * xh).astype(bf16))
            sum_ref[8:16] = nt(ones, g.astype(bf16))
            a = g * vec[:, 1:2]
            first = jnp.sum(a, axis=0, keepdims=True) * (1.0 / width)
            second = jnp.sum(a * xh, axis=0, keepdims=True) * (1.0 / width)
            go = (r1_ref[0:1] * (a - first - xh * second)).astype(bf16)
            go_ref[...] = go
            sum_ref[16:24] = nt(ones, go)

    return call(
        body, [((width, tokens), bf16), ((24, width), f32)], (gu, gf, xh1, r1, vecs, *pieces), "up_back", (steps,),
        [pl.BlockSpec((2, hb, tokens), lambda s: (0, s, 0))] + [whole(a) for a in (gf, xh1, r1, vecs)] + weight_specs(pieces, hb, 1),
        [whole_out((width, tokens)), whole_out((24, width))], [pltpu.VMEM((width, tokens), f32)],
    )


def attention_mid(go, att, inv, fq, near, other, heads, head_width):
    width, tokens = go.shape
    feats = fq.shape[0] // heads
    hb = heads * head_width // 2
    rows = head_width + PAD
    nn_, no = len(near), len(other)
    pieces = (*near, *other)

    def body(go_ref, att_ref, inv_ref, fq_ref, *refs):
        gn_ref, kv_ref = refs[nn_ + no :]
        g = go_ref[...]
        zeros = jnp.zeros((PAD - 1, tokens), f32)
        for i, w in enumerate((refs[:nn_], refs[nn_ : nn_ + no])):
            ga = tn(rows_of(w), g)
            for hl in range(heads // 2):
                h = i * (heads // 2) + hl
                gh = ga[hl * head_width : (hl + 1) * head_width]
                inverse = inv_ref[h : h + 1]
                a = att_ref[h * head_width : (h + 1) * head_width].astype(f32)
                gd = -jnp.sum(gh * a, axis=0, keepdims=True) * inverse
                both = jnp.concatenate((gh * inverse, gd, zeros), axis=0).astype(bf16)
                gn_ref[h * rows : (h + 1) * rows] = both
                kv_ref[h * rows : (h + 1) * rows] = nt(both, fq_ref[h * feats : (h + 1) * feats]).astype(bf16)

    outs = [((heads * rows, tokens), bf16), ((heads * rows, feats), bf16)]
    args = (go, att, inv, fq, *pieces)
    return call(
        body, outs, args, "attention_mid", (1,), [whole(a) for a in args[:4]] + fixed_specs(pieces, hb, 0),
        [whole_out(s) for s, _ in outs],
    )


def query_back(gn, kv, fq, uq, omegas, heads, head_width):
    n, tokens = uq.shape
    feats = fq.shape[0] // heads
    rows = head_width + PAD
    factor = head_width ** (-0.25)

    def body(gn_ref, kv_ref, fq_ref, uq_ref, om0_ref, om1_ref, gq_ref, sum_ref):
        for h in range(heads):
            om_ref = (om0_ref, om1_ref)[h // (heads // 2)]
            e = tn(kv_ref[h * rows : (h + 1) * rows], gn_ref[h * rows : (h + 1) * rows])
            e = e * fq_ref[h * feats : (h + 1) * feats].astype(f32)
            s = jnp.sum(e, axis=0, keepdims=True)
            u = uq_ref[h * head_width : (h + 1) * head_width].astype(f32)
            gq_ref[h * head_width : (h + 1) * head_width] = (
                factor * (nn(om_ref[h % (heads // 2)], e.astype(bf16)) - s * u)
            ).astype(bf16)
        sum_ref[...] = nt(ones_rows(tokens), gq_ref[...])

    return call(body, [((n, tokens), bf16), ((8, n), f32)], (gn, kv, fq, uq, *omegas), "query_back")


def key_back(gkv0, gkv1, fk, uk, v, omegas, heads, head_width):
    n, tokens = uk.shape
    feats = fk.shape[0] // heads
    rows = head_width + PAD
    factor = head_width ** (-0.25)
    hl_n = heads // 2
    hb = hl_n * head_width

    def body(gkv0_ref, gkv1_ref, fk_ref, uk_ref, v_ref, om0_ref, om1_ref, g_ref, sum_ref):
        ones = jnp.ones((PAD, tokens), bf16)
        for h in range(heads):
            i, hl = divmod(h, hl_n)
            base = i * 2 * hb + hl * head_width
            kv = (gkv0_ref[h * rows : (h + 1) * rows].astype(f32) + gkv1_ref[h * rows : (h + 1) * rows].astype(f32)).astype(bf16)
            f = fk_ref[h * feats : (h + 1) * feats]
            at = h * head_width
            value = jnp.concatenate((v_ref[at : at + head_width], ones), axis=0)
            e = tn(kv, value) * f.astype(f32)
            s = jnp.sum(e, axis=0, keepdims=True)
            u = uk_ref[at : at + head_width].astype(f32)
            g_ref[base : base + head_width] = (
                factor * (nn((om0_ref, om1_ref)[i][hl], e.astype(bf16)) - s * u)
            ).astype(bf16)
            g_ref[base + hb : base + hb + head_width] = nn(kv[:head_width], f).astype(bf16)
        sum_ref[...] = nt(ones_rows(tokens), g_ref[...])

    return call(body, [((2 * n, tokens), bf16), ((8, 2 * n), f32)], (gkv0, gkv1, fk, uk, v, *omegas), "key_back")


def last_parts(x, g, sums, got, name):
    sum1, sum2, bd, bu, sum_q, sum_kv = sums
    n, tokens = x.shape
    q = n // 4
    k = g.shape[1]
    hb = k // 2
    hid_local = bu.shape[2]
    ups = hid_local // hb
    rows = q + EXTRA
    which = 0 if got is not None else 1

    def body(x_ref, g_ref, s1_ref, s2_ref, bd_ref, bu_ref, sq_ref, skv_ref, *refs):
        if got is None:
            o_ref, row_s, col_s = refs
        else:
            got_ref, keep_ref, send_ref, row_s, col_s = refs
        for m, v in enumerate((s1_ref[16:17], s1_ref[0:1], s1_ref[8:9], bd_ref[0:1], s2_ref[0:1], s2_ref[8:9], s2_ref[16:17])):
            row_s[m : m + 1] = v
        row_s[7:8] = jnp.zeros((1, n), f32)
        col_s[...] = jnp.zeros(col_s.shape, f32)
        for i in range(2):
            col_s[i, 0:1] = sq_ref[0:1, i * hb : (i + 1) * hb]
            col_s[i, 1:2] = skv_ref[0:1, i * k : i * k + hb]
            col_s[i, 2:3] = skv_ref[0:1, i * k + hb : (i + 1) * k]
            for u in range(ups):
                col_s[i, 3 + u : 4 + u] = bu_ref[i, 0:1, u * hb : (u + 1) * hb]
        for i in range(2):
            for jx in range(2):
                p = 2 * which + jx
                main = nt(x_ref[p * q : (p + 1) * q], g_ref[i])
                small = row_s[:, p * q : (p + 1) * q]
                small = jnp.concatenate((small, jnp.zeros((8, hb - q), f32), col_s[i]), axis=1)
                small = jnp.concatenate((small, jnp.zeros((EXTRA - 8, k), f32)), axis=0)
                if got is None:
                    o_ref[i, jx, :q] = main.astype(bf16)
                    o_ref[i, jx, q:] = small.astype(bf16)
                else:
                    o = send_ref if jx else keep_ref
                    o[i * rows : i * rows + q] = (main + got_ref[i, jx, :q].astype(f32)).astype(bf16)
                    o[i * rows + q : (i + 1) * rows] = (small + got_ref[i, jx, q:].astype(f32)).astype(bf16)

    outs = [((2, 2, rows, k), bf16)] if got is None else [((2 * rows, k), bf16)] * 2
    args = (x, g, *sums) if got is None else (x, g, *sums, got)
    return call(body, outs, args, name, scratch=[pltpu.VMEM((8, n), f32), pltpu.VMEM((2, 8, hb), f32)])


def input_grad(gq, g, go, near, other):
    width, tokens = go.shape
    hb = gq.shape[1]
    k = width // 4
    nn_, no = len(near), len(other)

    def body(gq_ref, g_ref, go_ref, *refs):
        total = go_ref[...].astype(f32)
        for i, w in enumerate((refs[:nn_], refs[nn_ : nn_ + no])):
            w = jnp.concatenate([r[:k] for r in w], axis=0)
            total = total + nn(w[:, :hb], gq_ref[i]) + nn(w[:, hb:], g_ref[i])
        for p, o_ref in enumerate(refs[nn_ + no :]):
            o_ref[...] = total[p * k : (p + 1) * k].astype(bf16)

    return call(body, [((k, tokens), bf16)] * 4, (gq, g, go, *near, *other), "input_grad")


def swap(value, axis, mask):
    size = lax.axis_size(axis)
    return lax.ppermute(value, axis, [(s, s ^ mask) for s in range(size)])


def after(value, *others):
    return lax.optimization_barrier((value, *others))[0]


class Fold:
    def __init__(self, value):
        self.value = value
        self.four = lax.axis_size("dp") == 4
        if not self.four:
            self.value = lax.psum(value, "dp")
            return
        self.odd = lax.axis_index("dp") % 2 == 1
        n = value.shape[1] // 2
        low, high = value[:, :n], value[:, n:]
        self.value = jnp.where(self.odd, high, low)
        self.got = swap(jnp.where(self.odd, low, high), "dp", 1)

    def step(self, order, mask):
        if not self.four:
            return order
        self.value = after(self.value, order) + self.got
        self.got = swap(self.value, "dp", mask)
        return self.value

    def middle(self, order):
        return self.step(order, 2)

    def back(self, order):
        return self.step(order, 1)

    def result(self):
        if not self.four:
            return self.value.astype(f32)
        a, b = self.value.astype(f32), self.got.astype(f32)
        return jnp.concatenate((jnp.where(self.odd, b, a), jnp.where(self.odd, a, b)), axis=1)


def total(keep, got, last):
    n = keep.shape[0] // 2
    return keep[:n] + got[:n] + last


def far_half(keep, got):
    n = keep.shape[0] // 2
    return keep[n:] + got[n:]


def exchange(blocks):
    return [blocks[0]] + [swap(blocks[j], "row", j) for j in (1, 2, 3)]


def reduce_small(value, axis):
    step = 1
    while step < lax.axis_size(axis):
        value = value + swap(value, axis, step)
        step *= 2
    return value


def shards(
    inputs, teacher, lengths, omega,
    w_query, b_query, w_key, b_key, w_value, b_value, w_out, b_out,
    norm1_gain, norm1_bias, w_up, up_bias, w_down, b_down, norm2_gain, norm2_bias,
):
    row_parts = lax.axis_size("row")
    feat_local, seq_length = inputs.shape
    width = feat_local * row_parts
    head_local, head_width, feats = omega.shape
    heads = head_local * lax.axis_size("col")
    tokens = seq_length // row_parts
    hb = head_local * head_width
    hid_local = w_up.shape[1]
    row = lax.axis_index("row")
    col = lax.axis_index("col")
    row_ref = row.astype(jnp.int32).reshape(1)

    omegas = (omega, swap(omega, "col", 1))
    vecs = (b_out, norm1_gain, norm1_bias, b_down, norm2_gain, norm2_bias)
    ins = split_positions(inputs, row_ref, row_parts)
    ins_got = exchange(ins)
    xs = [ins_got[j] for j in (0, 2, 1, 3)]
    own_a = narrow_small((after(w_query, *ins), w_key, w_value), vecs, (b_query, b_key, b_value), up_bias, "narrow_a")
    a_y = swap(own_a, "col", 1)
    a_x = swap(own_a, "row", 2)
    a_far = swap(after(a_x, a_y, omegas[1]), "col", 1)
    near_a = (own_a, a_x, swap(own_a, "row", 1), swap(a_x, "row", 1))
    other_a = (a_y, a_far, swap(a_y, "row", 1), swap(a_far, "row", 1))
    count = reduce_small(jnp.sum(lengths).astype(f32).reshape(1, 1) + jnp.zeros((8, 128), f32), "dp")
    own_b = narrow((after(w_out, own_a), w_up, w_down), 3, "narrow_b")
    b_x = swap(after(own_b, a_x, ins_got[2], ins_got[3]), "row", 2)
    b_y = swap(after(own_b, a_far), "col", 1)
    length = lax.dynamic_index_in_dim(lengths, col, 0, False)
    keep = ((row * tokens + jnp.arange(tokens, dtype=jnp.int32)) < length).astype(f32)
    keep = after(jnp.broadcast_to(keep[None, :], (8, tokens)), count)
    scale = (2.0 * LOSS_SCALE) / (count * width)

    x, fq, fk, uq, uk, v, kv, vecs, up_bias_all = attention_in(
        xs, near_a, other_a, omegas, keep, head_local, head_width, hid_local
    )
    kv0 = kv + swap(kv, "row", 1)
    kv1 = swap(kv0, "row", 2)
    theirs = split_positions(after(teacher, kv0), row_ref, row_parts)
    teach = exchange(theirs)
    target = [teach[j] for j in (0, 2, 1, 3)]
    b_x = after(b_x, kv0, theirs[0])
    b_y = after(b_y, kv0, theirs[0])
    b_far_y = swap(b_x[CUT:], "col", 1)
    b_far_x = swap(b_y[:CUT], "row", 2)
    near_b = (own_b, b_x)
    near_b = near_b + tuple(swap(p, "row", 1) for p in near_b)
    other_b = (b_y, b_far_x, after(b_far_y, kv1, b_far_x, teach[2], teach[3]))
    other_b = other_b + tuple(swap(p, "row", 1) for p in other_b)
    kv, att, inv, xh1, r1, x1, hid, slope, gf, sum2, *out = middle(
        kv0, kv1, fq, x, near_b, other_b, vecs, up_bias_all, target, keep, scale, heads, head_width, hid_local
    )
    out = exchange([out[j] for j in (0, 2, 1, 3)])

    theirs = grad_theirs(gf, hid, hb, "down_theirs")
    got1 = swap(theirs, "row", 1)
    gu, bu, bd = down_back(after(gf, theirs), slope, near_b, other_b, hb, hid_local)
    kept0, kept1, send0, send1 = grad_mine(after(gf, gu), hid, got1, hb, "down_mine")
    down = ((kept0, swap(send0, "col", 1)), (kept1, swap(send1, "col", 1)))
    go, sum1 = up_back(after(gu, send0), gf, xh1, r1, vecs, near_b, other_b, hb)
    gn, gkv = attention_mid(go, att, inv, fq, near_b, other_b, heads, head_width)
    gkv0 = gkv + swap(gkv, "row", 1)
    gkv1 = swap(gkv0, "row", 2)
    far = far_half(after(down[0][0], gn, *out), down[0][1])
    r_down0 = swap(far, "row", 2)
    theirs = grad_theirs(after(x1, far), gu, hb, "up_theirs")
    got2 = swap(theirs, "row", 1)
    gq, sum_q = query_back(after(gn, theirs), kv, fq, uq, omegas, heads, head_width)
    down0 = total(after(down[0][0], gq), down[0][1], r_down0)
    z_down0 = Fold(down0)
    kept0, kept1, send0, send1 = grad_mine(after(x1, down0, gkv0), gu, got2, hb, "up_mine")
    up = ((kept0, swap(send0, "col", 1)), (kept1, swap(send1, "col", 1)))
    far = far_half(after(down[1][0], send0), down[1][1])
    r_down1 = swap(far, "row", 2)
    gq = gq.reshape(2, hb, tokens)
    att2 = att.reshape(2, hb, tokens)
    theirs = pair_theirs(after(x, far), gq, go, att2, "pair_theirs")
    got3 = swap(theirs, "row", 1)
    g, sum_kv = key_back(after(gkv0, theirs), gkv1, fk, uk, v, omegas, heads, head_width)
    g = g.reshape(2, 2 * hb, tokens)
    sums = (sum1, sum2, bd, bu, sum_q, sum_kv)
    far = far_half(after(up[0][0], g), up[0][1])
    r_up0 = swap(far, "row", 2)
    down1 = total(after(down[1][0], far), down[1][1], r_down1)
    z_down1 = Fold(down1)
    order = z_down0.middle(down1)
    theirs = last_parts(after(x, order), g, sums, None, "last_theirs")[0]
    got4 = swap(theirs, "row", 1)
    keep3, send3 = pair_mine(after(x, theirs), gq, go, att2, got3, "pair_mine")
    r_y3 = swap(send3, "col", 1)
    up0 = total(after(up[0][0], send3), up[0][1], r_up0)
    z_up0 = Fold(up0)
    keep4, send4 = last_parts(after(x, up0), g, sums, got4, "last_mine")
    r_x4 = swap(send4, "row", 2)
    far = far_half(after(up[1][0], send4), up[1][1])
    r_up1 = swap(far, "row", 2)
    order = z_down1.middle(far)
    order = z_down0.back(order)
    gin = input_grad(gq, g, after(go, order), near_a, other_a)
    far = far_half(after(keep4, gin[0]), r_x4)
    r_y4 = swap(far, "col", 1)
    far = far_half(after(keep3, far), r_y3)
    r_x3 = swap(far, "row", 2)
    up1 = total(after(up[1][0], far), up[1][1], r_up1)
    z_up1 = Fold(up1)
    order = z_up0.middle(up1)
    gin = exchange([after(gin[j], far) for j in (0, 2, 1, 3)])
    order = z_down1.back(order)
    last = total(after(keep4, order), r_x4, r_y4)
    last = jnp.concatenate((last, total(keep3, r_y3, r_x3)), axis=0)
    z_last = Fold(last)
    order = z_up1.middle(last)
    order = z_up0.back(order)
    order = z_last.middle(order)
    order = z_up1.back(order)
    order = z_last.back(order)
    out[0] = after(out[0], order)
    out = join_positions(out, row_ref)
    grad_in = join_positions([after(gin[0], out), *gin[1:]], row_ref)
    grad_down = jnp.concatenate((z_down0.result(), z_down1.result()), axis=1)
    grad_up = jnp.concatenate((z_up0.result(), z_up1.result()), axis=1)
    last = z_last.result()
    grad_pair = last[keep4.shape[0] // 2 :]

    extra = last[feat_local : keep4.shape[0] // 2]
    rows = extra[:7, :feat_local]
    cols = extra[:7, hb:]
    loss = rows[6, 0] / (count[0, 0] * width)
    return (
        out,
        loss,
        grad_in,
        grad_pair[:, :hb],
        cols[0],
        last[:feat_local, :hb],
        cols[1],
        last[:feat_local, hb:],
        cols[2],
        grad_pair[:, hb:],
        rows[0],
        rows[1],
        rows[2],
        grad_up,
        cols[3:].reshape(hid_local),
        grad_down,
        rows[3],
        rows[4],
        rows[5],
    )


def solution(mesh):
    both = P("row", ("dp", "col"))
    in_specs = (
        both, both, P("dp"), P("col", None, None),
        P("row", "col"), P("col"), P("row", "col"), P("col"), P("row", "col"), P("col"),
        P("row", "col"), P("row"), P("row"), P("row"),
        P("row", "col"), P("col"), P("row", "col"), P("row"), P("row"), P("row"),
    )
    out_specs = (
        both, P(), both,
        P("row", "col"), P("col"), P("row", "col"), P("col"), P("row", "col"), P("col"),
        P("row", "col"), P("row"), P("row"), P("row"),
        P("row", "col"), P("col"), P("row", "col"), P("row"), P("row"), P("row"),
    )
    return jax.shard_map(shards, mesh=mesh, in_specs=in_specs, out_specs=out_specs, check_vma=False)
```

```python
import jax
import jax.numpy as jnp
from jax import lax
from jax.experimental import pallas as pl
from jax.experimental.pallas import tpu as pltpu
from jax.sharding import PartitionSpec as P

LOSS_SCALE = 16777216
stabilizer = 2.0
norm_eps = 1e-12
root_half = 0.7071067811865476
inv_root_two_pi = 0.3989422804014327
f32 = jnp.float32
bf16 = jnp.bfloat16
PAD = 8
EXTRA = 16
CUT = 48
ASIDE = 256


def dot(a, b, dims):
    return lax.dot_general(a, b, (dims, ((), ())), preferred_element_type=f32)


def nn(a, b):
    return dot(a, b, ((1,), (0,)))


def nt(a, b):
    return dot(a, b, ((1,), (1,)))


def tn(a, b):
    return dot(a, b, ((0,), (0,)))


def ones_rows(tokens):
    return jnp.ones((8, tokens), bf16)


def call(body, outs, args, name, grid=None, in_specs=None, out_specs=None, scratch=(), limit=40, pinned=False):
    if grid is None:
        grid = (1,)
        in_specs = [single(a.shape) for a in args] if in_specs is None else in_specs
        out_specs = [single(s) for s, _ in outs]
    extra = dict(grid=grid, in_specs=in_specs, out_specs=out_specs)
    if pinned:
        args = [a if p is SMEM else pltpu.with_memory_space_constraint(a, pltpu.HBM) for a, p in zip(args, in_specs)]
    make = pltpu.HBM if pinned else jax.ShapeDtypeStruct
    return pl.pallas_call(
        body,
        out_shape=[make(s, d) for s, d in outs],
        scratch_shapes=list(scratch),
        compiler_params=pltpu.CompilerParams(vmem_limit_bytes=limit * 1024 * 1024),
        cost_estimate=pl.CostEstimate(flops=1000, bytes_accessed=1000, transcendentals=0),
        name=name,
        **extra,
    )(*args)


def single(shape):
    zeros = (0,) * len(shape)
    return pl.BlockSpec(shape, lambda s: zeros, pipeline_mode=pl.Buffered(1))


def whole(a):
    zeros = (0,) * a.ndim
    return pl.BlockSpec(a.shape, lambda s: zeros)


def whole_out(shape):
    zeros = (0,) * len(shape)
    return pl.BlockSpec(shape, lambda s: zeros)


SMEM = pl.BlockSpec(memory_space=pltpu.SMEM)


def split_positions(shard, row, row_parts):
    k, length = shard.shape
    n = length // row_parts

    def body(row_ref, in_ref, *out_refs):
        r = row_ref[0]
        for j, o_ref in enumerate(out_refs):
            at = pl.multiple_of(jnp.bitwise_xor(r, j) * n, n)
            o_ref[...] = in_ref[:, pl.ds(at, n)].astype(bf16)

    rows = k // 3
    return call(
        body, [((k, n), bf16)] * row_parts, (row, shard), "split_positions", (3,),
        [SMEM, pl.BlockSpec((rows, length), lambda s: (s, 0))], [pl.BlockSpec((rows, n), lambda s: (s, 0))] * row_parts, pinned=True,
    )


def join_positions(blocks, row):
    k, n = blocks[0].shape
    parts = len(blocks)

    def body(row_ref, *refs):
        r = row_ref[0]
        o_ref = refs[parts]
        for j in range(parts):
            at = pl.multiple_of(jnp.bitwise_xor(r, j) * n, n)
            o_ref[:, pl.ds(at, n)] = refs[j][...].astype(f32)

    rows = k // 3
    return call(
        body, [((k, n * parts), f32)], (row, *blocks), "join_positions", (3,),
        [SMEM] + [pl.BlockSpec((rows, n), lambda s: (s, 0))] * parts, [pl.BlockSpec((rows, n * parts), lambda s: (s, 0))],
    )[0]


def narrow(parts, steps, name):
    n = parts[0].shape[0]
    widths = [p.shape[1] for p in parts]

    def body(*refs):
        at = 0
        for ref, w in zip(refs, widths):
            refs[-1][:, at : at + w] = ref[...].astype(bf16)
            at += w

    return call(
        body, [((n, sum(widths)), bf16)], parts, name, (steps,),
        [pl.BlockSpec((n // steps, w), lambda s: (s, 0)) for w in widths],
        [pl.BlockSpec((n // steps, sum(widths)), lambda s: (s, 0))],
        pinned=True,
    )[0]


def narrow_small(parts, vecs, biases, up_bias, name):
    n, hb = parts[0].shape
    width = hb * len(parts)
    nv = len(vecs)
    rest = up_bias.shape[0] - width
    small = [v.reshape(1, v.shape[0]) for v in vecs] + [jnp.concatenate((*biases, up_bias)).reshape(-1, hb)]

    def body(*refs):
        p_refs = refs[: len(parts)]
        v_refs = refs[len(parts) : len(parts) + nv]
        b_ref, o_ref, small_ref = refs[len(parts) + nv :]
        small_ref[...] = jnp.zeros(small_ref.shape, f32)
        for m, ref in enumerate(v_refs):
            small_ref[m : m + 1, :n] = ref[...]
        for m, ref in enumerate(p_refs):
            o_ref[:n, m * hb : (m + 1) * hb] = ref[...].astype(bf16)
            small_ref[nv : nv + 1, m * hb : (m + 1) * hb] = b_ref[m : m + 1]
            small_ref[nv + 1 : nv + 2, m * hb : (m + 1) * hb] = b_ref[len(parts) + m : len(parts) + m + 1]
        small_ref[0:1, ASIDE : ASIDE + rest] = b_ref[2 * len(parts) : 2 * len(parts) + 1]
        value = small_ref[...]
        high = value.astype(bf16).astype(f32)
        o_ref[n:] = jnp.concatenate((high, value - high), axis=0).astype(bf16)

    scratch = [pltpu.VMEM((8, width), f32)]
    return call(body, [((n + EXTRA, width), bf16)], (*parts, *small), name, scratch=scratch, pinned=True)[0]


def small_rows(ref, k):
    v = ref[k : k + EXTRA].astype(f32)
    return v[0:8] + v[8:16]


def attention_in(xs, near, other, omegas, keep, head_local, head_width, hid_local):
    k, tokens = xs[0].shape
    feats = omegas[0].shape[2]
    heads = 2 * head_local
    hb = head_local * head_width
    rows = head_width + PAD
    factor = head_width ** (-0.25)
    n_near, n_other = len(near), len(other)

    def body(*refs):
        x_in = refs[:4]
        near_refs = refs[4 : 4 + n_near]
        other_refs = refs[4 + n_near : 4 + n_near + n_other]
        (om0_ref, om1_ref, keep_ref, x_ref, fq_ref, fk_ref, uq_ref, uk_ref, v_ref, kv_ref, vec_ref, up_ref) = refs[
            4 + n_near + n_other :
        ]
        for p in range(4):
            vec_ref[:, p * k : (p + 1) * k] = small_rows(near_refs[p], k)[:, :k]
        up_ref[...] = jnp.zeros(up_ref.shape, f32)
        for p in range(4):
            x_ref[p * k : (p + 1) * k] = x_in[p][...]
        xv = x_ref[...]
        ones = jnp.ones((PAD, tokens), bf16)
        for i, pieces in enumerate((near_refs, other_refs)):
            omega_ref = (om0_ref, om1_ref)[i]
            small = small_rows(pieces[0], k)
            up_ref[i : i + 1, : 3 * hb] = small[7:8]
            up_ref[i : i + 1, 3 * hb :] = small[0:1, ASIDE : ASIDE + hid_local - 3 * hb]
            triple = tn(jnp.concatenate([p[:k] for p in pieces], axis=0), xv) + jnp.transpose(small)[:, 6:7]
            for hl in range(head_local):
                h = i * head_local + hl
                at = h * head_width
                lo = hl * head_width
                value = triple[2 * hb + lo : 2 * hb + lo + head_width].astype(bf16)
                v_ref[at : at + head_width] = value
                for base, u_ref, f_ref, mask in ((0, uq_ref, fq_ref, False), (hb, uk_ref, fk_ref, True)):
                    u = triple[base + lo : base + lo + head_width] * factor
                    ub = u.astype(bf16)
                    u_ref[at : at + head_width] = ub
                    z = tn(omega_ref[hl], ub)
                    feat = jnp.exp(z - (0.5 * jnp.sum(u * u, axis=0, keepdims=True) + stabilizer))
                    if mask:
                        feat = feat * keep_ref[0:1]
                    feat = feat.astype(bf16)
                    f_ref[h * feats : (h + 1) * feats] = feat
                kv_ref[h * rows : (h + 1) * rows] = nt(jnp.concatenate((value, ones), axis=0), feat).astype(bf16)

    n = heads * head_width
    outs = [((4 * k, tokens), bf16)] + [((heads * feats, tokens), bf16)] * 2 + [((n, tokens), bf16)] * 3
    outs += [((heads * rows, feats), bf16), ((8, 4 * k), f32), ((8, hid_local), f32)]
    return call(body, outs, (*xs, *near, *other, *omegas, keep), "attention_in", pinned=True)


def weight_specs(pieces, block, first):
    return [pl.BlockSpec((p.shape[0], block), lambda s, f=first: (0, f + s)) for p in pieces]


def fixed_specs(pieces, block, at):
    return [pl.BlockSpec((p.shape[0], block), lambda s: (0, at)) for p in pieces]


def rows_of(refs):
    return jnp.concatenate([r[...] for r in refs], axis=0)


def middle(kv0, kv1, fq, x, near, other, vecs, up_bias, target, keep, scale, heads, head_width, hid_local):
    width, tokens = x.shape
    feats = kv0.shape[1]
    rows = head_width + PAD
    hb = heads * head_width // 2
    steps = hid_local // hb
    k = width // 4
    nn_, no = len(near), len(other)
    np_ = nn_ + no

    def body(*refs):
        kv0_ref, kv1_ref, fq_ref, x_ref = refs[:4]
        out_w = refs[4 : 4 + np_]
        up_w = refs[4 + np_ : 4 + 2 * np_]
        down_w = refs[4 + 2 * np_ : 4 + 3 * np_]
        (vec_ref, upb_ref, t0, t1, t2, t3, keep_ref, scale_ref,
         kv_ref, att_ref, inv_ref, xh1_ref, r1_ref, x1_ref, hid_ref, slope_ref, gf_ref, sum_ref,
         o0, o1, o2, o3, acc_ref, vec_s) = refs[4 + 3 * np_ :]
        step = pl.program_id(0)

        @pl.when(step == 0)
        def _():
            vec = jnp.transpose(vec_ref[...])
            vec_s[...] = vec
            kv_ref[...] = (kv0_ref[...].astype(f32) + kv1_ref[...].astype(f32)).astype(bf16)
            for h in range(heads):
                both = nn(kv_ref[h * rows : (h + 1) * rows], fq_ref[h * feats : (h + 1) * feats])
                inverse = 1.0 / both[head_width : head_width + 1]
                inv_ref[h : h + 1] = inverse
                att_ref[h * head_width : (h + 1) * head_width] = (both[:head_width] * inverse).astype(bf16)
            w = jnp.concatenate((rows_of(out_w[:nn_]), rows_of(out_w[nn_:])), axis=1)
            h1 = nn(w, att_ref[...]) + x_ref[...].astype(f32) + vec[:, 0:1]
            mean = jnp.sum(h1, axis=0, keepdims=True) * (1.0 / width)
            h1 = h1 - mean
            r1 = lax.rsqrt(jnp.sum(h1 * h1, axis=0, keepdims=True) * (1.0 / width) + norm_eps)
            h1 = h1 * r1
            r1_ref[...] = jnp.broadcast_to(r1, (8, tokens))
            xh1_ref[...] = h1.astype(bf16)
            x1 = h1 * vec[:, 1:2] + vec[:, 2:3]
            x1_ref[...] = x1.astype(bf16)
            acc_ref[...] = x1 + vec[:, 3:4]

        x1b = x1_ref[...]
        bias = jnp.transpose(upb_ref[...])
        total = acc_ref[...]
        for i, (a, b) in enumerate(((0, nn_), (nn_, np_))):
            up = tn(rows_of(up_w[a:b]), x1b) + bias[:, i : i + 1]
            gate = 0.5 * (1.0 + lax.erf(up * root_half))
            slope_ref[i] = (gate + up * inv_root_two_pi * jnp.exp(-0.5 * up * up)).astype(bf16)
            hid = (up * gate).astype(bf16)
            hid_ref[i] = hid
            total = total + nn(rows_of(down_w[a:b]), hid)
        acc_ref[...] = total

        @pl.when(step == steps - 1)
        def _():
            vec = vec_s[...]
            h2 = acc_ref[...]
            mean = jnp.sum(h2, axis=0, keepdims=True) * (1.0 / width)
            h2 = h2 - mean
            r2 = lax.rsqrt(jnp.sum(h2 * h2, axis=0, keepdims=True) * (1.0 / width) + norm_eps)
            h2 = h2 * r2
            out = h2 * vec[:, 4:5] + vec[:, 5:6]
            for p, o_ref in enumerate((o0, o1, o2, o3)):
                o_ref[...] = out[p * k : (p + 1) * k].astype(bf16)
            target = jnp.concatenate((t0[...], t1[...], t2[...], t3[...]), axis=0).astype(f32)
            diff = (out - target) * keep_ref[0:1]
            g = diff * scale_ref[0:1, 0:1]
            ones = ones_rows(tokens)
            sum_ref[0:8] = nt(ones, (g * h2).astype(bf16))
            sum_ref[8:16] = nt(ones, g.astype(bf16))
            sum_ref[16:24] = jnp.full((8, width), jnp.sum(diff * diff), f32)
            a = g * vec[:, 4:5]
            first = jnp.sum(a, axis=0, keepdims=True) * (1.0 / width)
            second = jnp.sum(a * h2, axis=0, keepdims=True) * (1.0 / width)
            gf_ref[...] = (r2 * (a - first - h2 * second)).astype(bf16)

    outs = [
        ((heads * rows, feats), bf16), ((width, tokens), bf16), ((16, tokens), f32), ((width, tokens), bf16),
        ((8, tokens), f32), ((width, tokens), bf16), ((2, hid_local, tokens), bf16), ((2, hid_local, tokens), bf16),
        ((width, tokens), bf16), ((24, width), f32),
    ] + [((k, tokens), bf16)] * 4
    pieces = (*near, *other)
    args = (kv0, kv1, fq, x, *pieces, *pieces, *pieces, vecs, up_bias, *target, keep, scale)
    in_specs = [whole(a) for a in (kv0, kv1, fq, x)]
    in_specs += fixed_specs(pieces, hb, 0) + weight_specs(pieces, hb, 1) + weight_specs(pieces, hb, 1 + steps)
    in_specs += [whole(vecs), pl.BlockSpec((8, hb), lambda s: (0, s))] + [whole(t) for t in target] + [whole(keep), whole(scale)]
    out_specs = [whole_out(s) for s, _ in outs]
    out_specs[6] = out_specs[7] = pl.BlockSpec((2, hb, tokens), lambda s: (0, s, 0))
    scratch = [pltpu.VMEM((width, tokens), f32), pltpu.VMEM((width, 8), f32)]
    return call(body, outs, args, "middle", (steps,), in_specs, out_specs, scratch, limit=56, pinned=True)


def grad_theirs(left, right, block, name):
    n, tokens = left.shape
    k = right.shape[1]
    half = n // 2

    def body(l_ref, r_ref, o_ref):
        for i in range(2):
            o_ref[i] = nt(l_ref[...], r_ref[i]).astype(bf16)

    return call(
        body, [((2, half, k), bf16)], (left, right), name, (k // block,),
        [pl.BlockSpec((half, tokens), lambda s: (1, 0)), pl.BlockSpec((2, block, tokens), lambda s: (0, s, 0))],
        [pl.BlockSpec((2, half, block), lambda s: (0, 0, s))],
    )[0]


def grad_mine(left, right, got, block, name):
    n, tokens = left.shape
    k = right.shape[1]
    half = n // 2
    share = k // block // 2

    def body(l_ref, r_ref, got_ref, keep0, keep1, send0, send1):
        step = pl.program_id(0)

        sums = [(nt(l_ref[...], r_ref[i]) + got_ref[i].astype(f32)).astype(bf16) for i in range(2)]

        def store(*refs):
            for ref, value in zip(refs, sums):
                ref[...] = value

        pl.when(step < share)(lambda: store(keep0, send0))
        pl.when(step >= share)(lambda: store(keep1, send1))

    first = pl.BlockSpec((half, block), lambda s: (0, jnp.minimum(s, share - 1)))
    second = pl.BlockSpec((half, block), lambda s: (0, jnp.maximum(s - share, 0)))
    return call(
        body, [((half, k // 2), bf16)] * 4, (left, right, got), name, (2 * share,),
        [
            pl.BlockSpec((half, tokens), lambda s: (0, 0)),
            pl.BlockSpec((2, block, tokens), lambda s: (0, s, 0)),
            pl.BlockSpec((2, half, block), lambda s: (0, 0, s)),
        ],
        [first, second, first, second],
    )


def pair_theirs(x, gq, go, att, name):
    n, tokens = x.shape
    half = n // 2
    k = gq.shape[1]

    def body(x_ref, gq_ref, go_ref, att_ref, o_ref):
        for i in range(2):
            o_ref[i, :, :k] = nt(x_ref[half:], gq_ref[i]).astype(bf16)
            o_ref[i, :, k:] = nt(go_ref[half:], att_ref[i]).astype(bf16)

    return call(body, [((2, half, 2 * k), bf16)], (x, gq, go, att), name)[0]


def pair_mine(x, gq, go, att, got, name):
    n, tokens = x.shape
    half = n // 2
    k = gq.shape[1]

    def body(x_ref, gq_ref, go_ref, att_ref, got_ref, keep_ref, send_ref):
        for i, o_ref in enumerate((keep_ref, send_ref)):
            o_ref[:, :k] = (nt(x_ref[:half], gq_ref[i]) + got_ref[i, :, :k].astype(f32)).astype(bf16)
            o_ref[:, k:] = (nt(go_ref[:half], att_ref[i]) + got_ref[i, :, k:].astype(f32)).astype(bf16)

    return call(body, [((half, 2 * k), bf16)] * 2, (x, gq, go, att, got), name)


def down_back(gf, slope, near, other, hb, hid_local):
    width, tokens = gf.shape
    steps = hid_local // hb
    nn_, no = len(near), len(other)
    pieces = (*near, *other)

    def body(gf_ref, slope_ref, *refs):
        gu_ref, sum_ref, bd_ref = refs[nn_ + no :]
        g = gf_ref[...]
        ones = ones_rows(tokens)

        @pl.when(pl.program_id(0) == 0)
        def _():
            bd_ref[...] = nt(ones, g)

        for i, w in enumerate((refs[:nn_], refs[nn_ : nn_ + no])):
            v = (tn(rows_of(w), g) * slope_ref[i].astype(f32)).astype(bf16)
            gu_ref[i] = v
            sum_ref[i] = nt(ones, v)

    spec = pl.BlockSpec((2, hb, tokens), lambda s: (0, s, 0))
    return call(
        body, [((2, hid_local, tokens), bf16), ((2, 8, hid_local), f32), ((8, width), f32)], (gf, slope, *pieces), "down_back",
        (steps,), [whole(gf), spec] + weight_specs(pieces, hb, 1 + steps),
        [spec, pl.BlockSpec((2, 8, hb), lambda s: (0, 0, s)), whole_out((8, width))],
    )


def up_back(gu, gf, xh1, r1, vecs, near, other, hb):
    width, tokens = gf.shape
    steps = gu.shape[1] // hb
    nn_, no = len(near), len(other)
    pieces = (*near, *other)

    def body(gu_ref, gf_ref, xh_ref, r1_ref, vec_ref, *refs):
        go_ref, sum_ref, acc_ref = refs[nn_ + no :]
        step = pl.program_id(0)

        @pl.when(step == 0)
        def _():
            acc_ref[...] = gf_ref[...].astype(f32)

        acc_ref[...] += nn(rows_of(refs[:nn_]), gu_ref[0]) + nn(rows_of(refs[nn_ : nn_ + no]), gu_ref[1])

        @pl.when(step == steps - 1)
        def _():
            vec = jnp.transpose(vec_ref[...])
            g = acc_ref[...]
            xh = xh_ref[...].astype(f32)
            ones = ones_rows(tokens)
            sum_ref[0:8] = nt(ones, (g * xh).astype(bf16))
            sum_ref[8:16] = nt(ones, g.astype(bf16))
            a = g * vec[:, 1:2]
            first = jnp.sum(a, axis=0, keepdims=True) * (1.0 / width)
            second = jnp.sum(a * xh, axis=0, keepdims=True) * (1.0 / width)
            go = (r1_ref[0:1] * (a - first - xh * second)).astype(bf16)
            go_ref[...] = go
            sum_ref[16:24] = nt(ones, go)

    return call(
        body, [((width, tokens), bf16), ((24, width), f32)], (gu, gf, xh1, r1, vecs, *pieces), "up_back", (steps,),
        [pl.BlockSpec((2, hb, tokens), lambda s: (0, s, 0))] + [whole(a) for a in (gf, xh1, r1, vecs)] + weight_specs(pieces, hb, 1),
        [whole_out((width, tokens)), whole_out((24, width))], [pltpu.VMEM((width, tokens), f32)],
    )


def attention_mid(go, att, inv, fq, near, other, heads, head_width):
    width, tokens = go.shape
    feats = fq.shape[0] // heads
    hb = heads * head_width // 2
    rows = head_width + PAD
    nn_, no = len(near), len(other)
    pieces = (*near, *other)

    def body(go_ref, att_ref, inv_ref, fq_ref, *refs):
        gn_ref, kv_ref = refs[nn_ + no :]
        g = go_ref[...]
        zeros = jnp.zeros((PAD - 1, tokens), f32)
        for i, w in enumerate((refs[:nn_], refs[nn_ : nn_ + no])):
            ga = tn(rows_of(w), g)
            for hl in range(heads // 2):
                h = i * (heads // 2) + hl
                gh = ga[hl * head_width : (hl + 1) * head_width]
                inverse = inv_ref[h : h + 1]
                a = att_ref[h * head_width : (h + 1) * head_width].astype(f32)
                gd = -jnp.sum(gh * a, axis=0, keepdims=True) * inverse
                both = jnp.concatenate((gh * inverse, gd, zeros), axis=0).astype(bf16)
                gn_ref[h * rows : (h + 1) * rows] = both
                kv_ref[h * rows : (h + 1) * rows] = nt(both, fq_ref[h * feats : (h + 1) * feats]).astype(bf16)

    outs = [((heads * rows, tokens), bf16), ((heads * rows, feats), bf16)]
    args = (go, att, inv, fq, *pieces)
    return call(
        body, outs, args, "attention_mid", (1,), [whole(a) for a in args[:4]] + fixed_specs(pieces, hb, 0),
        [whole_out(s) for s, _ in outs],
    )


def query_back(gn, kv, fq, uq, omegas, heads, head_width):
    n, tokens = uq.shape
    feats = fq.shape[0] // heads
    rows = head_width + PAD
    factor = head_width ** (-0.25)

    def body(gn_ref, kv_ref, fq_ref, uq_ref, om0_ref, om1_ref, gq_ref, sum_ref):
        for h in range(heads):
            om_ref = (om0_ref, om1_ref)[h // (heads // 2)]
            e = tn(kv_ref[h * rows : (h + 1) * rows], gn_ref[h * rows : (h + 1) * rows])
            e = e * fq_ref[h * feats : (h + 1) * feats].astype(f32)
            s = jnp.sum(e, axis=0, keepdims=True)
            u = uq_ref[h * head_width : (h + 1) * head_width].astype(f32)
            gq_ref[h * head_width : (h + 1) * head_width] = (
                factor * (nn(om_ref[h % (heads // 2)], e.astype(bf16)) - s * u)
            ).astype(bf16)
        sum_ref[...] = nt(ones_rows(tokens), gq_ref[...])

    return call(body, [((n, tokens), bf16), ((8, n), f32)], (gn, kv, fq, uq, *omegas), "query_back")


def key_back(gkv0, gkv1, fk, uk, v, omegas, heads, head_width):
    n, tokens = uk.shape
    feats = fk.shape[0] // heads
    rows = head_width + PAD
    factor = head_width ** (-0.25)
    hl_n = heads // 2
    hb = hl_n * head_width

    def body(gkv0_ref, gkv1_ref, fk_ref, uk_ref, v_ref, om0_ref, om1_ref, g_ref, sum_ref):
        ones = jnp.ones((PAD, tokens), bf16)
        for h in range(heads):
            i, hl = divmod(h, hl_n)
            base = i * 2 * hb + hl * head_width
            kv = (gkv0_ref[h * rows : (h + 1) * rows].astype(f32) + gkv1_ref[h * rows : (h + 1) * rows].astype(f32)).astype(bf16)
            f = fk_ref[h * feats : (h + 1) * feats]
            at = h * head_width
            value = jnp.concatenate((v_ref[at : at + head_width], ones), axis=0)
            e = tn(kv, value) * f.astype(f32)
            s = jnp.sum(e, axis=0, keepdims=True)
            u = uk_ref[at : at + head_width].astype(f32)
            g_ref[base : base + head_width] = (
                factor * (nn((om0_ref, om1_ref)[i][hl], e.astype(bf16)) - s * u)
            ).astype(bf16)
            g_ref[base + hb : base + hb + head_width] = nn(kv[:head_width], f).astype(bf16)
        sum_ref[...] = nt(ones_rows(tokens), g_ref[...])

    return call(body, [((2 * n, tokens), bf16), ((8, 2 * n), f32)], (gkv0, gkv1, fk, uk, v, *omegas), "key_back")


def last_parts(x, g, sums, got, name):
    sum1, sum2, bd, bu, sum_q, sum_kv = sums
    n, tokens = x.shape
    q = n // 4
    k = g.shape[1]
    hb = k // 2
    hid_local = bu.shape[2]
    ups = hid_local // hb
    rows = q + EXTRA
    which = 0 if got is not None else 1

    def body(x_ref, g_ref, s1_ref, s2_ref, bd_ref, bu_ref, sq_ref, skv_ref, *refs):
        if got is None:
            o_ref, row_s, col_s = refs
        else:
            got_ref, keep_ref, send_ref, row_s, col_s = refs
        for m, v in enumerate((s1_ref[16:17], s1_ref[0:1], s1_ref[8:9], bd_ref[0:1], s2_ref[0:1], s2_ref[8:9], s2_ref[16:17])):
            row_s[m : m + 1] = v
        row_s[7:8] = jnp.zeros((1, n), f32)
        col_s[...] = jnp.zeros(col_s.shape, f32)
        for i in range(2):
            col_s[i, 0:1] = sq_ref[0:1, i * hb : (i + 1) * hb]
            col_s[i, 1:2] = skv_ref[0:1, i * k : i * k + hb]
            col_s[i, 2:3] = skv_ref[0:1, i * k + hb : (i + 1) * k]
            for u in range(ups):
                col_s[i, 3 + u : 4 + u] = bu_ref[i, 0:1, u * hb : (u + 1) * hb]
        for i in range(2):
            for jx in range(2):
                p = 2 * which + jx
                main = nt(x_ref[p * q : (p + 1) * q], g_ref[i])
                small = row_s[:, p * q : (p + 1) * q]
                small = jnp.concatenate((small, jnp.zeros((8, hb - q), f32), col_s[i]), axis=1)
                small = jnp.concatenate((small, jnp.zeros((EXTRA - 8, k), f32)), axis=0)
                if got is None:
                    o_ref[i, jx, :q] = main.astype(bf16)
                    o_ref[i, jx, q:] = small.astype(bf16)
                else:
                    o = send_ref if jx else keep_ref
                    o[i * rows : i * rows + q] = (main + got_ref[i, jx, :q].astype(f32)).astype(bf16)
                    o[i * rows + q : (i + 1) * rows] = (small + got_ref[i, jx, q:].astype(f32)).astype(bf16)

    outs = [((2, 2, rows, k), bf16)] if got is None else [((2 * rows, k), bf16)] * 2
    args = (x, g, *sums) if got is None else (x, g, *sums, got)
    return call(body, outs, args, name, scratch=[pltpu.VMEM((8, n), f32), pltpu.VMEM((2, 8, hb), f32)])


def input_grad(gq, g, go, near, other):
    width, tokens = go.shape
    hb = gq.shape[1]
    k = width // 4
    nn_, no = len(near), len(other)

    def body(gq_ref, g_ref, go_ref, *refs):
        total = go_ref[...].astype(f32)
        for i, w in enumerate((refs[:nn_], refs[nn_ : nn_ + no])):
            w = jnp.concatenate([r[:k] for r in w], axis=0)
            total = total + nn(w[:, :hb], gq_ref[i]) + nn(w[:, hb:], g_ref[i])
        for p, o_ref in enumerate(refs[nn_ + no :]):
            o_ref[...] = total[p * k : (p + 1) * k].astype(bf16)

    return call(body, [((k, tokens), bf16)] * 4, (gq, g, go, *near, *other), "input_grad")


def swap(value, axis, mask):
    size = lax.axis_size(axis)
    return lax.ppermute(value, axis, [(s, s ^ mask) for s in range(size)])


def after(value, *others):
    return lax.optimization_barrier((value, *others))[0]


class Fold:
    def __init__(self, value):
        self.value = value
        self.four = lax.axis_size("dp") == 4
        if not self.four:
            self.value = lax.psum(value, "dp")
            return
        self.odd = lax.axis_index("dp") % 2 == 1
        n = value.shape[1] // 2
        low, high = value[:, :n], value[:, n:]
        self.value = jnp.where(self.odd, high, low)
        self.got = swap(jnp.where(self.odd, low, high), "dp", 1)

    def step(self, order, mask):
        if not self.four:
            return order
        self.value = after(self.value, order) + self.got
        self.got = swap(self.value, "dp", mask)
        return self.value

    def middle(self, order):
        return self.step(order, 2)

    def back(self, order):
        return self.step(order, 1)

    def result(self):
        if not self.four:
            return self.value.astype(f32)
        a, b = self.value.astype(f32), self.got.astype(f32)
        return jnp.concatenate((jnp.where(self.odd, b, a), jnp.where(self.odd, a, b)), axis=1)


def total(keep, got, last):
    n = keep.shape[0] // 2
    return keep[:n] + got[:n] + last


def far_half(keep, got):
    n = keep.shape[0] // 2
    return keep[n:] + got[n:]


def exchange(blocks):
    return [blocks[0]] + [swap(blocks[j], "row", j) for j in (1, 2, 3)]


def reduce_small(value, axis):
    step = 1
    while step < lax.axis_size(axis):
        value = value + swap(value, axis, step)
        step *= 2
    return value


def shards(
    inputs, teacher, lengths, omega,
    w_query, b_query, w_key, b_key, w_value, b_value, w_out, b_out,
    norm1_gain, norm1_bias, w_up, up_bias, w_down, b_down, norm2_gain, norm2_bias,
):
    row_parts = lax.axis_size("row")
    feat_local, seq_length = inputs.shape
    width = feat_local * row_parts
    head_local, head_width, feats = omega.shape
    heads = head_local * lax.axis_size("col")
    tokens = seq_length // row_parts
    hb = head_local * head_width
    hid_local = w_up.shape[1]
    row = lax.axis_index("row")
    col = lax.axis_index("col")
    row_ref = row.astype(jnp.int32).reshape(1)

    omegas = (omega, swap(omega, "col", 1))
    vecs = (b_out, norm1_gain, norm1_bias, b_down, norm2_gain, norm2_bias)
    ins = split_positions(inputs, row_ref, row_parts)
    ins_got = exchange(ins)
    xs = [ins_got[j] for j in (0, 2, 1, 3)]
    own_a = narrow_small((after(w_query, *ins), w_key, w_value), vecs, (b_query, b_key, b_value), up_bias, "narrow_a")
    a_y = swap(own_a, "col", 1)
    a_x = swap(own_a, "row", 2)
    a_far = swap(after(a_x, a_y, omegas[1]), "col", 1)
    near_a = (own_a, a_x, swap(own_a, "row", 1), swap(a_x, "row", 1))
    other_a = (a_y, a_far, swap(a_y, "row", 1), swap(a_far, "row", 1))
    count = reduce_small(jnp.sum(lengths).astype(f32).reshape(1, 1) + jnp.zeros((8, 128), f32), "dp")
    own_b = narrow((after(w_out, own_a, count), w_up, w_down), 3, "narrow_b")
    b_x = swap(after(own_b, a_x, ins_got[2], ins_got[3]), "row", 2)
    b_y = swap(after(own_b, a_far), "col", 1)
    length = lax.dynamic_index_in_dim(lengths, col, 0, False)
    keep = ((row * tokens + jnp.arange(tokens, dtype=jnp.int32)) < length).astype(f32)
    keep = jnp.broadcast_to(keep[None, :], (8, tokens))
    scale = (2.0 * LOSS_SCALE) / (count * width)

    x, fq, fk, uq, uk, v, kv, vecs, up_bias_all = attention_in(
        xs, near_a, other_a, omegas, keep, head_local, head_width, hid_local
    )
    kv0 = kv + swap(kv, "row", 1)
    kv1 = swap(kv0, "row", 2)
    theirs = split_positions(after(teacher, kv0), row_ref, row_parts)
    teach = exchange(theirs)
    target = [teach[j] for j in (0, 2, 1, 3)]
    b_x = after(b_x, kv0, theirs[0])
    b_y = after(b_y, kv0, theirs[0])
    b_far_y = swap(b_x[CUT:], "col", 1)
    b_far_x = swap(b_y[:CUT], "row", 2)
    near_b = (own_b, b_x)
    near_b = near_b + tuple(swap(p, "row", 1) for p in near_b)
    other_b = (b_y, b_far_x, after(b_far_y, kv1, b_far_x, teach[2], teach[3]))
    other_b = other_b + tuple(swap(p, "row", 1) for p in other_b)
    kv, att, inv, xh1, r1, x1, hid, slope, gf, sum2, *out = middle(
        kv0, kv1, fq, x, near_b, other_b, vecs, up_bias_all, target, keep, scale, heads, head_width, hid_local
    )
    out = exchange([out[j] for j in (0, 2, 1, 3)])

    theirs = grad_theirs(gf, hid, hb, "down_theirs")
    got1 = swap(theirs, "row", 1)
    gu, bu, bd = down_back(after(gf, theirs), slope, near_b, other_b, hb, hid_local)
    kept0, kept1, send0, send1 = grad_mine(after(gf, gu), hid, got1, hb, "down_mine")
    down = ((kept0, swap(send0, "col", 1)), (kept1, swap(send1, "col", 1)))
    go, sum1 = up_back(after(gu, send0), gf, xh1, r1, vecs, near_b, other_b, hb)
    gn, gkv = attention_mid(go, att, inv, fq, near_b, other_b, heads, head_width)
    gkv0 = gkv + swap(gkv, "row", 1)
    gkv1 = swap(gkv0, "row", 2)
    far = far_half(after(down[0][0], gn, *out), down[0][1])
    r_down0 = swap(far, "row", 2)
    theirs = grad_theirs(after(x1, far), gu, hb, "up_theirs")
    got2 = swap(theirs, "row", 1)
    gq, sum_q = query_back(after(gn, theirs), kv, fq, uq, omegas, heads, head_width)
    down0 = total(after(down[0][0], gq), down[0][1], r_down0)
    z_down0 = Fold(down0)
    kept0, kept1, send0, send1 = grad_mine(after(x1, down0, gkv0), gu, got2, hb, "up_mine")
    up = ((kept0, swap(send0, "col", 1)), (kept1, swap(send1, "col", 1)))
    far = far_half(after(down[1][0], send0), down[1][1])
    r_down1 = swap(far, "row", 2)
    gq = gq.reshape(2, hb, tokens)
    att2 = att.reshape(2, hb, tokens)
    theirs = pair_theirs(after(x, far), gq, go, att2, "pair_theirs")
    got3 = swap(theirs, "row", 1)
    g, sum_kv = key_back(after(gkv0, theirs), gkv1, fk, uk, v, omegas, heads, head_width)
    g = g.reshape(2, 2 * hb, tokens)
    sums = (sum1, sum2, bd, bu, sum_q, sum_kv)
    far = far_half(after(up[0][0], g), up[0][1])
    r_up0 = swap(far, "row", 2)
    down1 = total(after(down[1][0], far), down[1][1], r_down1)
    z_down1 = Fold(down1)
    order = z_down0.middle(down1)
    theirs = last_parts(after(x, order), g, sums, None, "last_theirs")[0]
    got4 = swap(theirs, "row", 1)
    keep3, send3 = pair_mine(after(x, theirs), gq, go, att2, got3, "pair_mine")
    r_y3 = swap(send3, "col", 1)
    up0 = total(after(up[0][0], send3), up[0][1], r_up0)
    z_up0 = Fold(up0)
    keep4, send4 = last_parts(after(x, up0), g, sums, got4, "last_mine")
    r_x4 = swap(send4, "row", 2)
    far = far_half(after(up[1][0], send4), up[1][1])
    r_up1 = swap(far, "row", 2)
    order = z_down1.middle(far)
    order = z_down0.back(order)
    gin = input_grad(gq, g, after(go, order), near_a, other_a)
    far = far_half(after(keep4, gin[0]), r_x4)
    r_y4 = swap(far, "col", 1)
    far = far_half(after(keep3, far), r_y3)
    r_x3 = swap(far, "row", 2)
    up1 = total(after(up[1][0], far), up[1][1], r_up1)
    z_up1 = Fold(up1)
    order = z_up0.middle(up1)
    gin = exchange([after(gin[j], far) for j in (0, 2, 1, 3)])
    order = z_down1.back(order)
    last = total(after(keep4, order), r_x4, r_y4)
    last = jnp.concatenate((last, total(keep3, r_y3, r_x3)), axis=0)
    z_last = Fold(last)
    order = z_up1.middle(last)
    order = z_up0.back(order)
    order = z_last.middle(order)
    order = z_up1.back(order)
    order = z_last.back(order)
    out[0] = after(out[0], order)
    out = join_positions(out, row_ref)
    grad_in = join_positions([after(gin[0], out), *gin[1:]], row_ref)
    grad_down = jnp.concatenate((z_down0.result(), z_down1.result()), axis=1)
    grad_up = jnp.concatenate((z_up0.result(), z_up1.result()), axis=1)
    last = z_last.result()
    grad_pair = last[keep4.shape[0] // 2 :]

    extra = last[feat_local : keep4.shape[0] // 2]
    rows = extra[:7, :feat_local]
    cols = extra[:7, hb:]
    loss = rows[6, 0] / (count[0, 0] * width)
    return (
        out,
        loss,
        grad_in,
        grad_pair[:, :hb],
        cols[0],
        last[:feat_local, :hb],
        cols[1],
        last[:feat_local, hb:],
        cols[2],
        grad_pair[:, hb:],
        rows[0],
        rows[1],
        rows[2],
        grad_up,
        cols[3:].reshape(hid_local),
        grad_down,
        rows[3],
        rows[4],
        rows[5],
    )


def solution(mesh):
    both = P("row", ("dp", "col"))
    in_specs = (
        both, both, P("dp"), P("col", None, None),
        P("row", "col"), P("col"), P("row", "col"), P("col"), P("row", "col"), P("col"),
        P("row", "col"), P("row"), P("row"), P("row"),
        P("row", "col"), P("col"), P("row", "col"), P("row"), P("row"), P("row"),
    )
    out_specs = (
        both, P(), both,
        P("row", "col"), P("col"), P("row", "col"), P("col"), P("row", "col"), P("col"),
        P("row", "col"), P("row"), P("row"), P("row"),
        P("row", "col"), P("col"), P("row", "col"), P("row"), P("row"), P("row"),
    )
    return jax.shard_map(shards, mesh=mesh, in_specs=in_specs, out_specs=out_specs, check_vma=False)
```
